32 devices in a mesh: dp: 8 (over y, x, core), tensor: 4 (over z).
Axes of the slice: x: 2, y: 2, z: 4, core: 2. Of those that a mesh axis runs over, the one named last changes fastest.
Arguments:
- inputs: bfloat16 [2, 8, 512, 1024], P(None, 'dp', 'tensor'), may hold values from -6 to 6
- lengths: int32 [2, 8], P(None, 'dp'), may hold values from 1 to 512, 2560 in all within a row
- cotangent: bfloat16 [2, 8, 512, 1024], P(None, 'dp', 'tensor'), may hold values from -6 to 6
- first_expand: bfloat16 [1024, 4096], P('dp', 'tensor'), may hold values from -0.1875 to 0.1875
- first_reduce: bfloat16 [1024, 4096], P('dp', 'tensor'), may hold values from -0.09375 to 0.09375
- heads_project: bfloat16 [1024, 3, 1024], P('dp', None, 'tensor'), may hold values from -0.1875 to 0.1875
- heads_merge: bfloat16 [1024, 1024], P('dp', 'tensor'), may hold values from -0.75 to 0.75
- filter_expand: bfloat16 [1024, 2, 1024], P('dp', None, 'tensor'), may hold values from -0.1875 to 0.1875
- filter_reduce: bfloat16 [1024, 1024], P('dp', 'tensor'), may hold values from -0.1875 to 0.1875
- second_expand: bfloat16 [1024, 4096], P('dp', 'tensor'), may hold values from -0.1875 to 0.1875
- second_reduce: bfloat16 [1024, 4096], P('dp', 'tensor'), may hold values from -0.09375 to 0.09375
- norm_gains: bfloat16 [6, 1024], replicated, may hold values from 0.25 to 1.75
- biases: bfloat16 [19, 1024], replicated, may hold values from -3 to 3
- kernel: bfloat16 [31, 1024], replicated, may hold values from -1 to 1
- distance_table: bfloat16 [73, 64], replicated, may hold values from -6 to 6
Outputs:
- outputs: bfloat16 [2, 8, 512, 1024], P(None, 'dp', 'tensor')
- input_grad: float32 [2, 8, 512, 1024], P(None, 'dp', 'tensor')
- first_expand_grad: float32 [1024, 4096], P('dp', 'tensor')
- first_reduce_grad: float32 [1024, 4096], P('dp', 'tensor')
- heads_project_grad: float32 [1024, 3, 1024], P('dp', None, 'tensor')
- heads_merge_grad: float32 [1024, 1024], P('dp', 'tensor')
- filter_expand_grad: float32 [1024, 2, 1024], P('dp', None, 'tensor')
- filter_reduce_grad: float32 [1024, 1024], P('dp', 'tensor')
- second_expand_grad: float32 [1024, 4096], P('dp', 'tensor')
- second_reduce_grad: float32 [1024, 4096], P('dp', 'tensor')
- norm_gains_grad: float32 [6, 1024], replicated
- biases_grad: float32 [19, 1024], replicated
- kernel_grad: float32 [31, 1024], replicated
- distance_table_grad: float32 [73, 64], replicated
The draws below stay inside these ranges and needn't reach their ends.
Inputs may be any that keep to these rules, and one draw needn't show every extreme that they name: In each micro-batch the clip lengths sum to 2560, and some clip has 512 live tokens.
All inputs are finite; a program needn't handle non-finite values. No bound on the sum of `lengths` on one device may be relied on, other than what follows from the above.
Results may differ from the reference program's by a relative error of at most 0.025.
Values may be sent and summed in bfloat16 or wider, within the bound.
No kernel may reach another device: no remote copies, remote signals or barrier semaphores. Data moves between devices by JAX's collectives and lax.ppermute only.
A program may use at most 256 MiB of HBM per device.

```python
import math
import jax
import jax.numpy as jnp
import numpy as np
from jax import lax

D = 1024
HEADS = 16
HD = 64
FF = 4096
KW = 31
LEFT = 64
RIGHT = 8
LEN = 512
MB = 2
NGAIN = 6
CLIPS = 8
BUCKETS = 73
NBIAS = 19
FILLED = 2560


def shard_levels(own_key, dims, pieces, low, largest):
    gain = 1.0
    for dim, parts in pieces:
        heights = jax.random.uniform(jax.random.fold_in(jax.random.fold_in(own_key, 6), dim), (parts,), jnp.float32, low / len(pieces), largest / len(pieces))
        gain = gain * jnp.repeat(jnp.exp(heights), dims[dim] // parts).reshape((-1,) + (1,) * (len(dims) - 1 - dim))
    return gain


def profile(number_of, total, most, skew):
    loads = [(1 << 20) // math.isqrt(grade ** skew) + 1 for grade in range(2, number_of + 1)]
    rest, given = total - most - (number_of - 1), [1] * (number_of - 1)
    while rest > 0:
        candidates = [i for i in range(number_of - 1) if given[i] < most]
        pool, remaining = sum([loads[i] for i in candidates]), rest
        for i in candidates:
            extra = min(most - given[i], max(1, remaining * loads[i] // pool), rest)
            given[i] = given[i] + extra
            rest = rest - extra
    return np.array([most] + given)


def ragged_sizes(own_key, count, total, bound, skew):
    if count == 2:
        one = jax.random.randint(own_key, (), max(1, total - bound), min(bound, total - 1) + 1)
        return jnp.stack([one, total - one])
    sizes = jnp.asarray(profile(count, total, bound, skew), jnp.int32)
    pairs = (count - 1) // 2
    giver, taker = sizes[1:1 + 2 * pairs:2], sizes[2:2 + 2 * pairs:2]
    margin = jnp.minimum(giver - 1, bound - taker)
    moved = jax.random.randint(jax.random.fold_in(own_key, 1), (pairs,), 0, 1 << 20) % (margin + 1)
    sizes = sizes.at[1:1 + 2 * pairs:2].set(giver - moved).at[2:2 + 2 * pairs:2].set(taker + moved)
    return sizes[jax.random.permutation(jax.random.fold_in(own_key, 2), count)]


def scatter_about(own_key, dims, scale, reach, cuts=(), dtype=jnp.bfloat16):
    drawn = jax.random.normal(own_key, dims, jnp.float32) * scale
    if len(cuts) > 0:
        drawn = shard_levels(own_key, dims, cuts, -0.22, 0.18) * drawn
    return jnp.clip(drawn, min=-reach, max=reach).astype(dtype)


def setup_inputs(seed: int = 0) -> dict:
    key_list = jax.random.split(jax.random.key(seed), 16)
    inputs = scatter_about(key_list[0], (MB, CLIPS, LEN, D), 1.0, 6.0, ((1, 8), (2, 4)))
    lengths = jax.vmap(lambda own: ragged_sizes(own, CLIPS, FILLED, LEN, 2))(jax.random.split(key_list[1], MB)).reshape((MB, CLIPS)).astype(jnp.int32)
    cotangent = scatter_about(key_list[2], (MB, CLIPS, LEN, D), 1.0, 6.0, ((1, 8), (2, 4)))
    first_expand = scatter_about(key_list[3], (D, FF), D ** -0.5, 0.1875, ((0, 8), (1, 4)))
    first_reduce = scatter_about(key_list[4], (D, FF), FF ** -0.5, 0.09375, ((0, 8), (1, 4)))
    heads_project = scatter_about(key_list[5], (D, 3, D), D ** -0.5, 0.1875, ((0, 8), (2, 4)))
    heads_merge = scatter_about(key_list[6], (D, D), (D // 16) ** -0.5, 0.75, ((0, 8), (1, 4)))
    filter_expand = scatter_about(key_list[7], (D, 2, D), D ** -0.5, 0.1875, ((0, 8), (2, 4)))
    filter_reduce = scatter_about(key_list[8], (D, D), D ** -0.5, 0.1875, ((0, 8), (1, 4)))
    second_expand = scatter_about(key_list[9], (D, FF), D ** -0.5, 0.1875, ((0, 8), (1, 4)))
    second_reduce = scatter_about(key_list[10], (D, FF), FF ** -0.5, 0.09375, ((0, 8), (1, 4)))
    norm_gains = jnp.clip(1.0 + 0.15 * jax.random.normal(key_list[11], (NGAIN, D), jnp.float32), 0.25, 1.75).astype(jnp.bfloat16)
    biases = scatter_about(key_list[12], (NBIAS, D), 0.5, 3.0)
    kernel = scatter_about(key_list[13], (KW, D), KW ** -0.5, 1.0)
    distance_table = scatter_about(key_list[14], (BUCKETS, HD), 1.0, 6.0)
    return {"inputs": inputs, "lengths": lengths, "cotangent": cotangent, "first_expand": first_expand, "first_reduce": first_reduce, "heads_project": heads_project, "heads_merge": heads_merge, "filter_expand": filter_expand, "filter_reduce": filter_reduce, "second_expand": second_expand, "second_reduce": second_reduce, "norm_gains": norm_gains, "biases": biases, "kernel": kernel, "distance_table": distance_table}


@jax.custom_vjp
def low(v):
    return lax.optimization_barrier(v.astype(jnp.bfloat16)).astype(jnp.float32)

@jax.custom_vjp
def low_back(v):
    return v

def low_keep(v):
    return (low(v), None)

def low_pass(kept, grad):
    return (grad,)

def back_keep(v):
    return (v, None)

def back_low(kept, grad):
    return (low(grad),)
low.defvjp(low_keep, low_pass)
low_back.defvjp(back_keep, back_low)
EPSILON = 1e-05
MASKED = -1e+30
HIGHEST = lax.Precision.HIGHEST

def matmul(left_side, right_side):
    return jnp.dot(left_side, right_side, precision=HIGHEST)

def row_norm(stream, gain_row, bias_row):
    center = stream - lax.optimization_barrier(jnp.mean(stream, axis=-1, keepdims=True))
    variance = lax.optimization_barrier(jnp.mean(center * center, axis=-1, keepdims=True))
    return center * lax.rsqrt(variance + EPSILON) * gain_row + bias_row

def swish(values):
    return values * jax.nn.sigmoid(values)

def feed_forward(stream, gain_row, bias_row, expand, shrink, hidden_bias, out_bias):
    normed = low(row_norm(stream, gain_row, bias_row))
    hidden = low_back(matmul(normed, expand) + hidden_bias)
    active = low(swish(hidden))
    branch = low_back(matmul(active, shrink.T))
    return stream + 0.5 * (branch + out_bias)

def bucket_index(row_count):
    positions = jnp.arange(row_count)
    return jnp.clip(positions[None, :] - positions[:, None], -LEFT, RIGHT) + LEFT

def attention(stream, gain_row, bias_row, project, merge, query_bias, value_bias, merge_bias, distance, key_live):
    row_count = stream.shape[0]
    normed = low(row_norm(stream, gain_row, bias_row))
    projected = jnp.einsum('nd,dke->nke', normed, project, precision=HIGHEST)
    queries = low(low_back(projected[:, 0] + query_bias)).reshape(row_count, HEADS, HD)
    key_rows = low(low_back(projected[:, 1])).reshape(row_count, HEADS, HD)
    values = low(low_back(projected[:, 2] + value_bias)).reshape(row_count, HEADS, HD)
    near_scores = jnp.einsum('qhe,be->hqb', queries, distance, precision=HIGHEST)
    buckets = jnp.broadcast_to(bucket_index(row_count)[None], (HEADS, row_count, row_count))
    relative = jnp.take_along_axis(near_scores, buckets, axis=2)
    scores = (jnp.einsum('qhe,khe->hqk', queries, key_rows, precision=HIGHEST) + relative) * HD ** (-0.5)
    scores = low_back(jnp.where(key_live[None, None, :], scores, MASKED))
    chances = low(jax.nn.softmax(scores, axis=-1))
    merged = jnp.einsum('hqk,khe->qhe', chances, values, precision=HIGHEST).reshape(row_count, HEADS * HD)
    merged = low(low_back(merged))
    branch = low_back(matmul(merged, merge.T))
    return stream + branch + merge_bias

def causal_mix(signal, kernel_rows):
    tap_count = kernel_rows.shape[0]
    row_count = signal.shape[0]
    padded = jnp.pad(signal, ((tap_count - 1, 0), (0, 0)))
    mixed_rows = jnp.zeros_like(signal)
    for tap_index in range(tap_count):
        mixed_rows = mixed_rows + kernel_rows[tap_index] * padded[tap_index:tap_index + row_count]
    return mixed_rows

def convolution(stream, gain_row, bias_row, expand, kernel_rows, depth_gain, depth_bias, shrink):
    normed = low(row_norm(stream, gain_row, bias_row))
    projected = low_back(jnp.einsum('nd,dke->nke', normed, expand, precision=HIGHEST))
    gated_rows = projected[:, 0] * jax.nn.sigmoid(projected[:, 1])
    mixed_rows = causal_mix(gated_rows, kernel_rows)
    active = low(swish(row_norm(mixed_rows, depth_gain, depth_bias)))
    branch = low_back(matmul(active, shrink.T))
    return stream + branch

def forward(clip_rows, clip_length, weights_in):
    first_expand, first_reduce, heads_project, heads_merge, filter_expand, filter_reduce, second_expand, second_reduce, norm_gains, biases, kernel, distance = weights_in
    row_count = clip_rows.shape[0]
    stride = FF // D
    key_live = jnp.arange(row_count) < clip_length
    stream = feed_forward(clip_rows, norm_gains[0], biases[0], first_expand, first_reduce, biases[11:11 + stride].reshape(-1), biases[9])
    stream = attention(stream, norm_gains[1], biases[1], heads_project, heads_merge, biases[6], biases[7], biases[8], distance, key_live)
    stream = convolution(stream, norm_gains[2], biases[2], filter_expand, kernel, norm_gains[3], biases[3], filter_reduce)
    stream = feed_forward(stream, norm_gains[4], biases[4], second_expand, second_reduce, biases[11 + stride:11 + 2 * stride].reshape(-1), biases[10])
    live_rows = key_live.astype(jnp.float32)[:, None]
    return row_norm(stream, norm_gains[5], biases[5]) * live_rows

def add_terms(first_term, second_term):
    return first_term + second_term

def reference(inputs, lengths, cotangent, first_expand, first_reduce, heads_project, heads_merge, filter_expand, filter_reduce, second_expand, second_reduce, norm_gains, biases, kernel, distance_table):
    weights_in = (first_expand.astype(jnp.float32), first_reduce.astype(jnp.float32), heads_project.astype(jnp.float32), heads_merge.astype(jnp.float32), filter_expand.astype(jnp.float32), filter_reduce.astype(jnp.float32), second_expand.astype(jnp.float32), second_reduce.astype(jnp.float32), norm_gains.astype(jnp.float32), biases.astype(jnp.float32), kernel.astype(jnp.float32), distance_table.astype(jnp.float32))
    clip_count = inputs.shape[0] * inputs.shape[1]
    rows_all = inputs.astype(jnp.float32).reshape(clip_count, inputs.shape[2], inputs.shape[3])
    cot_all = cotangent.astype(jnp.float32).reshape(clip_count, inputs.shape[2], inputs.shape[3])
    length_all = lengths.reshape(clip_count).astype(jnp.int32)

    def one_clip(totals, item):
        clip_rows, clip_length, clip_cot = item

        def local_forward(rows_in, params_in):
            return forward(rows_in, clip_length, params_in)
        result, pull = jax.vjp(local_forward, clip_rows, weights_in)
        rows_grad, param_grads = pull(clip_cot)
        return (jax.tree.map(add_terms, totals, param_grads), (result, rows_grad))
    zeros_start = jax.tree.map(jnp.zeros_like, weights_in)
    totals, (results, rows_grads) = lax.scan(one_clip, zeros_start, (rows_all, length_all, cot_all))
    return (results.reshape(inputs.shape).astype(jnp.bfloat16), rows_grads.reshape(inputs.shape), totals[0], totals[1], totals[2], totals[3], totals[4], totals[5], totals[6], totals[7], totals[8], totals[9], totals[10], totals[11])
```

```python
import functools

import jax
import jax.numpy as jnp
from jax import lax
from jax.experimental import pallas as pl
from jax.experimental.pallas import tpu as pltpu
from jax.sharding import Mesh
from jax.sharding import PartitionSpec as P

HD = 64
LEFT = 64
RIGHT = 8
EPSILON = 1e-05
MASKED = -1e30
WIDE = jnp.float32
NARROW = jnp.bfloat16
CHUNK = 64
QROWS = 128
NEAR = 128
VMEM_BYTES = 48 * 1024 * 1024
PLANE_BLOCKS = 4
LANES = 128
COST_PART = 0.0005
PAD = 32


def sds(shape, dtype):
    return jax.ShapeDtypeStruct(shape, dtype)


def params(parallel=1):
    return pltpu.CompilerParams(
        dimension_semantics=("arbitrary",) * parallel, vmem_limit_bytes=VMEM_BYTES
    )


def cost(flops, moved, exps=0):
    return pl.CostEstimate(
        flops=int(flops * COST_PART), bytes_accessed=int(moved * COST_PART), transcendentals=0
    )


def whole(shape):
    return pl.BlockSpec(shape, lambda *_: (0,) * len(shape))


def rel_cols(p, r, width):
    return pl.ds(pl.multiple_of(jnp.bitwise_xor(p, r) * width, width), width)


def weight_specs(w, cols, col_block):
    if len(w) == PLANE_BLOCKS:
        shape = (1, 1, w[0].shape[2], cols)
        return [
            pl.BlockSpec(shape, functools.partial(lambda r, t, p: (t, r, 0, col_block), r))
            for r in range(PLANE_BLOCKS)
        ]
    shape = (1, w[0].shape[1], cols)
    return [
        pl.BlockSpec(shape, lambda t, p: (t, 0, col_block)),
        pl.BlockSpec(shape, lambda t, p: (t, 0, col_block)),
        pl.BlockSpec(shape, lambda t, p: (t, 0, col_block)),
        pl.BlockSpec(shape, lambda t, p: (jnp.minimum(t, 1), 0, col_block)),
        pl.BlockSpec(shape, lambda t, p: (jnp.maximum(t - 2, 0), 0, col_block)),
    ]


def weight_blocks(w_refs, t):
    if len(w_refs) == PLANE_BLOCKS:
        return [ref[0, 0] for ref in w_refs]
    own, wx, wy, da, db = w_refs
    return own[0], wx[0], wy[0], jnp.where(t < 2, da[0], db[0])


def sigmoid(v):
    return 1.0 / (1.0 + jnp.exp(-v))


def norm_stats(v):
    mean = jnp.mean(v, axis=-1, keepdims=True)
    center = v - mean
    inv_std = lax.rsqrt(jnp.mean(center * center, axis=-1, keepdims=True) + EPSILON)
    return center * inv_std, inv_std


def expand_body(kind, merged, scale, nw, p_ref, *refs):
    refs = list(refs)
    x_ref = refs.pop(0)
    if merged:
        pa_ref, pb_ref, ob_ref = refs[:3]
        refs = refs[3:]
    g_ref, b_ref = refs[:2]
    w_refs = refs[2 : 2 + nw]
    refs = refs[2 + nw :]
    if kind != "conv":
        hb_ref = refs.pop(0)
    if merged:
        xn_ref = refs.pop(0)
    a_ref = refs.pop(0)
    outs = refs
    t = pl.program_id(0)
    p = p_ref[0]
    width = x_ref.shape[1] // PLANE_BLOCKS

    @pl.when(t == 0)
    def _():
        def step(i, carry):
            rows = pl.ds(pl.multiple_of(i * CHUNK, CHUNK), CHUNK)
            v = x_ref[rows, :]
            if merged:
                branch = pa_ref[rows, :].astype(WIDE) + pb_ref[rows, :].astype(WIDE)
                v = v + scale * (branch + ob_ref[...])
                xn_ref[rows, :] = v
            unit, _ = norm_stats(v)
            a_ref[rows, :] = (unit * g_ref[...] + b_ref[...]).astype(NARROW)
            return carry

        lax.fori_loop(0, x_ref.shape[0] // CHUNK, step, 0)

    acc = None
    for r, w in enumerate(weight_blocks(w_refs, t)):
        term = jnp.dot(a_ref[:, rel_cols(p, r, width)], w, preferred_element_type=WIDE)
        acc = term if acc is None else acc + term
    if kind == "ff":
        u = acc + hb_ref[...]
        outs[0][...] = u
        outs[1][...] = (u * sigmoid(u)).astype(NARROW)
    elif kind == "qkv":
        outs[0][...] = (acc + hb_ref[...]).astype(NARROW)
    else:
        half = acc.shape[1] // 2
        gate = sigmoid(acc[:, half:])
        outs[0][...] = gate
        outs[1][...] = acc[:, :half] * gate


def norm_expand(kind, x, merge, scale, gain, bias, w, cols, col_block, p, hidden_bias):
    rows, width = x.shape
    merged = merge is not None
    ins = [x]
    specs = [whole((rows, width))]
    if merged:
        ins += list(merge)
        specs += [whole((rows, width)), whole((rows, width)), whole((1, width))]
    ins += [gain, bias, *w]
    specs += [whole((1, width)), whole((1, width)), *weight_specs(w, cols, col_block)]
    if kind != "conv":
        ins.append(hidden_bias)
        specs.append(pl.BlockSpec((1, cols), lambda t, p: (0, t)))
    shapes, out_specs = [], []
    if merged:
        shapes.append(sds((rows, width), WIDE))
        out_specs.append(whole((rows, width)))
    shapes.append(sds((rows, width), NARROW))
    out_specs.append(whole((rows, width)))
    if kind == "ff":
        outs = [(cols, WIDE), (cols, NARROW)]
    elif kind == "qkv":
        outs = [(cols, NARROW)]
    else:
        outs = [(cols // 2, WIDE), (cols // 2, WIDE)]
    for out_cols, dtype in outs:
        shapes.append(sds((rows, 4 * out_cols), dtype))
        out_specs.append(pl.BlockSpec((rows, out_cols), lambda t, p: (0, t)))
    return pl.pallas_call(
        functools.partial(expand_body, kind, merged, scale, len(w)),
        grid_spec=pltpu.PrefetchScalarGridSpec(
            num_scalar_prefetch=1, grid=(4,), in_specs=specs, out_specs=out_specs
        ),
        out_shape=shapes,
        compiler_params=params(),
        cost_estimate=cost(2 * rows * width * 4 * cols, 8 * width * cols + 12 * rows * width),
        name="norm_expand_" + kind,
    )(p, *ins)


def reduce_body(nw, p_ref, s_ref, *refs):
    w_refs = refs[:nw]
    out_ref, acc_ref = refs[nw:]
    t = pl.program_id(0)
    p = p_ref[0]
    width = out_ref.shape[1] // PLANE_BLOCKS
    s = s_ref[...]

    @pl.when(t == 0)
    def _():
        acc_ref[...] = jnp.zeros_like(acc_ref)

    for r, w in enumerate(weight_blocks(w_refs, t)):
        cols = rel_cols(p, r, width)
        acc_ref[:, cols] += lax.dot_general(
            s, w, (((1,), (1,)), ((), ())), preferred_element_type=WIDE
        )

    @pl.when(t == 3)
    def _():
        out_ref[...] = acc_ref[...].astype(NARROW)


def reduce_mm(s, w, cols, col_block, p, width):
    rows = s.shape[0]
    return pl.pallas_call(
        functools.partial(reduce_body, len(w)),
        grid_spec=pltpu.PrefetchScalarGridSpec(
            num_scalar_prefetch=1,
            grid=(4,),
            in_specs=[
                pl.BlockSpec((rows, cols), lambda t, p: (0, t)),
                *weight_specs(w, cols, col_block),
            ],
            out_specs=whole((rows, width)),
            scratch_shapes=[pltpu.VMEM((rows, width), WIDE)],
        ),
        out_shape=sds((rows, width), NARROW),
        compiler_params=params(),
        cost_estimate=cost(2 * rows * width * 4 * cols, 8 * width * cols + 2 * rows * width),
        name="reduce_mm",
    )(p, s, *w)


def back_body(kind, nw, p_ref, g_ref, *refs):
    w_refs = refs[:nw]
    rest = refs[nw:]
    t = pl.program_id(0)
    p = p_ref[0]
    width = g_ref.shape[1] // PLANE_BLOCKS
    acc = None
    for r, w in enumerate(weight_blocks(w_refs, t)):
        term = jnp.dot(g_ref[:, rel_cols(p, r, width)], w, preferred_element_type=WIDE)
        acc = term if acc is None else acc + term
    if kind == "ff":
        u_ref, gu_ref, gc_ref = rest
        u = u_ref[...]
        logistic = sigmoid(u)
        gu = acc * (logistic * (1.0 + u * (1.0 - logistic)))
        gu_ref[...] = gu.astype(NARROW)
        gc_ref[...] = jnp.sum(gu, axis=0, keepdims=True)
    else:
        (out_ref,) = rest
        out_ref[...] = acc.astype(out_ref.dtype)


def back_expand(kind, g, w, cols, col_block, p, u=None):
    rows, width = g.shape
    ins = [g, *w]
    block = pl.BlockSpec((rows, cols), lambda t, p: (0, t))
    specs = [whole((rows, width)), *weight_specs(w, cols, col_block)]
    if kind == "ff":
        ins.append(u)
        specs.append(block)
        shapes = [sds((rows, 4 * cols), NARROW), sds((1, 4 * cols), WIDE)]
        out_specs = [block, pl.BlockSpec((1, cols), lambda t, p: (0, t))]
    else:
        shapes = sds((rows, 4 * cols), NARROW if kind == "low" else WIDE)
        out_specs = block
    return pl.pallas_call(
        functools.partial(back_body, kind, len(w)),
        grid_spec=pltpu.PrefetchScalarGridSpec(
            num_scalar_prefetch=1, grid=(4,), in_specs=specs, out_specs=out_specs
        ),
        out_shape=shapes,
        compiler_params=params(),
        cost_estimate=cost(2 * rows * width * 4 * cols, 8 * width * cols + 12 * rows * cols),
        name="back_expand_" + kind,
    )(p, *ins)


def wgrad_body(count, p_ref, *refs):
    x_refs = refs[:count]
    s_refs = refs[count : 2 * count]
    own_ref, sx_ref, kx_ref, sy_ref, ky_ref = refs[2 * count :]
    t = pl.program_id(0)
    p = p_ref[0]

    def grad(r, put):
        start = 0
        for x_ref, s_ref in zip(x_refs, s_refs):
            width = x_ref.shape[1] // PLANE_BLOCKS
            cols = s_ref.shape[1]
            term = lax.dot_general(
                x_ref[:, rel_cols(p, r, width)],
                s_ref[...],
                (((0,), (0,)), ((), ())),
                preferred_element_type=WIDE,
            ).astype(NARROW)
            put(start, cols, term)
            start += cols

    def put_own(start, cols, term):
        own_ref[0, :, start : start + cols] = term

    grad(0, put_own)

    @pl.when(t < 2)
    def _():
        def put_x(start, cols, term):
            sx_ref[0, 0, :, start : start + cols] = term

        def put_d(start, cols, term):
            sx_ref[1, 0, :, start : start + cols] = term

        def put_y(start, cols, term):
            ky_ref[0, :, start : start + cols] = term

        grad(1, put_x)
        grad(3, put_d)
        grad(2, put_y)

    @pl.when(t >= 2)
    def _():
        def put_y(start, cols, term):
            sy_ref[0, 0, :, start : start + cols] = term

        def put_d(start, cols, term):
            sy_ref[1, 0, :, start : start + cols] = term

        def put_x(start, cols, term):
            kx_ref[0, :, start : start + cols] = term

        grad(2, put_y)
        grad(3, put_d)
        grad(1, put_x)


def wgrad(xs, ss, p):
    rows, width = xs[0].shape
    wrows = width // PLANE_BLOCKS
    widths = [s.shape[1] // 4 for s in ss]
    cols = sum(widths)
    first = lambda t: jnp.minimum(t, 1)
    last = lambda t: jnp.maximum(t - 2, 0)
    return pl.pallas_call(
        functools.partial(wgrad_body, len(xs)),
        grid_spec=pltpu.PrefetchScalarGridSpec(
            num_scalar_prefetch=1,
            grid=(4,),
            in_specs=[whole((rows, width)) for _ in xs]
            + [pl.BlockSpec((rows, c), lambda t, p: (0, t)) for c in widths],
            out_specs=[
                pl.BlockSpec((1, wrows, cols), lambda t, p: (t, 0, 0)),
                pl.BlockSpec((2, 1, wrows, cols), lambda t, p: (0, first(t), 0, 0)),
                pl.BlockSpec((1, wrows, cols), lambda t, p: (last(t), 0, 0)),
                pl.BlockSpec((2, 1, wrows, cols), lambda t, p: (0, last(t), 0, 0)),
                pl.BlockSpec((1, wrows, cols), lambda t, p: (first(t), 0, 0)),
            ],
        ),
        out_shape=[
            sds((4, wrows, cols), NARROW),
            sds((2, 2, wrows, cols), NARROW),
            sds((2, wrows, cols), NARROW),
            sds((2, 2, wrows, cols), NARROW),
            sds((2, wrows, cols), NARROW),
        ],
        compiler_params=params(),
        cost_estimate=cost(2 * rows * width * 4 * cols, 8 * width * cols + 4 * rows * width),
        name="wgrad",
    )(p, *xs, *ss)


def wgrad_flat_body(p_ref, x_ref, s_ref, out_ref):
    p = p_ref[0]
    width = x_ref.shape[1] // PLANE_BLOCKS
    for r in range(PLANE_BLOCKS):
        out_ref[0, r] = lax.dot_general(
            x_ref[:, rel_cols(p, r, width)],
            s_ref[...],
            (((0,), (0,)), ((), ())),
            preferred_element_type=WIDE,
        ).astype(NARROW)


def wgrad_flat(x, s, p):
    rows, width = x.shape
    wrows = width // PLANE_BLOCKS
    cols = s.shape[1] // 4
    return pl.pallas_call(
        wgrad_flat_body,
        grid_spec=pltpu.PrefetchScalarGridSpec(
            num_scalar_prefetch=1,
            grid=(4,),
            in_specs=[whole((rows, width)), pl.BlockSpec((rows, cols), lambda t, p: (0, t))],
            out_specs=pl.BlockSpec((1, PLANE_BLOCKS, wrows, cols), lambda t, p: (t, 0, 0, 0)),
        ),
        out_shape=sds((4, PLANE_BLOCKS, wrows, cols), NARROW),
        compiler_params=params(),
        cost_estimate=cost(2 * rows * width * 4 * cols, 8 * width * cols + 4 * rows * width),
        name="wgrad_flat",
    )(p, x, s)


def combine_body(own_ref, rx_ref, ry_ref, fx_ref, fy_ref, out_ref):
    t = pl.program_id(0)
    near = jnp.where(t < 2, rx_ref[0, 0], ry_ref[0, 0])
    far = jnp.where(t < 2, fx_ref[0], fy_ref[0])
    total = own_ref[0].astype(WIDE) + near.astype(WIDE) + far.astype(WIDE)
    out_ref[0] = total.astype(NARROW)


def combine(own, rx, ry, fx, fy):
    rows, cols = own.shape[1:]
    first = lambda t: jnp.minimum(t, 1)
    last = lambda t: jnp.maximum(t - 2, 0)
    return pl.pallas_call(
        combine_body,
        grid=(4,),
        in_specs=[
            pl.BlockSpec((1, rows, cols), lambda t: (t, 0, 0)),
            pl.BlockSpec((1, 1, rows, cols), lambda t: (0, first(t), 0, 0)),
            pl.BlockSpec((1, 1, rows, cols), lambda t: (0, last(t), 0, 0)),
            pl.BlockSpec((1, rows, cols), lambda t: (first(t), 0, 0)),
            pl.BlockSpec((1, rows, cols), lambda t: (last(t), 0, 0)),
        ],
        out_specs=pl.BlockSpec((1, rows, cols), lambda t: (t, 0, 0)),
        out_shape=sds(own.shape, NARROW),
        compiler_params=params(),
        cost_estimate=cost(8 * rows * cols, 32 * rows * cols),
        name="combine",
    )(own, rx, ry, fx, fy)


def norm_back_body(scale, x_ref, gx_ref, pa_ref, pb_ref, g_ref, out_ref, low_ref, sums_ref):
    @pl.when(pl.program_id(0) == 0)
    def _():
        sums_ref[...] = jnp.zeros_like(sums_ref)

    unit, inv_std = norm_stats(x_ref[...])
    grad = pa_ref[...].astype(WIDE) + pb_ref[...].astype(WIDE)
    scaled = grad * g_ref[...]
    gx = gx_ref[...] + inv_std * (
        scaled
        - jnp.mean(scaled, axis=-1, keepdims=True)
        - unit * jnp.mean(scaled * unit, axis=-1, keepdims=True)
    )
    out_ref[...] = gx
    branch = scale * gx
    low_ref[...] = branch.astype(NARROW)
    sums_ref[0:1, :] += jnp.sum(grad * unit, axis=0, keepdims=True)
    sums_ref[1:2, :] += jnp.sum(grad, axis=0, keepdims=True)
    sums_ref[2:3, :] += jnp.sum(branch, axis=0, keepdims=True)


def norm_back(scale, x, gx, pa, pb, gain):
    rows, width = x.shape
    block = pl.BlockSpec((CHUNK, width), lambda i: (i, 0))
    return pl.pallas_call(
        functools.partial(norm_back_body, scale),
        grid=(rows // CHUNK,),
        in_specs=[block, block, block, block, whole((1, width))],
        out_specs=[block, block, whole((8, width))],
        out_shape=[sds((rows, width), WIDE), sds((rows, width), NARROW), sds((8, width), WIDE)],
        compiler_params=params(),
        cost_estimate=cost(20 * rows * width, 18 * rows * width),
        name="norm_back",
    )(x, gx, pa, pb, gain)


def final_body(
    x_ref, pa_ref, pb_ref, ob_ref, cot_ref, live_ref, g_ref, b_ref, y_ref, gx_ref, low_ref, sums_ref
):
    @pl.when(pl.program_id(0) == 0)
    def _():
        sums_ref[...] = jnp.zeros_like(sums_ref)

    branch = pa_ref[...].astype(WIDE) + pb_ref[...].astype(WIDE)
    v = x_ref[...] + 0.5 * (branch + ob_ref[...])
    unit, inv_std = norm_stats(v)
    live = live_ref[...]
    y_ref[...] = ((unit * g_ref[...] + b_ref[...]) * live).astype(NARROW)
    grad = cot_ref[...].astype(WIDE) * live
    scaled = grad * g_ref[...]
    gx = inv_std * (
        scaled
        - jnp.mean(scaled, axis=-1, keepdims=True)
        - unit * jnp.mean(scaled * unit, axis=-1, keepdims=True)
    )
    gx_ref[...] = gx
    half = 0.5 * gx
    low_ref[...] = half.astype(NARROW)
    sums_ref[0:1, :] += jnp.sum(grad * unit, axis=0, keepdims=True)
    sums_ref[1:2, :] += jnp.sum(grad, axis=0, keepdims=True)
    sums_ref[2:3, :] += jnp.sum(half, axis=0, keepdims=True)


def final_norm(x, pa, pb, ob, cot, live, gain, bias):
    rows, width = x.shape
    block = pl.BlockSpec((CHUNK, width), lambda i: (i, 0))
    row = whole((1, width))
    return pl.pallas_call(
        final_body,
        grid=(rows // CHUNK,),
        in_specs=[
            block, block, block, row, block,
            pl.BlockSpec((CHUNK, 1), lambda i: (i, 0)), row, row,
        ],
        out_specs=[block, block, block, whole((8, width))],
        out_shape=[
            sds((rows, width), NARROW),
            sds((rows, width), WIDE),
            sds((rows, width), NARROW),
            sds((8, width), WIDE),
        ],
        compiler_params=params(),
        cost_estimate=cost(24 * rows * width, 18 * rows * width),
        name="final_norm",
    )(x, pa, pb, ob, cot, live, gain, bias)


def distances(i0, keys):
    rows = lax.broadcasted_iota(jnp.int32, (QROWS, keys), 0) + i0
    cols = lax.broadcasted_iota(jnp.int32, (QROWS, keys), 1)
    return cols - rows, cols


def attend_body(len_ref, qkv_ref, table_ref, o_ref, p_out_ref):
    keys = qkv_ref.shape[0]
    width = qkv_ref.shape[1] // 3
    length = len_ref[0]
    table = table_ref[...]

    key_live = lax.broadcasted_iota(jnp.int32, (QROWS, keys), 1) < length
    for n in range(keys // QROWS):
        i0 = n * QROWS
        rows = slice(i0, i0 + QROWS)
        begin = max(0, i0 - QROWS)
        end = min(keys, i0 + 2 * QROWS)
        span = end - begin
        apart = distances(i0 - begin, span)[0]
        far_left = apart <= -LEFT
        far_right = apart >= RIGHT
        for e in range(width // HD):
            q = qkv_ref[rows, e * HD : (e + 1) * HD]
            k = qkv_ref[:, width + e * HD : width + (e + 1) * HD]
            v = qkv_ref[:, 2 * width + e * HD : 2 * width + (e + 1) * HD]
            near = lax.dot_general(q, table, (((1,), (1,)), ((), ())), preferred_element_type=WIDE)
            left, right = near[:, 0:1], near[:, LEFT + RIGHT : LEFT + RIGHT + 1]
            band = jnp.concatenate([near, jnp.zeros((QROWS, span - NEAR), WIDE)], axis=1)
            band = pltpu.roll(band, (i0 - begin + span - LEFT) % span, 1, stride=1, stride_axis=0)
            pieces = [jnp.where(far_left, left, jnp.where(far_right, right, band))]
            if begin > 0:
                pieces.insert(0, jnp.broadcast_to(left, (QROWS, begin)))
            if end < keys:
                pieces.append(jnp.broadcast_to(right, (QROWS, keys - end)))
            rel = jnp.concatenate(pieces, axis=1) if len(pieces) > 1 else pieces[0]
            s = lax.dot_general(q, k, (((1,), (1,)), ((), ())), preferred_element_type=WIDE)
            s = jnp.where(key_live, (s + rel) * HD ** (-0.5), MASKED)
            top = jnp.max(s, axis=-1, keepdims=True)
            ex = jnp.exp(s - top)
            chance = (ex * (1.0 / row_sum(ex))).astype(NARROW)
            p_out_ref[e, rows, :] = chance
            o_ref[rows, e * HD : (e + 1) * HD] = jnp.dot(
                chance, v, preferred_element_type=WIDE
            ).astype(NARROW)


def attend(qkv, table, length):
    rows = qkv.shape[0]
    width = qkv.shape[1] // 12
    heads = width // HD
    return pl.pallas_call(
        attend_body,
        grid_spec=pltpu.PrefetchScalarGridSpec(
            num_scalar_prefetch=1,
            grid=(4,),
            in_specs=[
                pl.BlockSpec((rows, 3 * width), lambda t, n: (0, t)),
                whole(table.shape),
            ],
            out_specs=[
                pl.BlockSpec((rows, width), lambda t, n: (0, t)),
                pl.BlockSpec((heads, rows, rows), lambda t, n: (t, 0, 0)),
            ],
        ),
        out_shape=[sds((rows, 4 * width), NARROW), sds((4 * heads, rows, rows), NARROW)],
        compiler_params=params(),
        cost_estimate=cost(16 * heads * rows * rows * HD, 10 * heads * rows * rows, 4 * heads * rows * rows),
        name="attend",
    )(length, qkv, table)


def attend_back_body(qkv_ref, go_ref, p_ref, table_ref, out_ref, sums_ref, dist_ref, gk_ref, gv_ref):
    keys = qkv_ref.shape[0]
    width = qkv_ref.shape[1] // 3
    table = table_ref[...]
    scale = HD ** (-0.5)
    nt = (((1,), (1,)), ((), ()))
    flip = (
        lax.broadcasted_iota(jnp.int32, (QROWS, QROWS), 0)
        + lax.broadcasted_iota(jnp.int32, (QROWS, QROWS), 1)
        == QROWS - 1
    ).astype(NARROW)
    bucket = lax.broadcasted_iota(jnp.int32, (QROWS, NEAR), 1)
    first_row = table[0:1, :].astype(WIDE)
    last_row = table[LEFT + RIGHT : LEFT + RIGHT + 1, :].astype(WIDE)

    @pl.when(pl.program_id(0) == 0)
    def _():
        dist_ref[...] = jnp.zeros_like(dist_ref)

    q_turned = jnp.transpose(qkv_ref[:, :width])
    go_turned = jnp.transpose(go_ref[...])
    for n in range(keys // QROWS):
        i0 = n * QROWS
        rows = slice(i0, i0 + QROWS)
        begin = max(0, i0 - QROWS)
        end = min(keys, i0 + 2 * QROWS)
        span = end - begin
        apart = distances(i0 - begin, span)[0]
        far_left = apart <= -LEFT
        far_right = apart >= RIGHT
        key_of = lax.broadcasted_iota(jnp.int32, (QROWS, NEAR), 0) + bucket + (i0 - LEFT)
        inside = (bucket > 0) & (bucket < LEFT + RIGHT) & (key_of >= 0) & (key_of < keys)
        for e in range(width // HD):
            lanes = slice(e * HD, (e + 1) * HD)
            q = qkv_ref[rows, lanes]
            k = qkv_ref[:, width + e * HD : width + (e + 1) * HD]
            v = qkv_ref[:, 2 * width + e * HD : 2 * width + (e + 1) * HD]
            go = go_ref[rows, lanes]
            chance = p_ref[e, rows, :]
            wide = chance.astype(WIDE)
            gp = lax.dot_general(go, v, nt, preferred_element_type=WIDE)
            gs = (wide * (gp - jnp.sum(gp * wide, axis=-1, keepdims=True))).astype(NARROW)
            gsw = gs.astype(WIDE)
            window = gsw[:, begin:end]
            turned = jnp.dot(flip, gs[:, begin:end], preferred_element_type=WIDE)
            turned = pltpu.roll(
                turned, (LEFT + 1 - QROWS - (i0 - begin)) % span, 1, stride=1, stride_axis=0
            )[:, :NEAR]
            back = jnp.dot(flip, turned.astype(NARROW), preferred_element_type=WIDE)
            left_sum = row_sum(jnp.where(far_left, window, 0.0))
            right_sum = row_sum(jnp.where(far_right, window, 0.0))
            if begin > 0:
                left_sum += row_sum(gsw[:, :begin])
            if end < keys:
                right_sum += row_sum(gsw[:, end:])
            left_sum *= scale
            right_sum *= scale
            near = (jnp.where(inside, back, 0.0) * scale).astype(NARROW)
            gq = jnp.dot(gs, k, preferred_element_type=WIDE) * scale
            gq += jnp.dot(near, table, preferred_element_type=WIDE)
            gq += left_sum * first_row + right_sum * last_row
            out_ref[rows, lanes] = gq.astype(NARROW)
            q_part = q_turned[lanes, rows]
            qw = q.astype(WIDE)
            dist_ref[:HD, :] += jnp.dot(q_part, near, preferred_element_type=WIDE)
            dist_ref[HD : HD + 1, :HD] += jnp.sum(left_sum * qw, axis=0, keepdims=True)
            dist_ref[HD + 1 : HD + 2, :HD] += jnp.sum(right_sum * qw, axis=0, keepdims=True)
            gk = jnp.dot(q_part, gs, preferred_element_type=WIDE)
            gv = jnp.dot(go_turned[lanes, rows], chance, preferred_element_type=WIDE)
            if n == 0:
                gk_ref[lanes, :] = gk
                gv_ref[lanes, :] = gv
            else:
                gk_ref[lanes, :] += gk
                gv_ref[lanes, :] += gv

    out_ref[:, width : 2 * width] = jnp.transpose(gk_ref[...] * scale).astype(NARROW)
    out_ref[:, 2 * width :] = jnp.transpose(gv_ref[...]).astype(NARROW)
    sums_ref[...] = jnp.sum(out_ref[...].astype(WIDE), axis=0, keepdims=True)


def attend_back(qkv, go, chances, table):
    rows = qkv.shape[0]
    width = qkv.shape[1] // 12
    heads = width // HD
    return pl.pallas_call(
        attend_back_body,
        grid=(4,),
        in_specs=[
            pl.BlockSpec((rows, 3 * width), lambda t: (0, t)),
            pl.BlockSpec((rows, width), lambda t: (0, t)),
            pl.BlockSpec((heads, rows, rows), lambda t: (t, 0, 0)),
            whole(table.shape),
        ],
        out_specs=[
            pl.BlockSpec((rows, 3 * width), lambda t: (0, t)),
            pl.BlockSpec((1, 3 * width), lambda t: (0, t)),
            whole((HD + 8, NEAR)),
        ],
        out_shape=[
            sds((rows, 12 * width), NARROW),
            sds((1, 12 * width), WIDE),
            sds((HD + 8, NEAR), WIDE),
        ],
        scratch_shapes=[pltpu.VMEM((width, rows), WIDE), pltpu.VMEM((width, rows), WIDE)],
        compiler_params=params(),
        cost_estimate=cost(40 * heads * rows * rows * HD, 10 * heads * rows * rows),
        name="attend_back",
    )(qkv, go, chances, table)


def lane_pair(first, second, rows):
    lane = lax.broadcasted_iota(jnp.int32, (rows, LANES), 1)
    return jnp.where(lane == 0, first, jnp.where(lane == 1, second, 0.0))


def row_sum(v):
    return jnp.sum(v, axis=-1, keepdims=True)


def mix_body(taps_count, z_ref, taps_ref, y_ref, sums_ref, pad_ref):
    rows = z_ref.shape[0]

    @pl.when(pl.program_id(0) == 0)
    def _():
        sums_ref[...] = jnp.zeros_like(sums_ref)

    pad_ref[0:PAD, :] = jnp.zeros((PAD, pad_ref.shape[1]), WIDE)
    pad_ref[PAD:, :] = z_ref[...]
    for start in range(0, rows, CHUNK):
        total = None
        for i in range(taps_count):
            begin = start + PAD - taps_count + 1 + i
            term = taps_ref[i : i + 1, :] * pad_ref[begin : begin + CHUNK, :]
            total = term if total is None else total + term
        here = slice(start, start + CHUNK)
        y_ref[here, :] = total
        sums_ref[here, :] += lane_pair(row_sum(total), row_sum(total * total), CHUNK)


def causal_mix(z, taps, taps_count):
    rows, cols = z.shape
    block = pl.BlockSpec((rows, cols // 4), lambda t: (0, t))
    return pl.pallas_call(
        functools.partial(mix_body, taps_count),
        grid=(4,),
        in_specs=[block, pl.BlockSpec((taps.shape[0], cols // 4), lambda t: (0, t))],
        out_specs=[block, whole((rows, LANES))],
        out_shape=[sds((rows, cols), WIDE), sds((rows, LANES), WIDE)],
        scratch_shapes=[pltpu.VMEM((rows + PAD, cols // 4), WIDE)],
        compiler_params=params(),
        cost_estimate=cost(2 * taps_count * rows * cols, 8 * rows * cols),
        name="causal_mix",
    )(z, taps)


def depth_stats(sa_ref, sb_ref, here, width):
    sums = (sa_ref[here, :] + sb_ref[here, :]) * (1.0 / width)
    mean = sums[:, 0:1]
    return mean, lax.rsqrt(sums[:, 1:2] - mean * mean + EPSILON)


def filter_out_body(p_ref, y_ref, sa_ref, sb_ref, g_ref, b_ref, *refs):
    w_refs = refs[:5]
    out_ref, low_ref, acc_ref = refs[5:]
    t = pl.program_id(0)
    p = p_ref[0]
    width = out_ref.shape[1]
    mean, std = depth_stats(sa_ref, sb_ref, slice(None), width)
    yn = (y_ref[...] - mean) * std * g_ref[...] + b_ref[...]
    low = (yn * sigmoid(yn)).astype(NARROW)
    low_ref[...] = low

    @pl.when(t == 0)
    def _():
        acc_ref[...] = jnp.zeros_like(acc_ref)

    for r, w in enumerate(weight_blocks(w_refs, t)):
        cols = rel_cols(p, r, width // PLANE_BLOCKS)
        acc_ref[:, cols] += lax.dot_general(
            low, w, (((1,), (1,)), ((), ())), preferred_element_type=WIDE
        )

    @pl.when(t == 3)
    def _():
        out_ref[...] = acc_ref[...].astype(NARROW)


def filter_out(y, sums, gain, bias, w, cols, col_block, p, width):
    rows = y.shape[0]
    block = pl.BlockSpec((rows, cols), lambda t, p: (0, t))
    row = pl.BlockSpec((1, cols), lambda t, p: (0, t))
    return pl.pallas_call(
        filter_out_body,
        grid_spec=pltpu.PrefetchScalarGridSpec(
            num_scalar_prefetch=1,
            grid=(4,),
            in_specs=[
                block, whole((rows, LANES)), whole((rows, LANES)), row, row,
                *weight_specs(w, cols, col_block),
            ],
            out_specs=[whole((rows, width)), block],
            scratch_shapes=[pltpu.VMEM((rows, width), WIDE)],
        ),
        out_shape=[sds((rows, width), NARROW), sds(y.shape, NARROW)],
        compiler_params=params(),
        cost_estimate=cost(2 * rows * width * 4 * cols, 8 * width * cols + 6 * rows * width),
        name="filter_out",
    )(p, y, *sums, gain, bias, *w)


def filter_in_body(p_ref, grad_ref, y_ref, sa_ref, sb_ref, g_ref, b_ref, *refs):
    w_refs = refs[:5]
    gyn_ref, cols_ref, rows_ref = refs[5:]
    t = pl.program_id(0)
    p = p_ref[0]
    width = grad_ref.shape[1]
    acc = None
    for r, w in enumerate(weight_blocks(w_refs, t)):
        cols = rel_cols(p, r, width // PLANE_BLOCKS)
        term = jnp.dot(grad_ref[:, cols], w, preferred_element_type=WIDE)
        acc = term if acc is None else acc + term
    mean, std = depth_stats(sa_ref, sb_ref, slice(None), width)
    unit = (y_ref[...] - mean) * std
    yn = unit * g_ref[...] + b_ref[...]
    logistic = sigmoid(yn)
    gyn = acc * (logistic * (1.0 + yn * (1.0 - logistic)))
    gyn_ref[...] = gyn
    cols_ref[0:1, :] = jnp.sum(gyn * unit, axis=0, keepdims=True)
    cols_ref[1:2, :] = jnp.sum(gyn, axis=0, keepdims=True)
    scaled = gyn * g_ref[...]
    pair = lane_pair(row_sum(scaled), row_sum(scaled * unit), gyn.shape[0])

    @pl.when(t == 0)
    def _():
        rows_ref[...] = pair

    @pl.when(t > 0)
    def _():
        rows_ref[...] += pair


def filter_in(grad, y, sums, gain, bias, w, cols, col_block, p):
    rows, width = grad.shape
    block = pl.BlockSpec((rows, cols), lambda t, p: (0, t))
    row = pl.BlockSpec((1, cols), lambda t, p: (0, t))
    return pl.pallas_call(
        filter_in_body,
        grid_spec=pltpu.PrefetchScalarGridSpec(
            num_scalar_prefetch=1,
            grid=(4,),
            in_specs=[
                whole((rows, width)), block, whole((rows, LANES)), whole((rows, LANES)), row, row,
                *weight_specs(w, cols, col_block),
            ],
            out_specs=[
                block,
                pl.BlockSpec((8, cols), lambda t, p: (0, t)),
                whole((rows, LANES)),
            ],
        ),
        out_shape=[sds(y.shape, WIDE), sds((8, 4 * cols), WIDE), sds((rows, LANES), WIDE)],
        compiler_params=params(),
        cost_estimate=cost(2 * rows * width * 4 * cols, 8 * width * cols + 6 * rows * width),
        name="filter_in",
    )(p, grad, y, *sums, gain, bias, *w)


def mix_back_body(
    taps_count, width, gyn_ref, y_ref, sa_ref, sb_ref, ra_ref, rb_ref, g_ref, z_ref, gate_ref,
    taps_ref, out_ref, grad_ref, gpad_ref, zpad_ref,
):
    rows, cols = z_ref.shape
    zpad_ref[0:PAD, :] = jnp.zeros((PAD, cols), WIDE)
    zpad_ref[PAD:, :] = z_ref[...]
    gpad_ref[rows:, :] = jnp.zeros((PAD, cols), WIDE)
    mean, std = depth_stats(sa_ref, sb_ref, slice(None), width)
    pair = (ra_ref[...] + rb_ref[...]) * (1.0 / width)
    unit = (y_ref[...] - mean) * std
    gpad_ref[0:rows, :] = std * (gyn_ref[...] * g_ref[...] - pair[:, 0:1] - unit * pair[:, 1:2])
    sums = [None] * taps_count
    for start in range(0, rows, CHUNK):
        here = slice(start, start + CHUNK)
        gy = gpad_ref[here, :]
        total = None
        for i in range(taps_count):
            begin = start + taps_count - 1 - i
            term = taps_ref[i : i + 1, :] * gpad_ref[begin : begin + CHUNK, :]
            total = term if total is None else total + term
        for i in range(taps_count):
            begin = start + PAD - taps_count + 1 + i
            part = zpad_ref[begin : begin + CHUNK, :] * gy
            part = jnp.sum(part.reshape(CHUNK // 8, 8, cols), axis=0)
            sums[i] = part if sums[i] is None else sums[i] + part
        gate = gate_ref[here, :]
        first = total * gate
        out_ref[here, :cols] = first.astype(NARROW)
        out_ref[here, cols:] = (total * z_ref[here, :] * (1.0 - gate)).astype(NARROW)
    for i in range(taps_count):
        grad_ref[i : i + 1, :] = jnp.sum(sums[i], axis=0, keepdims=True)


def mix_back(gyn, y, sums, pairs, gain, z, gate, taps, taps_count, width):
    rows, cols = z.shape
    n = cols // 4
    block = pl.BlockSpec((rows, n), lambda t: (0, t))
    row = pl.BlockSpec((1, n), lambda t: (0, t))
    lanes = whole((rows, LANES))
    tap_block = pl.BlockSpec((taps.shape[0], n), lambda t: (0, t))
    return pl.pallas_call(
        functools.partial(mix_back_body, taps_count, width),
        grid=(4,),
        in_specs=[block, block, lanes, lanes, lanes, lanes, row, block, block, tap_block],
        out_specs=[pl.BlockSpec((rows, 2 * n), lambda t: (0, t)), tap_block],
        out_shape=[sds((rows, 2 * cols), NARROW), sds(taps.shape, WIDE)],
        scratch_shapes=[pltpu.VMEM((rows + PAD, n), WIDE), pltpu.VMEM((rows + PAD, n), WIDE)],
        compiler_params=params(),
        cost_estimate=cost(4 * taps_count * rows * cols, 20 * rows * cols),
        name="mix_back",
    )(gyn, y, *sums, *pairs, gain, z, gate, taps)


def halve_body(groups, core_ref, *refs):
    count = sum(len(g) for g in groups)
    ins = list(refs[:count])
    keeps = refs[count : count + len(groups)]
    sends = refs[count + len(groups) :]
    low = core_ref[0] == 0
    for group, keep, send in zip(groups, keeps, sends):
        start = 0
        for n in group:
            ref = ins.pop(0)
            left, right = ref[:, :n], ref[:, n:]
            keep[:, start : start + n] = jnp.where(low, left, right)
            send[:, start : start + n] = jnp.where(low, right, left)
            start += n


def halve(groups, core):
    rows = groups[0][0].shape[0]
    halves = tuple(tuple(w.shape[1] // 2 for w in g) for g in groups)
    flat = [w for g in groups for w in g]
    shapes = [sds((rows, sum(h)), NARROW) for h in halves] * 2
    out = pl.pallas_call(
        functools.partial(halve_body, halves),
        grid_spec=pltpu.PrefetchScalarGridSpec(
            num_scalar_prefetch=1,
            grid=(1,),
            in_specs=[whole(w.shape) for w in flat],
            out_specs=[whole(s.shape) for s in shapes],
        ),
        out_shape=shapes,
        compiler_params=params(),
        cost_estimate=cost(0, 4 * sum(w.size for w in flat)),
        name="halve",
    )(core, *flat)
    return out[: len(groups)], out[len(groups) :]


def join_body(core_ref, keep_ref, came_ref, out_ref):
    low = core_ref[0] == 0
    rows = keep_ref.shape[0]
    keep, came = keep_ref[...], came_ref[...]
    out_ref[:rows, :] = jnp.where(low, keep, came)
    out_ref[rows:, :] = jnp.where(low, came, keep)


def join(keep, came, core):
    rows, cols = keep.shape
    return pl.pallas_call(
        join_body,
        grid_spec=pltpu.PrefetchScalarGridSpec(
            num_scalar_prefetch=1,
            grid=(1,),
            in_specs=[whole((rows, cols)), whole((rows, cols))],
            out_specs=whole((2 * rows, cols)),
        ),
        out_shape=sds((2 * rows, cols), keep.dtype),
        compiler_params=params(),
        cost_estimate=cost(0, 8 * rows * cols),
        name="join",
    )(core, keep, came)


def pack_body(lead, plan, core_ref, *refs):
    out_ref = refs[-1]
    low = core_ref[0] == 0
    out_ref[...] = jnp.zeros_like(out_ref)
    for ref, items in zip(refs[:-1], plan):
        for kind, src, dst in items:
            if kind == "once":
                v = ref[src : src + 1, :]
                out_ref[dst : dst + 1, :] = jnp.where(low, v, 0.0)
            elif kind == "all":
                out_ref[dst : dst + 8, :] = ref[...]
            elif kind == "taps":
                n = ref.shape[1] // 4
                for t in range(4):
                    v = ref[: src, t * n : (t + 1) * n]
                    out_ref[dst : dst + src, 2 * t * n : (2 * t + 1) * n] = jnp.where(low, v, 0.0)
                    out_ref[dst : dst + src, (2 * t + 1) * n : (2 * t + 2) * n] = jnp.where(low, 0.0, v)
            elif kind == "hidden":
                n = ref.shape[1] // 4
                for t in range(4):
                    v = ref[0:1, t * n : (t + 1) * n]
                    out_ref[dst + t : dst + t + 1, :n] = jnp.where(low, v, 0.0)
                    out_ref[dst + t : dst + t + 1, n:] = jnp.where(low, 0.0, v)
            else:
                row, first, step, n = src
                for t in range(4):
                    begin = t * step + first
                    v = ref[row : row + 1, begin : begin + n]
                    out_ref[dst : dst + 1, 2 * t * n : (2 * t + 1) * n] = jnp.where(low, v, 0.0)
                    out_ref[dst : dst + 1, (2 * t + 1) * n : (2 * t + 2) * n] = jnp.where(low, 0.0, v)


def pack(rows, width, core, sources):
    arrays = [a for a, _ in sources]
    plan = tuple(tuple(items) for _, items in sources)
    return pl.pallas_call(
        functools.partial(pack_body, rows, plan),
        grid_spec=pltpu.PrefetchScalarGridSpec(
            num_scalar_prefetch=1,
            grid=(1,),
            in_specs=[whole(a.shape) for a in arrays],
            out_specs=whole((rows, width)),
        ),
        out_shape=sds((rows, width), WIDE),
        compiler_params=params(),
        cost_estimate=cost(0, 8 * rows * width),
        name="pack",
    )(core, *arrays)


def on_device(planes, inputs, lengths, cotangent, *weights_and_rest):
    shards = weights_and_rest[:8]
    norm_gains, biases, kernel, distance_table = weights_and_rest[8:]
    batches, _, rows_here, width = inputs.shape
    parts = 4
    core = lax.axis_index("pair")
    plane = lax.axis_index("plane")
    part = lax.axis_index("tensor")
    quick = planes == PLANE_BLOCKS
    place = plane if quick else plane * 0
    p = place.astype(jnp.int32).reshape(1)

    def other_core(v):
        return lax.ppermute(v, "pair", [(0, 1), (1, 0)])

    def step_x(v):
        return lax.ppermute(v, "plane", [(i, i ^ 1) for i in range(planes)])

    def step_y(v):
        return lax.ppermute(v, "plane", [(i, i ^ 2) for i in range(planes)])

    def over_planes(v):
        if quick:
            return v + step_x(v) + step_y(v) + lax.ppermute(v, "plane", [(i, i ^ 3) for i in range(4)])
        bit = 1
        while bit < planes:
            v = v + lax.ppermute(v, "plane", [(i, i ^ bit) for i in range(planes)])
            bit *= 2
        return v

    def over_parts(v):
        def turn(k):
            return lax.ppermute(v, "tensor", [(i, i ^ k) for i in range(parts)])

        one, two, three = turn(1), turn(2), turn(3)
        return (v + one) + (two + three)

    def fence(*values):
        return lax.optimization_barrier(values) if quick else values

    def column_of(shard):
        return lax.all_gather(shard, "tensor", axis=0)

    def planes_of(column):
        every = lax.all_gather(column, "plane", axis=0)
        rows, cols = column.shape[1:]
        every = every.reshape(PLANE_BLOCKS, planes // PLANE_BLOCKS, parts, rows, cols)
        every = every.transpose(0, 2, 1, 3, 4).reshape(PLANE_BLOCKS, parts, -1, cols)
        return every[0], every[1], every[2], every[3, :2], every[3, 2:]

    def near(column):
        return step_x(column), step_y(column)

    def far(pair):
        return step_y(pair[0][:2]), step_x(pair[1][2:])

    def share(total):
        n = total.shape[0] // 2
        keep = lax.dynamic_slice_in_dim(total, core * n, n, 0)
        came = other_core(lax.dynamic_slice_in_dim(total, (1 - core) * n, n, 0))
        first = jnp.where(core == 0, keep, came).astype(WIDE)
        second = jnp.where(core == 0, came, keep).astype(WIDE)
        return first, second

    def tensor_sum(total):
        return lax.psum_scatter(total, "tensor", scatter_dimension=0)

    def hop1(grads):
        return (step_x(grads[1]), step_y(grads[3])) if quick else ()

    def hop2(grads, came):
        if not quick:
            return ()
        return step_y(add(grads[4], came[0][1])), step_x(add(grads[2], came[1][1]))

    def hop3(grads, came, last):
        own, sx, kx, sy, ky = grads
        if quick:
            return tensor_sum(combine(own, came[0], came[1], last[0], last[1]))
        blocks = [
            own,
            jnp.concatenate([sx[0], kx]),
            jnp.concatenate([ky, sy[0]]),
            jnp.concatenate([sx[1], sy[1]]),
        ]
        every = jnp.stack(blocks)
        rows = width // planes
        cols = own.shape[-1]
        every = every.reshape(PLANE_BLOCKS, parts, planes // PLANE_BLOCKS, rows, cols)
        every = every.transpose(0, 2, 1, 3, 4).reshape(planes, parts, rows, cols)
        return tensor_sum(lax.psum_scatter(every, "plane", scatter_dimension=0))

    def add(a, b):
        return (a.astype(WIDE) + b.astype(WIDE)).astype(NARROW)

    def rejoin(halves, start, cols, groups):
        pieces = [h[:, start : start + cols].reshape(h.shape[0], groups, -1) for h in halves]
        joined = jnp.concatenate(pieces, axis=2)
        return joined[:, 0] if groups == 1 else joined

    def spot(c, t):
        return c * parts + t

    def route(turn):
        pairs = []
        for c in range(2):
            for t in range(parts):
                mb = (turn + t) % 2
                pairs.append((spot(c, t), spot(t // 2, 2 * mb + c)))
        return pairs

    def bring(v):
        blocks = []
        for turn in range(2):
            mb = lax.rem(turn + part, 2)
            block = lax.dynamic_index_in_dim(v[:, 0], mb, 0, False)
            blocks.append(lax.ppermute(block, ("pair", "tensor"), route(turn)))
        return blocks

    def settle(blocks):
        swap = part // 2 == 1
        mine = jnp.concatenate(
            [jnp.where(swap, blocks[1], blocks[0]), jnp.where(swap, blocks[0], blocks[1])], axis=0
        )
        theirs = other_core(mine)
        return jnp.concatenate(
            [jnp.where(core == 0, mine, theirs), jnp.where(core == 0, theirs, mine)], axis=0
        )

    def send_home(v):
        half = v.shape[0] // 2
        mine = lax.dynamic_slice_in_dim(v, core * half, half, 0)
        first, second = mine[: half // 2], mine[half // 2 :]
        swap = part // 2 == 1
        blocks = [jnp.where(swap, second, first), jnp.where(swap, first, second)]
        came = []
        for turn in range(2):
            back = [(b, a) for a, b in route(turn)]
            came.append(lax.ppermute(blocks[turn], ("pair", "tensor"), back))
        odd = lax.rem(part, 2) == 1
        return jnp.stack([jnp.where(odd, came[1], came[0]), jnp.where(odd, came[0], came[1])])[:, None]

    (w_e1, w_r1, w_proj, w_merge, w_fe, w_fr, w_e2, w_r2) = shards
    core1 = core.astype(jnp.int32).reshape(1)
    ffc = w_e1.shape[1] // 2
    qc = w_proj.shape[2] // 2
    cc = w_fe.shape[2] // 2
    groups = [
        [w_e1],
        [w_r1],
        [w_proj[:, 0], w_proj[:, 1], w_proj[:, 2], w_merge],
        [w_fe[:, 0], w_fe[:, 1], w_fr, w_e2],
        [w_r2],
    ]
    keeps, sends = halve(groups, core1)
    pieces = fence(*[join(k, other_core(v), core1) for k, v in zip(keeps, sends)])

    gains = norm_gains.astype(WIDE)
    bias = biases.astype(WIDE)
    gain_row = lambda i: gains[i : i + 1]
    bias_row = lambda i: bias[i : i + 1]
    stride = w_e1.shape[1] * parts // width

    def pick(v):
        lead = v.shape[0]
        v = v.reshape(lead, parts, 2, -1)
        return lax.dynamic_index_in_dim(v, core, 2, False).reshape(lead, -1)

    hidden1 = pick(bias[11 : 11 + stride].reshape(1, -1))
    hidden2 = pick(bias[11 + stride : 11 + 2 * stride].reshape(1, -1))
    qb = pick(bias_row(6)).reshape(parts, 1, -1)
    vb = pick(bias_row(7)).reshape(parts, 1, -1)
    qkv_bias = jnp.concatenate([qb, jnp.zeros_like(qb), vb], axis=1).reshape(1, -1)
    taps_count = kernel.shape[0]
    taps = jnp.pad(pick(kernel.astype(WIDE)), ((0, PAD - taps_count), (0, 0)))
    depth_gain = pick(gain_row(3))
    depth_bias = pick(bias_row(3))
    buckets = distance_table.shape[0]
    table = jnp.pad(distance_table, ((0, NEAR - buckets), (0, 0)))

    pair_lengths = jnp.stack([lengths[:, 0], other_core(lengths[:, 0])])
    from_pair = jnp.bitwise_xor(lax.rem(part, 2), core)
    length = pair_lengths[from_pair, part // 2]
    rows_all = parts * inputs.shape[2]
    live = (jnp.arange(rows_all) < length).astype(WIDE)[:, None]

    col_e1 = column_of(pieces[0])
    r1c = column_of(pieces[1])
    attc = column_of(pieces[2])
    col_c = column_of(pieces[3])
    if quick:
        sd = pieces[4]
        sx, sy = step_x(sd), step_y(sd)
        sz = step_y(sx)
        col_e1, sx, sy, sz, source = fence(col_e1, sx, sy, sz, inputs)
        r2 = (column_of(jnp.stack([sd, sx, sy, sz])),) * PLANE_BLOCKS
        e1n, blocks = near(col_e1), bring(source)
        e1n, r1c, blocks = fence(e1n, r1c, blocks)
        e1f, r1n, x0 = far(e1n), near(r1c), settle(blocks)
        e1f, e1n, r1n, attc, x0 = fence(e1f, e1n, r1n, attc, x0)
        e1 = (col_e1, *e1n, *e1f)
        r1f, attn = far(r1n), near(attc)
    else:
        rows, cols = pieces[4].shape
        every = lax.all_gather(pieces[4], "plane", axis=0).reshape(PLANE_BLOCKS, -1, cols)
        r2 = (column_of(every),) * PLANE_BLOCKS
        x0 = settle(bring(inputs))
        e1 = planes_of(col_e1)
        r1 = planes_of(r1c)
        att = planes_of(attc)
        fil = planes_of(col_c[:, :, : 3 * cc])
        e2 = planes_of(col_c[:, :, 3 * cc :])
    x0 = x0.astype(WIDE)
    a1, u1, s1 = norm_expand("ff", x0, None, 0.5, gain_row(0), bias_row(0), e1, ffc, 0, p, hidden1)
    if quick:
        r1f, r1n, attn, s1 = fence(r1f, r1n, attn, s1)
        r1, attf = (r1c, *r1n, *r1f), far(attn)
    f1 = reduce_mm(s1, r1, ffc, 0, p, width)
    if quick:
        attf, attn, f1, col_c = fence(attf, attn, f1, col_c)
        att = (attc, *attn, *attf)
    f1o = other_core(f1)
    x1, bn, qkv = norm_expand(
        "qkv", x0, (f1, f1o, bias_row(9)), 0.5, gain_row(1), bias_row(1), att, 3 * qc, 0, p, qkv_bias
    )
    if quick:
        qkv, col_c = fence(qkv, col_c)
        filc, e2c = col_c[:, :, : 3 * cc], col_c[:, :, 3 * cc :]
        filn = near(filc)
    o, chances = attend(qkv, table, length.reshape(1))
    if quick:
        filn, o, e2c = fence(filn, o, e2c)
        filf, e2n = far(filn), near(e2c)
    f2 = reduce_mm(o, att, qc, 3, p, width)
    if quick:
        filf, filn, f2 = fence(filf, filn, f2)
        fil = (filc, *filn, *filf)
    f2o = other_core(f2)
    x2, cn, gate, z = norm_expand(
        "conv", x1, (f2, f2o, bias_row(8)), 1.0, gain_row(2), bias_row(2), fil, 2 * cc, 0, p, None
    )
    y, y_sums = causal_mix(z, taps, taps_count)
    if quick:
        e2n, y_sums, cot_source = fence(e2n, y_sums, cotangent)
        e2f = far(e2n)
        cot = bring(cot_source)
    y_sums = (y_sums, other_core(y_sums))
    f3, w = filter_out(y, y_sums, depth_gain, depth_bias, fil, cc, 2, p, width)
    if quick:
        e2f, cot, f3 = fence(e2f, cot, f3)
        cot = settle(cot)
        e2 = (e2c, *e2n, *e2f)
    else:
        cot = settle(bring(cotangent))
    f3o = other_core(f3)
    x3, a2, u2, s2 = norm_expand(
        "ff", x2, (f3, f3o, jnp.zeros((1, width), WIDE)), 1.0, gain_row(4), bias_row(4),
        e2, ffc, 0, p, hidden2,
    )
    f4 = reduce_mm(s2, r2, ffc, 0, p, width)
    out_rows, gx4, gf2, sums_final = final_norm(
        x3, f4, other_core(f4), bias_row(10), cot, live, gain_row(5), bias_row(5)
    )

    g_r2 = wgrad_flat(gf2, s2, p)
    g_r2, gf2 = fence(g_r2, gf2)
    z_r2 = tensor_sum(g_r2)
    gu2, gc2 = back_expand("ff", gf2, r2, ffc, 0, p, u2)
    g_e2 = wgrad([a2], [gu2], p)
    g_e2, gu2 = fence(g_e2, gu2)
    e2h1 = hop1(g_e2)
    b4 = reduce_mm(gu2, e2, ffc, 0, p, width)
    gx3, gw, sums3 = norm_back(1.0, x3, gx4, b4, other_core(b4), gain_row(4))
    gyn, depth_cols, depth_rows = filter_in(
        gw, y, y_sums, depth_gain, depth_bias, fil, cc, 2, p
    )
    depth_rows = (depth_rows, other_core(depth_rows))
    gg, taps_grad = mix_back(
        gyn, y, y_sums, depth_rows, depth_gain, z, gate, taps, taps_count, width
    )
    e2h1, gg = fence(e2h1, gg)
    e2h2 = hop2(g_e2, e2h1)
    g_fil = wgrad([cn, gw], [gg, w], p)
    filh1 = hop1(g_fil)
    b3 = reduce_mm(gg, fil, 2 * cc, 0, p, width)
    e2h2, b3, g_fil = fence(e2h2, b3, g_fil)
    z_e2 = hop3(g_e2, e2h1, e2h2)
    outputs = send_home(out_rows)
    gx2, gm, sums2 = norm_back(1.0, x2, gx3, b3, other_core(b3), gain_row(2))
    go = back_expand("low", gm, att, qc, 3, p)
    gqkv, gqkv_sums, table_grad = attend_back(qkv, go, chances, table)
    filh1, gqkv, outputs = fence(filh1, gqkv, outputs)
    filh2 = hop2(g_fil, filh1)
    g_att = wgrad([bn, gm], [gqkv, o], p)
    g_att, gqkv = fence(g_att, gqkv)
    atth1 = hop1(g_att)
    b2 = reduce_mm(gqkv, att, 3 * qc, 0, p, width)
    gx1, gf1, sums1 = norm_back(0.5, x1, gx2, b2, other_core(b2), gain_row(1))
    g_r1 = wgrad([gf1], [s1], p)

    table_rows = -(-buckets // 8)
    tail = jnp.transpose(table_grad[:HD])[1 : buckets - 1]
    ends = table_grad[HD : HD + 2, :HD]
    tail = jnp.concatenate([ends[:1], tail, ends[1:]], axis=0)
    tail = jnp.pad(tail, ((0, 8 * table_rows - buckets), (0, 0)))
    tail = tail.reshape(table_rows, 8, HD).transpose(1, 0, 2).reshape(8, table_rows * HD)
    tail = jnp.pad(tail, ((0, 0), (0, width - table_rows * HD)))
    early = pack(
        64, width, core1,
        [
            (sums_final, [("once", 0, 5), ("once", 1, 11), ("once", 2, 16)]),
            (sums3, [("once", 0, 4), ("once", 1, 10)]),
            (sums2, [("once", 0, 2), ("once", 1, 8), ("once", 2, 14)]),
            (sums1, [("once", 0, 1), ("once", 1, 7), ("once", 2, 15)]),
            (gqkv_sums, [("row", (0, 0, 3 * qc, qc), 12), ("row", (0, 2 * qc, 3 * qc, qc), 13)]),
            (depth_cols, [("row", (0, 0, cc, cc), 3), ("row", (1, 0, cc, cc), 9)]),
            (gc2, [("hidden", 0, 21)]),
            (taps_grad, [("taps", taps_count, 25)]),
            (tail, [("all", 0, 56)]),
        ],
    )
    filh2, g_r1, gf1, z_r2, early = fence(filh2, g_r1, gf1, z_r2, early)
    r1h1 = hop1(g_r1)
    z_fil = hop3(g_fil, filh1, filh2)
    half = early.shape[0] // 2
    mine = lax.dynamic_slice_in_dim(early, core * half, half, 0)
    theirs = lax.dynamic_slice_in_dim(early, (1 - core) * half, half, 0)
    gu1, gc1 = back_expand("ff", gf1, r1, ffc, 0, p, u1)
    g_e1 = wgrad([a1], [gu1], p)
    atth1, g_e1, gu1, z_e2, mine = fence(atth1, g_e1, gu1, z_e2, mine)
    atth2 = hop2(g_att, atth1)
    e1h1 = hop1(g_e1)
    early = mine + other_core(theirs)
    b1 = reduce_mm(gu1, e1, ffc, 0, p, width)
    r1h1, atth2, b1 = fence(r1h1, atth2, b1)
    r1h2 = hop2(g_r1, r1h1)
    z_att = hop3(g_att, atth1, atth2)
    gx0, _, sums0 = norm_back(1.0, x0, gx1, b1, other_core(b1), gain_row(0))
    late = pack(
        8, width, core1,
        [(sums0, [("once", 0, 0), ("once", 1, 1)]), (gc1, [("hidden", 0, 2)])],
    )
    e1h1, gx0, late, z_fil = fence(e1h1, gx0, late, z_fil)
    e1h2 = hop2(g_e1, e1h1)
    homeward = send_home(gx0.astype(NARROW))
    late = late + other_core(late)
    early = over_planes(early)
    r1h2, early, late = fence(r1h2, early, late)
    z_r1 = hop3(g_r1, r1h1, r1h2)
    late = over_planes(late)
    e1h2, late, early = fence(e1h2, late, early)
    z_e1 = hop3(g_e1, e1h1, e1h2)
    early, late = over_parts(early), over_parts(late)
    early_other = other_core(early)
    early = jnp.concatenate(
        [jnp.where(core == 0, early, early_other), jnp.where(core == 0, early_other, early)], axis=0
    )
    input_grad = homeward.astype(WIDE)
    if quick:
        rx = step_x(z_r2[1::2])
        ry = step_y(add(z_r2[2], rx[1]))
        z_r2 = (z_r2[0].astype(WIDE) + rx[0].astype(WIDE) + ry.astype(WIDE)).astype(NARROW)
    else:
        z_r2 = lax.psum_scatter(
            z_r2.reshape(planes, -1, z_r2.shape[-1]), "plane", scatter_dimension=0
        )
    e1_grad, r1_grad, att_grad, fil_grad, e2_grad, r2_grad = [
        share(v) for v in (z_e1, z_r1, z_att, z_fil, z_e2, z_r2)
    ]

    gains_grad = jnp.concatenate([late[0:1], early[1:6]], axis=0)
    bias_grad = jnp.concatenate([late[1:2], early[7:17], late[2:6], early[21:25]], axis=0)
    taps_t = early[25 : 25 + taps_count]
    table_t = early[56:64, : table_rows * HD].reshape(8, table_rows, HD).transpose(1, 0, 2)
    table_t = table_t.reshape(8 * table_rows, HD)[:buckets]
    return (
        outputs,
        input_grad,
        rejoin(e1_grad, 0, ffc, 1),
        rejoin(r1_grad, 0, ffc, 1),
        rejoin(att_grad, 0, 3 * qc, 3),
        rejoin(att_grad, 3 * qc, qc, 1),
        rejoin(fil_grad, 0, 2 * cc, 2),
        rejoin(fil_grad, 2 * cc, cc, 1),
        rejoin(e2_grad, 0, ffc, 1),
        rejoin(r2_grad, 0, ffc, 1),
        gains_grad,
        bias_grad,
        taps_t,
        table_t,
    )


def solution(mesh):
    dp = mesh.shape["dp"]
    tensor = mesh.shape["tensor"]
    split = Mesh(mesh.devices.reshape(dp // 2, 2, tensor), ("plane", "pair", "tensor"))
    both = ("plane", "pair")
    rows = P(None, both, "tensor", None)
    flat = P(both, "tensor")
    deep = P(both, None, "tensor")
    weights = (flat, flat, deep, flat, deep, flat, flat, flat)
    small = (P(), P(), P(), P())
    return jax.shard_map(
        functools.partial(on_device, dp // 2),
        mesh=split,
        in_specs=(rows, P(None, both), rows, *weights, *small),
        out_specs=(rows, rows, *weights, *small),
        check_vma=False,
    )
```

```python
import functools

import jax
import jax.numpy as jnp
from jax import lax
from jax.experimental import pallas as pl
from jax.experimental.pallas import tpu as pltpu
from jax.sharding import Mesh
from jax.sharding import PartitionSpec as P

HD = 64
LEFT = 64
RIGHT = 8
EPSILON = 1e-05
MASKED = -1e30
WIDE = jnp.float32
NARROW = jnp.bfloat16
CHUNK = 64
QROWS = 128
NEAR = 128
VMEM_BYTES = 48 * 1024 * 1024
PLANE_BLOCKS = 4
LANES = 128
COST_PART = 0.0005
PAD = 32


def sds(shape, dtype):
    return jax.ShapeDtypeStruct(shape, dtype)


def params(parallel=1):
    return pltpu.CompilerParams(
        dimension_semantics=("arbitrary",) * parallel, vmem_limit_bytes=VMEM_BYTES
    )


def cost(flops, moved, exps=0):
    return pl.CostEstimate(
        flops=int(flops * COST_PART), bytes_accessed=int(moved * COST_PART), transcendentals=0
    )


def whole(shape):
    return pl.BlockSpec(shape, lambda *_: (0,) * len(shape))


def rel_cols(p, r, width):
    return pl.ds(pl.multiple_of(jnp.bitwise_xor(p, r) * width, width), width)


def weight_specs(w, cols, col_block):
    if len(w) == PLANE_BLOCKS:
        shape = (1, 1, w[0].shape[2], cols)
        return [
            pl.BlockSpec(shape, functools.partial(lambda r, t, p: (t, r, 0, col_block), r))
            for r in range(PLANE_BLOCKS)
        ]
    shape = (1, w[0].shape[1], cols)
    return [
        pl.BlockSpec(shape, lambda t, p: (t, 0, col_block)),
        pl.BlockSpec(shape, lambda t, p: (t, 0, col_block)),
        pl.BlockSpec(shape, lambda t, p: (t, 0, col_block)),
        pl.BlockSpec(shape, lambda t, p: (jnp.minimum(t, 1), 0, col_block)),
        pl.BlockSpec(shape, lambda t, p: (jnp.maximum(t - 2, 0), 0, col_block)),
    ]


def weight_blocks(w_refs, t):
    if len(w_refs) == PLANE_BLOCKS:
        return [ref[0, 0] for ref in w_refs]
    own, wx, wy, da, db = w_refs
    return own[0], wx[0], wy[0], jnp.where(t < 2, da[0], db[0])


def sigmoid(v):
    return 1.0 / (1.0 + jnp.exp(-v))


def norm_stats(v):
    mean = jnp.mean(v, axis=-1, keepdims=True)
    center = v - mean
    inv_std = lax.rsqrt(jnp.mean(center * center, axis=-1, keepdims=True) + EPSILON)
    return center * inv_std, inv_std


def expand_body(kind, merged, scale, nw, p_ref, *refs):
    refs = list(refs)
    x_ref = refs.pop(0)
    if merged:
        pa_ref, pb_ref, ob_ref = refs[:3]
        refs = refs[3:]
    g_ref, b_ref = refs[:2]
    w_refs = refs[2 : 2 + nw]
    refs = refs[2 + nw :]
    if kind != "conv":
        hb_ref = refs.pop(0)
    if merged:
        xn_ref = refs.pop(0)
    a_ref = refs.pop(0)
    outs = refs
    t = pl.program_id(0)
    p = p_ref[0]
    width = x_ref.shape[1] // PLANE_BLOCKS

    @pl.when(t == 0)
    def _():
        def step(i, carry):
            rows = pl.ds(pl.multiple_of(i * CHUNK, CHUNK), CHUNK)
            v = x_ref[rows, :]
            if merged:
                branch = pa_ref[rows, :].astype(WIDE) + pb_ref[rows, :].astype(WIDE)
                v = v + scale * (branch + ob_ref[...])
                xn_ref[rows, :] = v
            unit, _ = norm_stats(v)
            a_ref[rows, :] = (unit * g_ref[...] + b_ref[...]).astype(NARROW)
            return carry

        lax.fori_loop(0, x_ref.shape[0] // CHUNK, step, 0)

    acc = None
    for r, w in enumerate(weight_blocks(w_refs, t)):
        term = jnp.dot(a_ref[:, rel_cols(p, r, width)], w, preferred_element_type=WIDE)
        acc = term if acc is None else acc + term
    if kind == "ff":
        u = acc + hb_ref[...]
        outs[0][...] = u
        outs[1][...] = (u * sigmoid(u)).astype(NARROW)
    elif kind == "qkv":
        outs[0][...] = (acc + hb_ref[...]).astype(NARROW)
    else:
        half = acc.shape[1] // 2
        gate = sigmoid(acc[:, half:])
        outs[0][...] = gate
        outs[1][...] = acc[:, :half] * gate


def norm_expand(kind, x, merge, scale, gain, bias, w, cols, col_block, p, hidden_bias):
    rows, width = x.shape
    merged = merge is not None
    ins = [x]
    specs = [whole((rows, width))]
    if merged:
        ins += list(merge)
        specs += [whole((rows, width)), whole((rows, width)), whole((1, width))]
    ins += [gain, bias, *w]
    specs += [whole((1, width)), whole((1, width)), *weight_specs(w, cols, col_block)]
    if kind != "conv":
        ins.append(hidden_bias)
        specs.append(pl.BlockSpec((1, cols), lambda t, p: (0, t)))
    shapes, out_specs = [], []
    if merged:
        shapes.append(sds((rows, width), WIDE))
        out_specs.append(whole((rows, width)))
    shapes.append(sds((rows, width), NARROW))
    out_specs.append(whole((rows, width)))
    if kind == "ff":
        outs = [(cols, WIDE), (cols, NARROW)]
    elif kind == "qkv":
        outs = [(cols, NARROW)]
    else:
        outs = [(cols // 2, WIDE), (cols // 2, WIDE)]
    for out_cols, dtype in outs:
        shapes.append(sds((rows, 4 * out_cols), dtype))
        out_specs.append(pl.BlockSpec((rows, out_cols), lambda t, p: (0, t)))
    return pl.pallas_call(
        functools.partial(expand_body, kind, merged, scale, len(w)),
        grid_spec=pltpu.PrefetchScalarGridSpec(
            num_scalar_prefetch=1, grid=(4,), in_specs=specs, out_specs=out_specs
        ),
        out_shape=shapes,
        compiler_params=params(),
        cost_estimate=cost(2 * rows * width * 4 * cols, 8 * width * cols + 12 * rows * width),
        name="norm_expand_" + kind,
    )(p, *ins)


def reduce_body(nw, p_ref, s_ref, *refs):
    w_refs = refs[:nw]
    out_ref, acc_ref = refs[nw:]
    t = pl.program_id(0)
    p = p_ref[0]
    width = out_ref.shape[1] // PLANE_BLOCKS
    s = s_ref[...]

    @pl.when(t == 0)
    def _():
        acc_ref[...] = jnp.zeros_like(acc_ref)

    for r, w in enumerate(weight_blocks(w_refs, t)):
        cols = rel_cols(p, r, width)
        acc_ref[:, cols] += lax.dot_general(
            s, w, (((1,), (1,)), ((), ())), preferred_element_type=WIDE
        )

    @pl.when(t == 3)
    def _():
        out_ref[...] = acc_ref[...].astype(NARROW)


def reduce_mm(s, w, cols, col_block, p, width):
    rows = s.shape[0]
    return pl.pallas_call(
        functools.partial(reduce_body, len(w)),
        grid_spec=pltpu.PrefetchScalarGridSpec(
            num_scalar_prefetch=1,
            grid=(4,),
            in_specs=[
                pl.BlockSpec((rows, cols), lambda t, p: (0, t)),
                *weight_specs(w, cols, col_block),
            ],
            out_specs=whole((rows, width)),
            scratch_shapes=[pltpu.VMEM((rows, width), WIDE)],
        ),
        out_shape=sds((rows, width), NARROW),
        compiler_params=params(),
        cost_estimate=cost(2 * rows * width * 4 * cols, 8 * width * cols + 2 * rows * width),
        name="reduce_mm",
    )(p, s, *w)


def back_body(kind, nw, p_ref, g_ref, *refs):
    w_refs = refs[:nw]
    rest = refs[nw:]
    t = pl.program_id(0)
    p = p_ref[0]
    width = g_ref.shape[1] // PLANE_BLOCKS
    acc = None
    for r, w in enumerate(weight_blocks(w_refs, t)):
        term = jnp.dot(g_ref[:, rel_cols(p, r, width)], w, preferred_element_type=WIDE)
        acc = term if acc is None else acc + term
    if kind == "ff":
        u_ref, gu_ref, gc_ref = rest
        u = u_ref[...]
        logistic = sigmoid(u)
        gu = acc * (logistic * (1.0 + u * (1.0 - logistic)))
        gu_ref[...] = gu.astype(NARROW)
        gc_ref[...] = jnp.sum(gu, axis=0, keepdims=True)
    else:
        (out_ref,) = rest
        out_ref[...] = acc.astype(out_ref.dtype)


def back_expand(kind, g, w, cols, col_block, p, u=None):
    rows, width = g.shape
    ins = [g, *w]
    block = pl.BlockSpec((rows, cols), lambda t, p: (0, t))
    specs = [whole((rows, width)), *weight_specs(w, cols, col_block)]
    if kind == "ff":
        ins.append(u)
        specs.append(block)
        shapes = [sds((rows, 4 * cols), NARROW), sds((1, 4 * cols), WIDE)]
        out_specs = [block, pl.BlockSpec((1, cols), lambda t, p: (0, t))]
    else:
        shapes = sds((rows, 4 * cols), NARROW if kind == "low" else WIDE)
        out_specs = block
    return pl.pallas_call(
        functools.partial(back_body, kind, len(w)),
        grid_spec=pltpu.PrefetchScalarGridSpec(
            num_scalar_prefetch=1, grid=(4,), in_specs=specs, out_specs=out_specs
        ),
        out_shape=shapes,
        compiler_params=params(),
        cost_estimate=cost(2 * rows * width * 4 * cols, 8 * width * cols + 12 * rows * cols),
        name="back_expand_" + kind,
    )(p, *ins)


def wgrad_body(count, p_ref, *refs):
    x_refs = refs[:count]
    s_refs = refs[count : 2 * count]
    own_ref, sx_ref, kx_ref, sy_ref, ky_ref = refs[2 * count :]
    t = pl.program_id(0)
    p = p_ref[0]

    def grad(r, put):
        start = 0
        for x_ref, s_ref in zip(x_refs, s_refs):
            width = x_ref.shape[1] // PLANE_BLOCKS
            cols = s_ref.shape[1]
            term = lax.dot_general(
                x_ref[:, rel_cols(p, r, width)],
                s_ref[...],
                (((0,), (0,)), ((), ())),
                preferred_element_type=WIDE,
            ).astype(NARROW)
            put(start, cols, term)
            start += cols

    def put_own(start, cols, term):
        own_ref[0, :, start : start + cols] = term

    grad(0, put_own)

    @pl.when(t < 2)
    def _():
        def put_x(start, cols, term):
            sx_ref[0, 0, :, start : start + cols] = term

        def put_d(start, cols, term):
            sx_ref[1, 0, :, start : start + cols] = term

        def put_y(start, cols, term):
            ky_ref[0, :, start : start + cols] = term

        grad(1, put_x)
        grad(3, put_d)
        grad(2, put_y)

    @pl.when(t >= 2)
    def _():
        def put_y(start, cols, term):
            sy_ref[0, 0, :, start : start + cols] = term

        def put_d(start, cols, term):
            sy_ref[1, 0, :, start : start + cols] = term

        def put_x(start, cols, term):
            kx_ref[0, :, start : start + cols] = term

        grad(2, put_y)
        grad(3, put_d)
        grad(1, put_x)


def wgrad(xs, ss, p):
    rows, width = xs[0].shape
    wrows = width // PLANE_BLOCKS
    widths = [s.shape[1] // 4 for s in ss]
    cols = sum(widths)
    first = lambda t: jnp.minimum(t, 1)
    last = lambda t: jnp.maximum(t - 2, 0)
    return pl.pallas_call(
        functools.partial(wgrad_body, len(xs)),
        grid_spec=pltpu.PrefetchScalarGridSpec(
            num_scalar_prefetch=1,
            grid=(4,),
            in_specs=[whole((rows, width)) for _ in xs]
            + [pl.BlockSpec((rows, c), lambda t, p: (0, t)) for c in widths],
            out_specs=[
                pl.BlockSpec((1, wrows, cols), lambda t, p: (t, 0, 0)),
                pl.BlockSpec((2, 1, wrows, cols), lambda t, p: (0, first(t), 0, 0)),
                pl.BlockSpec((1, wrows, cols), lambda t, p: (last(t), 0, 0)),
                pl.BlockSpec((2, 1, wrows, cols), lambda t, p: (0, last(t), 0, 0)),
                pl.BlockSpec((1, wrows, cols), lambda t, p: (first(t), 0, 0)),
            ],
        ),
        out_shape=[
            sds((4, wrows, cols), NARROW),
            sds((2, 2, wrows, cols), NARROW),
            sds((2, wrows, cols), NARROW),
            sds((2, 2, wrows, cols), NARROW),
            sds((2, wrows, cols), NARROW),
        ],
        compiler_params=params(),
        cost_estimate=cost(2 * rows * width * 4 * cols, 8 * width * cols + 4 * rows * width),
        name="wgrad",
    )(p, *xs, *ss)


def wgrad_flat_body(count, p_ref, *refs):
    p = p_ref[0]
    out_ref = refs[-1]
    for r in range(PLANE_BLOCKS):
        start = 0
        for x_ref, s_ref in zip(refs[:count], refs[count : 2 * count]):
            width = x_ref.shape[1] // PLANE_BLOCKS
            cols = s_ref.shape[1]
            out_ref[0, r, :, start : start + cols] = lax.dot_general(
                x_ref[:, rel_cols(p, r, width)],
                s_ref[...],
                (((0,), (0,)), ((), ())),
                preferred_element_type=WIDE,
            ).astype(NARROW)
            start += cols


def wgrad_flat(xs, ss, p):
    rows, width = xs[0].shape
    wrows = width // PLANE_BLOCKS
    widths = [s.shape[1] // 4 for s in ss]
    cols = sum(widths)
    return pl.pallas_call(
        functools.partial(wgrad_flat_body, len(xs)),
        grid_spec=pltpu.PrefetchScalarGridSpec(
            num_scalar_prefetch=1,
            grid=(4,),
            in_specs=[whole((rows, width)) for _ in xs]
            + [pl.BlockSpec((rows, c), lambda t, p: (0, t)) for c in widths],
            out_specs=pl.BlockSpec((1, PLANE_BLOCKS, wrows, cols), lambda t, p: (t, 0, 0, 0)),
        ),
        out_shape=sds((4, PLANE_BLOCKS, wrows, cols), NARROW),
        compiler_params=params(),
        cost_estimate=cost(2 * rows * width * 4 * cols, 8 * width * cols + 4 * rows * width),
        name="wgrad_flat",
    )(p, *xs, *ss)


def combine_body(own_ref, rx_ref, ry_ref, fx_ref, fy_ref, out_ref):
    t = pl.program_id(0)
    near = jnp.where(t < 2, rx_ref[0, 0], ry_ref[0, 0])
    far = jnp.where(t < 2, fx_ref[0], fy_ref[0])
    total = own_ref[0].astype(WIDE) + near.astype(WIDE) + far.astype(WIDE)
    out_ref[0] = total.astype(NARROW)


def combine(own, rx, ry, fx, fy):
    rows, cols = own.shape[1:]
    first = lambda t: jnp.minimum(t, 1)
    last = lambda t: jnp.maximum(t - 2, 0)
    return pl.pallas_call(
        combine_body,
        grid=(4,),
        in_specs=[
            pl.BlockSpec((1, rows, cols), lambda t: (t, 0, 0)),
            pl.BlockSpec((1, 1, rows, cols), lambda t: (0, first(t), 0, 0)),
            pl.BlockSpec((1, 1, rows, cols), lambda t: (0, last(t), 0, 0)),
            pl.BlockSpec((1, rows, cols), lambda t: (first(t), 0, 0)),
            pl.BlockSpec((1, rows, cols), lambda t: (last(t), 0, 0)),
        ],
        out_specs=pl.BlockSpec((1, rows, cols), lambda t: (t, 0, 0)),
        out_shape=sds(own.shape, NARROW),
        compiler_params=params(),
        cost_estimate=cost(8 * rows * cols, 32 * rows * cols),
        name="combine",
    )(own, rx, ry, fx, fy)


def norm_back_body(scale, x_ref, gx_ref, pa_ref, pb_ref, g_ref, out_ref, low_ref, sums_ref):
    @pl.when(pl.program_id(0) == 0)
    def _():
        sums_ref[...] = jnp.zeros_like(sums_ref)

    unit, inv_std = norm_stats(x_ref[...])
    grad = pa_ref[...].astype(WIDE) + pb_ref[...].astype(WIDE)
    scaled = grad * g_ref[...]
    gx = gx_ref[...] + inv_std * (
        scaled
        - jnp.mean(scaled, axis=-1, keepdims=True)
        - unit * jnp.mean(scaled * unit, axis=-1, keepdims=True)
    )
    out_ref[...] = gx
    branch = scale * gx
    low_ref[...] = branch.astype(NARROW)
    sums_ref[0:1, :] += jnp.sum(grad * unit, axis=0, keepdims=True)
    sums_ref[1:2, :] += jnp.sum(grad, axis=0, keepdims=True)
    sums_ref[2:3, :] += jnp.sum(branch, axis=0, keepdims=True)


def norm_back(scale, x, gx, pa, pb, gain):
    rows, width = x.shape
    block = pl.BlockSpec((CHUNK, width), lambda i: (i, 0))
    return pl.pallas_call(
        functools.partial(norm_back_body, scale),
        grid=(rows // CHUNK,),
        in_specs=[block, block, block, block, whole((1, width))],
        out_specs=[block, block, whole((8, width))],
        out_shape=[sds((rows, width), WIDE), sds((rows, width), NARROW), sds((8, width), WIDE)],
        compiler_params=params(),
        cost_estimate=cost(20 * rows * width, 18 * rows * width),
        name="norm_back",
    )(x, gx, pa, pb, gain)


def final_body(
    x_ref, pa_ref, pb_ref, ob_ref, cot_ref, live_ref, g_ref, b_ref, y_ref, gx_ref, low_ref, sums_ref
):
    @pl.when(pl.program_id(0) == 0)
    def _():
        sums_ref[...] = jnp.zeros_like(sums_ref)

    branch = pa_ref[...].astype(WIDE) + pb_ref[...].astype(WIDE)
    v = x_ref[...] + 0.5 * (branch + ob_ref[...])
    unit, inv_std = norm_stats(v)
    live = live_ref[...]
    y_ref[...] = ((unit * g_ref[...] + b_ref[...]) * live).astype(NARROW)
    grad = cot_ref[...].astype(WIDE) * live
    scaled = grad * g_ref[...]
    gx = inv_std * (
        scaled
        - jnp.mean(scaled, axis=-1, keepdims=True)
        - unit * jnp.mean(scaled * unit, axis=-1, keepdims=True)
    )
    gx_ref[...] = gx
    half = 0.5 * gx
    low_ref[...] = half.astype(NARROW)
    sums_ref[0:1, :] += jnp.sum(grad * unit, axis=0, keepdims=True)
    sums_ref[1:2, :] += jnp.sum(grad, axis=0, keepdims=True)
    sums_ref[2:3, :] += jnp.sum(half, axis=0, keepdims=True)


def final_norm(x, pa, pb, ob, cot, live, gain, bias):
    rows, width = x.shape
    block = pl.BlockSpec((CHUNK, width), lambda i: (i, 0))
    row = whole((1, width))
    return pl.pallas_call(
        final_body,
        grid=(rows // CHUNK,),
        in_specs=[
            block, block, block, row, block,
            pl.BlockSpec((CHUNK, 1), lambda i: (i, 0)), row, row,
        ],
        out_specs=[block, block, block, whole((8, width))],
        out_shape=[
            sds((rows, width), NARROW),
            sds((rows, width), WIDE),
            sds((rows, width), NARROW),
            sds((8, width), WIDE),
        ],
        compiler_params=params(),
        cost_estimate=cost(24 * rows * width, 18 * rows * width),
        name="final_norm",
    )(x, pa, pb, ob, cot, live, gain, bias)


def distances(i0, keys):
    rows = lax.broadcasted_iota(jnp.int32, (QROWS, keys), 0) + i0
    cols = lax.broadcasted_iota(jnp.int32, (QROWS, keys), 1)
    return cols - rows, cols


def attend_body(len_ref, qkv_ref, table_ref, o_ref, p_out_ref):
    keys = qkv_ref.shape[0]
    width = qkv_ref.shape[1] // 3
    length = len_ref[0]
    table = table_ref[...]

    key_live = lax.broadcasted_iota(jnp.int32, (QROWS, keys), 1) < length
    for n in range(keys // QROWS):
        i0 = n * QROWS
        rows = slice(i0, i0 + QROWS)
        begin = max(0, i0 - QROWS)
        end = min(keys, i0 + 2 * QROWS)
        span = end - begin
        apart = distances(i0 - begin, span)[0]
        far_left = apart <= -LEFT
        far_right = apart >= RIGHT
        for e in range(width // HD):
            q = qkv_ref[rows, e * HD : (e + 1) * HD]
            k = qkv_ref[:, width + e * HD : width + (e + 1) * HD]
            v = qkv_ref[:, 2 * width + e * HD : 2 * width + (e + 1) * HD]
            near = lax.dot_general(q, table, (((1,), (1,)), ((), ())), preferred_element_type=WIDE)
            left, right = near[:, 0:1], near[:, LEFT + RIGHT : LEFT + RIGHT + 1]
            band = jnp.concatenate([near, jnp.zeros((QROWS, span - NEAR), WIDE)], axis=1)
            band = pltpu.roll(band, (i0 - begin + span - LEFT) % span, 1, stride=1, stride_axis=0)
            pieces = [jnp.where(far_left, left, jnp.where(far_right, right, band))]
            if begin > 0:
                pieces.insert(0, jnp.broadcast_to(left, (QROWS, begin)))
            if end < keys:
                pieces.append(jnp.broadcast_to(right, (QROWS, keys - end)))
            rel = jnp.concatenate(pieces, axis=1) if len(pieces) > 1 else pieces[0]
            s = lax.dot_general(q, k, (((1,), (1,)), ((), ())), preferred_element_type=WIDE)
            s = jnp.where(key_live, (s + rel) * HD ** (-0.5), MASKED)
            top = jnp.max(s, axis=-1, keepdims=True)
            ex = jnp.exp(s - top)
            chance = (ex * (1.0 / row_sum(ex))).astype(NARROW)
            p_out_ref[e, rows, :] = chance
            o_ref[rows, e * HD : (e + 1) * HD] = jnp.dot(
                chance, v, preferred_element_type=WIDE
            ).astype(NARROW)


def attend(qkv, table, length):
    rows = qkv.shape[0]
    width = qkv.shape[1] // 12
    heads = width // HD
    return pl.pallas_call(
        attend_body,
        grid_spec=pltpu.PrefetchScalarGridSpec(
            num_scalar_prefetch=1,
            grid=(4,),
            in_specs=[
                pl.BlockSpec((rows, 3 * width), lambda t, n: (0, t)),
                whole(table.shape),
            ],
            out_specs=[
                pl.BlockSpec((rows, width), lambda t, n: (0, t)),
                pl.BlockSpec((heads, rows, rows), lambda t, n: (t, 0, 0)),
            ],
        ),
        out_shape=[sds((rows, 4 * width), NARROW), sds((4 * heads, rows, rows), NARROW)],
        compiler_params=params(),
        cost_estimate=cost(16 * heads * rows * rows * HD, 10 * heads * rows * rows, 4 * heads * rows * rows),
        name="attend",
    )(length, qkv, table)


def attend_back_body(qkv_ref, go_ref, p_ref, table_ref, out_ref, sums_ref, dist_ref, gk_ref, gv_ref):
    keys = qkv_ref.shape[0]
    width = qkv_ref.shape[1] // 3
    table = table_ref[...]
    scale = HD ** (-0.5)
    nt = (((1,), (1,)), ((), ()))
    flip = (
        lax.broadcasted_iota(jnp.int32, (QROWS, QROWS), 0)
        + lax.broadcasted_iota(jnp.int32, (QROWS, QROWS), 1)
        == QROWS - 1
    ).astype(NARROW)
    bucket = lax.broadcasted_iota(jnp.int32, (QROWS, NEAR), 1)
    first_row = table[0:1, :].astype(WIDE)
    last_row = table[LEFT + RIGHT : LEFT + RIGHT + 1, :].astype(WIDE)

    @pl.when(pl.program_id(0) == 0)
    def _():
        dist_ref[...] = jnp.zeros_like(dist_ref)

    q_turned = jnp.transpose(qkv_ref[:, :width])
    go_turned = jnp.transpose(go_ref[...])
    for n in range(keys // QROWS):
        i0 = n * QROWS
        rows = slice(i0, i0 + QROWS)
        begin = max(0, i0 - QROWS)
        end = min(keys, i0 + 2 * QROWS)
        span = end - begin
        apart = distances(i0 - begin, span)[0]
        far_left = apart <= -LEFT
        far_right = apart >= RIGHT
        key_of = lax.broadcasted_iota(jnp.int32, (QROWS, NEAR), 0) + bucket + (i0 - LEFT)
        inside = (bucket > 0) & (bucket < LEFT + RIGHT) & (key_of >= 0) & (key_of < keys)
        for e in range(width // HD):
            lanes = slice(e * HD, (e + 1) * HD)
            q = qkv_ref[rows, lanes]
            k = qkv_ref[:, width + e * HD : width + (e + 1) * HD]
            v = qkv_ref[:, 2 * width + e * HD : 2 * width + (e + 1) * HD]
            go = go_ref[rows, lanes]
            chance = p_ref[e, rows, :]
            wide = chance.astype(WIDE)
            gp = lax.dot_general(go, v, nt, preferred_element_type=WIDE)
            gs = (wide * (gp - jnp.sum(gp * wide, axis=-1, keepdims=True))).astype(NARROW)
            gsw = gs.astype(WIDE)
            window = gsw[:, begin:end]
            turned = jnp.dot(flip, gs[:, begin:end], preferred_element_type=WIDE)
            turned = pltpu.roll(
                turned, (LEFT + 1 - QROWS - (i0 - begin)) % span, 1, stride=1, stride_axis=0
            )[:, :NEAR]
            back = jnp.dot(flip, turned.astype(NARROW), preferred_element_type=WIDE)
            left_sum = row_sum(jnp.where(far_left, window, 0.0))
            right_sum = row_sum(jnp.where(far_right, window, 0.0))
            if begin > 0:
                left_sum += row_sum(gsw[:, :begin])
            if end < keys:
                right_sum += row_sum(gsw[:, end:])
            left_sum *= scale
            right_sum *= scale
            near = (jnp.where(inside, back, 0.0) * scale).astype(NARROW)
            gq = jnp.dot(gs, k, preferred_element_type=WIDE) * scale
            gq += jnp.dot(near, table, preferred_element_type=WIDE)
            gq += left_sum * first_row + right_sum * last_row
            out_ref[rows, lanes] = gq.astype(NARROW)
            q_part = q_turned[lanes, rows]
            qw = q.astype(WIDE)
            dist_ref[:HD, :] += jnp.dot(q_part, near, preferred_element_type=WIDE)
            dist_ref[HD : HD + 1, :HD] += jnp.sum(left_sum * qw, axis=0, keepdims=True)
            dist_ref[HD + 1 : HD + 2, :HD] += jnp.sum(right_sum * qw, axis=0, keepdims=True)
            gk = jnp.dot(q_part, gs, preferred_element_type=WIDE)
            gv = jnp.dot(go_turned[lanes, rows], chance, preferred_element_type=WIDE)
            if n == 0:
                gk_ref[lanes, :] = gk
                gv_ref[lanes, :] = gv
            else:
                gk_ref[lanes, :] += gk
                gv_ref[lanes, :] += gv

    out_ref[:, width : 2 * width] = jnp.transpose(gk_ref[...] * scale).astype(NARROW)
    out_ref[:, 2 * width :] = jnp.transpose(gv_ref[...]).astype(NARROW)
    sums_ref[...] = jnp.sum(out_ref[...].astype(WIDE), axis=0, keepdims=True)


def attend_back(qkv, go, chances, table):
    rows = qkv.shape[0]
    width = qkv.shape[1] // 12
    heads = width // HD
    return pl.pallas_call(
        attend_back_body,
        grid=(4,),
        in_specs=[
            pl.BlockSpec((rows, 3 * width), lambda t: (0, t)),
            pl.BlockSpec((rows, width), lambda t: (0, t)),
            pl.BlockSpec((heads, rows, rows), lambda t: (t, 0, 0)),
            whole(table.shape),
        ],
        out_specs=[
            pl.BlockSpec((rows, 3 * width), lambda t: (0, t)),
            pl.BlockSpec((1, 3 * width), lambda t: (0, t)),
            whole((HD + 8, NEAR)),
        ],
        out_shape=[
            sds((rows, 12 * width), NARROW),
            sds((1, 12 * width), WIDE),
            sds((HD + 8, NEAR), WIDE),
        ],
        scratch_shapes=[pltpu.VMEM((width, rows), WIDE), pltpu.VMEM((width, rows), WIDE)],
        compiler_params=params(),
        cost_estimate=cost(40 * heads * rows * rows * HD, 10 * heads * rows * rows),
        name="attend_back",
    )(qkv, go, chances, table)


def lane_pair(first, second, rows):
    lane = lax.broadcasted_iota(jnp.int32, (rows, LANES), 1)
    return jnp.where(lane == 0, first, jnp.where(lane == 1, second, 0.0))


def row_sum(v):
    return jnp.sum(v, axis=-1, keepdims=True)


def mix_body(taps_count, z_ref, taps_ref, y_ref, sums_ref, pad_ref):
    rows = z_ref.shape[0]

    @pl.when(pl.program_id(0) == 0)
    def _():
        sums_ref[...] = jnp.zeros_like(sums_ref)

    pad_ref[0:PAD, :] = jnp.zeros((PAD, pad_ref.shape[1]), WIDE)
    pad_ref[PAD:, :] = z_ref[...]
    for start in range(0, rows, CHUNK):
        total = None
        for i in range(taps_count):
            begin = start + PAD - taps_count + 1 + i
            term = taps_ref[i : i + 1, :] * pad_ref[begin : begin + CHUNK, :]
            total = term if total is None else total + term
        here = slice(start, start + CHUNK)
        y_ref[here, :] = total
        sums_ref[here, :] += lane_pair(row_sum(total), row_sum(total * total), CHUNK)


def causal_mix(z, taps, taps_count):
    rows, cols = z.shape
    block = pl.BlockSpec((rows, cols // 4), lambda t: (0, t))
    return pl.pallas_call(
        functools.partial(mix_body, taps_count),
        grid=(4,),
        in_specs=[block, pl.BlockSpec((taps.shape[0], cols // 4), lambda t: (0, t))],
        out_specs=[block, whole((rows, LANES))],
        out_shape=[sds((rows, cols), WIDE), sds((rows, LANES), WIDE)],
        scratch_shapes=[pltpu.VMEM((rows + PAD, cols // 4), WIDE)],
        compiler_params=params(),
        cost_estimate=cost(2 * taps_count * rows * cols, 8 * rows * cols),
        name="causal_mix",
    )(z, taps)


def depth_stats(sa_ref, sb_ref, here, width):
    sums = (sa_ref[here, :] + sb_ref[here, :]) * (1.0 / width)
    mean = sums[:, 0:1]
    return mean, lax.rsqrt(sums[:, 1:2] - mean * mean + EPSILON)


def filter_out_body(p_ref, y_ref, sa_ref, sb_ref, g_ref, b_ref, *refs):
    w_refs = refs[:5]
    out_ref, low_ref, acc_ref = refs[5:]
    t = pl.program_id(0)
    p = p_ref[0]
    width = out_ref.shape[1]
    mean, std = depth_stats(sa_ref, sb_ref, slice(None), width)
    yn = (y_ref[...] - mean) * std * g_ref[...] + b_ref[...]
    low = (yn * sigmoid(yn)).astype(NARROW)
    low_ref[...] = low

    @pl.when(t == 0)
    def _():
        acc_ref[...] = jnp.zeros_like(acc_ref)

    for r, w in enumerate(weight_blocks(w_refs, t)):
        cols = rel_cols(p, r, width // PLANE_BLOCKS)
        acc_ref[:, cols] += lax.dot_general(
            low, w, (((1,), (1,)), ((), ())), preferred_element_type=WIDE
        )

    @pl.when(t == 3)
    def _():
        out_ref[...] = acc_ref[...].astype(NARROW)


def filter_out(y, sums, gain, bias, w, cols, col_block, p, width):
    rows = y.shape[0]
    block = pl.BlockSpec((rows, cols), lambda t, p: (0, t))
    row = pl.BlockSpec((1, cols), lambda t, p: (0, t))
    return pl.pallas_call(
        filter_out_body,
        grid_spec=pltpu.PrefetchScalarGridSpec(
            num_scalar_prefetch=1,
            grid=(4,),
            in_specs=[
                block, whole((rows, LANES)), whole((rows, LANES)), row, row,
                *weight_specs(w, cols, col_block),
            ],
            out_specs=[whole((rows, width)), block],
            scratch_shapes=[pltpu.VMEM((rows, width), WIDE)],
        ),
        out_shape=[sds((rows, width), NARROW), sds(y.shape, NARROW)],
        compiler_params=params(),
        cost_estimate=cost(2 * rows * width * 4 * cols, 8 * width * cols + 6 * rows * width),
        name="filter_out",
    )(p, y, *sums, gain, bias, *w)


def filter_in_body(p_ref, grad_ref, y_ref, sa_ref, sb_ref, g_ref, b_ref, *refs):
    w_refs = refs[:5]
    gyn_ref, cols_ref, rows_ref = refs[5:]
    t = pl.program_id(0)
    p = p_ref[0]
    width = grad_ref.shape[1]
    acc = None
    for r, w in enumerate(weight_blocks(w_refs, t)):
        cols = rel_cols(p, r, width // PLANE_BLOCKS)
        term = jnp.dot(grad_ref[:, cols], w, preferred_element_type=WIDE)
        acc = term if acc is None else acc + term
    mean, std = depth_stats(sa_ref, sb_ref, slice(None), width)
    unit = (y_ref[...] - mean) * std
    yn = unit * g_ref[...] + b_ref[...]
    logistic = sigmoid(yn)
    gyn = acc * (logistic * (1.0 + yn * (1.0 - logistic)))
    gyn_ref[...] = gyn
    cols_ref[0:1, :] = jnp.sum(gyn * unit, axis=0, keepdims=True)
    cols_ref[1:2, :] = jnp.sum(gyn, axis=0, keepdims=True)
    scaled = gyn * g_ref[...]
    pair = lane_pair(row_sum(scaled), row_sum(scaled * unit), gyn.shape[0])

    @pl.when(t == 0)
    def _():
        rows_ref[...] = pair

    @pl.when(t > 0)
    def _():
        rows_ref[...] += pair


def filter_in(grad, y, sums, gain, bias, w, cols, col_block, p):
    rows, width = grad.shape
    block = pl.BlockSpec((rows, cols), lambda t, p: (0, t))
    row = pl.BlockSpec((1, cols), lambda t, p: (0, t))
    return pl.pallas_call(
        filter_in_body,
        grid_spec=pltpu.PrefetchScalarGridSpec(
            num_scalar_prefetch=1,
            grid=(4,),
            in_specs=[
                whole((rows, width)), block, whole((rows, LANES)), whole((rows, LANES)), row, row,
                *weight_specs(w, cols, col_block),
            ],
            out_specs=[
                block,
                pl.BlockSpec((8, cols), lambda t, p: (0, t)),
                whole((rows, LANES)),
            ],
        ),
        out_shape=[sds(y.shape, WIDE), sds((8, 4 * cols), WIDE), sds((rows, LANES), WIDE)],
        compiler_params=params(),
        cost_estimate=cost(2 * rows * width * 4 * cols, 8 * width * cols + 6 * rows * width),
        name="filter_in",
    )(p, grad, y, *sums, gain, bias, *w)


def mix_back_body(
    taps_count, width, gyn_ref, y_ref, sa_ref, sb_ref, ra_ref, rb_ref, g_ref, z_ref, gate_ref,
    taps_ref, out_ref, grad_ref, gpad_ref, zpad_ref,
):
    rows, cols = z_ref.shape
    zpad_ref[0:PAD, :] = jnp.zeros((PAD, cols), WIDE)
    zpad_ref[PAD:, :] = z_ref[...]
    gpad_ref[rows:, :] = jnp.zeros((PAD, cols), WIDE)
    mean, std = depth_stats(sa_ref, sb_ref, slice(None), width)
    pair = (ra_ref[...] + rb_ref[...]) * (1.0 / width)
    unit = (y_ref[...] - mean) * std
    gpad_ref[0:rows, :] = std * (gyn_ref[...] * g_ref[...] - pair[:, 0:1] - unit * pair[:, 1:2])
    sums = [None] * taps_count
    for start in range(0, rows, CHUNK):
        here = slice(start, start + CHUNK)
        gy = gpad_ref[here, :]
        total = None
        for i in range(taps_count):
            begin = start + taps_count - 1 - i
            term = taps_ref[i : i + 1, :] * gpad_ref[begin : begin + CHUNK, :]
            total = term if total is None else total + term
        for i in range(taps_count):
            begin = start + PAD - taps_count + 1 + i
            part = zpad_ref[begin : begin + CHUNK, :] * gy
            part = jnp.sum(part.reshape(CHUNK // 8, 8, cols), axis=0)
            sums[i] = part if sums[i] is None else sums[i] + part
        gate = gate_ref[here, :]
        first = total * gate
        out_ref[here, :cols] = first.astype(NARROW)
        out_ref[here, cols:] = (total * z_ref[here, :] * (1.0 - gate)).astype(NARROW)
    for i in range(taps_count):
        grad_ref[i : i + 1, :] = jnp.sum(sums[i], axis=0, keepdims=True)


def mix_back(gyn, y, sums, pairs, gain, z, gate, taps, taps_count, width):
    rows, cols = z.shape
    n = cols // 4
    block = pl.BlockSpec((rows, n), lambda t: (0, t))
    row = pl.BlockSpec((1, n), lambda t: (0, t))
    lanes = whole((rows, LANES))
    tap_block = pl.BlockSpec((taps.shape[0], n), lambda t: (0, t))
    return pl.pallas_call(
        functools.partial(mix_back_body, taps_count, width),
        grid=(4,),
        in_specs=[block, block, lanes, lanes, lanes, lanes, row, block, block, tap_block],
        out_specs=[pl.BlockSpec((rows, 2 * n), lambda t: (0, t)), tap_block],
        out_shape=[sds((rows, 2 * cols), NARROW), sds(taps.shape, WIDE)],
        scratch_shapes=[pltpu.VMEM((rows + PAD, n), WIDE), pltpu.VMEM((rows + PAD, n), WIDE)],
        compiler_params=params(),
        cost_estimate=cost(4 * taps_count * rows * cols, 20 * rows * cols),
        name="mix_back",
    )(gyn, y, *sums, *pairs, gain, z, gate, taps)


def halve_body(groups, core_ref, *refs):
    count = sum(len(g) for g in groups)
    ins = list(refs[:count])
    keeps = refs[count : count + len(groups)]
    sends = refs[count + len(groups) :]
    low = core_ref[0] == 0
    for group, keep, send in zip(groups, keeps, sends):
        start = 0
        for n in group:
            ref = ins.pop(0)
            left, right = ref[:, :n], ref[:, n:]
            keep[:, start : start + n] = jnp.where(low, left, right)
            send[:, start : start + n] = jnp.where(low, right, left)
            start += n


def halve(groups, core):
    rows = groups[0][0].shape[0]
    halves = tuple(tuple(w.shape[1] // 2 for w in g) for g in groups)
    flat = [w for g in groups for w in g]
    shapes = [sds((rows, sum(h)), NARROW) for h in halves] * 2
    out = pl.pallas_call(
        functools.partial(halve_body, halves),
        grid_spec=pltpu.PrefetchScalarGridSpec(
            num_scalar_prefetch=1,
            grid=(1,),
            in_specs=[whole(w.shape) for w in flat],
            out_specs=[whole(s.shape) for s in shapes],
        ),
        out_shape=shapes,
        compiler_params=params(),
        cost_estimate=cost(0, 4 * sum(w.size for w in flat)),
        name="halve",
    )(core, *flat)
    return out[: len(groups)], out[len(groups) :]


def join_body(core_ref, keep_ref, came_ref, out_ref):
    low = core_ref[0] == 0
    rows = keep_ref.shape[0]
    keep, came = keep_ref[...], came_ref[...]
    out_ref[:rows, :] = jnp.where(low, keep, came)
    out_ref[rows:, :] = jnp.where(low, came, keep)


def join(keep, came, core):
    rows, cols = keep.shape
    return pl.pallas_call(
        join_body,
        grid_spec=pltpu.PrefetchScalarGridSpec(
            num_scalar_prefetch=1,
            grid=(1,),
            in_specs=[whole((rows, cols)), whole((rows, cols))],
            out_specs=whole((2 * rows, cols)),
        ),
        out_shape=sds((2 * rows, cols), keep.dtype),
        compiler_params=params(),
        cost_estimate=cost(0, 8 * rows * cols),
        name="join",
    )(core, keep, came)


def pack_body(lead, plan, core_ref, *refs):
    out_ref = refs[-1]
    low = core_ref[0] == 0
    out_ref[...] = jnp.zeros_like(out_ref)
    for ref, items in zip(refs[:-1], plan):
        for kind, src, dst in items:
            if kind == "once":
                v = ref[src : src + 1, :]
                out_ref[dst : dst + 1, :] = jnp.where(low, v, 0.0)
            elif kind == "all":
                out_ref[dst : dst + 8, :] = ref[...]
            elif kind == "taps":
                n = ref.shape[1] // 4
                for t in range(4):
                    v = ref[: src, t * n : (t + 1) * n]
                    out_ref[dst : dst + src, 2 * t * n : (2 * t + 1) * n] = jnp.where(low, v, 0.0)
                    out_ref[dst : dst + src, (2 * t + 1) * n : (2 * t + 2) * n] = jnp.where(low, 0.0, v)
            elif kind == "hidden":
                n = ref.shape[1] // 4
                for t in range(4):
                    v = ref[0:1, t * n : (t + 1) * n]
                    out_ref[dst + t : dst + t + 1, :n] = jnp.where(low, v, 0.0)
                    out_ref[dst + t : dst + t + 1, n:] = jnp.where(low, 0.0, v)
            else:
                row, first, step, n = src
                for t in range(4):
                    begin = t * step + first
                    v = ref[row : row + 1, begin : begin + n]
                    out_ref[dst : dst + 1, 2 * t * n : (2 * t + 1) * n] = jnp.where(low, v, 0.0)
                    out_ref[dst : dst + 1, (2 * t + 1) * n : (2 * t + 2) * n] = jnp.where(low, 0.0, v)


def pack(rows, width, core, sources):
    arrays = [a for a, _ in sources]
    plan = tuple(tuple(items) for _, items in sources)
    return pl.pallas_call(
        functools.partial(pack_body, rows, plan),
        grid_spec=pltpu.PrefetchScalarGridSpec(
            num_scalar_prefetch=1,
            grid=(1,),
            in_specs=[whole(a.shape) for a in arrays],
            out_specs=whole((rows, width)),
        ),
        out_shape=sds((rows, width), WIDE),
        compiler_params=params(),
        cost_estimate=cost(0, 8 * rows * width),
        name="pack",
    )(core, *arrays)


def on_device(planes, inputs, lengths, cotangent, *weights_and_rest):
    shards = weights_and_rest[:8]
    norm_gains, biases, kernel, distance_table = weights_and_rest[8:]
    batches, _, rows_here, width = inputs.shape
    parts = 4
    core = lax.axis_index("pair")
    plane = lax.axis_index("plane")
    part = lax.axis_index("tensor")
    quick = planes == PLANE_BLOCKS
    place = plane if quick else plane * 0
    p = place.astype(jnp.int32).reshape(1)

    def other_core(v):
        return lax.ppermute(v, "pair", [(0, 1), (1, 0)])

    def step_x(v):
        return lax.ppermute(v, "plane", [(i, i ^ 1) for i in range(planes)])

    def step_y(v):
        return lax.ppermute(v, "plane", [(i, i ^ 2) for i in range(planes)])

    def over_planes(v):
        if quick:
            return v + step_x(v) + step_y(v) + lax.ppermute(v, "plane", [(i, i ^ 3) for i in range(4)])
        bit = 1
        while bit < planes:
            v = v + lax.ppermute(v, "plane", [(i, i ^ bit) for i in range(planes)])
            bit *= 2
        return v

    def over_parts(v):
        def turn(k):
            return lax.ppermute(v, "tensor", [(i, i ^ k) for i in range(parts)])

        one, two, three = turn(1), turn(2), turn(3)
        return (v + one) + (two + three)

    def fence(*values):
        return lax.optimization_barrier(values) if quick else values

    def column_of(shard):
        return lax.all_gather(shard, "tensor", axis=0)

    def planes_of(column):
        every = lax.all_gather(column, "plane", axis=0)
        rows, cols = column.shape[1:]
        every = every.reshape(PLANE_BLOCKS, planes // PLANE_BLOCKS, parts, rows, cols)
        every = every.transpose(0, 2, 1, 3, 4).reshape(PLANE_BLOCKS, parts, -1, cols)
        return every[0], every[1], every[2], every[3, :2], every[3, 2:]

    def near(column):
        return step_x(column), step_y(column)

    def far(pair):
        return step_y(pair[0][:2]), step_x(pair[1][2:])

    def share(total):
        n = total.shape[0] // 2
        keep = lax.dynamic_slice_in_dim(total, core * n, n, 0)
        came = other_core(lax.dynamic_slice_in_dim(total, (1 - core) * n, n, 0))
        first = jnp.where(core == 0, keep, came).astype(WIDE)
        second = jnp.where(core == 0, came, keep).astype(WIDE)
        return first, second

    def tensor_sum(total):
        return lax.psum_scatter(total, "tensor", scatter_dimension=0)

    def across_x(every):
        return step_x(every[1::2]) if quick else ()

    def across_y(every, rx):
        return step_y(add(every[2], rx[1])) if quick else ()

    def across_end(every, rx, ry):
        if quick:
            return (every[0].astype(WIDE) + rx[0].astype(WIDE) + ry.astype(WIDE)).astype(NARROW)
        return lax.psum_scatter(
            every.reshape(planes, -1, every.shape[-1]), "plane", scatter_dimension=0
        )

    def hop1(grads):
        return (step_x(grads[1]), step_y(grads[3])) if quick else ()

    def hop2(grads, came):
        if not quick:
            return ()
        return step_y(add(grads[4], came[0][1])), step_x(add(grads[2], came[1][1]))

    def hop3(grads, came, last):
        return tensor_sum(gathered(grads, came, last))

    def gathered(grads, came, last):
        own, sx, kx, sy, ky = grads
        if quick:
            return combine(own, came[0], came[1], last[0], last[1])
        blocks = [
            own,
            jnp.concatenate([sx[0], kx]),
            jnp.concatenate([ky, sy[0]]),
            jnp.concatenate([sx[1], sy[1]]),
        ]
        every = jnp.stack(blocks)
        rows = width // planes
        cols = own.shape[-1]
        every = every.reshape(PLANE_BLOCKS, parts, planes // PLANE_BLOCKS, rows, cols)
        every = every.transpose(0, 2, 1, 3, 4).reshape(planes, parts, rows, cols)
        return lax.psum_scatter(every, "plane", scatter_dimension=0)

    def add(a, b):
        return (a.astype(WIDE) + b.astype(WIDE)).astype(NARROW)

    def rejoin(halves, start, cols, groups):
        pieces = [h[:, start : start + cols].reshape(h.shape[0], groups, -1) for h in halves]
        joined = jnp.concatenate(pieces, axis=2)
        return joined[:, 0] if groups == 1 else joined

    def spot(c, t):
        return c * parts + t

    def route(turn):
        pairs = []
        for c in range(2):
            for t in range(parts):
                mb = (turn + t) % 2
                pairs.append((spot(c, t), spot(t // 2, 2 * mb + c)))
        return pairs

    def bring(v):
        blocks = []
        for turn in range(2):
            mb = lax.rem(turn + part, 2)
            block = lax.dynamic_index_in_dim(v[:, 0], mb, 0, False)
            blocks.append(lax.ppermute(block, ("pair", "tensor"), route(turn)))
        return blocks

    def settle(blocks):
        swap = part // 2 == 1
        mine = jnp.concatenate(
            [jnp.where(swap, blocks[1], blocks[0]), jnp.where(swap, blocks[0], blocks[1])], axis=0
        )
        theirs = other_core(mine)
        return jnp.concatenate(
            [jnp.where(core == 0, mine, theirs), jnp.where(core == 0, theirs, mine)], axis=0
        )

    def send_home(v):
        half = v.shape[0] // 2
        mine = lax.dynamic_slice_in_dim(v, core * half, half, 0)
        first, second = mine[: half // 2], mine[half // 2 :]
        swap = part // 2 == 1
        blocks = [jnp.where(swap, second, first), jnp.where(swap, first, second)]
        came = []
        for turn in range(2):
            back = [(b, a) for a, b in route(turn)]
            came.append(lax.ppermute(blocks[turn], ("pair", "tensor"), back))
        return came

    def home(came):
        odd = lax.rem(part, 2) == 1
        return jnp.stack([jnp.where(odd, came[1], came[0]), jnp.where(odd, came[0], came[1])])[:, None]

    (w_e1, w_r1, w_proj, w_merge, w_fe, w_fr, w_e2, w_r2) = shards
    core1 = core.astype(jnp.int32).reshape(1)
    ffc = w_e1.shape[1] // 2
    qc = w_proj.shape[2] // 2
    cc = w_fe.shape[2] // 2
    groups = [
        [w_e1],
        [w_r1],
        [w_proj[:, 0], w_proj[:, 1], w_proj[:, 2], w_merge],
        [w_fe[:, 0], w_fe[:, 1], w_fr, w_e2],
        [w_r2],
    ]
    keeps, sends = halve(groups, core1)
    pieces = fence(*[join(k, other_core(v), core1) for k, v in zip(keeps, sends)])

    gains = norm_gains.astype(WIDE)
    bias = biases.astype(WIDE)
    gain_row = lambda i: gains[i : i + 1]
    bias_row = lambda i: bias[i : i + 1]
    stride = w_e1.shape[1] * parts // width

    def pick(v):
        lead = v.shape[0]
        v = v.reshape(lead, parts, 2, -1)
        return lax.dynamic_index_in_dim(v, core, 2, False).reshape(lead, -1)

    hidden1 = pick(bias[11 : 11 + stride].reshape(1, -1))
    hidden2 = pick(bias[11 + stride : 11 + 2 * stride].reshape(1, -1))
    qb = pick(bias_row(6)).reshape(parts, 1, -1)
    vb = pick(bias_row(7)).reshape(parts, 1, -1)
    qkv_bias = jnp.concatenate([qb, jnp.zeros_like(qb), vb], axis=1).reshape(1, -1)
    taps_count = kernel.shape[0]
    taps = jnp.pad(pick(kernel.astype(WIDE)), ((0, PAD - taps_count), (0, 0)))
    depth_gain = pick(gain_row(3))
    depth_bias = pick(bias_row(3))
    buckets = distance_table.shape[0]
    table = jnp.pad(distance_table, ((0, NEAR - buckets), (0, 0)))

    pair_lengths = jnp.stack([lengths[:, 0], other_core(lengths[:, 0])])
    from_pair = jnp.bitwise_xor(lax.rem(part, 2), core)
    length = pair_lengths[from_pair, part // 2]
    rows_all = parts * inputs.shape[2]
    live = (jnp.arange(rows_all) < length).astype(WIDE)[:, None]

    col_e1 = column_of(pieces[0])
    r1c = column_of(pieces[1])
    attc = column_of(pieces[2])
    col_c = column_of(pieces[3])
    if quick:
        sd = pieces[4]
        sx, sy = step_x(sd), step_y(sd)
        sz = step_y(sx)
        col_e1, sx, sy, sz, source = fence(col_e1, sx, sy, sz, inputs)
        r2 = (column_of(jnp.stack([sd, sx, sy, sz])),) * PLANE_BLOCKS
        e1n, blocks = near(col_e1), bring(source)
        e1n, r1c, blocks, source = fence(e1n, r1c, blocks, cotangent)
        e1f, r1n, x0 = far(e1n), near(r1c), settle(blocks)
        cot = bring(source)
        e1f, e1n, r1n, attc, x0, cot = fence(e1f, e1n, r1n, attc, x0, cot)
        e1 = (col_e1, *e1n, *e1f)
        r1f, attn = far(r1n), near(attc)
    else:
        rows, cols = pieces[4].shape
        every = lax.all_gather(pieces[4], "plane", axis=0).reshape(PLANE_BLOCKS, -1, cols)
        r2 = (column_of(every),) * PLANE_BLOCKS
        x0 = settle(bring(inputs))
        e1 = planes_of(col_e1)
        r1 = planes_of(r1c)
        att = planes_of(attc)
        fil = planes_of(col_c[:, :, : 3 * cc])
        e2 = planes_of(col_c[:, :, 3 * cc :])
    x0 = x0.astype(WIDE)
    a1, u1, s1 = norm_expand("ff", x0, None, 0.5, gain_row(0), bias_row(0), e1, ffc, 0, p, hidden1)
    if quick:
        cot = settle(cot)
        r1f, r1n, attn, s1, cot = fence(r1f, r1n, attn, s1, cot)
        r1, attf = (r1c, *r1n, *r1f), far(attn)
    f1 = reduce_mm(s1, r1, ffc, 0, p, width)
    if quick:
        attf, attn, f1, col_c = fence(attf, attn, f1, col_c)
        att = (attc, *attn, *attf)
    f1o = other_core(f1)
    x1, bn, qkv = norm_expand(
        "qkv", x0, (f1, f1o, bias_row(9)), 0.5, gain_row(1), bias_row(1), att, 3 * qc, 0, p, qkv_bias
    )
    if quick:
        qkv, col_c = fence(qkv, col_c)
        filc, e2c = col_c[:, :, : 3 * cc], col_c[:, :, 3 * cc :]
        filn = near(filc)
    o, chances = attend(qkv, table, length.reshape(1))
    if quick:
        filn, o, e2c = fence(filn, o, e2c)
        filf, e2n = far(filn), near(e2c)
    f2 = reduce_mm(o, att, qc, 3, p, width)
    if quick:
        filf, filn, f2 = fence(filf, filn, f2)
        fil = (filc, *filn, *filf)
    f2o = other_core(f2)
    x2, cn, gate, z = norm_expand(
        "conv", x1, (f2, f2o, bias_row(8)), 1.0, gain_row(2), bias_row(2), fil, 2 * cc, 0, p, None
    )
    y, y_sums = causal_mix(z, taps, taps_count)
    if quick:
        e2n, y_sums = fence(e2n, y_sums)
        e2f = far(e2n)
    y_sums = (y_sums, other_core(y_sums))
    f3, w = filter_out(y, y_sums, depth_gain, depth_bias, fil, cc, 2, p, width)
    if quick:
        e2f, f3 = fence(e2f, f3)
        e2 = (e2c, *e2n, *e2f)
    else:
        cot = settle(bring(cotangent))
    f3o = other_core(f3)
    x3, a2, u2, s2 = norm_expand(
        "ff", x2, (f3, f3o, jnp.zeros((1, width), WIDE)), 1.0, gain_row(4), bias_row(4),
        e2, ffc, 0, p, hidden2,
    )
    f4 = reduce_mm(s2, r2, ffc, 0, p, width)
    out_rows, gx4, gf2, sums_final = final_norm(
        x3, f4, other_core(f4), bias_row(10), cot, live, gain_row(5), bias_row(5)
    )

    g_r2 = wgrad_flat([gf2], [s2], p)
    g_r2, gf2 = fence(g_r2, gf2)
    z_r2 = tensor_sum(g_r2)
    gu2, gc2 = back_expand("ff", gf2, r2, ffc, 0, p, u2)
    g_e2 = wgrad([a2], [gu2], p)
    g_e2, gu2 = fence(g_e2, gu2)
    e2h1 = hop1(g_e2)
    b4 = reduce_mm(gu2, e2, ffc, 0, p, width)
    gx3, gw, sums3 = norm_back(1.0, x3, gx4, b4, other_core(b4), gain_row(4))
    gyn, depth_cols, depth_rows = filter_in(
        gw, y, y_sums, depth_gain, depth_bias, fil, cc, 2, p
    )
    depth_rows = (depth_rows, other_core(depth_rows))
    gg, taps_grad = mix_back(
        gyn, y, y_sums, depth_rows, depth_gain, z, gate, taps, taps_count, width
    )
    e2h1, gg = fence(e2h1, gg)
    e2h2 = hop2(g_e2, e2h1)
    g_fil = wgrad_flat([cn, gw], [gg, w], p)
    z_fil = tensor_sum(g_fil)
    b3 = reduce_mm(gg, fil, 2 * cc, 0, p, width)
    e2h2, b3, g_fil = fence(e2h2, b3, g_fil)
    z_e2 = hop3(g_e2, e2h1, e2h2)
    gx2, gm, sums2 = norm_back(1.0, x2, gx3, b3, other_core(b3), gain_row(2))
    go = back_expand("low", gm, att, qc, 3, p)
    go, z_r2 = fence(go, z_r2)
    r2x = across_x(z_r2)
    gqkv, gqkv_sums, table_grad = attend_back(qkv, go, chances, table)
    g_att = wgrad([bn, gm], [gqkv, o], p)
    g_att, gqkv, r2x = fence(g_att, gqkv, r2x)
    atth1 = hop1(g_att)
    b2 = reduce_mm(gqkv, att, 3 * qc, 0, p, width)
    gx1, gf1, sums1 = norm_back(0.5, x1, gx2, b2, other_core(b2), gain_row(1))
    g_r1 = wgrad([gf1], [s1], p)
    g_r1, gf1, atth1 = fence(g_r1, gf1, atth1)
    r1h1 = hop1(g_r1)
    atth2 = hop2(g_att, atth1)
    gu1, gc1 = back_expand("ff", gf1, r1, ffc, 0, p, u1)
    g_e1 = wgrad([a1], [gu1], p)
    outputs = send_home(out_rows)
    atth2, r1h1, g_e1, gu1, z_fil, outputs = fence(atth2, r1h1, g_e1, gu1, z_fil, outputs)
    e1h1 = hop1(g_e1)
    r1h2 = hop2(g_r1, r1h1)
    z_att = hop3(g_att, atth1, atth2)
    b1 = reduce_mm(gu1, e1, ffc, 0, p, width)
    gx0, _, sums0 = norm_back(1.0, x0, gx1, b1, other_core(b1), gain_row(0))

    table_rows = -(-buckets // 8)
    tail = jnp.transpose(table_grad[:HD])[1 : buckets - 1]
    ends = table_grad[HD : HD + 2, :HD]
    tail = jnp.concatenate([ends[:1], tail, ends[1:]], axis=0)
    tail = jnp.pad(tail, ((0, 8 * table_rows - buckets), (0, 0)))
    tail = tail.reshape(table_rows, 8, HD).transpose(1, 0, 2).reshape(8, table_rows * HD)
    tail = jnp.pad(tail, ((0, 0), (0, width - table_rows * HD)))
    small = pack(
        64, width, core1,
        [
            (sums_final, [("once", 0, 5), ("once", 1, 11), ("once", 2, 16)]),
            (sums3, [("once", 0, 4), ("once", 1, 10)]),
            (sums2, [("once", 0, 2), ("once", 1, 8), ("once", 2, 14)]),
            (sums1, [("once", 0, 1), ("once", 1, 7), ("once", 2, 15)]),
            (sums0, [("once", 0, 0), ("once", 1, 6)]),
            (gqkv_sums, [("row", (0, 0, 3 * qc, qc), 12), ("row", (0, 2 * qc, 3 * qc, qc), 13)]),
            (depth_cols, [("row", (0, 0, cc, cc), 3), ("row", (1, 0, cc, cc), 9)]),
            (gc1, [("hidden", 0, 17)]),
            (gc2, [("hidden", 0, 21)]),
            (taps_grad, [("taps", taps_count, 25)]),
            (tail, [("all", 0, 56)]),
        ],
    )
    half = small.shape[0] // 2
    mine = lax.dynamic_slice_in_dim(small, core * half, half, 0)
    came = other_core(lax.dynamic_slice_in_dim(small, (1 - core) * half, half, 0))
    r1h2, e1h1, gx0, came, z_e2 = fence(r1h2, e1h1, gx0, came, z_e2)
    e1h2 = hop2(g_e1, e1h1)
    z_r1 = hop3(g_r1, r1h1, r1h2)
    planes_came = over_planes(mine + came)
    e1h2, planes_came = fence(e1h2, planes_came)
    t_e1, planes_came = fence(gathered(g_e1, e1h1, e1h2), planes_came)
    z_e1 = tensor_sum(t_e1)
    filx, r2y = across_x(z_fil), across_y(z_r2, r2x)
    homeward = send_home(gx0.astype(NARROW))
    mine = over_parts(planes_came)
    filx, r2y, mine, homeward, z_att = fence(filx, r2y, mine, homeward, z_att)
    fily = across_y(z_fil, filx)
    e2_grad, att_grad = share(z_e2), share(z_att)
    theirs = other_core(mine)
    r2_grad = share(across_end(z_r2, r2x, r2y))
    fil_grad = share(across_end(z_fil, filx, fily))
    small = jnp.concatenate(
        [jnp.where(core == 0, mine, theirs), jnp.where(core == 0, theirs, mine)], axis=0
    )
    outputs = home(outputs)
    input_grad = home(homeward).astype(WIDE)
    r1_grad, e1_grad = share(z_r1), share(z_e1)
    gains_grad = small[0:6]
    bias_grad = small[6:25]
    taps_t = small[25 : 25 + taps_count]
    table_t = small[56:64, : table_rows * HD].reshape(8, table_rows, HD).transpose(1, 0, 2)
    table_t = table_t.reshape(8 * table_rows, HD)[:buckets]
    return (
        outputs,
        input_grad,
        rejoin(e1_grad, 0, ffc, 1),
        rejoin(r1_grad, 0, ffc, 1),
        rejoin(att_grad, 0, 3 * qc, 3),
        rejoin(att_grad, 3 * qc, qc, 1),
        rejoin(fil_grad, 0, 2 * cc, 2),
        rejoin(fil_grad, 2 * cc, cc, 1),
        rejoin(e2_grad, 0, ffc, 1),
        rejoin(r2_grad, 0, ffc, 1),
        gains_grad,
        bias_grad,
        taps_t,
        table_t,
    )


def solution(mesh):
    dp = mesh.shape["dp"]
    tensor = mesh.shape["tensor"]
    split = Mesh(mesh.devices.reshape(dp // 2, 2, tensor), ("plane", "pair", "tensor"))
    both = ("plane", "pair")
    rows = P(None, both, "tensor", None)
    flat = P(both, "tensor")
    deep = P(both, None, "tensor")
    weights = (flat, flat, deep, flat, deep, flat, flat, flat)
    small = (P(), P(), P(), P())
    return jax.shard_map(
        functools.partial(on_device, dp // 2),
        mesh=split,
        in_specs=(rows, P(None, both), rows, *weights, *small),
        out_specs=(rows, rows, *weights, *small),
        check_vma=False,
    )
```

```python
import functools

import jax
import jax.numpy as jnp
from jax import lax
from jax.experimental import pallas as pl
from jax.experimental.pallas import tpu as pltpu
from jax.sharding import Mesh
from jax.sharding import PartitionSpec as P

HD = 64
LEFT = 64
RIGHT = 8
EPSILON = 1e-05
MASKED = -1e30
WIDE = jnp.float32
NARROW = jnp.bfloat16
CHUNK = 256
MIX_CHUNK = 64
QROWS = 256
BROWS = 512
NEAR = 128
VMEM_BYTES = 48 * 1024 * 1024
PLANE_BLOCKS = 4
LANES = 128
COST_PART = 0.0005
PAD = 32


def sds(shape, dtype):
    return jax.ShapeDtypeStruct(shape, dtype)


def params(parallel=1):
    return pltpu.CompilerParams(
        dimension_semantics=("arbitrary",) * parallel, vmem_limit_bytes=VMEM_BYTES
    )


def cost(flops, moved, exps=0):
    return pl.CostEstimate(
        flops=int(flops * COST_PART), bytes_accessed=int(moved * COST_PART), transcendentals=0
    )


def whole(shape):
    return pl.BlockSpec(shape, lambda *_: (0,) * len(shape))


def rel_cols(p, r, width):
    return pl.ds(pl.multiple_of(jnp.bitwise_xor(p, r) * width, width), width)


def weight_specs(w, cols, col_block):
    if len(w) == PLANE_BLOCKS:
        shape = (1, 1, w[0].shape[2], cols)
        return [
            pl.BlockSpec(shape, functools.partial(lambda r, t, p: (t, r, 0, col_block), r))
            for r in range(PLANE_BLOCKS)
        ]
    shape = (1, w[0].shape[1], cols)
    return [
        pl.BlockSpec(shape, lambda t, p: (t, 0, col_block)),
        pl.BlockSpec(shape, lambda t, p: (t, 0, col_block)),
        pl.BlockSpec(shape, lambda t, p: (t, 0, col_block)),
        pl.BlockSpec(shape, lambda t, p: (jnp.minimum(t, 1), 0, col_block)),
        pl.BlockSpec(shape, lambda t, p: (jnp.maximum(t - 2, 0), 0, col_block)),
    ]


def weight_blocks(w_refs, t):
    if len(w_refs) == PLANE_BLOCKS:
        return [ref[0, 0] for ref in w_refs]
    own, wx, wy, da, db = w_refs
    return own[0], wx[0], wy[0], jnp.where(t < 2, da[0], db[0])


def sigmoid(v):
    return 1.0 / (1.0 + jnp.exp(-v))


def norm_stats(v):
    mean = jnp.mean(v, axis=-1, keepdims=True)
    center = v - mean
    inv_std = lax.rsqrt(jnp.mean(center * center, axis=-1, keepdims=True) + EPSILON)
    return center * inv_std, inv_std


def expand_body(kind, merged, scale, nw, p_ref, *refs):
    refs = list(refs)
    x_ref = refs.pop(0)
    if merged:
        pa_ref, pb_ref, ob_ref = refs[:3]
        refs = refs[3:]
    g_ref, b_ref = refs[:2]
    w_refs = refs[2 : 2 + nw]
    refs = refs[2 + nw :]
    if kind != "conv":
        hb_ref = refs.pop(0)
    if merged:
        xn_ref = refs.pop(0)
    a_ref = refs.pop(0)
    outs = refs
    t = pl.program_id(0)
    p = p_ref[0]
    width = x_ref.shape[1] // PLANE_BLOCKS

    @pl.when(t == 0)
    def _():
        def step(i, carry):
            rows = pl.ds(pl.multiple_of(i * CHUNK, CHUNK), CHUNK)
            v = x_ref[rows, :]
            if merged:
                branch = pa_ref[rows, :].astype(WIDE) + pb_ref[rows, :].astype(WIDE)
                v = v + scale * (branch + ob_ref[...])
                xn_ref[rows, :] = v
            unit, _ = norm_stats(v)
            a_ref[rows, :] = (unit * g_ref[...] + b_ref[...]).astype(NARROW)
            return carry

        lax.fori_loop(0, x_ref.shape[0] // CHUNK, step, 0)

    acc = None
    for r, w in enumerate(weight_blocks(w_refs, t)):
        term = jnp.dot(a_ref[:, rel_cols(p, r, width)], w, preferred_element_type=WIDE)
        acc = term if acc is None else acc + term
    if kind == "ff":
        u = acc + hb_ref[...]
        outs[0][...] = u
        outs[1][...] = (u * sigmoid(u)).astype(NARROW)
    elif kind == "qkv":
        outs[0][...] = (acc + hb_ref[...]).astype(NARROW)
    else:
        half = acc.shape[1] // 2
        gate = sigmoid(acc[:, half:])
        outs[0][...] = gate
        outs[1][...] = acc[:, :half] * gate


def norm_expand(kind, x, merge, scale, gain, bias, w, cols, col_block, p, hidden_bias):
    rows, width = x.shape
    merged = merge is not None
    ins = [x]
    specs = [whole((rows, width))]
    if merged:
        ins += list(merge)
        specs += [whole((rows, width)), whole((rows, width)), whole((1, width))]
    ins += [gain, bias, *w]
    specs += [whole((1, width)), whole((1, width)), *weight_specs(w, cols, col_block)]
    if kind != "conv":
        ins.append(hidden_bias)
        specs.append(pl.BlockSpec((1, cols), lambda t, p: (0, t)))
    shapes, out_specs = [], []
    if merged:
        shapes.append(sds((rows, width), WIDE))
        out_specs.append(whole((rows, width)))
    shapes.append(sds((rows, width), NARROW))
    out_specs.append(whole((rows, width)))
    if kind == "ff":
        outs = [(cols, WIDE), (cols, NARROW)]
    elif kind == "qkv":
        outs = [(cols, NARROW)]
    else:
        outs = [(cols // 2, WIDE), (cols // 2, WIDE)]
    for out_cols, dtype in outs:
        shapes.append(sds((rows, 4 * out_cols), dtype))
        out_specs.append(pl.BlockSpec((rows, out_cols), lambda t, p: (0, t)))
    return pl.pallas_call(
        functools.partial(expand_body, kind, merged, scale, len(w)),
        grid_spec=pltpu.PrefetchScalarGridSpec(
            num_scalar_prefetch=1, grid=(4,), in_specs=specs, out_specs=out_specs
        ),
        out_shape=shapes,
        compiler_params=params(),
        cost_estimate=cost(2 * rows * width * 4 * cols, 8 * width * cols + 12 * rows * width),
        name="norm_expand_" + kind,
    )(p, *ins)


def reduce_body(nw, p_ref, s_ref, *refs):
    w_refs = refs[:nw]
    out_ref, acc_ref = refs[nw:]
    t = pl.program_id(0)
    p = p_ref[0]
    width = out_ref.shape[1] // PLANE_BLOCKS
    s = s_ref[...]

    @pl.when(t == 0)
    def _():
        acc_ref[...] = jnp.zeros_like(acc_ref)

    for r, w in enumerate(weight_blocks(w_refs, t)):
        cols = rel_cols(p, r, width)
        acc_ref[:, cols] += lax.dot_general(
            s, w, (((1,), (1,)), ((), ())), preferred_element_type=WIDE
        )

    @pl.when(t == 3)
    def _():
        out_ref[...] = acc_ref[...].astype(NARROW)


def reduce_mm(s, w, cols, col_block, p, width):
    rows = s.shape[0]
    return pl.pallas_call(
        functools.partial(reduce_body, len(w)),
        grid_spec=pltpu.PrefetchScalarGridSpec(
            num_scalar_prefetch=1,
            grid=(4,),
            in_specs=[
                pl.BlockSpec((rows, cols), lambda t, p: (0, t)),
                *weight_specs(w, cols, col_block),
            ],
            out_specs=whole((rows, width)),
            scratch_shapes=[pltpu.VMEM((rows, width), WIDE)],
        ),
        out_shape=sds((rows, width), NARROW),
        compiler_params=params(),
        cost_estimate=cost(2 * rows * width * 4 * cols, 8 * width * cols + 2 * rows * width),
        name="reduce_mm",
    )(p, s, *w)


def combine_body(own_ref, rx_ref, ry_ref, fx_ref, fy_ref, out_ref):
    t = pl.program_id(0)
    near = jnp.where(t < 2, rx_ref[0, 0], ry_ref[0, 0])
    far = jnp.where(t < 2, fx_ref[0], fy_ref[0])
    total = own_ref[0].astype(WIDE) + near.astype(WIDE) + far.astype(WIDE)
    out_ref[0] = total.astype(NARROW)


def combine(own, rx, ry, fx, fy):
    rows, cols = own.shape[1:]
    first = lambda t: jnp.minimum(t, 1)
    last = lambda t: jnp.maximum(t - 2, 0)
    return pl.pallas_call(
        combine_body,
        grid=(4,),
        in_specs=[
            pl.BlockSpec((1, rows, cols), lambda t: (t, 0, 0)),
            pl.BlockSpec((1, 1, rows, cols), lambda t: (0, first(t), 0, 0)),
            pl.BlockSpec((1, 1, rows, cols), lambda t: (0, last(t), 0, 0)),
            pl.BlockSpec((1, rows, cols), lambda t: (first(t), 0, 0)),
            pl.BlockSpec((1, rows, cols), lambda t: (last(t), 0, 0)),
        ],
        out_specs=pl.BlockSpec((1, rows, cols), lambda t: (t, 0, 0)),
        out_shape=sds(own.shape, NARROW),
        compiler_params=params(),
        cost_estimate=cost(8 * rows * cols, 32 * rows * cols),
        name="combine",
    )(own, rx, ry, fx, fy)


def write_grads(t, p, pairs, refs):
    def grad(r, put):
        start = 0
        for x_ref, value in pairs:
            width = x_ref.shape[1] // PLANE_BLOCKS
            cols = value.shape[1]
            term = lax.dot_general(
                x_ref[:, rel_cols(p, r, width)],
                value,
                (((0,), (0,)), ((), ())),
                preferred_element_type=WIDE,
            ).astype(NARROW)
            put(slice(start, start + cols), term)
            start += cols

    def into(ref, *place):
        def put(cols, term):
            ref[(*place, slice(None), cols)] = term

        return put

    if len(refs) == 1:
        for r in range(PLANE_BLOCKS):
            grad(r, into(refs[0], 0, r))
        return
    own_ref, sx_ref, kx_ref, sy_ref, ky_ref = refs
    grad(0, into(own_ref, 0))

    @pl.when(t < 2)
    def _():
        grad(1, into(sx_ref, 0, 0))
        grad(3, into(sx_ref, 1, 0))
        grad(2, into(ky_ref, 0))

    @pl.when(t >= 2)
    def _():
        grad(2, into(sy_ref, 0, 0))
        grad(3, into(sy_ref, 1, 0))
        grad(1, into(kx_ref, 0))


def grad_outs(wrows, cols, flat):
    if flat:
        shape = (4, PLANE_BLOCKS, wrows, cols)
        spec = pl.BlockSpec((1, PLANE_BLOCKS, wrows, cols), lambda t, p: (t, 0, 0, 0))
        return [spec], [sds(shape, NARROW)]
    first = lambda t: jnp.minimum(t, 1)
    last = lambda t: jnp.maximum(t - 2, 0)
    specs = [
        pl.BlockSpec((1, wrows, cols), lambda t, p: (t, 0, 0)),
        pl.BlockSpec((2, 1, wrows, cols), lambda t, p: (0, first(t), 0, 0)),
        pl.BlockSpec((1, wrows, cols), lambda t, p: (last(t), 0, 0)),
        pl.BlockSpec((2, 1, wrows, cols), lambda t, p: (0, last(t), 0, 0)),
        pl.BlockSpec((1, wrows, cols), lambda t, p: (first(t), 0, 0)),
    ]
    shapes = [
        sds((4, wrows, cols), NARROW),
        sds((2, 2, wrows, cols), NARROW),
        sds((2, wrows, cols), NARROW),
        sds((2, 2, wrows, cols), NARROW),
        sds((2, wrows, cols), NARROW),
    ]
    return specs, shapes


def expand_from(g_ref, w_refs, t, p):
    width = g_ref.shape[1] // PLANE_BLOCKS
    acc = None
    for r, w in enumerate(weight_blocks(w_refs, t)):
        term = jnp.dot(g_ref[:, rel_cols(p, r, width)], w, preferred_element_type=WIDE)
        acc = term if acc is None else acc + term
    return acc


def reduce_into(acc_ref, value, w_refs, t, p):
    width = acc_ref.shape[1] // PLANE_BLOCKS

    @pl.when(t == 0)
    def _():
        acc_ref[...] = jnp.zeros_like(acc_ref)

    for r, w in enumerate(weight_blocks(w_refs, t)):
        acc_ref[:, rel_cols(p, r, width)] += lax.dot_general(
            value, w, (((1,), (1,)), ((), ())), preferred_element_type=WIDE
        )


def ff_back_body(nr, ne, fr, p_ref, g_ref, a_ref, u_ref, *refs):
    r_refs, e_refs = refs[:nr], refs[nr : nr + ne]
    b_ref, gc_ref = refs[nr + ne : nr + ne + 2]
    outs, acc_ref = refs[nr + ne + 2 : -1], refs[-1]
    t = pl.program_id(0)
    p = p_ref[0]
    grad = expand_from(g_ref, r_refs, t, p)
    u = u_ref[...]
    logistic = sigmoid(u)
    gu = grad * (logistic * (1.0 + u * (1.0 - logistic)))
    gc_ref[...] = jnp.sum(gu, axis=0, keepdims=True)
    low = gu.astype(NARROW)
    reduce_into(acc_ref, low, e_refs, t, p)
    write_grads(t, p, [(g_ref, (u * logistic).astype(NARROW))], outs[:fr])
    write_grads(t, p, [(a_ref, low)], outs[fr:])

    @pl.when(t == 3)
    def _():
        b_ref[...] = acc_ref[...].astype(NARROW)


def ff_back(g, a, u, wr, we, p, flat):
    rows, width = g.shape
    cols = u.shape[1] // 4
    wrows = width // PLANE_BLOCKS
    r_specs, r_shapes = grad_outs(wrows, cols, flat)
    e_specs, e_shapes = grad_outs(wrows, cols, False)
    out = pl.pallas_call(
        functools.partial(ff_back_body, len(wr), len(we), len(r_specs)),
        grid_spec=pltpu.PrefetchScalarGridSpec(
            num_scalar_prefetch=1,
            grid=(4,),
            in_specs=[
                whole((rows, width)),
                whole((rows, width)),
                pl.BlockSpec((rows, cols), lambda t, p: (0, t)),
                *weight_specs(wr, cols, 0),
                *weight_specs(we, cols, 0),
            ],
            out_specs=[
                whole((rows, width)),
                pl.BlockSpec((1, cols), lambda t, p: (0, t)),
                *r_specs,
                *e_specs,
            ],
            scratch_shapes=[pltpu.VMEM((rows, width), WIDE)],
        ),
        out_shape=[sds((rows, width), NARROW), sds((1, 4 * cols), WIDE), *r_shapes, *e_shapes],
        compiler_params=params(),
        cost_estimate=cost(32 * rows * width * cols, 32 * width * cols),
        name="ff_back",
    )(p, g, a, u, *wr, *we)
    g_r = out[2 : 2 + len(r_specs)]
    return out[0], out[1], (g_r[0] if flat else g_r), out[2 + len(r_specs) :]


def norm_back_body(scale, x_ref, gx_ref, pa_ref, pb_ref, g_ref, out_ref, low_ref, sums_ref):
    @pl.when(pl.program_id(0) == 0)
    def _():
        sums_ref[...] = jnp.zeros_like(sums_ref)

    unit, inv_std = norm_stats(x_ref[...])
    grad = pa_ref[...].astype(WIDE) + pb_ref[...].astype(WIDE)
    scaled = grad * g_ref[...]
    gx = gx_ref[...] + inv_std * (
        scaled
        - jnp.mean(scaled, axis=-1, keepdims=True)
        - unit * jnp.mean(scaled * unit, axis=-1, keepdims=True)
    )
    out_ref[...] = gx
    branch = scale * gx
    low_ref[...] = branch.astype(NARROW)
    sums_ref[0:1, :] += jnp.sum(grad * unit, axis=0, keepdims=True)
    sums_ref[1:2, :] += jnp.sum(grad, axis=0, keepdims=True)
    sums_ref[2:3, :] += jnp.sum(branch, axis=0, keepdims=True)


def norm_back(scale, x, gx, pa, pb, gain):
    rows, width = x.shape
    block = pl.BlockSpec((CHUNK, width), lambda i: (i, 0))
    return pl.pallas_call(
        functools.partial(norm_back_body, scale),
        grid=(rows // CHUNK,),
        in_specs=[block, block, block, block, whole((1, width))],
        out_specs=[block, block, whole((8, width))],
        out_shape=[sds((rows, width), WIDE), sds((rows, width), NARROW), sds((8, width), WIDE)],
        compiler_params=params(),
        cost_estimate=cost(20 * rows * width, 18 * rows * width),
        name="norm_back",
    )(x, gx, pa, pb, gain)


def final_body(
    x_ref, pa_ref, pb_ref, ob_ref, cot_ref, live_ref, g_ref, b_ref, y_ref, gx_ref, low_ref, sums_ref
):
    @pl.when(pl.program_id(0) == 0)
    def _():
        sums_ref[...] = jnp.zeros_like(sums_ref)

    branch = pa_ref[...].astype(WIDE) + pb_ref[...].astype(WIDE)
    v = x_ref[...] + 0.5 * (branch + ob_ref[...])
    unit, inv_std = norm_stats(v)
    live = live_ref[...]
    y_ref[...] = ((unit * g_ref[...] + b_ref[...]) * live).astype(NARROW)
    grad = cot_ref[...].astype(WIDE) * live
    scaled = grad * g_ref[...]
    gx = inv_std * (
        scaled
        - jnp.mean(scaled, axis=-1, keepdims=True)
        - unit * jnp.mean(scaled * unit, axis=-1, keepdims=True)
    )
    gx_ref[...] = gx
    half = 0.5 * gx
    low_ref[...] = half.astype(NARROW)
    sums_ref[0:1, :] += jnp.sum(grad * unit, axis=0, keepdims=True)
    sums_ref[1:2, :] += jnp.sum(grad, axis=0, keepdims=True)
    sums_ref[2:3, :] += jnp.sum(half, axis=0, keepdims=True)


def final_norm(x, pa, pb, ob, cot, live, gain, bias):
    rows, width = x.shape
    block = pl.BlockSpec((CHUNK, width), lambda i: (i, 0))
    row = whole((1, width))
    return pl.pallas_call(
        final_body,
        grid=(rows // CHUNK,),
        in_specs=[
            block, block, block, row, block,
            pl.BlockSpec((CHUNK, 1), lambda i: (i, 0)), row, row,
        ],
        out_specs=[block, block, block, whole((8, width))],
        out_shape=[
            sds((rows, width), NARROW),
            sds((rows, width), WIDE),
            sds((rows, width), NARROW),
            sds((8, width), WIDE),
        ],
        compiler_params=params(),
        cost_estimate=cost(24 * rows * width, 18 * rows * width),
        name="final_norm",
    )(x, pa, pb, ob, cot, live, gain, bias)


def distances(i0, keys, rows_here):
    rows = lax.broadcasted_iota(jnp.int32, (rows_here, keys), 0) + i0
    cols = lax.broadcasted_iota(jnp.int32, (rows_here, keys), 1)
    return cols - rows, cols


def head_lanes(rows, width, e):
    lane = lax.broadcasted_iota(jnp.int32, (rows, width), 1)
    return (lane >= e * HD) & (lane < (e + 1) * HD)


def doubled(table, heads):
    return jnp.concatenate([table] * heads, axis=1)


def attend_body(len_ref, qkv_ref, table_ref, o_ref, p_out_ref):
    keys = qkv_ref.shape[0]
    width = qkv_ref.shape[1] // 3
    heads = width // HD
    length = len_ref[0]
    table_turned = jnp.transpose(doubled(table_ref[...], heads))
    k_turned = jnp.transpose(qkv_ref[:, width : 2 * width])
    v = qkv_ref[:, 2 * width :]
    key_live = lax.broadcasted_iota(jnp.int32, (QROWS, keys), 1) < length
    masks = [head_lanes(QROWS, width, e) for e in range(heads)]
    for n in range(keys // QROWS):
        i0 = n * QROWS
        rows = slice(i0, i0 + QROWS)
        begin = max(0, i0 - NEAR)
        end = min(keys, i0 + QROWS + NEAR)
        span = end - begin
        apart = distances(i0 - begin, span, QROWS)[0]
        far_left = apart <= -LEFT
        far_right = apart >= RIGHT
        q_all = qkv_ref[rows, :width]
        merged = None
        for e in range(heads):
            q = jnp.where(masks[e], q_all, jnp.zeros_like(q_all))
            near = jnp.dot(q, table_turned, preferred_element_type=WIDE)
            left, right = near[:, 0:1], near[:, LEFT + RIGHT : LEFT + RIGHT + 1]
            band = jnp.concatenate([near, jnp.zeros((QROWS, span - NEAR), WIDE)], axis=1)
            band = pltpu.roll(band, (i0 - begin + span - LEFT) % span, 1, stride=1, stride_axis=0)
            pieces = [jnp.where(far_left, left, jnp.where(far_right, right, band))]
            if begin > 0:
                pieces.insert(0, jnp.broadcast_to(left, (QROWS, begin)))
            if end < keys:
                pieces.append(jnp.broadcast_to(right, (QROWS, keys - end)))
            rel = jnp.concatenate(pieces, axis=1) if len(pieces) > 1 else pieces[0]
            s = jnp.dot(q, k_turned, preferred_element_type=WIDE)
            s = jnp.where(key_live, (s + rel) * HD ** (-0.5), MASKED)
            top = jnp.max(s, axis=-1, keepdims=True)
            ex = jnp.exp(s - top)
            chance = (ex * (1.0 / row_sum(ex))).astype(NARROW)
            p_out_ref[e, rows, :] = chance
            part = jnp.dot(chance, v, preferred_element_type=WIDE)
            merged = part if merged is None else jnp.where(masks[e], part, merged)
        o_ref[rows, :] = merged.astype(NARROW)


def attend(qkv, table, length):
    rows = qkv.shape[0]
    width = qkv.shape[1] // 12
    heads = width // HD
    return pl.pallas_call(
        attend_body,
        grid_spec=pltpu.PrefetchScalarGridSpec(
            num_scalar_prefetch=1,
            grid=(4,),
            in_specs=[
                pl.BlockSpec((rows, 3 * width), lambda t, n: (0, t)),
                whole(table.shape),
            ],
            out_specs=[
                pl.BlockSpec((rows, width), lambda t, n: (0, t)),
                pl.BlockSpec((heads, rows, rows), lambda t, n: (t, 0, 0)),
            ],
        ),
        out_shape=[sds((rows, 4 * width), NARROW), sds((4 * heads, rows, rows), NARROW)],
        compiler_params=params(),
        cost_estimate=cost(16 * heads * rows * rows * HD, 10 * heads * rows * rows, 4 * heads * rows * rows),
        name="attend",
    )(length, qkv, table)


def attend_back_parts(qkv_ref, go_ref, p_ref, table_ref, out_ref, sums_ref, dist_ref, gk_ref, gv_ref):
    keys = qkv_ref.shape[0]
    width = qkv_ref.shape[1] // 3
    heads = width // HD
    table = doubled(table_ref[...], heads)
    scale = HD ** (-0.5)
    flip = (
        lax.broadcasted_iota(jnp.int32, (BROWS, BROWS), 0)
        + lax.broadcasted_iota(jnp.int32, (BROWS, BROWS), 1)
        == BROWS - 1
    ).astype(NARROW)
    bucket = lax.broadcasted_iota(jnp.int32, (BROWS, NEAR), 1)
    first_row = table[0:1, :].astype(WIDE)
    last_row = table[LEFT + RIGHT : LEFT + RIGHT + 1, :].astype(WIDE)
    masks = [head_lanes(BROWS, width, e) for e in range(heads)]

    @pl.when(pl.program_id(0) == 0)
    def _():
        dist_ref[...] = jnp.zeros_like(dist_ref)

    q_turned = jnp.transpose(qkv_ref[:, :width])
    go_turned = jnp.transpose(go_ref[...])
    v_turned = jnp.transpose(qkv_ref[:, 2 * width :])
    k = qkv_ref[:, width : 2 * width]
    for n in range(keys // BROWS):
        i0 = n * BROWS
        rows = slice(i0, i0 + BROWS)
        begin = max(0, i0 - NEAR)
        end = min(keys, i0 + BROWS + NEAR)
        span = end - begin
        apart = distances(i0 - begin, span, BROWS)[0]
        far_left = apart <= -LEFT
        far_right = apart >= RIGHT
        key_of = lax.broadcasted_iota(jnp.int32, (BROWS, NEAR), 0) + bucket + (i0 - LEFT)
        inside = (bucket > 0) & (bucket < LEFT + RIGHT) & (key_of >= 0) & (key_of < keys)
        q_wide = qkv_ref[rows, :width].astype(WIDE)
        go_all = go_ref[rows, :]
        merged = None
        for e in range(heads):
            some = slice(e * HD, (e + 1) * HD)
            go = jnp.where(masks[e], go_all, jnp.zeros_like(go_all))
            chance = p_ref[e, rows, :]
            wide = chance.astype(WIDE)
            gp = jnp.dot(go, v_turned, preferred_element_type=WIDE)
            gs = (wide * (gp - row_sum(gp * wide))).astype(NARROW)
            gsw = gs.astype(WIDE)
            window = gsw[:, begin:end]
            turned = jnp.dot(flip, gs[:, begin:end], preferred_element_type=WIDE)
            turned = pltpu.roll(
                turned, (LEFT + 1 - BROWS - (i0 - begin)) % span, 1, stride=1, stride_axis=0
            )[:, :NEAR]
            back = jnp.dot(flip, turned.astype(NARROW), preferred_element_type=WIDE)
            left_sum = row_sum(jnp.where(far_left, window, 0.0))
            right_sum = row_sum(jnp.where(far_right, window, 0.0))
            if begin > 0:
                left_sum += row_sum(gsw[:, :begin])
            if end < keys:
                right_sum += row_sum(gsw[:, end:])
            left_sum *= scale
            right_sum *= scale
            near = (jnp.where(inside, back, 0.0) * scale).astype(NARROW)
            gq = jnp.dot(gs, k, preferred_element_type=WIDE) * scale
            gq += jnp.dot(near, table, preferred_element_type=WIDE)
            gq += left_sum * first_row + right_sum * last_row
            merged = gq if merged is None else jnp.where(masks[e], gq, merged)
            q_part = q_turned[some, rows]
            dist_ref[:HD, :] += jnp.dot(q_part, near, preferred_element_type=WIDE)
            ends = HD + 2 * e
            dist_ref[ends : ends + 1, :] += jnp.sum(left_sum * q_wide, axis=0, keepdims=True)
            dist_ref[ends + 1 : ends + 2, :] += jnp.sum(right_sum * q_wide, axis=0, keepdims=True)
            gk = jnp.dot(q_part, gs, preferred_element_type=WIDE)
            gv = jnp.dot(go_turned[some, rows], chance, preferred_element_type=WIDE)
            if n == 0:
                gk_ref[some, :] = gk
                gv_ref[some, :] = gv
            else:
                gk_ref[some, :] += gk
                gv_ref[some, :] += gv
        out_ref[rows, :width] = merged.astype(NARROW)

    out_ref[:, width : 2 * width] = jnp.transpose(gk_ref[...] * scale).astype(NARROW)
    out_ref[:, 2 * width :] = jnp.transpose(gv_ref[...]).astype(NARROW)
    sums_ref[...] = jnp.sum(out_ref[...].astype(WIDE), axis=0, keepdims=True)


def attend_back_body(
    nw, s_ref, gm_ref, bn_ref, qkv_ref, chance_ref, o_ref, table_ref, *refs
):
    m_refs, w_refs = refs[:nw], refs[nw : 2 * nw]
    b_ref, sums_ref, dist_ref = refs[2 * nw : 2 * nw + 3]
    outs = refs[2 * nw + 3 : -5]
    acc_ref, go_ref, out_ref, gk_ref, gv_ref = refs[-5:]
    t = pl.program_id(0)
    p = s_ref[0]
    go_ref[...] = expand_from(gm_ref, m_refs, t, p).astype(NARROW)
    attend_back_parts(
        qkv_ref, go_ref, chance_ref, table_ref, out_ref, sums_ref, dist_ref, gk_ref, gv_ref
    )
    grad = out_ref[...]
    reduce_into(acc_ref, grad, w_refs, t, p)
    write_grads(t, p, [(bn_ref, grad), (gm_ref, o_ref[...])], outs)

    @pl.when(t == 3)
    def _():
        b_ref[...] = acc_ref[...].astype(NARROW)


def attend_back(gm, bn, qkv, chances, o, table, w, p):
    rows, width = gm.shape
    wrows = width // PLANE_BLOCKS
    cols = qkv.shape[1] // 12
    heads = cols // HD
    g_specs, g_shapes = grad_outs(wrows, 4 * cols, False)
    out = pl.pallas_call(
        functools.partial(attend_back_body, len(w)),
        grid_spec=pltpu.PrefetchScalarGridSpec(
            num_scalar_prefetch=1,
            grid=(4,),
            in_specs=[
                whole((rows, width)),
                whole((rows, width)),
                pl.BlockSpec((rows, 3 * cols), lambda t, p: (0, t)),
                pl.BlockSpec((heads, rows, rows), lambda t, p: (t, 0, 0)),
                pl.BlockSpec((rows, cols), lambda t, p: (0, t)),
                whole(table.shape),
                *weight_specs(w, cols, 3),
                *weight_specs(w, 3 * cols, 0),
            ],
            out_specs=[
                whole((rows, width)),
                pl.BlockSpec((1, 3 * cols), lambda t, p: (0, t)),
                whole((HD + 8, NEAR)),
                *g_specs,
            ],
            scratch_shapes=[
                pltpu.VMEM((rows, width), WIDE),
                pltpu.VMEM((rows, cols), NARROW),
                pltpu.VMEM((rows, 3 * cols), NARROW),
                pltpu.VMEM((cols, rows), WIDE),
                pltpu.VMEM((cols, rows), WIDE),
            ],
        ),
        out_shape=[
            sds((rows, width), NARROW),
            sds((1, 12 * cols), WIDE),
            sds((HD + 8, NEAR), WIDE),
            *g_shapes,
        ],
        compiler_params=params(),
        cost_estimate=cost(40 * heads * rows * rows * HD, 10 * heads * rows * rows),
        name="attend_back",
    )(p, gm, bn, qkv, chances, o, table, *w, *w)
    return out[0], out[1], out[2], out[3:]


def lane_pair(first, second, rows):
    lane = lax.broadcasted_iota(jnp.int32, (rows, LANES), 1)
    return jnp.where(lane == 0, first, jnp.where(lane == 1, second, 0.0))


def row_sum(v):
    return jnp.sum(v, axis=-1, keepdims=True)


def mix_body(taps_count, z_ref, taps_ref, y_ref, sums_ref, pad_ref):
    rows = z_ref.shape[0]

    @pl.when(pl.program_id(0) == 0)
    def _():
        sums_ref[...] = jnp.zeros_like(sums_ref)

    pad_ref[0:PAD, :] = jnp.zeros((PAD, pad_ref.shape[1]), WIDE)
    pad_ref[PAD:, :] = z_ref[...]
    for start in range(0, rows, MIX_CHUNK):
        total = None
        for i in range(taps_count):
            begin = start + PAD - taps_count + 1 + i
            term = taps_ref[i : i + 1, :] * pad_ref[begin : begin + MIX_CHUNK, :]
            total = term if total is None else total + term
        here = slice(start, start + MIX_CHUNK)
        y_ref[here, :] = total
        sums_ref[here, :] += lane_pair(row_sum(total), row_sum(total * total), MIX_CHUNK)


def causal_mix(z, taps, taps_count):
    rows, cols = z.shape
    block = pl.BlockSpec((rows, cols // 4), lambda t: (0, t))
    return pl.pallas_call(
        functools.partial(mix_body, taps_count),
        grid=(4,),
        in_specs=[block, pl.BlockSpec((taps.shape[0], cols // 4), lambda t: (0, t))],
        out_specs=[block, whole((rows, LANES))],
        out_shape=[sds((rows, cols), WIDE), sds((rows, LANES), WIDE)],
        scratch_shapes=[pltpu.VMEM((rows + PAD, cols // 4), WIDE)],
        compiler_params=params(),
        cost_estimate=cost(2 * taps_count * rows * cols, 8 * rows * cols),
        name="causal_mix",
    )(z, taps)


def depth_stats(sa_ref, sb_ref, here, width):
    sums = (sa_ref[here, :] + sb_ref[here, :]) * (1.0 / width)
    mean = sums[:, 0:1]
    return mean, lax.rsqrt(sums[:, 1:2] - mean * mean + EPSILON)


def filter_out_body(p_ref, y_ref, sa_ref, sb_ref, g_ref, b_ref, *refs):
    w_refs = refs[:5]
    out_ref, low_ref, acc_ref = refs[5:]
    t = pl.program_id(0)
    p = p_ref[0]
    width = out_ref.shape[1]
    mean, std = depth_stats(sa_ref, sb_ref, slice(None), width)
    yn = (y_ref[...] - mean) * std * g_ref[...] + b_ref[...]
    low = (yn * sigmoid(yn)).astype(NARROW)
    low_ref[...] = low

    @pl.when(t == 0)
    def _():
        acc_ref[...] = jnp.zeros_like(acc_ref)

    for r, w in enumerate(weight_blocks(w_refs, t)):
        cols = rel_cols(p, r, width // PLANE_BLOCKS)
        acc_ref[:, cols] += lax.dot_general(
            low, w, (((1,), (1,)), ((), ())), preferred_element_type=WIDE
        )

    @pl.when(t == 3)
    def _():
        out_ref[...] = acc_ref[...].astype(NARROW)


def filter_out(y, sums, gain, bias, w, cols, col_block, p, width):
    rows = y.shape[0]
    block = pl.BlockSpec((rows, cols), lambda t, p: (0, t))
    row = pl.BlockSpec((1, cols), lambda t, p: (0, t))
    return pl.pallas_call(
        filter_out_body,
        grid_spec=pltpu.PrefetchScalarGridSpec(
            num_scalar_prefetch=1,
            grid=(4,),
            in_specs=[
                block, whole((rows, LANES)), whole((rows, LANES)), row, row,
                *weight_specs(w, cols, col_block),
            ],
            out_specs=[whole((rows, width)), block],
            scratch_shapes=[pltpu.VMEM((rows, width), WIDE)],
        ),
        out_shape=[sds((rows, width), NARROW), sds(y.shape, NARROW)],
        compiler_params=params(),
        cost_estimate=cost(2 * rows * width * 4 * cols, 8 * width * cols + 6 * rows * width),
        name="filter_out",
    )(p, y, *sums, gain, bias, *w)


def filter_in_body(p_ref, grad_ref, y_ref, sa_ref, sb_ref, g_ref, b_ref, *refs):
    w_refs = refs[:5]
    gyn_ref, cols_ref, rows_ref = refs[5:]
    t = pl.program_id(0)
    p = p_ref[0]
    width = grad_ref.shape[1]
    acc = None
    for r, w in enumerate(weight_blocks(w_refs, t)):
        cols = rel_cols(p, r, width // PLANE_BLOCKS)
        term = jnp.dot(grad_ref[:, cols], w, preferred_element_type=WIDE)
        acc = term if acc is None else acc + term
    mean, std = depth_stats(sa_ref, sb_ref, slice(None), width)
    unit = (y_ref[...] - mean) * std
    yn = unit * g_ref[...] + b_ref[...]
    logistic = sigmoid(yn)
    gyn = acc * (logistic * (1.0 + yn * (1.0 - logistic)))
    gyn_ref[...] = gyn
    cols_ref[0:1, :] = jnp.sum(gyn * unit, axis=0, keepdims=True)
    cols_ref[1:2, :] = jnp.sum(gyn, axis=0, keepdims=True)
    scaled = gyn * g_ref[...]
    pair = lane_pair(row_sum(scaled), row_sum(scaled * unit), gyn.shape[0])

    @pl.when(t == 0)
    def _():
        rows_ref[...] = pair

    @pl.when(t > 0)
    def _():
        rows_ref[...] += pair


def filter_in(grad, y, sums, gain, bias, w, cols, col_block, p):
    rows, width = grad.shape
    block = pl.BlockSpec((rows, cols), lambda t, p: (0, t))
    row = pl.BlockSpec((1, cols), lambda t, p: (0, t))
    return pl.pallas_call(
        filter_in_body,
        grid_spec=pltpu.PrefetchScalarGridSpec(
            num_scalar_prefetch=1,
            grid=(4,),
            in_specs=[
                whole((rows, width)), block, whole((rows, LANES)), whole((rows, LANES)), row, row,
                *weight_specs(w, cols, col_block),
            ],
            out_specs=[
                block,
                pl.BlockSpec((8, cols), lambda t, p: (0, t)),
                whole((rows, LANES)),
            ],
        ),
        out_shape=[sds(y.shape, WIDE), sds((8, 4 * cols), WIDE), sds((rows, LANES), WIDE)],
        compiler_params=params(),
        cost_estimate=cost(2 * rows * width * 4 * cols, 8 * width * cols + 6 * rows * width),
        name="filter_in",
    )(p, grad, y, *sums, gain, bias, *w)


def mix_back_parts(
    taps_count, width, gyn_ref, y_ref, sa_ref, sb_ref, ra_ref, rb_ref, g_ref, z_ref, gate_ref,
    taps_ref, out_ref, grad_ref, gpad_ref, zpad_ref,
):
    rows, cols = z_ref.shape
    zpad_ref[0:PAD, :] = jnp.zeros((PAD, cols), WIDE)
    zpad_ref[PAD:, :] = z_ref[...]
    gpad_ref[rows:, :] = jnp.zeros((PAD, cols), WIDE)
    mean, std = depth_stats(sa_ref, sb_ref, slice(None), width)
    pair = (ra_ref[...] + rb_ref[...]) * (1.0 / width)
    unit = (y_ref[...] - mean) * std
    gpad_ref[0:rows, :] = std * (gyn_ref[...] * g_ref[...] - pair[:, 0:1] - unit * pair[:, 1:2])
    sums = [None] * taps_count
    for start in range(0, rows, MIX_CHUNK):
        here = slice(start, start + MIX_CHUNK)
        gy = gpad_ref[here, :]
        total = None
        for i in range(taps_count):
            begin = start + taps_count - 1 - i
            term = taps_ref[i : i + 1, :] * gpad_ref[begin : begin + MIX_CHUNK, :]
            total = term if total is None else total + term
        for i in range(taps_count):
            begin = start + PAD - taps_count + 1 + i
            part = zpad_ref[begin : begin + MIX_CHUNK, :] * gy
            part = jnp.sum(part.reshape(MIX_CHUNK // 8, 8, cols), axis=0)
            sums[i] = part if sums[i] is None else sums[i] + part
        gate = gate_ref[here, :]
        first = total * gate
        out_ref[here, :cols] = first.astype(NARROW)
        out_ref[here, cols:] = (total * z_ref[here, :] * (1.0 - gate)).astype(NARROW)
    for i in range(taps_count):
        grad_ref[i : i + 1, :] = jnp.sum(sums[i], axis=0, keepdims=True)


def mix_back_body(taps_count, width, nw, s_ref, *refs):
    parts, gate_taps = refs[:8], refs[8:10]
    cn_ref, gw_ref, wact_ref = refs[10:13]
    w_refs = refs[13 : 13 + nw]
    b_ref, grad_ref, flat_ref = refs[13 + nw : 16 + nw]
    acc_ref, out_ref, gpad_ref, zpad_ref = refs[16 + nw :]
    t = pl.program_id(0)
    p = s_ref[0]
    mix_back_parts(
        taps_count, width, *parts, *gate_taps, out_ref, grad_ref, gpad_ref, zpad_ref
    )
    grad = out_ref[...]
    reduce_into(acc_ref, grad, w_refs, t, p)
    write_grads(t, p, [(cn_ref, grad), (gw_ref, wact_ref[...])], [flat_ref])

    @pl.when(t == 3)
    def _():
        b_ref[...] = acc_ref[...].astype(NARROW)


def mix_back(gyn, y, sums, pairs, gain, z, gate, taps, taps_count, cn, gw, act, w, p):
    rows, cols = z.shape
    width = cn.shape[1]
    wrows = width // PLANE_BLOCKS
    n = cols // 4
    block = pl.BlockSpec((rows, n), lambda t, p: (0, t))
    row = pl.BlockSpec((1, n), lambda t, p: (0, t))
    lanes = whole((rows, LANES))
    tap_block = pl.BlockSpec((taps.shape[0], n), lambda t, p: (0, t))
    g_specs, g_shapes = grad_outs(wrows, 3 * n, True)
    return pl.pallas_call(
        functools.partial(mix_back_body, taps_count, width, len(w)),
        grid_spec=pltpu.PrefetchScalarGridSpec(
            num_scalar_prefetch=1,
            grid=(4,),
            in_specs=[
                block, block, lanes, lanes, lanes, lanes, row, block, block, tap_block,
                whole((rows, width)), whole((rows, width)), block,
                *weight_specs(w, 2 * n, 0),
            ],
            out_specs=[whole((rows, width)), tap_block, *g_specs],
            scratch_shapes=[
                pltpu.VMEM((rows, width), WIDE),
                pltpu.VMEM((rows, 2 * n), NARROW),
                pltpu.VMEM((rows + PAD, n), WIDE),
                pltpu.VMEM((rows + PAD, n), WIDE),
            ],
        ),
        out_shape=[sds((rows, width), NARROW), sds(taps.shape, WIDE), *g_shapes],
        compiler_params=params(),
        cost_estimate=cost(4 * taps_count * rows * cols, 20 * rows * cols),
        name="mix_back",
    )(p, gyn, y, *sums, *pairs, gain, z, gate, taps, cn, gw, act, *w)


def halve_body(groups, core_ref, *refs):
    count = sum(len(g) for g in groups)
    ins = list(refs[:count])
    keeps = refs[count : count + len(groups)]
    sends = refs[count + len(groups) :]
    low = core_ref[0] == 0
    for group, keep, send in zip(groups, keeps, sends):
        start = 0
        for n in group:
            ref = ins.pop(0)
            left, right = ref[:, :n], ref[:, n:]
            keep[:, start : start + n] = jnp.where(low, left, right)
            send[:, start : start + n] = jnp.where(low, right, left)
            start += n


def halve(groups, core):
    rows = groups[0][0].shape[0]
    halves = tuple(tuple(w.shape[1] // 2 for w in g) for g in groups)
    flat = [w for g in groups for w in g]
    shapes = [sds((rows, sum(h)), NARROW) for h in halves] * 2
    out = pl.pallas_call(
        functools.partial(halve_body, halves),
        grid_spec=pltpu.PrefetchScalarGridSpec(
            num_scalar_prefetch=1,
            grid=(1,),
            in_specs=[whole(w.shape) for w in flat],
            out_specs=[whole(s.shape) for s in shapes],
        ),
        out_shape=shapes,
        compiler_params=params(),
        cost_estimate=cost(0, 4 * sum(w.size for w in flat)),
        name="halve",
    )(core, *flat)
    return out[: len(groups)], out[len(groups) :]


def join_body(core_ref, keep_ref, came_ref, out_ref):
    low = core_ref[0] == 0
    rows = keep_ref.shape[0]
    keep, came = keep_ref[...], came_ref[...]
    out_ref[:rows, :] = jnp.where(low, keep, came)
    out_ref[rows:, :] = jnp.where(low, came, keep)


def join(keep, came, core):
    rows, cols = keep.shape
    return pl.pallas_call(
        join_body,
        grid_spec=pltpu.PrefetchScalarGridSpec(
            num_scalar_prefetch=1,
            grid=(1,),
            in_specs=[whole((rows, cols)), whole((rows, cols))],
            out_specs=whole((2 * rows, cols)),
        ),
        out_shape=sds((2 * rows, cols), keep.dtype),
        compiler_params=params(),
        cost_estimate=cost(0, 8 * rows * cols),
        name="join",
    )(core, keep, came)


def pack_body(lead, plan, core_ref, *refs):
    out_ref = refs[-1]
    low = core_ref[0] == 0
    out_ref[...] = jnp.zeros_like(out_ref)
    for ref, items in zip(refs[:-1], plan):
        for kind, src, dst in items:
            if kind == "once":
                v = ref[src : src + 1, :]
                out_ref[dst : dst + 1, :] = jnp.where(low, v, 0.0)
            elif kind == "all":
                out_ref[dst : dst + 8, :] = ref[...]
            elif kind == "taps":
                n = ref.shape[1] // 4
                for t in range(4):
                    v = ref[: src, t * n : (t + 1) * n]
                    out_ref[dst : dst + src, 2 * t * n : (2 * t + 1) * n] = jnp.where(low, v, 0.0)
                    out_ref[dst : dst + src, (2 * t + 1) * n : (2 * t + 2) * n] = jnp.where(low, 0.0, v)
            elif kind == "hidden":
                n = ref.shape[1] // 4
                for t in range(4):
                    v = ref[0:1, t * n : (t + 1) * n]
                    out_ref[dst + t : dst + t + 1, :n] = jnp.where(low, v, 0.0)
                    out_ref[dst + t : dst + t + 1, n:] = jnp.where(low, 0.0, v)
            else:
                row, first, step, n = src
                for t in range(4):
                    begin = t * step + first
                    v = ref[row : row + 1, begin : begin + n]
                    out_ref[dst : dst + 1, 2 * t * n : (2 * t + 1) * n] = jnp.where(low, v, 0.0)
                    out_ref[dst : dst + 1, (2 * t + 1) * n : (2 * t + 2) * n] = jnp.where(low, 0.0, v)


def pack(rows, width, core, sources):
    arrays = [a for a, _ in sources]
    plan = tuple(tuple(items) for _, items in sources)
    return pl.pallas_call(
        functools.partial(pack_body, rows, plan),
        grid_spec=pltpu.PrefetchScalarGridSpec(
            num_scalar_prefetch=1,
            grid=(1,),
            in_specs=[whole(a.shape) for a in arrays],
            out_specs=whole((rows, width)),
        ),
        out_shape=sds((rows, width), WIDE),
        compiler_params=params(),
        cost_estimate=cost(0, 8 * rows * width),
        name="pack",
    )(core, *arrays)


def on_device(planes, inputs, lengths, cotangent, *weights_and_rest):
    shards = weights_and_rest[:8]
    norm_gains, biases, kernel, distance_table = weights_and_rest[8:]
    batches, _, rows_here, width = inputs.shape
    parts = 4
    core = lax.axis_index("pair")
    plane = lax.axis_index("plane")
    part = lax.axis_index("tensor")
    quick = planes == PLANE_BLOCKS
    place = plane if quick else plane * 0
    p = place.astype(jnp.int32).reshape(1)

    def other_core(v):
        return lax.ppermute(v, "pair", [(0, 1), (1, 0)])

    def step_x(v):
        return lax.ppermute(v, "plane", [(i, i ^ 1) for i in range(planes)])

    def step_y(v):
        return lax.ppermute(v, "plane", [(i, i ^ 2) for i in range(planes)])

    def over_planes(v):
        if quick:
            return v + step_x(v) + step_y(v) + lax.ppermute(v, "plane", [(i, i ^ 3) for i in range(4)])
        bit = 1
        while bit < planes:
            v = v + lax.ppermute(v, "plane", [(i, i ^ bit) for i in range(planes)])
            bit *= 2
        return v

    def over_parts(v):
        def turn(k):
            return lax.ppermute(v, "tensor", [(i, i ^ k) for i in range(parts)])

        one, two, three = turn(1), turn(2), turn(3)
        return (v + one) + (two + three)

    def fence(*values):
        return lax.optimization_barrier(values) if quick else values

    def column_of(shard):
        return lax.all_gather(shard, "tensor", axis=0)

    def planes_of(column):
        every = lax.all_gather(column, "plane", axis=0)
        rows, cols = column.shape[1:]
        every = every.reshape(PLANE_BLOCKS, planes // PLANE_BLOCKS, parts, rows, cols)
        every = every.transpose(0, 2, 1, 3, 4).reshape(PLANE_BLOCKS, parts, -1, cols)
        return every[0], every[1], every[2], every[3, :2], every[3, 2:]

    def near(column):
        return step_x(column), step_y(column)

    def far(pair):
        return step_y(pair[0][:2]), step_x(pair[1][2:])

    def share(total):
        n = total.shape[0] // 2
        keep = lax.dynamic_slice_in_dim(total, core * n, n, 0)
        came = other_core(lax.dynamic_slice_in_dim(total, (1 - core) * n, n, 0))
        first = jnp.where(core == 0, keep, came).astype(WIDE)
        second = jnp.where(core == 0, came, keep).astype(WIDE)
        return first, second

    def tensor_sum(total):
        return lax.psum_scatter(total, "tensor", scatter_dimension=0)

    def across_x(every):
        return step_x(every[1::2]) if quick else ()

    def across_y(every, rx):
        return step_y(add(every[2], rx[1])) if quick else ()

    def across_end(every, rx, ry):
        if quick:
            return (every[0].astype(WIDE) + rx[0].astype(WIDE) + ry.astype(WIDE)).astype(NARROW)
        return lax.psum_scatter(
            every.reshape(planes, -1, every.shape[-1]), "plane", scatter_dimension=0
        )

    def hop1(grads):
        return (step_x(grads[1]), step_y(grads[3])) if quick else ()

    def hop2(grads, came):
        if not quick:
            return ()
        return step_y(add(grads[4], came[0][1])), step_x(add(grads[2], came[1][1]))

    def hop3(grads, came, last):
        return tensor_sum(gathered(grads, came, last))

    def gathered(grads, came, last):
        own, sx, kx, sy, ky = grads
        if quick:
            return combine(own, came[0], came[1], last[0], last[1])
        blocks = [
            own,
            jnp.concatenate([sx[0], kx]),
            jnp.concatenate([ky, sy[0]]),
            jnp.concatenate([sx[1], sy[1]]),
        ]
        every = jnp.stack(blocks)
        rows = width // planes
        cols = own.shape[-1]
        every = every.reshape(PLANE_BLOCKS, parts, planes // PLANE_BLOCKS, rows, cols)
        every = every.transpose(0, 2, 1, 3, 4).reshape(planes, parts, rows, cols)
        return lax.psum_scatter(every, "plane", scatter_dimension=0)

    def add(a, b):
        return (a.astype(WIDE) + b.astype(WIDE)).astype(NARROW)

    def rejoin(halves, start, cols, groups):
        pieces = [h[:, start : start + cols].reshape(h.shape[0], groups, -1) for h in halves]
        joined = jnp.concatenate(pieces, axis=2)
        return joined[:, 0] if groups == 1 else joined

    def spot(c, t):
        return c * parts + t

    def route(turn):
        pairs = []
        for c in range(2):
            for t in range(parts):
                mb = (turn + t) % 2
                pairs.append((spot(c, t), spot(t // 2, 2 * mb + c)))
        return pairs

    def bring(v):
        blocks = []
        for turn in range(2):
            mb = lax.rem(turn + part, 2)
            block = lax.dynamic_index_in_dim(v[:, 0], mb, 0, False)
            blocks.append(lax.ppermute(block, ("pair", "tensor"), route(turn)))
        return blocks

    def settle(blocks):
        swap = part // 2 == 1
        mine = jnp.concatenate(
            [jnp.where(swap, blocks[1], blocks[0]), jnp.where(swap, blocks[0], blocks[1])], axis=0
        )
        theirs = other_core(mine)
        return jnp.concatenate(
            [jnp.where(core == 0, mine, theirs), jnp.where(core == 0, theirs, mine)], axis=0
        )

    def send_home(v):
        half = v.shape[0] // 2
        mine = lax.dynamic_slice_in_dim(v, core * half, half, 0)
        first, second = mine[: half // 2], mine[half // 2 :]
        swap = part // 2 == 1
        blocks = [jnp.where(swap, second, first), jnp.where(swap, first, second)]
        came = []
        for turn in range(2):
            back = [(b, a) for a, b in route(turn)]
            came.append(lax.ppermute(blocks[turn], ("pair", "tensor"), back))
        return came

    def home(came):
        odd = lax.rem(part, 2) == 1
        return jnp.stack([jnp.where(odd, came[1], came[0]), jnp.where(odd, came[0], came[1])])[:, None]

    (w_e1, w_r1, w_proj, w_merge, w_fe, w_fr, w_e2, w_r2) = shards
    core1 = core.astype(jnp.int32).reshape(1)
    ffc = w_e1.shape[1] // 2
    qc = w_proj.shape[2] // 2
    cc = w_fe.shape[2] // 2
    groups = [
        [w_e1],
        [w_r1],
        [w_proj[:, 0], w_proj[:, 1], w_proj[:, 2], w_merge],
        [w_fe[:, 0], w_fe[:, 1], w_fr, w_e2],
        [w_r2],
    ]
    keeps, sends = halve(groups, core1)
    pieces = fence(*[join(k, other_core(v), core1) for k, v in zip(keeps, sends)])

    gains = norm_gains.astype(WIDE)
    bias = biases.astype(WIDE)
    gain_row = lambda i: gains[i : i + 1]
    bias_row = lambda i: bias[i : i + 1]
    stride = w_e1.shape[1] * parts // width

    def pick(v):
        lead = v.shape[0]
        v = v.reshape(lead, parts, 2, -1)
        return lax.dynamic_index_in_dim(v, core, 2, False).reshape(lead, -1)

    hidden1 = pick(bias[11 : 11 + stride].reshape(1, -1))
    hidden2 = pick(bias[11 + stride : 11 + 2 * stride].reshape(1, -1))
    qb = pick(bias_row(6)).reshape(parts, 1, -1)
    vb = pick(bias_row(7)).reshape(parts, 1, -1)
    qkv_bias = jnp.concatenate([qb, jnp.zeros_like(qb), vb], axis=1).reshape(1, -1)
    taps_count = kernel.shape[0]
    taps = jnp.pad(pick(kernel.astype(WIDE)), ((0, PAD - taps_count), (0, 0)))
    depth_gain = pick(gain_row(3))
    depth_bias = pick(bias_row(3))
    buckets = distance_table.shape[0]
    table = jnp.pad(distance_table, ((0, NEAR - buckets), (0, 0)))

    pair_lengths = jnp.stack([lengths[:, 0], other_core(lengths[:, 0])])
    from_pair = jnp.bitwise_xor(lax.rem(part, 2), core)
    length = pair_lengths[from_pair, part // 2]
    rows_all = parts * inputs.shape[2]
    live = (jnp.arange(rows_all) < length).astype(WIDE)[:, None]

    col_e1 = column_of(pieces[0])
    r1c = column_of(pieces[1])
    attc = column_of(pieces[2])
    col_c = column_of(pieces[3])
    if quick:
        sd = pieces[4]
        sx, sy = step_x(sd), step_y(sd)
        sz = step_y(sx)
        col_e1, sx, sy, sz, source = fence(col_e1, sx, sy, sz, inputs)
        r2 = (column_of(jnp.stack([sd, sx, sy, sz])),) * PLANE_BLOCKS
        e1n, blocks = near(col_e1), bring(source)
        e1n, r1c, blocks, source = fence(e1n, r1c, blocks, cotangent)
        e1f, r1n, x0 = far(e1n), near(r1c), settle(blocks)
        cot = bring(source)
        e1f, e1n, r1n, attc, x0, cot = fence(e1f, e1n, r1n, attc, x0, cot)
        e1 = (col_e1, *e1n, *e1f)
        r1f, attn = far(r1n), near(attc)
    else:
        rows, cols = pieces[4].shape
        every = lax.all_gather(pieces[4], "plane", axis=0).reshape(PLANE_BLOCKS, -1, cols)
        r2 = (column_of(every),) * PLANE_BLOCKS
        x0 = settle(bring(inputs))
        e1 = planes_of(col_e1)
        r1 = planes_of(r1c)
        att = planes_of(attc)
        fil = planes_of(col_c[:, :, : 3 * cc])
        e2 = planes_of(col_c[:, :, 3 * cc :])
    x0 = x0.astype(WIDE)
    a1, u1, s1 = norm_expand("ff", x0, None, 0.5, gain_row(0), bias_row(0), e1, ffc, 0, p, hidden1)
    if quick:
        cot = settle(cot)
        r1f, r1n, attn, s1, cot = fence(r1f, r1n, attn, s1, cot)
        r1, attf = (r1c, *r1n, *r1f), far(attn)
    f1 = reduce_mm(s1, r1, ffc, 0, p, width)
    if quick:
        attf, attn, f1, col_c = fence(attf, attn, f1, col_c)
        att = (attc, *attn, *attf)
    f1o = other_core(f1)
    x1, bn, qkv = norm_expand(
        "qkv", x0, (f1, f1o, bias_row(9)), 0.5, gain_row(1), bias_row(1), att, 3 * qc, 0, p, qkv_bias
    )
    if quick:
        qkv, col_c = fence(qkv, col_c)
        filc, e2c = col_c[:, :, : 3 * cc], col_c[:, :, 3 * cc :]
        filn = near(filc)
    o, chances = attend(qkv, table, length.reshape(1))
    if quick:
        filn, o, e2c = fence(filn, o, e2c)
        filf, e2n = far(filn), near(e2c)
    f2 = reduce_mm(o, att, qc, 3, p, width)
    if quick:
        filf, filn, f2 = fence(filf, filn, f2)
        fil = (filc, *filn, *filf)
    f2o = other_core(f2)
    x2, cn, gate, z = norm_expand(
        "conv", x1, (f2, f2o, bias_row(8)), 1.0, gain_row(2), bias_row(2), fil, 2 * cc, 0, p, None
    )
    y, y_sums = causal_mix(z, taps, taps_count)
    if quick:
        e2n, y_sums = fence(e2n, y_sums)
        e2f = far(e2n)
    y_sums = (y_sums, other_core(y_sums))
    f3, w = filter_out(y, y_sums, depth_gain, depth_bias, fil, cc, 2, p, width)
    if quick:
        e2f, f3 = fence(e2f, f3)
        e2 = (e2c, *e2n, *e2f)
    else:
        cot = settle(bring(cotangent))
    f3o = other_core(f3)
    x3, a2, u2, s2 = norm_expand(
        "ff", x2, (f3, f3o, jnp.zeros((1, width), WIDE)), 1.0, gain_row(4), bias_row(4),
        e2, ffc, 0, p, hidden2,
    )
    f4 = reduce_mm(s2, r2, ffc, 0, p, width)
    out_rows, gx4, gf2, sums_final = final_norm(
        x3, f4, other_core(f4), bias_row(10), cot, live, gain_row(5), bias_row(5)
    )

    b4, gc2, g_r2, g_e2 = ff_back(gf2, a2, u2, r2, e2, p, True)
    g_r2, g_e2, b4 = fence(g_r2, g_e2, b4)
    z_r2 = tensor_sum(g_r2)
    e2h1 = hop1(g_e2)
    gx3, gw, sums3 = norm_back(1.0, x3, gx4, b4, other_core(b4), gain_row(4))
    gyn, depth_cols, depth_rows = filter_in(
        gw, y, y_sums, depth_gain, depth_bias, fil, cc, 2, p
    )
    depth_rows = (depth_rows, other_core(depth_rows))
    b3, taps_grad, g_fil = mix_back(
        gyn, y, y_sums, depth_rows, depth_gain, z, gate, taps, taps_count, cn, gw, w, fil, p
    )
    e2h1, b3, g_fil = fence(e2h1, b3, g_fil)
    e2h2 = hop2(g_e2, e2h1)
    z_fil = tensor_sum(g_fil)
    gx2, gm, sums2 = norm_back(1.0, x2, gx3, b3, other_core(b3), gain_row(2))
    e2h2, gm = fence(e2h2, gm)
    z_e2 = hop3(g_e2, e2h1, e2h2)
    b2, gqkv_sums, table_grad, g_att = attend_back(gm, bn, qkv, chances, o, table, att, p)
    g_att, b2, z_r2 = fence(g_att, b2, z_r2)
    atth1 = hop1(g_att)
    gx1, gf1, sums1 = norm_back(0.5, x1, gx2, b2, other_core(b2), gain_row(1))
    outputs = send_home(out_rows)
    b1, gc1, g_r1, g_e1 = ff_back(gf1, a1, u1, r1, e1, p, False)
    g_r1, g_e1, b1, atth1, outputs = fence(g_r1, g_e1, b1, atth1, outputs)
    r1h1 = hop1(g_r1)
    atth2 = hop2(g_att, atth1)
    gx0, _, sums0 = norm_back(1.0, x0, gx1, b1, other_core(b1), gain_row(0))
    atth2, r1h1, gx0, z_fil = fence(atth2, r1h1, gx0, z_fil)
    e1h1 = hop1(g_e1)
    r1h2 = hop2(g_r1, r1h1)
    z_att = hop3(g_att, atth1, atth2)

    table_rows = -(-buckets // 8)
    tail = jnp.transpose(table_grad[:HD])[1 : buckets - 1]
    ends = table_grad[HD : HD + 2, :HD]
    for e in range(1, qc // HD):
        ends = ends + table_grad[HD + 2 * e : HD + 2 * e + 2, e * HD : (e + 1) * HD]
    tail = jnp.concatenate([ends[:1], tail, ends[1:]], axis=0)
    tail = jnp.pad(tail, ((0, 8 * table_rows - buckets), (0, 0)))
    tail = tail.reshape(table_rows, 8, HD).transpose(1, 0, 2).reshape(8, table_rows * HD)
    tail = jnp.pad(tail, ((0, 0), (0, width - table_rows * HD)))
    small = pack(
        64, width, core1,
        [
            (sums_final, [("once", 0, 5), ("once", 1, 11), ("once", 2, 16)]),
            (sums3, [("once", 0, 4), ("once", 1, 10)]),
            (sums2, [("once", 0, 2), ("once", 1, 8), ("once", 2, 14)]),
            (sums1, [("once", 0, 1), ("once", 1, 7), ("once", 2, 15)]),
            (sums0, [("once", 0, 0), ("once", 1, 6)]),
            (gqkv_sums, [("row", (0, 0, 3 * qc, qc), 12), ("row", (0, 2 * qc, 3 * qc, qc), 13)]),
            (depth_cols, [("row", (0, 0, cc, cc), 3), ("row", (1, 0, cc, cc), 9)]),
            (gc1, [("hidden", 0, 17)]),
            (gc2, [("hidden", 0, 21)]),
            (taps_grad, [("taps", taps_count, 25)]),
            (tail, [("all", 0, 56)]),
        ],
    )
    half = small.shape[0] // 2
    mine = lax.dynamic_slice_in_dim(small, core * half, half, 0)
    came = other_core(lax.dynamic_slice_in_dim(small, (1 - core) * half, half, 0))
    r1h2, e1h1, gx0, came, z_e2 = fence(r1h2, e1h1, gx0, came, z_e2)
    e1h2 = hop2(g_e1, e1h1)
    z_r1 = hop3(g_r1, r1h1, r1h2)
    planes_came = over_planes(mine + came)
    e1h2, planes_came = fence(e1h2, planes_came)
    t_e1, planes_came = fence(gathered(g_e1, e1h1, e1h2), planes_came)
    z_e1 = tensor_sum(t_e1)
    filx, r2x = across_x(z_fil), across_x(z_r2)
    homeward = send_home(gx0.astype(NARROW))
    mine = over_parts(planes_came)
    filx, r2x, mine, homeward, z_att = fence(filx, r2x, mine, homeward, z_att)
    fily, r2y = across_y(z_fil, filx), across_y(z_r2, r2x)
    e2_grad, att_grad = share(z_e2), share(z_att)
    theirs = other_core(mine)
    r2_grad = share(across_end(z_r2, r2x, r2y))
    fil_grad = share(across_end(z_fil, filx, fily))
    small = jnp.concatenate(
        [jnp.where(core == 0, mine, theirs), jnp.where(core == 0, theirs, mine)], axis=0
    )
    outputs = home(outputs)
    input_grad = home(homeward).astype(WIDE)
    r1_grad, e1_grad = share(z_r1), share(z_e1)
    gains_grad = small[0:6]
    bias_grad = small[6:25]
    taps_t = small[25 : 25 + taps_count]
    table_t = small[56:64, : table_rows * HD].reshape(8, table_rows, HD).transpose(1, 0, 2)
    table_t = table_t.reshape(8 * table_rows, HD)[:buckets]
    return (
        outputs,
        input_grad,
        rejoin(e1_grad, 0, ffc, 1),
        rejoin(r1_grad, 0, ffc, 1),
        rejoin(att_grad, 0, 3 * qc, 3),
        rejoin(att_grad, 3 * qc, qc, 1),
        rejoin(fil_grad, 0, 2 * cc, 2),
        rejoin(fil_grad, 2 * cc, cc, 1),
        rejoin(e2_grad, 0, ffc, 1),
        rejoin(r2_grad, 0, ffc, 1),
        gains_grad,
        bias_grad,
        taps_t,
        table_t,
    )


def solution(mesh):
    dp = mesh.shape["dp"]
    tensor = mesh.shape["tensor"]
    split = Mesh(mesh.devices.reshape(dp // 2, 2, tensor), ("plane", "pair", "tensor"))
    both = ("plane", "pair")
    rows = P(None, both, "tensor", None)
    flat = P(both, "tensor")
    deep = P(both, None, "tensor")
    weights = (flat, flat, deep, flat, deep, flat, flat, flat)
    small = (P(), P(), P(), P())
    return jax.shard_map(
        functools.partial(on_device, dp // 2),
        mesh=split,
        in_specs=(rows, P(None, both), rows, *weights, *small),
        out_specs=(rows, rows, *weights, *small),
        check_vma=False,
    )
```

```python
import functools

import jax
import jax.numpy as jnp
from jax import lax
from jax.experimental import pallas as pl
from jax.experimental.pallas import tpu as pltpu
from jax.sharding import Mesh
from jax.sharding import PartitionSpec as P

HD = 64
LEFT = 64
RIGHT = 8
EPSILON = 1e-05
MASKED = -1e30
WIDE = jnp.float32
NARROW = jnp.bfloat16
CHUNK = 256
MIX_CHUNK = 64
QROWS = 256
BROWS = 512
NEAR = 128
VMEM_BYTES = 48 * 1024 * 1024
PLANE_BLOCKS = 4
LANES = 128
COST_PART = 0.0005
PAD = 32


def sds(shape, dtype):
    return jax.ShapeDtypeStruct(shape, dtype)


def params(parallel=1):
    return pltpu.CompilerParams(
        dimension_semantics=("arbitrary",) * parallel, vmem_limit_bytes=VMEM_BYTES
    )


def cost(flops, moved, exps=0):
    return pl.CostEstimate(
        flops=int(flops * COST_PART), bytes_accessed=int(moved * COST_PART), transcendentals=0
    )


def whole(shape):
    return pl.BlockSpec(shape, lambda *_: (0,) * len(shape))


def rel_cols(p, r, width):
    return pl.ds(pl.multiple_of(jnp.bitwise_xor(p, r) * width, width), width)


def weight_specs(w, cols, col_block):
    if len(w) == PLANE_BLOCKS:
        shape = (1, 1, w[0].shape[2], cols)
        return [
            pl.BlockSpec(shape, functools.partial(lambda r, t, p: (t, r, 0, col_block), r))
            for r in range(PLANE_BLOCKS)
        ]
    shape = (1, w[0].shape[1], cols)
    return [
        pl.BlockSpec(shape, lambda t, p: (t, 0, col_block)),
        pl.BlockSpec(shape, lambda t, p: (t, 0, col_block)),
        pl.BlockSpec(shape, lambda t, p: (t, 0, col_block)),
        pl.BlockSpec(shape, lambda t, p: (jnp.minimum(t, 1), 0, col_block)),
        pl.BlockSpec(shape, lambda t, p: (jnp.maximum(t - 2, 0), 0, col_block)),
    ]


def weight_blocks(w_refs, t):
    if len(w_refs) == PLANE_BLOCKS:
        return [ref[0, 0] for ref in w_refs]
    own, wx, wy, da, db = w_refs
    return own[0], wx[0], wy[0], jnp.where(t < 2, da[0], db[0])


def sigmoid(v):
    return 1.0 / (1.0 + jnp.exp(-v))


def norm_stats(v):
    mean = jnp.mean(v, axis=-1, keepdims=True)
    center = v - mean
    inv_std = lax.rsqrt(jnp.mean(center * center, axis=-1, keepdims=True) + EPSILON)
    return center * inv_std, inv_std


def expand_body(kind, merged, scale, nw, p_ref, *refs):
    refs = list(refs)
    x_ref = refs.pop(0)
    if merged:
        pa_ref, pb_ref, ob_ref = refs[:3]
        refs = refs[3:]
    g_ref, b_ref = refs[:2]
    w_refs = refs[2 : 2 + nw]
    refs = refs[2 + nw :]
    if kind != "conv":
        hb_ref = refs.pop(0)
    if merged:
        xn_ref = refs.pop(0)
    a_ref = refs.pop(0)
    outs = refs
    t = pl.program_id(0)
    p = p_ref[0]
    width = x_ref.shape[1] // PLANE_BLOCKS

    @pl.when(t == 0)
    def _():
        def step(i, carry):
            rows = pl.ds(pl.multiple_of(i * CHUNK, CHUNK), CHUNK)
            v = x_ref[rows, :]
            if merged:
                branch = pa_ref[rows, :].astype(WIDE) + pb_ref[rows, :].astype(WIDE)
                v = v + scale * (branch + ob_ref[...])
                xn_ref[rows, :] = v
            unit, _ = norm_stats(v)
            a_ref[rows, :] = (unit * g_ref[...] + b_ref[...]).astype(NARROW)
            return carry

        lax.fori_loop(0, x_ref.shape[0] // CHUNK, step, 0)

    acc = None
    for r, w in enumerate(weight_blocks(w_refs, t)):
        term = jnp.dot(a_ref[:, rel_cols(p, r, width)], w, preferred_element_type=WIDE)
        acc = term if acc is None else acc + term
    if kind == "ff":
        u = acc + hb_ref[...]
        outs[0][...] = u
        outs[1][...] = (u * sigmoid(u)).astype(NARROW)
    elif kind == "qkv":
        outs[0][...] = (acc + hb_ref[...]).astype(NARROW)
    else:
        half = acc.shape[1] // 2
        gate = sigmoid(acc[:, half:])
        outs[0][...] = gate
        outs[1][...] = acc[:, :half] * gate


def norm_expand(kind, x, merge, scale, gain, bias, w, cols, col_block, p, hidden_bias):
    rows, width = x.shape
    merged = merge is not None
    ins = [x]
    specs = [whole((rows, width))]
    if merged:
        ins += list(merge)
        specs += [whole((rows, width)), whole((rows, width)), whole((1, width))]
    ins += [gain, bias, *w]
    specs += [whole((1, width)), whole((1, width)), *weight_specs(w, cols, col_block)]
    if kind != "conv":
        ins.append(hidden_bias)
        specs.append(pl.BlockSpec((1, cols), lambda t, p: (0, t)))
    shapes, out_specs = [], []
    if merged:
        shapes.append(sds((rows, width), WIDE))
        out_specs.append(whole((rows, width)))
    shapes.append(sds((rows, width), NARROW))
    out_specs.append(whole((rows, width)))
    if kind == "ff":
        outs = [(cols, WIDE), (cols, NARROW)]
    elif kind == "qkv":
        outs = [(cols, NARROW)]
    else:
        outs = [(cols // 2, WIDE), (cols // 2, WIDE)]
    for out_cols, dtype in outs:
        shapes.append(sds((rows, 4 * out_cols), dtype))
        out_specs.append(pl.BlockSpec((rows, out_cols), lambda t, p: (0, t)))
    return pl.pallas_call(
        functools.partial(expand_body, kind, merged, scale, len(w)),
        grid_spec=pltpu.PrefetchScalarGridSpec(
            num_scalar_prefetch=1, grid=(4,), in_specs=specs, out_specs=out_specs
        ),
        out_shape=shapes,
        compiler_params=params(),
        cost_estimate=cost(2 * rows * width * 4 * cols, 8 * width * cols + 12 * rows * width),
        name="norm_expand_" + kind,
    )(p, *ins)


def reduce_body(nw, p_ref, s_ref, *refs):
    w_refs = refs[:nw]
    out_ref, acc_ref = refs[nw:]
    t = pl.program_id(0)
    p = p_ref[0]
    width = out_ref.shape[1] // PLANE_BLOCKS
    s = s_ref[...]

    @pl.when(t == 0)
    def _():
        acc_ref[...] = jnp.zeros_like(acc_ref)

    for r, w in enumerate(weight_blocks(w_refs, t)):
        cols = rel_cols(p, r, width)
        acc_ref[:, cols] += lax.dot_general(
            s, w, (((1,), (1,)), ((), ())), preferred_element_type=WIDE
        )

    @pl.when(t == 3)
    def _():
        out_ref[...] = acc_ref[...].astype(NARROW)


def reduce_mm(s, w, cols, col_block, p, width):
    rows = s.shape[0]
    return pl.pallas_call(
        functools.partial(reduce_body, len(w)),
        grid_spec=pltpu.PrefetchScalarGridSpec(
            num_scalar_prefetch=1,
            grid=(4,),
            in_specs=[
                pl.BlockSpec((rows, cols), lambda t, p: (0, t)),
                *weight_specs(w, cols, col_block),
            ],
            out_specs=whole((rows, width)),
            scratch_shapes=[pltpu.VMEM((rows, width), WIDE)],
        ),
        out_shape=sds((rows, width), NARROW),
        compiler_params=params(),
        cost_estimate=cost(2 * rows * width * 4 * cols, 8 * width * cols + 2 * rows * width),
        name="reduce_mm",
    )(p, s, *w)


def combine_body(own_ref, rx_ref, ry_ref, fx_ref, fy_ref, out_ref):
    t = pl.program_id(0)
    near = jnp.where(t < 2, rx_ref[0, 0], ry_ref[0, 0])
    far = jnp.where(t < 2, fx_ref[0], fy_ref[0])
    total = own_ref[0].astype(WIDE) + near.astype(WIDE) + far.astype(WIDE)
    out_ref[0] = total.astype(NARROW)


def combine(own, rx, ry, fx, fy):
    rows, cols = own.shape[1:]
    first = lambda t: jnp.minimum(t, 1)
    last = lambda t: jnp.maximum(t - 2, 0)
    return pl.pallas_call(
        combine_body,
        grid=(4,),
        in_specs=[
            pl.BlockSpec((1, rows, cols), lambda t: (t, 0, 0)),
            pl.BlockSpec((1, 1, rows, cols), lambda t: (0, first(t), 0, 0)),
            pl.BlockSpec((1, 1, rows, cols), lambda t: (0, last(t), 0, 0)),
            pl.BlockSpec((1, rows, cols), lambda t: (first(t), 0, 0)),
            pl.BlockSpec((1, rows, cols), lambda t: (last(t), 0, 0)),
        ],
        out_specs=pl.BlockSpec((1, rows, cols), lambda t: (t, 0, 0)),
        out_shape=sds(own.shape, NARROW),
        compiler_params=params(),
        cost_estimate=cost(8 * rows * cols, 32 * rows * cols),
        name="combine",
    )(own, rx, ry, fx, fy)


def write_grads(t, p, pairs, refs):
    def grad(r, put):
        start = 0
        for x_ref, value in pairs:
            width = x_ref.shape[1] // PLANE_BLOCKS
            cols = value.shape[1]
            term = lax.dot_general(
                x_ref[:, rel_cols(p, r, width)],
                value,
                (((0,), (0,)), ((), ())),
                preferred_element_type=WIDE,
            ).astype(NARROW)
            put(slice(start, start + cols), term)
            start += cols

    def into(ref, *place):
        def put(cols, term):
            ref[(*place, slice(None), cols)] = term

        return put

    if len(refs) == 1:
        for r in range(PLANE_BLOCKS):
            grad(r, into(refs[0], 0, r))
        return
    own_ref, sx_ref, kx_ref, sy_ref, ky_ref = refs
    grad(0, into(own_ref, 0))

    @pl.when(t < 2)
    def _():
        grad(1, into(sx_ref, 0, 0))
        grad(3, into(sx_ref, 1, 0))
        grad(2, into(ky_ref, 0))

    @pl.when(t >= 2)
    def _():
        grad(2, into(sy_ref, 0, 0))
        grad(3, into(sy_ref, 1, 0))
        grad(1, into(kx_ref, 0))


def grad_outs(wrows, cols, flat):
    if flat:
        shape = (4, PLANE_BLOCKS, wrows, cols)
        spec = pl.BlockSpec((1, PLANE_BLOCKS, wrows, cols), lambda t, p: (t, 0, 0, 0))
        return [spec], [sds(shape, NARROW)]
    first = lambda t: jnp.minimum(t, 1)
    last = lambda t: jnp.maximum(t - 2, 0)
    specs = [
        pl.BlockSpec((1, wrows, cols), lambda t, p: (t, 0, 0)),
        pl.BlockSpec((2, 1, wrows, cols), lambda t, p: (0, first(t), 0, 0)),
        pl.BlockSpec((1, wrows, cols), lambda t, p: (last(t), 0, 0)),
        pl.BlockSpec((2, 1, wrows, cols), lambda t, p: (0, last(t), 0, 0)),
        pl.BlockSpec((1, wrows, cols), lambda t, p: (first(t), 0, 0)),
    ]
    shapes = [
        sds((4, wrows, cols), NARROW),
        sds((2, 2, wrows, cols), NARROW),
        sds((2, wrows, cols), NARROW),
        sds((2, 2, wrows, cols), NARROW),
        sds((2, wrows, cols), NARROW),
    ]
    return specs, shapes


def expand_from(g_ref, w_refs, t, p):
    width = g_ref.shape[1] // PLANE_BLOCKS
    acc = None
    for r, w in enumerate(weight_blocks(w_refs, t)):
        term = jnp.dot(g_ref[:, rel_cols(p, r, width)], w, preferred_element_type=WIDE)
        acc = term if acc is None else acc + term
    return acc


def reduce_into(acc_ref, value, w_refs, t, p):
    width = acc_ref.shape[1] // PLANE_BLOCKS

    @pl.when(t == 0)
    def _():
        acc_ref[...] = jnp.zeros_like(acc_ref)

    for r, w in enumerate(weight_blocks(w_refs, t)):
        acc_ref[:, rel_cols(p, r, width)] += lax.dot_general(
            value, w, (((1,), (1,)), ((), ())), preferred_element_type=WIDE
        )


def ff_back_body(nr, ne, fr, p_ref, g_ref, a_ref, u_ref, *refs):
    r_refs, e_refs = refs[:nr], refs[nr : nr + ne]
    b_ref, gc_ref = refs[nr + ne : nr + ne + 2]
    outs, acc_ref = refs[nr + ne + 2 : -1], refs[-1]
    t = pl.program_id(0)
    p = p_ref[0]
    grad = expand_from(g_ref, r_refs, t, p)
    u = u_ref[...]
    logistic = sigmoid(u)
    gu = grad * (logistic * (1.0 + u * (1.0 - logistic)))
    gc_ref[...] = jnp.sum(gu, axis=0, keepdims=True)
    low = gu.astype(NARROW)
    reduce_into(acc_ref, low, e_refs, t, p)
    write_grads(t, p, [(g_ref, (u * logistic).astype(NARROW))], outs[:fr])
    write_grads(t, p, [(a_ref, low)], outs[fr:])

    @pl.when(t == 3)
    def _():
        b_ref[...] = acc_ref[...].astype(NARROW)


def ff_back(g, a, u, wr, we, p, flat):
    rows, width = g.shape
    cols = u.shape[1] // 4
    wrows = width // PLANE_BLOCKS
    r_specs, r_shapes = grad_outs(wrows, cols, flat)
    e_specs, e_shapes = grad_outs(wrows, cols, False)
    out = pl.pallas_call(
        functools.partial(ff_back_body, len(wr), len(we), len(r_specs)),
        grid_spec=pltpu.PrefetchScalarGridSpec(
            num_scalar_prefetch=1,
            grid=(4,),
            in_specs=[
                whole((rows, width)),
                whole((rows, width)),
                pl.BlockSpec((rows, cols), lambda t, p: (0, t)),
                *weight_specs(wr, cols, 0),
                *weight_specs(we, cols, 0),
            ],
            out_specs=[
                whole((rows, width)),
                pl.BlockSpec((1, cols), lambda t, p: (0, t)),
                *r_specs,
                *e_specs,
            ],
            scratch_shapes=[pltpu.VMEM((rows, width), WIDE)],
        ),
        out_shape=[sds((rows, width), NARROW), sds((1, 4 * cols), WIDE), *r_shapes, *e_shapes],
        compiler_params=params(),
        cost_estimate=cost(32 * rows * width * cols, 32 * width * cols),
        name="ff_back",
    )(p, g, a, u, *wr, *we)
    g_r = out[2 : 2 + len(r_specs)]
    return out[0], out[1], (g_r[0] if flat else g_r), out[2 + len(r_specs) :]


def norm_back_body(scale, x_ref, gx_ref, pa_ref, pb_ref, g_ref, out_ref, low_ref, sums_ref):
    @pl.when(pl.program_id(0) == 0)
    def _():
        sums_ref[...] = jnp.zeros_like(sums_ref)

    unit, inv_std = norm_stats(x_ref[...])
    grad = pa_ref[...].astype(WIDE) + pb_ref[...].astype(WIDE)
    scaled = grad * g_ref[...]
    gx = gx_ref[...] + inv_std * (
        scaled
        - jnp.mean(scaled, axis=-1, keepdims=True)
        - unit * jnp.mean(scaled * unit, axis=-1, keepdims=True)
    )
    out_ref[...] = gx
    branch = scale * gx
    low_ref[...] = branch.astype(NARROW)
    sums_ref[0:1, :] += jnp.sum(grad * unit, axis=0, keepdims=True)
    sums_ref[1:2, :] += jnp.sum(grad, axis=0, keepdims=True)
    sums_ref[2:3, :] += jnp.sum(branch, axis=0, keepdims=True)


def norm_back(scale, x, gx, pa, pb, gain):
    rows, width = x.shape
    block = pl.BlockSpec((CHUNK, width), lambda i: (i, 0))
    return pl.pallas_call(
        functools.partial(norm_back_body, scale),
        grid=(rows // CHUNK,),
        in_specs=[block, block, block, block, whole((1, width))],
        out_specs=[block, block, whole((8, width))],
        out_shape=[sds((rows, width), WIDE), sds((rows, width), NARROW), sds((8, width), WIDE)],
        compiler_params=params(),
        cost_estimate=cost(20 * rows * width, 18 * rows * width),
        name="norm_back",
    )(x, gx, pa, pb, gain)


def final_body(
    x_ref, pa_ref, pb_ref, ob_ref, cot_ref, live_ref, g_ref, b_ref, y_ref, gx_ref, low_ref, sums_ref
):
    @pl.when(pl.program_id(0) == 0)
    def _():
        sums_ref[...] = jnp.zeros_like(sums_ref)

    branch = pa_ref[...].astype(WIDE) + pb_ref[...].astype(WIDE)
    v = x_ref[...] + 0.5 * (branch + ob_ref[...])
    unit, inv_std = norm_stats(v)
    live = live_ref[...]
    y_ref[...] = ((unit * g_ref[...] + b_ref[...]) * live).astype(NARROW)
    grad = cot_ref[...].astype(WIDE) * live
    scaled = grad * g_ref[...]
    gx = inv_std * (
        scaled
        - jnp.mean(scaled, axis=-1, keepdims=True)
        - unit * jnp.mean(scaled * unit, axis=-1, keepdims=True)
    )
    gx_ref[...] = gx
    half = 0.5 * gx
    low_ref[...] = half.astype(NARROW)
    sums_ref[0:1, :] += jnp.sum(grad * unit, axis=0, keepdims=True)
    sums_ref[1:2, :] += jnp.sum(grad, axis=0, keepdims=True)
    sums_ref[2:3, :] += jnp.sum(half, axis=0, keepdims=True)


def final_norm(x, pa, pb, ob, cot, live, gain, bias):
    rows, width = x.shape
    block = pl.BlockSpec((CHUNK, width), lambda i: (i, 0))
    row = whole((1, width))
    return pl.pallas_call(
        final_body,
        grid=(rows // CHUNK,),
        in_specs=[
            block, block, block, row, block,
            pl.BlockSpec((CHUNK, 1), lambda i: (i, 0)), row, row,
        ],
        out_specs=[block, block, block, whole((8, width))],
        out_shape=[
            sds((rows, width), NARROW),
            sds((rows, width), WIDE),
            sds((rows, width), NARROW),
            sds((8, width), WIDE),
        ],
        compiler_params=params(),
        cost_estimate=cost(24 * rows * width, 18 * rows * width),
        name="final_norm",
    )(x, pa, pb, ob, cot, live, gain, bias)


def distances(i0, keys, rows_here):
    rows = lax.broadcasted_iota(jnp.int32, (rows_here, keys), 0) + i0
    cols = lax.broadcasted_iota(jnp.int32, (rows_here, keys), 1)
    return cols - rows, cols


def head_lanes(rows, width, e):
    lane = lax.broadcasted_iota(jnp.int32, (rows, width), 1)
    return (lane >= e * HD) & (lane < (e + 1) * HD)


def doubled(table, heads):
    return jnp.concatenate([table] * heads, axis=1)


def attend_body(len_ref, qkv_ref, table_ref, o_ref, p_out_ref):
    keys = qkv_ref.shape[0]
    width = qkv_ref.shape[1] // 3
    heads = width // HD
    length = len_ref[0]
    table_turned = jnp.transpose(doubled(table_ref[...], heads))
    k_turned = jnp.transpose(qkv_ref[:, width : 2 * width])
    v = qkv_ref[:, 2 * width :]
    key_live = lax.broadcasted_iota(jnp.int32, (QROWS, keys), 1) < length
    masks = [head_lanes(QROWS, width, e) for e in range(heads)]
    for n in range(keys // QROWS):
        i0 = n * QROWS
        rows = slice(i0, i0 + QROWS)
        begin = max(0, i0 - NEAR)
        end = min(keys, i0 + QROWS + NEAR)
        span = end - begin
        apart = distances(i0 - begin, span, QROWS)[0]
        far_left = apart <= -LEFT
        far_right = apart >= RIGHT
        q_all = qkv_ref[rows, :width]
        merged = None
        for e in range(heads):
            q = jnp.where(masks[e], q_all, jnp.zeros_like(q_all))
            near = jnp.dot(q, table_turned, preferred_element_type=WIDE)
            left, right = near[:, 0:1], near[:, LEFT + RIGHT : LEFT + RIGHT + 1]
            band = jnp.concatenate([near, jnp.zeros((QROWS, span - NEAR), WIDE)], axis=1)
            band = pltpu.roll(band, (i0 - begin + span - LEFT) % span, 1, stride=1, stride_axis=0)
            pieces = [jnp.where(far_left, left, jnp.where(far_right, right, band))]
            if begin > 0:
                pieces.insert(0, jnp.broadcast_to(left, (QROWS, begin)))
            if end < keys:
                pieces.append(jnp.broadcast_to(right, (QROWS, keys - end)))
            rel = jnp.concatenate(pieces, axis=1) if len(pieces) > 1 else pieces[0]
            s = jnp.dot(q, k_turned, preferred_element_type=WIDE)
            s = jnp.where(key_live, (s + rel) * HD ** (-0.5), MASKED)
            top = jnp.max(s, axis=-1, keepdims=True)
            ex = jnp.exp(s - top)
            chance = (ex * (1.0 / row_sum(ex))).astype(NARROW)
            p_out_ref[e, rows, :] = chance
            part = jnp.dot(chance, v, preferred_element_type=WIDE)
            merged = part if merged is None else jnp.where(masks[e], part, merged)
        o_ref[rows, :] = merged.astype(NARROW)


def attend(qkv, table, length):
    rows = qkv.shape[0]
    width = qkv.shape[1] // 12
    heads = width // HD
    return pl.pallas_call(
        attend_body,
        grid_spec=pltpu.PrefetchScalarGridSpec(
            num_scalar_prefetch=1,
            grid=(4,),
            in_specs=[
                pl.BlockSpec((rows, 3 * width), lambda t, n: (0, t)),
                whole(table.shape),
            ],
            out_specs=[
                pl.BlockSpec((rows, width), lambda t, n: (0, t)),
                pl.BlockSpec((heads, rows, rows), lambda t, n: (t, 0, 0)),
            ],
        ),
        out_shape=[sds((rows, 4 * width), NARROW), sds((4 * heads, rows, rows), NARROW)],
        compiler_params=params(),
        cost_estimate=cost(16 * heads * rows * rows * HD, 10 * heads * rows * rows, 4 * heads * rows * rows),
        name="attend",
    )(length, qkv, table)


def attend_back_parts(qkv_ref, go_ref, p_ref, table_ref, out_ref, sums_ref, dist_ref, gk_ref, gv_ref):
    keys = qkv_ref.shape[0]
    width = qkv_ref.shape[1] // 3
    heads = width // HD
    table = doubled(table_ref[...], heads)
    scale = HD ** (-0.5)
    flip = (
        lax.broadcasted_iota(jnp.int32, (BROWS, BROWS), 0)
        + lax.broadcasted_iota(jnp.int32, (BROWS, BROWS), 1)
        == BROWS - 1
    ).astype(NARROW)
    bucket = lax.broadcasted_iota(jnp.int32, (BROWS, NEAR), 1)
    first_row = table[0:1, :].astype(WIDE)
    last_row = table[LEFT + RIGHT : LEFT + RIGHT + 1, :].astype(WIDE)
    masks = [head_lanes(BROWS, width, e) for e in range(heads)]

    @pl.when(pl.program_id(0) == 0)
    def _():
        dist_ref[...] = jnp.zeros_like(dist_ref)

    q_turned = jnp.transpose(qkv_ref[:, :width])
    go_turned = jnp.transpose(go_ref[...])
    v_turned = jnp.transpose(qkv_ref[:, 2 * width :])
    k = qkv_ref[:, width : 2 * width]
    for n in range(keys // BROWS):
        i0 = n * BROWS
        rows = slice(i0, i0 + BROWS)
        begin = max(0, i0 - NEAR)
        end = min(keys, i0 + BROWS + NEAR)
        span = end - begin
        apart = distances(i0 - begin, span, BROWS)[0]
        far_left = apart <= -LEFT
        far_right = apart >= RIGHT
        key_of = lax.broadcasted_iota(jnp.int32, (BROWS, NEAR), 0) + bucket + (i0 - LEFT)
        inside = (bucket > 0) & (bucket < LEFT + RIGHT) & (key_of >= 0) & (key_of < keys)
        q_wide = qkv_ref[rows, :width].astype(WIDE)
        go_all = go_ref[rows, :]
        merged = None
        for e in range(heads):
            some = slice(e * HD, (e + 1) * HD)
            go = jnp.where(masks[e], go_all, jnp.zeros_like(go_all))
            chance = p_ref[e, rows, :]
            wide = chance.astype(WIDE)
            gp = jnp.dot(go, v_turned, preferred_element_type=WIDE)
            gs = (wide * (gp - row_sum(gp * wide))).astype(NARROW)
            gsw = gs.astype(WIDE)
            window = gsw[:, begin:end]
            turned = jnp.dot(flip, gs[:, begin:end], preferred_element_type=WIDE)
            turned = pltpu.roll(
                turned, (LEFT + 1 - BROWS - (i0 - begin)) % span, 1, stride=1, stride_axis=0
            )[:, :NEAR]
            back = jnp.dot(flip, turned.astype(NARROW), preferred_element_type=WIDE)
            left_sum = row_sum(jnp.where(far_left, window, 0.0))
            right_sum = row_sum(jnp.where(far_right, window, 0.0))
            if begin > 0:
                left_sum += row_sum(gsw[:, :begin])
            if end < keys:
                right_sum += row_sum(gsw[:, end:])
            left_sum *= scale
            right_sum *= scale
            near = (jnp.where(inside, back, 0.0) * scale).astype(NARROW)
            gq = jnp.dot(gs, k, preferred_element_type=WIDE) * scale
            gq += jnp.dot(near, table, preferred_element_type=WIDE)
            gq += left_sum * first_row + right_sum * last_row
            merged = gq if merged is None else jnp.where(masks[e], gq, merged)
            q_part = q_turned[some, rows]
            dist_ref[:HD, :] += jnp.dot(q_part, near, preferred_element_type=WIDE)
            ends = HD + 2 * e
            dist_ref[ends : ends + 1, :] += jnp.sum(left_sum * q_wide, axis=0, keepdims=True)
            dist_ref[ends + 1 : ends + 2, :] += jnp.sum(right_sum * q_wide, axis=0, keepdims=True)
            gk = jnp.dot(q_part, gs, preferred_element_type=WIDE)
            gv = jnp.dot(go_turned[some, rows], chance, preferred_element_type=WIDE)
            if n == 0:
                gk_ref[some, :] = gk
                gv_ref[some, :] = gv
            else:
                gk_ref[some, :] += gk
                gv_ref[some, :] += gv
        out_ref[rows, :width] = merged.astype(NARROW)

    out_ref[:, width : 2 * width] = jnp.transpose(gk_ref[...] * scale).astype(NARROW)
    out_ref[:, 2 * width :] = jnp.transpose(gv_ref[...]).astype(NARROW)
    sums_ref[...] = jnp.sum(out_ref[...].astype(WIDE), axis=0, keepdims=True)


def attend_back_body(
    nw, s_ref, gm_ref, bn_ref, qkv_ref, chance_ref, o_ref, table_ref, *refs
):
    m_refs, w_refs = refs[:nw], refs[nw : 2 * nw]
    b_ref, sums_ref, dist_ref = refs[2 * nw : 2 * nw + 3]
    outs = refs[2 * nw + 3 : -5]
    acc_ref, go_ref, out_ref, gk_ref, gv_ref = refs[-5:]
    t = pl.program_id(0)
    p = s_ref[0]
    go_ref[...] = expand_from(gm_ref, m_refs, t, p).astype(NARROW)
    attend_back_parts(
        qkv_ref, go_ref, chance_ref, table_ref, out_ref, sums_ref, dist_ref, gk_ref, gv_ref
    )
    grad = out_ref[...]
    reduce_into(acc_ref, grad, w_refs, t, p)
    write_grads(t, p, [(bn_ref, grad), (gm_ref, o_ref[...])], outs)

    @pl.when(t == 3)
    def _():
        b_ref[...] = acc_ref[...].astype(NARROW)


def attend_back(gm, bn, qkv, chances, o, table, w, p):
    rows, width = gm.shape
    wrows = width // PLANE_BLOCKS
    cols = qkv.shape[1] // 12
    heads = cols // HD
    g_specs, g_shapes = grad_outs(wrows, 4 * cols, False)
    out = pl.pallas_call(
        functools.partial(attend_back_body, len(w)),
        grid_spec=pltpu.PrefetchScalarGridSpec(
            num_scalar_prefetch=1,
            grid=(4,),
            in_specs=[
                whole((rows, width)),
                whole((rows, width)),
                pl.BlockSpec((rows, 3 * cols), lambda t, p: (0, t)),
                pl.BlockSpec((heads, rows, rows), lambda t, p: (t, 0, 0)),
                pl.BlockSpec((rows, cols), lambda t, p: (0, t)),
                whole(table.shape),
                *weight_specs(w, cols, 3),
                *weight_specs(w, 3 * cols, 0),
            ],
            out_specs=[
                whole((rows, width)),
                pl.BlockSpec((1, 3 * cols), lambda t, p: (0, t)),
                whole((HD + 8, NEAR)),
                *g_specs,
            ],
            scratch_shapes=[
                pltpu.VMEM((rows, width), WIDE),
                pltpu.VMEM((rows, cols), NARROW),
                pltpu.VMEM((rows, 3 * cols), NARROW),
                pltpu.VMEM((cols, rows), WIDE),
                pltpu.VMEM((cols, rows), WIDE),
            ],
        ),
        out_shape=[
            sds((rows, width), NARROW),
            sds((1, 12 * cols), WIDE),
            sds((HD + 8, NEAR), WIDE),
            *g_shapes,
        ],
        compiler_params=params(),
        cost_estimate=cost(40 * heads * rows * rows * HD, 10 * heads * rows * rows),
        name="attend_back",
    )(p, gm, bn, qkv, chances, o, table, *w, *w)
    return out[0], out[1], out[2], out[3:]


def lane_pair(first, second, rows):
    lane = lax.broadcasted_iota(jnp.int32, (rows, LANES), 1)
    return jnp.where(lane == 0, first, jnp.where(lane == 1, second, 0.0))


def row_sum(v):
    return jnp.sum(v, axis=-1, keepdims=True)


def mix_body(taps_count, z_ref, taps_ref, y_ref, sums_ref, pad_ref):
    rows = z_ref.shape[0]

    @pl.when(pl.program_id(0) == 0)
    def _():
        sums_ref[...] = jnp.zeros_like(sums_ref)

    pad_ref[0:PAD, :] = jnp.zeros((PAD, pad_ref.shape[1]), WIDE)
    pad_ref[PAD:, :] = z_ref[...]
    for start in range(0, rows, MIX_CHUNK):
        total = None
        for i in range(taps_count):
            begin = start + PAD - taps_count + 1 + i
            term = taps_ref[i : i + 1, :] * pad_ref[begin : begin + MIX_CHUNK, :]
            total = term if total is None else total + term
        here = slice(start, start + MIX_CHUNK)
        y_ref[here, :] = total
        sums_ref[here, :] += lane_pair(row_sum(total), row_sum(total * total), MIX_CHUNK)


def causal_mix(z, taps, taps_count):
    rows, cols = z.shape
    block = pl.BlockSpec((rows, cols // 4), lambda t: (0, t))
    return pl.pallas_call(
        functools.partial(mix_body, taps_count),
        grid=(4,),
        in_specs=[block, pl.BlockSpec((taps.shape[0], cols // 4), lambda t: (0, t))],
        out_specs=[block, whole((rows, LANES))],
        out_shape=[sds((rows, cols), WIDE), sds((rows, LANES), WIDE)],
        scratch_shapes=[pltpu.VMEM((rows + PAD, cols // 4), WIDE)],
        compiler_params=params(),
        cost_estimate=cost(2 * taps_count * rows * cols, 8 * rows * cols),
        name="causal_mix",
    )(z, taps)


def depth_stats(sa_ref, sb_ref, here, width):
    sums = (sa_ref[here, :] + sb_ref[here, :]) * (1.0 / width)
    mean = sums[:, 0:1]
    return mean, lax.rsqrt(sums[:, 1:2] - mean * mean + EPSILON)


def filter_out_body(p_ref, y_ref, sa_ref, sb_ref, g_ref, b_ref, *refs):
    w_refs = refs[:5]
    out_ref, low_ref, acc_ref = refs[5:]
    t = pl.program_id(0)
    p = p_ref[0]
    width = out_ref.shape[1]
    mean, std = depth_stats(sa_ref, sb_ref, slice(None), width)
    yn = (y_ref[...] - mean) * std * g_ref[...] + b_ref[...]
    low = (yn * sigmoid(yn)).astype(NARROW)
    low_ref[...] = low

    @pl.when(t == 0)
    def _():
        acc_ref[...] = jnp.zeros_like(acc_ref)

    for r, w in enumerate(weight_blocks(w_refs, t)):
        cols = rel_cols(p, r, width // PLANE_BLOCKS)
        acc_ref[:, cols] += lax.dot_general(
            low, w, (((1,), (1,)), ((), ())), preferred_element_type=WIDE
        )

    @pl.when(t == 3)
    def _():
        out_ref[...] = acc_ref[...].astype(NARROW)


def filter_out(y, sums, gain, bias, w, cols, col_block, p, width):
    rows = y.shape[0]
    block = pl.BlockSpec((rows, cols), lambda t, p: (0, t))
    row = pl.BlockSpec((1, cols), lambda t, p: (0, t))
    return pl.pallas_call(
        filter_out_body,
        grid_spec=pltpu.PrefetchScalarGridSpec(
            num_scalar_prefetch=1,
            grid=(4,),
            in_specs=[
                block, whole((rows, LANES)), whole((rows, LANES)), row, row,
                *weight_specs(w, cols, col_block),
            ],
            out_specs=[whole((rows, width)), block],
            scratch_shapes=[pltpu.VMEM((rows, width), WIDE)],
        ),
        out_shape=[sds((rows, width), NARROW), sds(y.shape, NARROW)],
        compiler_params=params(),
        cost_estimate=cost(2 * rows * width * 4 * cols, 8 * width * cols + 6 * rows * width),
        name="filter_out",
    )(p, y, *sums, gain, bias, *w)


def filter_in_body(p_ref, grad_ref, y_ref, sa_ref, sb_ref, g_ref, b_ref, *refs):
    w_refs = refs[:5]
    gyn_ref, cols_ref, rows_ref = refs[5:]
    t = pl.program_id(0)
    p = p_ref[0]
    width = grad_ref.shape[1]
    acc = None
    for r, w in enumerate(weight_blocks(w_refs, t)):
        cols = rel_cols(p, r, width // PLANE_BLOCKS)
        term = jnp.dot(grad_ref[:, cols], w, preferred_element_type=WIDE)
        acc = term if acc is None else acc + term
    mean, std = depth_stats(sa_ref, sb_ref, slice(None), width)
    unit = (y_ref[...] - mean) * std
    yn = unit * g_ref[...] + b_ref[...]
    logistic = sigmoid(yn)
    gyn = acc * (logistic * (1.0 + yn * (1.0 - logistic)))
    gyn_ref[...] = gyn
    cols_ref[0:1, :] = jnp.sum(gyn * unit, axis=0, keepdims=True)
    cols_ref[1:2, :] = jnp.sum(gyn, axis=0, keepdims=True)
    scaled = gyn * g_ref[...]
    pair = lane_pair(row_sum(scaled), row_sum(scaled * unit), gyn.shape[0])

    @pl.when(t == 0)
    def _():
        rows_ref[...] = pair

    @pl.when(t > 0)
    def _():
        rows_ref[...] += pair


def filter_in(grad, y, sums, gain, bias, w, cols, col_block, p):
    rows, width = grad.shape
    block = pl.BlockSpec((rows, cols), lambda t, p: (0, t))
    row = pl.BlockSpec((1, cols), lambda t, p: (0, t))
    return pl.pallas_call(
        filter_in_body,
        grid_spec=pltpu.PrefetchScalarGridSpec(
            num_scalar_prefetch=1,
            grid=(4,),
            in_specs=[
                whole((rows, width)), block, whole((rows, LANES)), whole((rows, LANES)), row, row,
                *weight_specs(w, cols, col_block),
            ],
            out_specs=[
                block,
                pl.BlockSpec((8, cols), lambda t, p: (0, t)),
                whole((rows, LANES)),
            ],
        ),
        out_shape=[sds(y.shape, WIDE), sds((8, 4 * cols), WIDE), sds((rows, LANES), WIDE)],
        compiler_params=params(),
        cost_estimate=cost(2 * rows * width * 4 * cols, 8 * width * cols + 6 * rows * width),
        name="filter_in",
    )(p, grad, y, *sums, gain, bias, *w)


def mix_back_parts(
    taps_count, width, gyn_ref, y_ref, sa_ref, sb_ref, ra_ref, rb_ref, g_ref, z_ref, gate_ref,
    taps_ref, out_ref, grad_ref, gpad_ref, zpad_ref,
):
    rows, cols = z_ref.shape
    zpad_ref[0:PAD, :] = jnp.zeros((PAD, cols), WIDE)
    zpad_ref[PAD:, :] = z_ref[...]
    gpad_ref[rows:, :] = jnp.zeros((PAD, cols), WIDE)
    mean, std = depth_stats(sa_ref, sb_ref, slice(None), width)
    pair = (ra_ref[...] + rb_ref[...]) * (1.0 / width)
    unit = (y_ref[...] - mean) * std
    gpad_ref[0:rows, :] = std * (gyn_ref[...] * g_ref[...] - pair[:, 0:1] - unit * pair[:, 1:2])
    sums = [None] * taps_count
    for start in range(0, rows, MIX_CHUNK):
        here = slice(start, start + MIX_CHUNK)
        gy = gpad_ref[here, :]
        total = None
        for i in range(taps_count):
            begin = start + taps_count - 1 - i
            term = taps_ref[i : i + 1, :] * gpad_ref[begin : begin + MIX_CHUNK, :]
            total = term if total is None else total + term
        for i in range(taps_count):
            begin = start + PAD - taps_count + 1 + i
            part = zpad_ref[begin : begin + MIX_CHUNK, :] * gy
            part = jnp.sum(part.reshape(MIX_CHUNK // 8, 8, cols), axis=0)
            sums[i] = part if sums[i] is None else sums[i] + part
        gate = gate_ref[here, :]
        first = total * gate
        out_ref[here, :cols] = first.astype(NARROW)
        out_ref[here, cols:] = (total * z_ref[here, :] * (1.0 - gate)).astype(NARROW)
    for i in range(taps_count):
        grad_ref[i : i + 1, :] = jnp.sum(sums[i], axis=0, keepdims=True)


def mix_back_body(taps_count, width, nw, s_ref, *refs):
    parts, gate_taps = refs[:8], refs[8:10]
    cn_ref, gw_ref, wact_ref = refs[10:13]
    w_refs = refs[13 : 13 + nw]
    b_ref, grad_ref, flat_ref = refs[13 + nw : 16 + nw]
    acc_ref, out_ref, gpad_ref, zpad_ref = refs[16 + nw :]
    t = pl.program_id(0)
    p = s_ref[0]
    mix_back_parts(
        taps_count, width, *parts, *gate_taps, out_ref, grad_ref, gpad_ref, zpad_ref
    )
    grad = out_ref[...]
    reduce_into(acc_ref, grad, w_refs, t, p)
    write_grads(t, p, [(cn_ref, grad), (gw_ref, wact_ref[...])], [flat_ref])

    @pl.when(t == 3)
    def _():
        b_ref[...] = acc_ref[...].astype(NARROW)


def mix_back(gyn, y, sums, pairs, gain, z, gate, taps, taps_count, cn, gw, act, w, p):
    rows, cols = z.shape
    width = cn.shape[1]
    wrows = width // PLANE_BLOCKS
    n = cols // 4
    block = pl.BlockSpec((rows, n), lambda t, p: (0, t))
    row = pl.BlockSpec((1, n), lambda t, p: (0, t))
    lanes = whole((rows, LANES))
    tap_block = pl.BlockSpec((taps.shape[0], n), lambda t, p: (0, t))
    g_specs, g_shapes = grad_outs(wrows, 3 * n, True)
    return pl.pallas_call(
        functools.partial(mix_back_body, taps_count, width, len(w)),
        grid_spec=pltpu.PrefetchScalarGridSpec(
            num_scalar_prefetch=1,
            grid=(4,),
            in_specs=[
                block, block, lanes, lanes, lanes, lanes, row, block, block, tap_block,
                whole((rows, width)), whole((rows, width)), block,
                *weight_specs(w, 2 * n, 0),
            ],
            out_specs=[whole((rows, width)), tap_block, *g_specs],
            scratch_shapes=[
                pltpu.VMEM((rows, width), WIDE),
                pltpu.VMEM((rows, 2 * n), NARROW),
                pltpu.VMEM((rows + PAD, n), WIDE),
                pltpu.VMEM((rows + PAD, n), WIDE),
            ],
        ),
        out_shape=[sds((rows, width), NARROW), sds(taps.shape, WIDE), *g_shapes],
        compiler_params=params(),
        cost_estimate=cost(4 * taps_count * rows * cols, 20 * rows * cols),
        name="mix_back",
    )(p, gyn, y, *sums, *pairs, gain, z, gate, taps, cn, gw, act, *w)


def halve_body(groups, core_ref, *refs):
    count = sum(len(g) for g in groups)
    ins = list(refs[:count])
    keeps = refs[count : count + len(groups)]
    sends = refs[count + len(groups) :]
    low = core_ref[0] == 0
    for group, keep, send in zip(groups, keeps, sends):
        start = 0
        for n in group:
            ref = ins.pop(0)
            left, right = ref[:, :n], ref[:, n:]
            keep[:, start : start + n] = jnp.where(low, left, right)
            send[:, start : start + n] = jnp.where(low, right, left)
            start += n


def halve(groups, core):
    rows = groups[0][0].shape[0]
    halves = tuple(tuple(w.shape[1] // 2 for w in g) for g in groups)
    flat = [w for g in groups for w in g]
    shapes = [sds((rows, sum(h)), NARROW) for h in halves] * 2
    out = pl.pallas_call(
        functools.partial(halve_body, halves),
        grid_spec=pltpu.PrefetchScalarGridSpec(
            num_scalar_prefetch=1,
            grid=(1,),
            in_specs=[whole(w.shape) for w in flat],
            out_specs=[whole(s.shape) for s in shapes],
        ),
        out_shape=shapes,
        compiler_params=params(),
        cost_estimate=cost(0, 4 * sum(w.size for w in flat)),
        name="halve",
    )(core, *flat)
    return out[: len(groups)], out[len(groups) :]


def join_body(core_ref, keep_ref, came_ref, out_ref):
    low = core_ref[0] == 0
    rows = keep_ref.shape[0]
    keep, came = keep_ref[...], came_ref[...]
    out_ref[:rows, :] = jnp.where(low, keep, came)
    out_ref[rows:, :] = jnp.where(low, came, keep)


def join(keep, came, core):
    rows, cols = keep.shape
    return pl.pallas_call(
        join_body,
        grid_spec=pltpu.PrefetchScalarGridSpec(
            num_scalar_prefetch=1,
            grid=(1,),
            in_specs=[whole((rows, cols)), whole((rows, cols))],
            out_specs=whole((2 * rows, cols)),
        ),
        out_shape=sds((2 * rows, cols), keep.dtype),
        compiler_params=params(),
        cost_estimate=cost(0, 8 * rows * cols),
        name="join",
    )(core, keep, came)


def pack_body(lead, plan, core_ref, *refs):
    out_ref = refs[-1]
    low = core_ref[0] == 0
    out_ref[...] = jnp.zeros_like(out_ref)
    for ref, items in zip(refs[:-1], plan):
        for kind, src, dst in items:
            if kind == "once":
                v = ref[src : src + 1, :]
                out_ref[dst : dst + 1, :] = jnp.where(low, v, 0.0)
            elif kind == "all":
                out_ref[dst : dst + 8, :] = ref[...]
            elif kind == "taps":
                n = ref.shape[1] // 4
                for t in range(4):
                    v = ref[: src, t * n : (t + 1) * n]
                    out_ref[dst : dst + src, 2 * t * n : (2 * t + 1) * n] = jnp.where(low, v, 0.0)
                    out_ref[dst : dst + src, (2 * t + 1) * n : (2 * t + 2) * n] = jnp.where(low, 0.0, v)
            elif kind == "hidden":
                n = ref.shape[1] // 4
                for t in range(4):
                    v = ref[0:1, t * n : (t + 1) * n]
                    out_ref[dst + t : dst + t + 1, :n] = jnp.where(low, v, 0.0)
                    out_ref[dst + t : dst + t + 1, n:] = jnp.where(low, 0.0, v)
            else:
                row, first, step, n = src
                for t in range(4):
                    begin = t * step + first
                    v = ref[row : row + 1, begin : begin + n]
                    out_ref[dst : dst + 1, 2 * t * n : (2 * t + 1) * n] = jnp.where(low, v, 0.0)
                    out_ref[dst : dst + 1, (2 * t + 1) * n : (2 * t + 2) * n] = jnp.where(low, 0.0, v)


def pack(rows, width, core, sources):
    arrays = [a for a, _ in sources]
    plan = tuple(tuple(items) for _, items in sources)
    return pl.pallas_call(
        functools.partial(pack_body, rows, plan),
        grid_spec=pltpu.PrefetchScalarGridSpec(
            num_scalar_prefetch=1,
            grid=(1,),
            in_specs=[whole(a.shape) for a in arrays],
            out_specs=whole((rows, width)),
        ),
        out_shape=sds((rows, width), WIDE),
        compiler_params=params(),
        cost_estimate=cost(0, 8 * rows * width),
        name="pack",
    )(core, *arrays)


def on_device(planes, inputs, lengths, cotangent, *weights_and_rest):
    shards = weights_and_rest[:8]
    norm_gains, biases, kernel, distance_table = weights_and_rest[8:]
    batches, _, rows_here, width = inputs.shape
    parts = 4
    core = lax.axis_index("pair")
    plane = lax.axis_index("plane")
    part = lax.axis_index("tensor")
    quick = planes == PLANE_BLOCKS
    place = plane if quick else plane * 0
    p = place.astype(jnp.int32).reshape(1)

    def other_core(v):
        return lax.ppermute(v, "pair", [(0, 1), (1, 0)])

    def step_x(v):
        return lax.ppermute(v, "plane", [(i, i ^ 1) for i in range(planes)])

    def step_y(v):
        return lax.ppermute(v, "plane", [(i, i ^ 2) for i in range(planes)])

    def over_planes(v):
        if quick:
            return v + step_x(v) + step_y(v) + lax.ppermute(v, "plane", [(i, i ^ 3) for i in range(4)])
        bit = 1
        while bit < planes:
            v = v + lax.ppermute(v, "plane", [(i, i ^ bit) for i in range(planes)])
            bit *= 2
        return v

    def over_parts(v):
        def turn(k):
            return lax.ppermute(v, "tensor", [(i, i ^ k) for i in range(parts)])

        one, two, three = turn(1), turn(2), turn(3)
        return (v + one) + (two + three)

    def fence(*values):
        return lax.optimization_barrier(values) if quick else values

    def column_of(shard):
        return lax.all_gather(shard, "tensor", axis=0)

    def planes_of(column):
        every = lax.all_gather(column, "plane", axis=0)
        rows, cols = column.shape[1:]
        every = every.reshape(PLANE_BLOCKS, planes // PLANE_BLOCKS, parts, rows, cols)
        every = every.transpose(0, 2, 1, 3, 4).reshape(PLANE_BLOCKS, parts, -1, cols)
        return every[0], every[1], every[2], every[3, :2], every[3, 2:]

    def near(column):
        return step_x(column), step_y(column)

    def far(pair):
        return step_y(pair[0][:2]), step_x(pair[1][2:])

    def share(total):
        n = total.shape[0] // 2
        keep = lax.dynamic_slice_in_dim(total, core * n, n, 0)
        came = other_core(lax.dynamic_slice_in_dim(total, (1 - core) * n, n, 0))
        first = jnp.where(core == 0, keep, came).astype(WIDE)
        second = jnp.where(core == 0, came, keep).astype(WIDE)
        return first, second

    def tensor_sum(total):
        return lax.psum_scatter(total, "tensor", scatter_dimension=0)

    def across_x(every):
        return step_x(every[1::2]) if quick else ()

    def across_y(every, rx):
        return step_y(add(every[2], rx[1])) if quick else ()

    def across_end(every, rx, ry):
        if quick:
            return (every[0].astype(WIDE) + rx[0].astype(WIDE) + ry.astype(WIDE)).astype(NARROW)
        return lax.psum_scatter(
            every.reshape(planes, -1, every.shape[-1]), "plane", scatter_dimension=0
        )

    def hop1(grads):
        return (step_x(grads[1]), step_y(grads[3])) if quick else ()

    def hop2(grads, came):
        if not quick:
            return ()
        return step_y(add(grads[4], came[0][1])), step_x(add(grads[2], came[1][1]))

    def hop3(grads, came, last):
        return tensor_sum(gathered(grads, came, last))

    def gathered(grads, came, last):
        own, sx, kx, sy, ky = grads
        if quick:
            return combine(own, came[0], came[1], last[0], last[1])
        blocks = [
            own,
            jnp.concatenate([sx[0], kx]),
            jnp.concatenate([ky, sy[0]]),
            jnp.concatenate([sx[1], sy[1]]),
        ]
        every = jnp.stack(blocks)
        rows = width // planes
        cols = own.shape[-1]
        every = every.reshape(PLANE_BLOCKS, parts, planes // PLANE_BLOCKS, rows, cols)
        every = every.transpose(0, 2, 1, 3, 4).reshape(planes, parts, rows, cols)
        return lax.psum_scatter(every, "plane", scatter_dimension=0)

    def add(a, b):
        return (a.astype(WIDE) + b.astype(WIDE)).astype(NARROW)

    def rejoin(halves, start, cols, groups):
        pieces = [h[:, start : start + cols].reshape(h.shape[0], groups, -1) for h in halves]
        joined = jnp.concatenate(pieces, axis=2)
        return joined[:, 0] if groups == 1 else joined

    def spot(c, t):
        return c * parts + t

    def route(turn):
        pairs = []
        for c in range(2):
            for t in range(parts):
                mb = (turn + t) % 2
                pairs.append((spot(c, t), spot(t // 2, 2 * mb + c)))
        return pairs

    def bring_one(v, turn):
        mb = lax.rem(turn + part, 2)
        block = lax.dynamic_index_in_dim(v[:, 0], mb, 0, False)
        return lax.ppermute(block, ("pair", "tensor"), route(turn))

    def bring(v):
        return [bring_one(v, turn) for turn in range(2)]

    def settle(blocks):
        swap = part // 2 == 1
        mine = jnp.concatenate(
            [jnp.where(swap, blocks[1], blocks[0]), jnp.where(swap, blocks[0], blocks[1])], axis=0
        )
        theirs = other_core(mine)
        return jnp.concatenate(
            [jnp.where(core == 0, mine, theirs), jnp.where(core == 0, theirs, mine)], axis=0
        )

    def send_home(v):
        half = v.shape[0] // 2
        mine = lax.dynamic_slice_in_dim(v, core * half, half, 0)
        first, second = mine[: half // 2], mine[half // 2 :]
        swap = part // 2 == 1
        blocks = [jnp.where(swap, second, first), jnp.where(swap, first, second)]
        came = []
        for turn in range(2):
            back = [(b, a) for a, b in route(turn)]
            came.append(lax.ppermute(blocks[turn], ("pair", "tensor"), back))
        return came

    def home(came):
        odd = lax.rem(part, 2) == 1
        return jnp.stack([jnp.where(odd, came[1], came[0]), jnp.where(odd, came[0], came[1])])[:, None]

    (w_e1, w_r1, w_proj, w_merge, w_fe, w_fr, w_e2, w_r2) = shards
    core1 = core.astype(jnp.int32).reshape(1)
    ffc = w_e1.shape[1] // 2
    qc = w_proj.shape[2] // 2
    cc = w_fe.shape[2] // 2
    groups = [
        [w_e1],
        [w_r1],
        [w_proj[:, 0], w_proj[:, 1], w_proj[:, 2], w_merge],
        [w_fe[:, 0], w_fe[:, 1], w_fr, w_e2],
        [w_r2],
    ]
    keeps, sends = halve(groups, core1)
    pieces = fence(*[join(k, other_core(v), core1) for k, v in zip(keeps, sends)])

    gains = norm_gains.astype(WIDE)
    bias = biases.astype(WIDE)
    gain_row = lambda i: gains[i : i + 1]
    bias_row = lambda i: bias[i : i + 1]
    stride = w_e1.shape[1] * parts // width

    def pick(v):
        lead = v.shape[0]
        v = v.reshape(lead, parts, 2, -1)
        return lax.dynamic_index_in_dim(v, core, 2, False).reshape(lead, -1)

    hidden1 = pick(bias[11 : 11 + stride].reshape(1, -1))
    hidden2 = pick(bias[11 + stride : 11 + 2 * stride].reshape(1, -1))
    qb = pick(bias_row(6)).reshape(parts, 1, -1)
    vb = pick(bias_row(7)).reshape(parts, 1, -1)
    qkv_bias = jnp.concatenate([qb, jnp.zeros_like(qb), vb], axis=1).reshape(1, -1)
    taps_count = kernel.shape[0]
    taps = jnp.pad(pick(kernel.astype(WIDE)), ((0, PAD - taps_count), (0, 0)))
    depth_gain = pick(gain_row(3))
    depth_bias = pick(bias_row(3))
    buckets = distance_table.shape[0]
    table = jnp.pad(distance_table, ((0, NEAR - buckets), (0, 0)))

    pair_lengths = jnp.stack([lengths[:, 0], other_core(lengths[:, 0])])
    from_pair = jnp.bitwise_xor(lax.rem(part, 2), core)
    length = pair_lengths[from_pair, part // 2]
    rows_all = parts * inputs.shape[2]
    live = (jnp.arange(rows_all) < length).astype(WIDE)[:, None]

    col_e1 = column_of(pieces[0])
    r1c = column_of(pieces[1])
    attc = column_of(pieces[2])
    col_c = column_of(pieces[3])
    if quick:
        sd = pieces[4]
        sx, sy = step_x(sd), step_y(sd)
        sz = step_y(sx)
        col_e1, sx, sy, sz, source = fence(col_e1, sx, sy, sz, inputs)
        r2 = (column_of(jnp.stack([sd, sx, sy, sz])),) * PLANE_BLOCKS
        e1n, block0 = near(col_e1), bring_one(source, 0)
        e1n, r1c, block0, source = fence(e1n, r1c, block0, source)
        e1f, r1n, block1 = far(e1n), near(r1c), bring_one(source, 1)
        e1f, e1n, r1n, attc, block1, source = fence(e1f, e1n, r1n, attc, block1, cotangent)
        x0, cot0 = settle([block0, block1]), bring_one(source, 0)
        e1 = (col_e1, *e1n, *e1f)
        r1f, attn = far(r1n), near(attc)
    else:
        rows, cols = pieces[4].shape
        every = lax.all_gather(pieces[4], "plane", axis=0).reshape(PLANE_BLOCKS, -1, cols)
        r2 = (column_of(every),) * PLANE_BLOCKS
        x0 = settle(bring(inputs))
        e1 = planes_of(col_e1)
        r1 = planes_of(r1c)
        att = planes_of(attc)
        fil = planes_of(col_c[:, :, : 3 * cc])
        e2 = planes_of(col_c[:, :, 3 * cc :])
    x0 = x0.astype(WIDE)
    a1, u1, s1 = norm_expand("ff", x0, None, 0.5, gain_row(0), bias_row(0), e1, ffc, 0, p, hidden1)
    if quick:
        r1f, r1n, attn, s1, cot0, source = fence(r1f, r1n, attn, s1, cot0, source)
        cot1 = bring_one(source, 1)
        r1, attf = (r1c, *r1n, *r1f), far(attn)
    f1 = reduce_mm(s1, r1, ffc, 0, p, width)
    if quick:
        attf, attn, f1, col_c, cot1 = fence(attf, attn, f1, col_c, cot1)
        cot = settle([cot0, cot1])
        att = (attc, *attn, *attf)
    f1o = other_core(f1)
    x1, bn, qkv = norm_expand(
        "qkv", x0, (f1, f1o, bias_row(9)), 0.5, gain_row(1), bias_row(1), att, 3 * qc, 0, p, qkv_bias
    )
    if quick:
        qkv, col_c = fence(qkv, col_c)
        filc, e2c = col_c[:, :, : 3 * cc], col_c[:, :, 3 * cc :]
        filn = near(filc)
    o, chances = attend(qkv, table, length.reshape(1))
    if quick:
        filn, o, e2c = fence(filn, o, e2c)
        filf, e2n = far(filn), near(e2c)
    f2 = reduce_mm(o, att, qc, 3, p, width)
    if quick:
        filf, filn, f2 = fence(filf, filn, f2)
        fil = (filc, *filn, *filf)
    f2o = other_core(f2)
    x2, cn, gate, z = norm_expand(
        "conv", x1, (f2, f2o, bias_row(8)), 1.0, gain_row(2), bias_row(2), fil, 2 * cc, 0, p, None
    )
    y, y_sums = causal_mix(z, taps, taps_count)
    if quick:
        e2n, y_sums = fence(e2n, y_sums)
        e2f = far(e2n)
    y_sums = (y_sums, other_core(y_sums))
    f3, w = filter_out(y, y_sums, depth_gain, depth_bias, fil, cc, 2, p, width)
    if quick:
        e2f, f3 = fence(e2f, f3)
        e2 = (e2c, *e2n, *e2f)
    else:
        cot = settle(bring(cotangent))
    f3o = other_core(f3)
    x3, a2, u2, s2 = norm_expand(
        "ff", x2, (f3, f3o, jnp.zeros((1, width), WIDE)), 1.0, gain_row(4), bias_row(4),
        e2, ffc, 0, p, hidden2,
    )
    f4 = reduce_mm(s2, r2, ffc, 0, p, width)
    out_rows, gx4, gf2, sums_final = final_norm(
        x3, f4, other_core(f4), bias_row(10), cot, live, gain_row(5), bias_row(5)
    )

    b4, gc2, g_r2, g_e2 = ff_back(gf2, a2, u2, r2, e2, p, True)
    g_r2, g_e2, b4 = fence(g_r2, g_e2, b4)
    z_r2 = tensor_sum(g_r2)
    e2h1 = hop1(g_e2)
    gx3, gw, sums3 = norm_back(1.0, x3, gx4, b4, other_core(b4), gain_row(4))
    gyn, depth_cols, depth_rows = filter_in(
        gw, y, y_sums, depth_gain, depth_bias, fil, cc, 2, p
    )
    depth_rows = (depth_rows, other_core(depth_rows))
    b3, taps_grad, g_fil = mix_back(
        gyn, y, y_sums, depth_rows, depth_gain, z, gate, taps, taps_count, cn, gw, w, fil, p
    )
    e2h1, b3, g_fil = fence(e2h1, b3, g_fil)
    e2h2 = hop2(g_e2, e2h1)
    z_fil = tensor_sum(g_fil)
    gx2, gm, sums2 = norm_back(1.0, x2, gx3, b3, other_core(b3), gain_row(2))
    e2h2, gm = fence(e2h2, gm)
    z_e2 = hop3(g_e2, e2h1, e2h2)
    b2, gqkv_sums, table_grad, g_att = attend_back(gm, bn, qkv, chances, o, table, att, p)
    g_att, b2, z_r2 = fence(g_att, b2, z_r2)
    atth1 = hop1(g_att)
    gx1, gf1, sums1 = norm_back(0.5, x1, gx2, b2, other_core(b2), gain_row(1))
    b1, gc1, g_r1, g_e1 = ff_back(gf1, a1, u1, r1, e1, p, False)
    g_r1, g_e1, b1, atth1 = fence(g_r1, g_e1, b1, atth1)
    outputs = send_home(out_rows)
    r1h1 = hop1(g_r1)
    atth2 = hop2(g_att, atth1)
    gx0, _, sums0 = norm_back(1.0, x0, gx1, b1, other_core(b1), gain_row(0))
    atth2, r1h1, gx0, z_fil, outputs = fence(atth2, r1h1, gx0, z_fil, outputs)
    e1h1 = hop1(g_e1)
    r1h2 = hop2(g_r1, r1h1)
    z_att = hop3(g_att, atth1, atth2)

    table_rows = -(-buckets // 8)
    tail = jnp.transpose(table_grad[:HD])[1 : buckets - 1]
    ends = table_grad[HD : HD + 2, :HD]
    for e in range(1, qc // HD):
        ends = ends + table_grad[HD + 2 * e : HD + 2 * e + 2, e * HD : (e + 1) * HD]
    tail = jnp.concatenate([ends[:1], tail, ends[1:]], axis=0)
    tail = jnp.pad(tail, ((0, 8 * table_rows - buckets), (0, 0)))
    tail = tail.reshape(table_rows, 8, HD).transpose(1, 0, 2).reshape(8, table_rows * HD)
    tail = jnp.pad(tail, ((0, 0), (0, width - table_rows * HD)))
    small = pack(
        64, width, core1,
        [
            (sums_final, [("once", 0, 5), ("once", 1, 11), ("once", 2, 16)]),
            (sums3, [("once", 0, 4), ("once", 1, 10)]),
            (sums2, [("once", 0, 2), ("once", 1, 8), ("once", 2, 14)]),
            (sums1, [("once", 0, 1), ("once", 1, 7), ("once", 2, 15)]),
            (sums0, [("once", 0, 0), ("once", 1, 6)]),
            (gqkv_sums, [("row", (0, 0, 3 * qc, qc), 12), ("row", (0, 2 * qc, 3 * qc, qc), 13)]),
            (depth_cols, [("row", (0, 0, cc, cc), 3), ("row", (1, 0, cc, cc), 9)]),
            (gc1, [("hidden", 0, 17)]),
            (gc2, [("hidden", 0, 21)]),
            (taps_grad, [("taps", taps_count, 25)]),
            (tail, [("all", 0, 56)]),
        ],
    )
    half = small.shape[0] // 2
    mine = lax.dynamic_slice_in_dim(small, core * half, half, 0)
    came = other_core(lax.dynamic_slice_in_dim(small, (1 - core) * half, half, 0))
    homeward = send_home(gx0.astype(NARROW))
    r1h2, e1h1, came, z_e2, homeward = fence(r1h2, e1h1, came, z_e2, homeward)
    e1h2 = hop2(g_e1, e1h1)
    z_r1 = hop3(g_r1, r1h1, r1h2)
    planes_came = over_planes(mine + came)
    e1h2, planes_came = fence(e1h2, planes_came)
    t_e1, planes_came = fence(gathered(g_e1, e1h1, e1h2), planes_came)
    z_e1 = tensor_sum(t_e1)
    filx, r2x = across_x(z_fil), across_x(z_r2)
    mine = over_parts(planes_came)
    filx, r2x, mine, z_att = fence(filx, r2x, mine, z_att)
    fily, r2y = across_y(z_fil, filx), across_y(z_r2, r2x)
    e2_grad, att_grad = share(z_e2), share(z_att)
    theirs = other_core(mine)
    r2_grad = share(across_end(z_r2, r2x, r2y))
    fil_grad = share(across_end(z_fil, filx, fily))
    small = jnp.concatenate(
        [jnp.where(core == 0, mine, theirs), jnp.where(core == 0, theirs, mine)], axis=0
    )
    outputs = home(outputs)
    input_grad = home(homeward).astype(WIDE)
    r1_grad, e1_grad = share(z_r1), share(z_e1)
    gains_grad = small[0:6]
    bias_grad = small[6:25]
    taps_t = small[25 : 25 + taps_count]
    table_t = small[56:64, : table_rows * HD].reshape(8, table_rows, HD).transpose(1, 0, 2)
    table_t = table_t.reshape(8 * table_rows, HD)[:buckets]
    return (
        outputs,
        input_grad,
        rejoin(e1_grad, 0, ffc, 1),
        rejoin(r1_grad, 0, ffc, 1),
        rejoin(att_grad, 0, 3 * qc, 3),
        rejoin(att_grad, 3 * qc, qc, 1),
        rejoin(fil_grad, 0, 2 * cc, 2),
        rejoin(fil_grad, 2 * cc, cc, 1),
        rejoin(e2_grad, 0, ffc, 1),
        rejoin(r2_grad, 0, ffc, 1),
        gains_grad,
        bias_grad,
        taps_t,
        table_t,
    )


def solution(mesh):
    dp = mesh.shape["dp"]
    tensor = mesh.shape["tensor"]
    split = Mesh(mesh.devices.reshape(dp // 2, 2, tensor), ("plane", "pair", "tensor"))
    both = ("plane", "pair")
    rows = P(None, both, "tensor", None)
    flat = P(both, "tensor")
    deep = P(both, None, "tensor")
    weights = (flat, flat, deep, flat, deep, flat, flat, flat)
    small = (P(), P(), P(), P())
    return jax.shard_map(
        functools.partial(on_device, dp // 2),
        mesh=split,
        in_specs=(rows, P(None, both), rows, *weights, *small),
        out_specs=(rows, rows, *weights, *small),
        check_vma=False,
    )
```

```python
import functools

import jax
import jax.numpy as jnp
from jax import lax
from jax.experimental import pallas as pl
from jax.experimental.pallas import tpu as pltpu
from jax.sharding import Mesh
from jax.sharding import PartitionSpec as P

HD = 64
LEFT = 64
RIGHT = 8
EPSILON = 1e-05
MASKED = -1e30
WIDE = jnp.float32
NARROW = jnp.bfloat16
CHUNK = 256
MIX_CHUNK = 64
QROWS = 256
BROWS = 512
NEAR = 128
VMEM_BYTES = 48 * 1024 * 1024
MOST_VMEM = 60 * 1024 * 1024
PLANE_BLOCKS = 4
LANES = 128
COST_PART = 0.0005
PAD = 32


def sds(shape, dtype):
    return jax.ShapeDtypeStruct(shape, dtype)


def params(limit=VMEM_BYTES):
    return pltpu.CompilerParams(dimension_semantics=("arbitrary",), vmem_limit_bytes=limit)


def cost(flops, moved, exps=0):
    return pl.CostEstimate(
        flops=int(flops * COST_PART), bytes_accessed=int(moved * COST_PART), transcendentals=0
    )


def whole(shape):
    return pl.BlockSpec(shape, lambda *_: (0,) * len(shape))


def rel_cols(p, r, width):
    return pl.ds(pl.multiple_of(jnp.bitwise_xor(p, r) * width, width), width)


def weight_specs(w, cols, col_block):
    if len(w) == PLANE_BLOCKS:
        shape = (1, 1, w[0].shape[2], cols)
        return [
            pl.BlockSpec(shape, functools.partial(lambda r, t, p: (t, r, 0, col_block), r))
            for r in range(PLANE_BLOCKS)
        ]
    shape = (1, w[0].shape[1], cols)
    return [
        pl.BlockSpec(shape, lambda t, p: (t, 0, col_block)),
        pl.BlockSpec(shape, lambda t, p: (t, 0, col_block)),
        pl.BlockSpec(shape, lambda t, p: (t, 0, col_block)),
        pl.BlockSpec(shape, lambda t, p: (jnp.minimum(t, 1), 0, col_block)),
        pl.BlockSpec(shape, lambda t, p: (jnp.maximum(t - 2, 0), 0, col_block)),
    ]


def weight_blocks(w_refs, t):
    if len(w_refs) == PLANE_BLOCKS:
        return [ref[0, 0] for ref in w_refs]
    own, wx, wy, da, db = w_refs
    return own[0], wx[0], wy[0], jnp.where(t < 2, da[0], db[0])


def sigmoid(v):
    return 1.0 / (1.0 + jnp.exp(-v))


def norm_stats(v):
    mean = jnp.mean(v, axis=-1, keepdims=True)
    center = v - mean
    inv_std = lax.rsqrt(jnp.mean(center * center, axis=-1, keepdims=True) + EPSILON)
    return center * inv_std, inv_std


def expand_body(kind, merged, scale, nw, nr, p_ref, *refs):
    refs = list(refs)
    x_ref = refs.pop(0)
    if merged:
        pa_ref, pb_ref, ob_ref = refs[:3]
        refs = refs[3:]
    g_ref, b_ref = refs[:2]
    w_refs = refs[2 : 2 + nw]
    r_refs = refs[2 + nw : 2 + nw + nr]
    refs = refs[2 + nw + nr :]
    if kind != "conv":
        hb_ref = refs.pop(0)
    if merged:
        xn_ref = refs.pop(0)
    a_ref = refs.pop(0)
    outs = refs
    t = pl.program_id(0)
    p = p_ref[0]
    width = x_ref.shape[1] // PLANE_BLOCKS

    @pl.when(t == 0)
    def _():
        def step(i, carry):
            rows = pl.ds(pl.multiple_of(i * CHUNK, CHUNK), CHUNK)
            v = x_ref[rows, :]
            if merged:
                branch = pa_ref[rows, :].astype(WIDE) + pb_ref[rows, :].astype(WIDE)
                v = v + scale * (branch + ob_ref[...])
                xn_ref[rows, :] = v
            unit, _ = norm_stats(v)
            a_ref[rows, :] = (unit * g_ref[...] + b_ref[...]).astype(NARROW)
            return carry

        lax.fori_loop(0, x_ref.shape[0] // CHUNK, step, 0)

    acc = None
    for r, w in enumerate(weight_blocks(w_refs, t)):
        term = jnp.dot(a_ref[:, rel_cols(p, r, width)], w, preferred_element_type=WIDE)
        acc = term if acc is None else acc + term
    if kind == "ff":
        u = acc + hb_ref[...]
        outs[0][...] = u
        s = (u * sigmoid(u)).astype(NARROW)
        if nr == 0:
            outs[1][...] = s
        else:
            f_ref, acc_ref = outs[1:]
            reduce_into(acc_ref, s, r_refs, t, p)

            @pl.when(t == 3)
            def _():
                f_ref[...] = acc_ref[...].astype(NARROW)
    elif kind == "qkv":
        outs[0][...] = (acc + hb_ref[...]).astype(NARROW)
    else:
        half = acc.shape[1] // 2
        gate = sigmoid(acc[:, half:])
        outs[0][...] = gate
        outs[1][...] = acc[:, :half] * gate


def norm_expand(kind, x, merge, scale, gain, bias, w, cols, col_block, p, hidden_bias, wr=()):
    rows, width = x.shape
    merged = merge is not None
    ins = [x]
    specs = [whole((rows, width))]
    if merged:
        ins += list(merge)
        specs += [whole((rows, width)), whole((rows, width)), whole((1, width))]
    ins += [gain, bias, *w, *wr]
    specs += [whole((1, width)), whole((1, width)), *weight_specs(w, cols, col_block)]
    if wr:
        specs += weight_specs(wr, cols, 0)
    if kind != "conv":
        ins.append(hidden_bias)
        specs.append(pl.BlockSpec((1, cols), lambda t, p: (0, t)))
    shapes, out_specs = [], []
    if merged:
        shapes.append(sds((rows, width), WIDE))
        out_specs.append(whole((rows, width)))
    shapes.append(sds((rows, width), NARROW))
    out_specs.append(whole((rows, width)))
    if kind == "ff":
        outs = [(cols, WIDE)] if wr else [(cols, WIDE), (cols, NARROW)]
    elif kind == "qkv":
        outs = [(cols, NARROW)]
    else:
        outs = [(cols // 2, WIDE), (cols // 2, WIDE)]
    for out_cols, dtype in outs:
        shapes.append(sds((rows, 4 * out_cols), dtype))
        out_specs.append(pl.BlockSpec((rows, out_cols), lambda t, p: (0, t)))
    if wr:
        shapes.append(sds((rows, width), NARROW))
        out_specs.append(whole((rows, width)))
    return pl.pallas_call(
        functools.partial(expand_body, kind, merged, scale, len(w), len(wr)),
        grid_spec=pltpu.PrefetchScalarGridSpec(
            num_scalar_prefetch=1, grid=(4,), in_specs=specs, out_specs=out_specs,
            scratch_shapes=[pltpu.VMEM((rows, width), WIDE)] if wr else [],
        ),
        out_shape=shapes,
        compiler_params=params(),
        cost_estimate=cost(2 * rows * width * 4 * cols, 8 * width * cols + 12 * rows * width),
        name="norm_expand_" + kind,
    )(p, *ins)


def reduce_body(nw, p_ref, s_ref, *refs):
    w_refs = refs[:nw]
    out_ref, acc_ref = refs[nw:]
    t = pl.program_id(0)
    p = p_ref[0]
    width = out_ref.shape[1] // PLANE_BLOCKS
    s = s_ref[...]

    @pl.when(t == 0)
    def _():
        acc_ref[...] = jnp.zeros_like(acc_ref)

    for r, w in enumerate(weight_blocks(w_refs, t)):
        cols = rel_cols(p, r, width)
        acc_ref[:, cols] += lax.dot_general(
            s, w, (((1,), (1,)), ((), ())), preferred_element_type=WIDE
        )

    @pl.when(t == 3)
    def _():
        out_ref[...] = acc_ref[...].astype(NARROW)


def reduce_mm(s, w, cols, col_block, p, width):
    rows = s.shape[0]
    return pl.pallas_call(
        functools.partial(reduce_body, len(w)),
        grid_spec=pltpu.PrefetchScalarGridSpec(
            num_scalar_prefetch=1,
            grid=(4,),
            in_specs=[
                pl.BlockSpec((rows, cols), lambda t, p: (0, t)),
                *weight_specs(w, cols, col_block),
            ],
            out_specs=whole((rows, width)),
            scratch_shapes=[pltpu.VMEM((rows, width), WIDE)],
        ),
        out_shape=sds((rows, width), NARROW),
        compiler_params=params(),
        cost_estimate=cost(2 * rows * width * 4 * cols, 8 * width * cols + 2 * rows * width),
        name="reduce_mm",
    )(p, s, *w)


def combine_body(own_ref, rx_ref, ry_ref, fx_ref, fy_ref, out_ref):
    t = pl.program_id(0)
    near = jnp.where(t < 2, rx_ref[0, 0], ry_ref[0, 0])
    far = jnp.where(t < 2, fx_ref[0], fy_ref[0])
    total = own_ref[0].astype(WIDE) + near.astype(WIDE) + far.astype(WIDE)
    out_ref[0] = total.astype(NARROW)


def combine(own, rx, ry, fx, fy):
    rows, cols = own.shape[1:]
    first = lambda t: jnp.minimum(t, 1)
    last = lambda t: jnp.maximum(t - 2, 0)
    return pl.pallas_call(
        combine_body,
        grid=(4,),
        in_specs=[
            pl.BlockSpec((1, rows, cols), lambda t: (t, 0, 0)),
            pl.BlockSpec((1, 1, rows, cols), lambda t: (0, first(t), 0, 0)),
            pl.BlockSpec((1, 1, rows, cols), lambda t: (0, last(t), 0, 0)),
            pl.BlockSpec((1, rows, cols), lambda t: (first(t), 0, 0)),
            pl.BlockSpec((1, rows, cols), lambda t: (last(t), 0, 0)),
        ],
        out_specs=pl.BlockSpec((1, rows, cols), lambda t: (t, 0, 0)),
        out_shape=sds(own.shape, NARROW),
        compiler_params=params(),
        cost_estimate=cost(8 * rows * cols, 32 * rows * cols),
        name="combine",
    )(own, rx, ry, fx, fy)


def write_grads(t, p, pairs, refs):
    def grad(r, put):
        start = 0
        for x_ref, value in pairs:
            width = x_ref.shape[1] // PLANE_BLOCKS
            cols = value.shape[1]
            term = lax.dot_general(
                x_ref[:, rel_cols(p, r, width)],
                value,
                (((0,), (0,)), ((), ())),
                preferred_element_type=WIDE,
            ).astype(NARROW)
            put(slice(start, start + cols), term)
            start += cols

    def into(ref, *place):
        def put(cols, term):
            ref[(*place, slice(None), cols)] = term

        return put

    if len(refs) == 1:
        for r in range(PLANE_BLOCKS):
            grad(r, into(refs[0], 0, r))
        return
    own_ref, sx_ref, kx_ref, sy_ref, ky_ref = refs
    grad(0, into(own_ref, 0))

    @pl.when(t < 2)
    def _():
        grad(1, into(sx_ref, 0, 0))
        grad(3, into(sx_ref, 1, 0))
        grad(2, into(ky_ref, 0))

    @pl.when(t >= 2)
    def _():
        grad(2, into(sy_ref, 0, 0))
        grad(3, into(sy_ref, 1, 0))
        grad(1, into(kx_ref, 0))


def grad_outs(wrows, cols, flat):
    if flat:
        shape = (4, PLANE_BLOCKS, wrows, cols)
        spec = pl.BlockSpec((1, PLANE_BLOCKS, wrows, cols), lambda t, p: (t, 0, 0, 0))
        return [spec], [sds(shape, NARROW)]
    first = lambda t: jnp.minimum(t, 1)
    last = lambda t: jnp.maximum(t - 2, 0)
    specs = [
        pl.BlockSpec((1, wrows, cols), lambda t, p: (t, 0, 0)),
        pl.BlockSpec((2, 1, wrows, cols), lambda t, p: (0, first(t), 0, 0)),
        pl.BlockSpec((1, wrows, cols), lambda t, p: (last(t), 0, 0)),
        pl.BlockSpec((2, 1, wrows, cols), lambda t, p: (0, last(t), 0, 0)),
        pl.BlockSpec((1, wrows, cols), lambda t, p: (first(t), 0, 0)),
    ]
    shapes = [
        sds((4, wrows, cols), NARROW),
        sds((2, 2, wrows, cols), NARROW),
        sds((2, wrows, cols), NARROW),
        sds((2, 2, wrows, cols), NARROW),
        sds((2, wrows, cols), NARROW),
    ]
    return specs, shapes


def expand_from(g_ref, w_refs, t, p):
    width = g_ref.shape[1] // PLANE_BLOCKS
    acc = None
    for r, w in enumerate(weight_blocks(w_refs, t)):
        term = jnp.dot(g_ref[:, rel_cols(p, r, width)], w, preferred_element_type=WIDE)
        acc = term if acc is None else acc + term
    return acc


def reduce_into(acc_ref, value, w_refs, t, p):
    width = acc_ref.shape[1] // PLANE_BLOCKS

    @pl.when(t == 0)
    def _():
        acc_ref[...] = jnp.zeros_like(acc_ref)

    for r, w in enumerate(weight_blocks(w_refs, t)):
        acc_ref[:, rel_cols(p, r, width)] += lax.dot_general(
            value, w, (((1,), (1,)), ((), ())), preferred_element_type=WIDE
        )


def ff_back_body(nr, ne, fr, p_ref, g_ref, a_ref, u_ref, *refs):
    r_refs, e_refs = refs[:nr], refs[nr : nr + ne]
    b_ref, gc_ref = refs[nr + ne : nr + ne + 2]
    outs, acc_ref = refs[nr + ne + 2 : -1], refs[-1]
    t = pl.program_id(0)
    p = p_ref[0]
    grad = expand_from(g_ref, r_refs, t, p)
    u = u_ref[...]
    logistic = sigmoid(u)
    gu = grad * (logistic * (1.0 + u * (1.0 - logistic)))
    gc_ref[...] = jnp.sum(gu, axis=0, keepdims=True)
    low = gu.astype(NARROW)
    reduce_into(acc_ref, low, e_refs, t, p)
    write_grads(t, p, [(g_ref, (u * logistic).astype(NARROW))], outs[:fr])
    write_grads(t, p, [(a_ref, low)], outs[fr:])

    @pl.when(t == 3)
    def _():
        b_ref[...] = acc_ref[...].astype(NARROW)


def ff_back(g, a, u, wr, we, p, flat):
    rows, width = g.shape
    cols = u.shape[1] // 4
    wrows = width // PLANE_BLOCKS
    r_specs, r_shapes = grad_outs(wrows, cols, flat)
    e_specs, e_shapes = grad_outs(wrows, cols, False)
    out = pl.pallas_call(
        functools.partial(ff_back_body, len(wr), len(we), len(r_specs)),
        grid_spec=pltpu.PrefetchScalarGridSpec(
            num_scalar_prefetch=1,
            grid=(4,),
            in_specs=[
                whole((rows, width)),
                whole((rows, width)),
                pl.BlockSpec((rows, cols), lambda t, p: (0, t)),
                *weight_specs(wr, cols, 0),
                *weight_specs(we, cols, 0),
            ],
            out_specs=[
                whole((rows, width)),
                pl.BlockSpec((1, cols), lambda t, p: (0, t)),
                *r_specs,
                *e_specs,
            ],
            scratch_shapes=[pltpu.VMEM((rows, width), WIDE)],
        ),
        out_shape=[sds((rows, width), NARROW), sds((1, 4 * cols), WIDE), *r_shapes, *e_shapes],
        compiler_params=params(MOST_VMEM),
        cost_estimate=cost(32 * rows * width * cols, 32 * width * cols),
        name="ff_back",
    )(p, g, a, u, *wr, *we)
    g_r = out[2 : 2 + len(r_specs)]
    return out[0], out[1], (g_r[0] if flat else g_r), out[2 + len(r_specs) :]


def norm_back_body(scale, x_ref, gx_ref, pa_ref, pb_ref, g_ref, out_ref, low_ref, sums_ref):
    @pl.when(pl.program_id(0) == 0)
    def _():
        sums_ref[...] = jnp.zeros_like(sums_ref)

    unit, inv_std = norm_stats(x_ref[...])
    grad = pa_ref[...].astype(WIDE) + pb_ref[...].astype(WIDE)
    scaled = grad * g_ref[...]
    gx = gx_ref[...] + inv_std * (
        scaled
        - jnp.mean(scaled, axis=-1, keepdims=True)
        - unit * jnp.mean(scaled * unit, axis=-1, keepdims=True)
    )
    out_ref[...] = gx
    branch = scale * gx
    low_ref[...] = branch.astype(NARROW)
    sums_ref[0:1, :] += jnp.sum(grad * unit, axis=0, keepdims=True)
    sums_ref[1:2, :] += jnp.sum(grad, axis=0, keepdims=True)
    sums_ref[2:3, :] += jnp.sum(branch, axis=0, keepdims=True)


def norm_back(scale, x, gx, pa, pb, gain):
    rows, width = x.shape
    block = pl.BlockSpec((CHUNK, width), lambda i: (i, 0))
    return pl.pallas_call(
        functools.partial(norm_back_body, scale),
        grid=(rows // CHUNK,),
        in_specs=[block, block, block, block, whole((1, width))],
        out_specs=[block, block, whole((8, width))],
        out_shape=[sds((rows, width), WIDE), sds((rows, width), NARROW), sds((8, width), WIDE)],
        compiler_params=params(),
        cost_estimate=cost(20 * rows * width, 18 * rows * width),
        name="norm_back",
    )(x, gx, pa, pb, gain)


def final_body(
    x_ref, pa_ref, pb_ref, ob_ref, cot_ref, live_ref, g_ref, b_ref, y_ref, gx_ref, low_ref, sums_ref
):
    @pl.when(pl.program_id(0) == 0)
    def _():
        sums_ref[...] = jnp.zeros_like(sums_ref)

    branch = pa_ref[...].astype(WIDE) + pb_ref[...].astype(WIDE)
    v = x_ref[...] + 0.5 * (branch + ob_ref[...])
    unit, inv_std = norm_stats(v)
    live = live_ref[...]
    y_ref[...] = ((unit * g_ref[...] + b_ref[...]) * live).astype(NARROW)
    grad = cot_ref[...].astype(WIDE) * live
    scaled = grad * g_ref[...]
    gx = inv_std * (
        scaled
        - jnp.mean(scaled, axis=-1, keepdims=True)
        - unit * jnp.mean(scaled * unit, axis=-1, keepdims=True)
    )
    gx_ref[...] = gx
    half = 0.5 * gx
    low_ref[...] = half.astype(NARROW)
    sums_ref[0:1, :] += jnp.sum(grad * unit, axis=0, keepdims=True)
    sums_ref[1:2, :] += jnp.sum(grad, axis=0, keepdims=True)
    sums_ref[2:3, :] += jnp.sum(half, axis=0, keepdims=True)


def final_norm(x, pa, pb, ob, cot, live, gain, bias):
    rows, width = x.shape
    block = pl.BlockSpec((CHUNK, width), lambda i: (i, 0))
    row = whole((1, width))
    return pl.pallas_call(
        final_body,
        grid=(rows // CHUNK,),
        in_specs=[
            block, block, block, row, block,
            pl.BlockSpec((CHUNK, 1), lambda i: (i, 0)), row, row,
        ],
        out_specs=[block, block, block, whole((8, width))],
        out_shape=[
            sds((rows, width), NARROW),
            sds((rows, width), WIDE),
            sds((rows, width), NARROW),
            sds((8, width), WIDE),
        ],
        compiler_params=params(),
        cost_estimate=cost(24 * rows * width, 18 * rows * width),
        name="final_norm",
    )(x, pa, pb, ob, cot, live, gain, bias)


def distances(i0, keys, rows_here):
    rows = lax.broadcasted_iota(jnp.int32, (rows_here, keys), 0) + i0
    cols = lax.broadcasted_iota(jnp.int32, (rows_here, keys), 1)
    return cols - rows, cols


def head_lanes(rows, width, e):
    lane = lax.broadcasted_iota(jnp.int32, (rows, width), 1)
    return (lane >= e * HD) & (lane < (e + 1) * HD)


def doubled(table, heads):
    return jnp.concatenate([table] * heads, axis=1)


def attend_body(len_ref, qkv_ref, table_ref, o_ref, p_out_ref):
    keys = qkv_ref.shape[0]
    width = qkv_ref.shape[1] // 3
    heads = width // HD
    length = len_ref[0]
    table_turned = jnp.transpose(doubled(table_ref[...], heads))
    k_turned = jnp.transpose(qkv_ref[:, width : 2 * width])
    v = qkv_ref[:, 2 * width :]
    key_live = lax.broadcasted_iota(jnp.int32, (QROWS, keys), 1) < length
    masks = [head_lanes(QROWS, width, e) for e in range(heads)]
    for n in range(keys // QROWS):
        i0 = n * QROWS
        rows = slice(i0, i0 + QROWS)
        begin = max(0, i0 - NEAR)
        end = min(keys, i0 + QROWS + NEAR)
        span = end - begin
        apart = distances(i0 - begin, span, QROWS)[0]
        far_left = apart <= -LEFT
        far_right = apart >= RIGHT
        q_all = qkv_ref[rows, :width]
        merged = None
        for e in range(heads):
            q = jnp.where(masks[e], q_all, jnp.zeros_like(q_all))
            near = jnp.dot(q, table_turned, preferred_element_type=WIDE)
            left, right = near[:, 0:1], near[:, LEFT + RIGHT : LEFT + RIGHT + 1]
            band = jnp.concatenate([near, jnp.zeros((QROWS, span - NEAR), WIDE)], axis=1)
            band = pltpu.roll(band, (i0 - begin + span - LEFT) % span, 1, stride=1, stride_axis=0)
            pieces = [jnp.where(far_left, left, jnp.where(far_right, right, band))]
            if begin > 0:
                pieces.insert(0, jnp.broadcast_to(left, (QROWS, begin)))
            if end < keys:
                pieces.append(jnp.broadcast_to(right, (QROWS, keys - end)))
            rel = jnp.concatenate(pieces, axis=1) if len(pieces) > 1 else pieces[0]
            s = jnp.dot(q, k_turned, preferred_element_type=WIDE)
            s = jnp.where(key_live, (s + rel) * HD ** (-0.5), MASKED)
            top = jnp.max(s, axis=-1, keepdims=True)
            ex = jnp.exp(s - top)
            chance = (ex * (1.0 / row_sum(ex))).astype(NARROW)
            p_out_ref[e, rows, :] = chance
            part = jnp.dot(chance, v, preferred_element_type=WIDE)
            merged = part if merged is None else jnp.where(masks[e], part, merged)
        o_ref[rows, :] = merged.astype(NARROW)


def attend(qkv, table, length):
    rows = qkv.shape[0]
    width = qkv.shape[1] // 12
    heads = width // HD
    return pl.pallas_call(
        attend_body,
        grid_spec=pltpu.PrefetchScalarGridSpec(
            num_scalar_prefetch=1,
            grid=(4,),
            in_specs=[
                pl.BlockSpec((rows, 3 * width), lambda t, n: (0, t)),
                whole(table.shape),
            ],
            out_specs=[
                pl.BlockSpec((rows, width), lambda t, n: (0, t)),
                pl.BlockSpec((heads, rows, rows), lambda t, n: (t, 0, 0)),
            ],
        ),
        out_shape=[sds((rows, 4 * width), NARROW), sds((4 * heads, rows, rows), NARROW)],
        compiler_params=params(),
        cost_estimate=cost(16 * heads * rows * rows * HD, 10 * heads * rows * rows, 4 * heads * rows * rows),
        name="attend",
    )(length, qkv, table)


def attend_back_parts(qkv_ref, go_ref, p_ref, table_ref, out_ref, sums_ref, dist_ref, gk_ref, gv_ref):
    keys = qkv_ref.shape[0]
    width = qkv_ref.shape[1] // 3
    heads = width // HD
    table = doubled(table_ref[...], heads)
    scale = HD ** (-0.5)
    flip = (
        lax.broadcasted_iota(jnp.int32, (BROWS, BROWS), 0)
        + lax.broadcasted_iota(jnp.int32, (BROWS, BROWS), 1)
        == BROWS - 1
    ).astype(NARROW)
    bucket = lax.broadcasted_iota(jnp.int32, (BROWS, NEAR), 1)
    first_row = table[0:1, :].astype(WIDE)
    last_row = table[LEFT + RIGHT : LEFT + RIGHT + 1, :].astype(WIDE)
    masks = [head_lanes(BROWS, width, e) for e in range(heads)]

    @pl.when(pl.program_id(0) == 0)
    def _():
        dist_ref[...] = jnp.zeros_like(dist_ref)

    q_turned = jnp.transpose(qkv_ref[:, :width])
    go_turned = jnp.transpose(go_ref[...])
    v_turned = jnp.transpose(qkv_ref[:, 2 * width :])
    k = qkv_ref[:, width : 2 * width]
    for n in range(keys // BROWS):
        i0 = n * BROWS
        rows = slice(i0, i0 + BROWS)
        begin = max(0, i0 - NEAR)
        end = min(keys, i0 + BROWS + NEAR)
        span = end - begin
        apart = distances(i0 - begin, span, BROWS)[0]
        far_left = apart <= -LEFT
        far_right = apart >= RIGHT
        key_of = lax.broadcasted_iota(jnp.int32, (BROWS, NEAR), 0) + bucket + (i0 - LEFT)
        inside = (bucket > 0) & (bucket < LEFT + RIGHT) & (key_of >= 0) & (key_of < keys)
        q_wide = qkv_ref[rows, :width].astype(WIDE)
        go_all = go_ref[rows, :]
        merged = None
        for e in range(heads):
            some = slice(e * HD, (e + 1) * HD)
            go = jnp.where(masks[e], go_all, jnp.zeros_like(go_all))
            chance = p_ref[e, rows, :]
            wide = chance.astype(WIDE)
            gp = jnp.dot(go, v_turned, preferred_element_type=WIDE)
            gs = (wide * (gp - row_sum(gp * wide))).astype(NARROW)
            gsw = gs.astype(WIDE)
            window = gsw[:, begin:end]
            turned = jnp.dot(flip, gs[:, begin:end], preferred_element_type=WIDE)
            turned = pltpu.roll(
                turned, (LEFT + 1 - BROWS - (i0 - begin)) % span, 1, stride=1, stride_axis=0
            )[:, :NEAR]
            back = jnp.dot(flip, turned.astype(NARROW), preferred_element_type=WIDE)
            left_sum = row_sum(jnp.where(far_left, window, 0.0))
            right_sum = row_sum(jnp.where(far_right, window, 0.0))
            if begin > 0:
                left_sum += row_sum(gsw[:, :begin])
            if end < keys:
                right_sum += row_sum(gsw[:, end:])
            left_sum *= scale
            right_sum *= scale
            near = (jnp.where(inside, back, 0.0) * scale).astype(NARROW)
            gq = jnp.dot(gs, k, preferred_element_type=WIDE) * scale
            gq += jnp.dot(near, table, preferred_element_type=WIDE)
            gq += left_sum * first_row + right_sum * last_row
            merged = gq if merged is None else jnp.where(masks[e], gq, merged)
            q_part = q_turned[some, rows]
            dist_ref[:HD, :] += jnp.dot(q_part, near, preferred_element_type=WIDE)
            ends = HD + 2 * e
            dist_ref[ends : ends + 1, :] += jnp.sum(left_sum * q_wide, axis=0, keepdims=True)
            dist_ref[ends + 1 : ends + 2, :] += jnp.sum(right_sum * q_wide, axis=0, keepdims=True)
            gk = jnp.dot(q_part, gs, preferred_element_type=WIDE)
            gv = jnp.dot(go_turned[some, rows], chance, preferred_element_type=WIDE)
            if n == 0:
                gk_ref[some, :] = gk
                gv_ref[some, :] = gv
            else:
                gk_ref[some, :] += gk
                gv_ref[some, :] += gv
        out_ref[rows, :width] = merged.astype(NARROW)

    out_ref[:, width : 2 * width] = jnp.transpose(gk_ref[...] * scale).astype(NARROW)
    out_ref[:, 2 * width :] = jnp.transpose(gv_ref[...]).astype(NARROW)
    sums_ref[...] = jnp.sum(out_ref[...].astype(WIDE), axis=0, keepdims=True)


def attend_back_body(
    nw, s_ref, gm_ref, bn_ref, qkv_ref, chance_ref, o_ref, table_ref, *refs
):
    m_refs, w_refs = refs[:nw], refs[nw : 2 * nw]
    b_ref, sums_ref, dist_ref = refs[2 * nw : 2 * nw + 3]
    outs = refs[2 * nw + 3 : -5]
    acc_ref, go_ref, out_ref, gk_ref, gv_ref = refs[-5:]
    t = pl.program_id(0)
    p = s_ref[0]
    go_ref[...] = expand_from(gm_ref, m_refs, t, p).astype(NARROW)
    attend_back_parts(
        qkv_ref, go_ref, chance_ref, table_ref, out_ref, sums_ref, dist_ref, gk_ref, gv_ref
    )
    grad = out_ref[...]
    reduce_into(acc_ref, grad, w_refs, t, p)
    write_grads(t, p, [(bn_ref, grad), (gm_ref, o_ref[...])], outs)

    @pl.when(t == 3)
    def _():
        b_ref[...] = acc_ref[...].astype(NARROW)


def attend_back(gm, bn, qkv, chances, o, table, w, p):
    rows, width = gm.shape
    wrows = width // PLANE_BLOCKS
    cols = qkv.shape[1] // 12
    heads = cols // HD
    g_specs, g_shapes = grad_outs(wrows, 4 * cols, False)
    out = pl.pallas_call(
        functools.partial(attend_back_body, len(w)),
        grid_spec=pltpu.PrefetchScalarGridSpec(
            num_scalar_prefetch=1,
            grid=(4,),
            in_specs=[
                whole((rows, width)),
                whole((rows, width)),
                pl.BlockSpec((rows, 3 * cols), lambda t, p: (0, t)),
                pl.BlockSpec((heads, rows, rows), lambda t, p: (t, 0, 0)),
                pl.BlockSpec((rows, cols), lambda t, p: (0, t)),
                whole(table.shape),
                *weight_specs(w, cols, 3),
                *weight_specs(w, 3 * cols, 0),
            ],
            out_specs=[
                whole((rows, width)),
                pl.BlockSpec((1, 3 * cols), lambda t, p: (0, t)),
                whole((HD + 8, NEAR)),
                *g_specs,
            ],
            scratch_shapes=[
                pltpu.VMEM((rows, width), WIDE),
                pltpu.VMEM((rows, cols), NARROW),
                pltpu.VMEM((rows, 3 * cols), NARROW),
                pltpu.VMEM((cols, rows), WIDE),
                pltpu.VMEM((cols, rows), WIDE),
            ],
        ),
        out_shape=[
            sds((rows, width), NARROW),
            sds((1, 12 * cols), WIDE),
            sds((HD + 8, NEAR), WIDE),
            *g_shapes,
        ],
        compiler_params=params(MOST_VMEM),
        cost_estimate=cost(40 * heads * rows * rows * HD, 10 * heads * rows * rows),
        name="attend_back",
    )(p, gm, bn, qkv, chances, o, table, *w, *w)
    return out[0], out[1], out[2], out[3:]


def lane_pair(first, second, rows):
    lane = lax.broadcasted_iota(jnp.int32, (rows, LANES), 1)
    return jnp.where(lane == 0, first, jnp.where(lane == 1, second, 0.0))


def row_sum(v):
    return jnp.sum(v, axis=-1, keepdims=True)


def mix_body(taps_count, z_ref, taps_ref, y_ref, sums_ref, pad_ref):
    rows = z_ref.shape[0]

    @pl.when(pl.program_id(0) == 0)
    def _():
        sums_ref[...] = jnp.zeros_like(sums_ref)

    pad_ref[0:PAD, :] = jnp.zeros((PAD, pad_ref.shape[1]), WIDE)
    pad_ref[PAD:, :] = z_ref[...]
    for start in range(0, rows, MIX_CHUNK):
        total = None
        for i in range(taps_count):
            begin = start + PAD - taps_count + 1 + i
            term = taps_ref[i : i + 1, :] * pad_ref[begin : begin + MIX_CHUNK, :]
            total = term if total is None else total + term
        here = slice(start, start + MIX_CHUNK)
        y_ref[here, :] = total
        sums_ref[here, :] += lane_pair(row_sum(total), row_sum(total * total), MIX_CHUNK)


def causal_mix(z, taps, taps_count):
    rows, cols = z.shape
    block = pl.BlockSpec((rows, cols // 4), lambda t: (0, t))
    return pl.pallas_call(
        functools.partial(mix_body, taps_count),
        grid=(4,),
        in_specs=[block, pl.BlockSpec((taps.shape[0], cols // 4), lambda t: (0, t))],
        out_specs=[block, whole((rows, LANES))],
        out_shape=[sds((rows, cols), WIDE), sds((rows, LANES), WIDE)],
        scratch_shapes=[pltpu.VMEM((rows + PAD, cols // 4), WIDE)],
        compiler_params=params(),
        cost_estimate=cost(2 * taps_count * rows * cols, 8 * rows * cols),
        name="causal_mix",
    )(z, taps)


def depth_stats(sa_ref, sb_ref, here, width):
    sums = (sa_ref[here, :] + sb_ref[here, :]) * (1.0 / width)
    mean = sums[:, 0:1]
    return mean, lax.rsqrt(sums[:, 1:2] - mean * mean + EPSILON)


def filter_out_body(p_ref, y_ref, sa_ref, sb_ref, g_ref, b_ref, *refs):
    w_refs = refs[:5]
    out_ref, low_ref, acc_ref = refs[5:]
    t = pl.program_id(0)
    p = p_ref[0]
    width = out_ref.shape[1]
    mean, std = depth_stats(sa_ref, sb_ref, slice(None), width)
    yn = (y_ref[...] - mean) * std * g_ref[...] + b_ref[...]
    low = (yn * sigmoid(yn)).astype(NARROW)
    low_ref[...] = low

    @pl.when(t == 0)
    def _():
        acc_ref[...] = jnp.zeros_like(acc_ref)

    for r, w in enumerate(weight_blocks(w_refs, t)):
        cols = rel_cols(p, r, width // PLANE_BLOCKS)
        acc_ref[:, cols] += lax.dot_general(
            low, w, (((1,), (1,)), ((), ())), preferred_element_type=WIDE
        )

    @pl.when(t == 3)
    def _():
        out_ref[...] = acc_ref[...].astype(NARROW)


def filter_out(y, sums, gain, bias, w, cols, col_block, p, width):
    rows = y.shape[0]
    block = pl.BlockSpec((rows, cols), lambda t, p: (0, t))
    row = pl.BlockSpec((1, cols), lambda t, p: (0, t))
    return pl.pallas_call(
        filter_out_body,
        grid_spec=pltpu.PrefetchScalarGridSpec(
            num_scalar_prefetch=1,
            grid=(4,),
            in_specs=[
                block, whole((rows, LANES)), whole((rows, LANES)), row, row,
                *weight_specs(w, cols, col_block),
            ],
            out_specs=[whole((rows, width)), block],
            scratch_shapes=[pltpu.VMEM((rows, width), WIDE)],
        ),
        out_shape=[sds((rows, width), NARROW), sds(y.shape, NARROW)],
        compiler_params=params(),
        cost_estimate=cost(2 * rows * width * 4 * cols, 8 * width * cols + 6 * rows * width),
        name="filter_out",
    )(p, y, *sums, gain, bias, *w)


def filter_in_body(p_ref, grad_ref, y_ref, sa_ref, sb_ref, g_ref, b_ref, *refs):
    w_refs = refs[:5]
    gyn_ref, cols_ref, rows_ref = refs[5:]
    t = pl.program_id(0)
    p = p_ref[0]
    width = grad_ref.shape[1]
    acc = None
    for r, w in enumerate(weight_blocks(w_refs, t)):
        cols = rel_cols(p, r, width // PLANE_BLOCKS)
        term = jnp.dot(grad_ref[:, cols], w, preferred_element_type=WIDE)
        acc = term if acc is None else acc + term
    mean, std = depth_stats(sa_ref, sb_ref, slice(None), width)
    unit = (y_ref[...] - mean) * std
    yn = unit * g_ref[...] + b_ref[...]
    logistic = sigmoid(yn)
    gyn = acc * (logistic * (1.0 + yn * (1.0 - logistic)))
    gyn_ref[...] = gyn
    cols_ref[0:1, :] = jnp.sum(gyn * unit, axis=0, keepdims=True)
    cols_ref[1:2, :] = jnp.sum(gyn, axis=0, keepdims=True)
    scaled = gyn * g_ref[...]
    pair = lane_pair(row_sum(scaled), row_sum(scaled * unit), gyn.shape[0])

    @pl.when(t == 0)
    def _():
        rows_ref[...] = pair

    @pl.when(t > 0)
    def _():
        rows_ref[...] += pair


def filter_in(grad, y, sums, gain, bias, w, cols, col_block, p):
    rows, width = grad.shape
    block = pl.BlockSpec((rows, cols), lambda t, p: (0, t))
    row = pl.BlockSpec((1, cols), lambda t, p: (0, t))
    return pl.pallas_call(
        filter_in_body,
        grid_spec=pltpu.PrefetchScalarGridSpec(
            num_scalar_prefetch=1,
            grid=(4,),
            in_specs=[
                whole((rows, width)), block, whole((rows, LANES)), whole((rows, LANES)), row, row,
                *weight_specs(w, cols, col_block),
            ],
            out_specs=[
                block,
                pl.BlockSpec((8, cols), lambda t, p: (0, t)),
                whole((rows, LANES)),
            ],
        ),
        out_shape=[sds(y.shape, WIDE), sds((8, 4 * cols), WIDE), sds((rows, LANES), WIDE)],
        compiler_params=params(),
        cost_estimate=cost(2 * rows * width * 4 * cols, 8 * width * cols + 6 * rows * width),
        name="filter_in",
    )(p, grad, y, *sums, gain, bias, *w)


def mix_back_parts(
    taps_count, width, gyn_ref, y_ref, sa_ref, sb_ref, ra_ref, rb_ref, g_ref, z_ref, gate_ref,
    taps_ref, out_ref, grad_ref, gpad_ref, zpad_ref,
):
    rows, cols = z_ref.shape
    zpad_ref[0:PAD, :] = jnp.zeros((PAD, cols), WIDE)
    zpad_ref[PAD:, :] = z_ref[...]
    gpad_ref[rows:, :] = jnp.zeros((PAD, cols), WIDE)
    mean, std = depth_stats(sa_ref, sb_ref, slice(None), width)
    pair = (ra_ref[...] + rb_ref[...]) * (1.0 / width)
    unit = (y_ref[...] - mean) * std
    gpad_ref[0:rows, :] = std * (gyn_ref[...] * g_ref[...] - pair[:, 0:1] - unit * pair[:, 1:2])
    sums = [None] * taps_count
    for start in range(0, rows, MIX_CHUNK):
        here = slice(start, start + MIX_CHUNK)
        gy = gpad_ref[here, :]
        total = None
        for i in range(taps_count):
            begin = start + taps_count - 1 - i
            term = taps_ref[i : i + 1, :] * gpad_ref[begin : begin + MIX_CHUNK, :]
            total = term if total is None else total + term
        for i in range(taps_count):
            begin = start + PAD - taps_count + 1 + i
            part = zpad_ref[begin : begin + MIX_CHUNK, :] * gy
            part = jnp.sum(part.reshape(MIX_CHUNK // 8, 8, cols), axis=0)
            sums[i] = part if sums[i] is None else sums[i] + part
        gate = gate_ref[here, :]
        first = total * gate
        out_ref[here, :cols] = first.astype(NARROW)
        out_ref[here, cols:] = (total * z_ref[here, :] * (1.0 - gate)).astype(NARROW)
    for i in range(taps_count):
        grad_ref[i : i + 1, :] = jnp.sum(sums[i], axis=0, keepdims=True)


def mix_back_body(taps_count, width, nw, s_ref, *refs):
    parts, gate_taps = refs[:8], refs[8:10]
    cn_ref, gw_ref, wact_ref = refs[10:13]
    w_refs = refs[13 : 13 + nw]
    b_ref, grad_ref, flat_ref = refs[13 + nw : 16 + nw]
    acc_ref, out_ref, gpad_ref, zpad_ref = refs[16 + nw :]
    t = pl.program_id(0)
    p = s_ref[0]
    mix_back_parts(
        taps_count, width, *parts, *gate_taps, out_ref, grad_ref, gpad_ref, zpad_ref
    )
    grad = out_ref[...]
    reduce_into(acc_ref, grad, w_refs, t, p)
    write_grads(t, p, [(cn_ref, grad), (gw_ref, wact_ref[...])], [flat_ref])

    @pl.when(t == 3)
    def _():
        b_ref[...] = acc_ref[...].astype(NARROW)


def mix_back(gyn, y, sums, pairs, gain, z, gate, taps, taps_count, cn, gw, act, w, p):
    rows, cols = z.shape
    width = cn.shape[1]
    wrows = width // PLANE_BLOCKS
    n = cols // 4
    block = pl.BlockSpec((rows, n), lambda t, p: (0, t))
    row = pl.BlockSpec((1, n), lambda t, p: (0, t))
    lanes = whole((rows, LANES))
    tap_block = pl.BlockSpec((taps.shape[0], n), lambda t, p: (0, t))
    g_specs, g_shapes = grad_outs(wrows, 3 * n, True)
    return pl.pallas_call(
        functools.partial(mix_back_body, taps_count, width, len(w)),
        grid_spec=pltpu.PrefetchScalarGridSpec(
            num_scalar_prefetch=1,
            grid=(4,),
            in_specs=[
                block, block, lanes, lanes, lanes, lanes, row, block, block, tap_block,
                whole((rows, width)), whole((rows, width)), block,
                *weight_specs(w, 2 * n, 0),
            ],
            out_specs=[whole((rows, width)), tap_block, *g_specs],
            scratch_shapes=[
                pltpu.VMEM((rows, width), WIDE),
                pltpu.VMEM((rows, 2 * n), NARROW),
                pltpu.VMEM((rows + PAD, n), WIDE),
                pltpu.VMEM((rows + PAD, n), WIDE),
            ],
        ),
        out_shape=[sds((rows, width), NARROW), sds(taps.shape, WIDE), *g_shapes],
        compiler_params=params(MOST_VMEM),
        cost_estimate=cost(4 * taps_count * rows * cols, 20 * rows * cols),
        name="mix_back",
    )(p, gyn, y, *sums, *pairs, gain, z, gate, taps, cn, gw, act, *w)


def halve_body(groups, core_ref, *refs):
    count = sum(len(g) for g in groups)
    ins = list(refs[:count])
    keeps = refs[count : count + len(groups)]
    sends = refs[count + len(groups) :]
    low = core_ref[0] == 0
    for group, keep, send in zip(groups, keeps, sends):
        start = 0
        for n in group:
            ref = ins.pop(0)
            left, right = ref[:, :n], ref[:, n:]
            keep[:, start : start + n] = jnp.where(low, left, right)
            send[:, start : start + n] = jnp.where(low, right, left)
            start += n


def halve(groups, core):
    rows = groups[0][0].shape[0]
    halves = tuple(tuple(w.shape[1] // 2 for w in g) for g in groups)
    flat = [w for g in groups for w in g]
    shapes = [sds((rows, sum(h)), NARROW) for h in halves] * 2
    out = pl.pallas_call(
        functools.partial(halve_body, halves),
        grid_spec=pltpu.PrefetchScalarGridSpec(
            num_scalar_prefetch=1,
            grid=(1,),
            in_specs=[whole(w.shape) for w in flat],
            out_specs=[whole(s.shape) for s in shapes],
        ),
        out_shape=shapes,
        compiler_params=params(),
        cost_estimate=cost(0, 4 * sum(w.size for w in flat)),
        name="halve",
    )(core, *flat)
    return out[: len(groups)], out[len(groups) :]


def join_body(core_ref, keep_ref, came_ref, out_ref):
    low = core_ref[0] == 0
    rows = keep_ref.shape[0]
    keep, came = keep_ref[...], came_ref[...]
    out_ref[:rows, :] = jnp.where(low, keep, came)
    out_ref[rows:, :] = jnp.where(low, came, keep)


def join(keep, came, core):
    rows, cols = keep.shape
    return pl.pallas_call(
        join_body,
        grid_spec=pltpu.PrefetchScalarGridSpec(
            num_scalar_prefetch=1,
            grid=(1,),
            in_specs=[whole((rows, cols)), whole((rows, cols))],
            out_specs=whole((2 * rows, cols)),
        ),
        out_shape=sds((2 * rows, cols), keep.dtype),
        compiler_params=params(),
        cost_estimate=cost(0, 8 * rows * cols),
        name="join",
    )(core, keep, came)


def pack_body(lead, plan, core_ref, *refs):
    out_ref = refs[-1]
    low = core_ref[0] == 0
    out_ref[...] = jnp.zeros_like(out_ref)
    for ref, items in zip(refs[:-1], plan):
        for kind, src, dst in items:
            if kind == "once":
                v = ref[src : src + 1, :]
                out_ref[dst : dst + 1, :] = jnp.where(low, v, 0.0)
            elif kind == "all":
                out_ref[dst : dst + 8, :] = ref[...]
            elif kind == "taps":
                n = ref.shape[1] // 4
                for t in range(4):
                    v = ref[: src, t * n : (t + 1) * n]
                    out_ref[dst : dst + src, 2 * t * n : (2 * t + 1) * n] = jnp.where(low, v, 0.0)
                    out_ref[dst : dst + src, (2 * t + 1) * n : (2 * t + 2) * n] = jnp.where(low, 0.0, v)
            elif kind == "hidden":
                n = ref.shape[1] // 4
                for t in range(4):
                    v = ref[0:1, t * n : (t + 1) * n]
                    out_ref[dst + t : dst + t + 1, :n] = jnp.where(low, v, 0.0)
                    out_ref[dst + t : dst + t + 1, n:] = jnp.where(low, 0.0, v)
            else:
                row, first, step, n = src
                for t in range(4):
                    begin = t * step + first
                    v = ref[row : row + 1, begin : begin + n]
                    out_ref[dst : dst + 1, 2 * t * n : (2 * t + 1) * n] = jnp.where(low, v, 0.0)
                    out_ref[dst : dst + 1, (2 * t + 1) * n : (2 * t + 2) * n] = jnp.where(low, 0.0, v)


def pack(rows, width, core, sources):
    arrays = [a for a, _ in sources]
    plan = tuple(tuple(items) for _, items in sources)
    return pl.pallas_call(
        functools.partial(pack_body, rows, plan),
        grid_spec=pltpu.PrefetchScalarGridSpec(
            num_scalar_prefetch=1,
            grid=(1,),
            in_specs=[whole(a.shape) for a in arrays],
            out_specs=whole((rows, width)),
        ),
        out_shape=sds((rows, width), WIDE),
        compiler_params=params(),
        cost_estimate=cost(0, 8 * rows * width),
        name="pack",
    )(core, *arrays)


def on_device(planes, inputs, lengths, cotangent, *weights_and_rest):
    shards = weights_and_rest[:8]
    norm_gains, biases, kernel, distance_table = weights_and_rest[8:]
    batches, _, rows_here, width = inputs.shape
    parts = 4
    core = lax.axis_index("pair")
    plane = lax.axis_index("plane")
    part = lax.axis_index("tensor")
    quick = planes == PLANE_BLOCKS
    place = plane if quick else plane * 0
    p = place.astype(jnp.int32).reshape(1)

    def other_core(v):
        return lax.ppermute(v, "pair", [(0, 1), (1, 0)])

    def step_x(v):
        return lax.ppermute(v, "plane", [(i, i ^ 1) for i in range(planes)])

    def step_y(v):
        return lax.ppermute(v, "plane", [(i, i ^ 2) for i in range(planes)])

    def over_planes(v):
        if quick:
            return v + step_x(v) + step_y(v) + lax.ppermute(v, "plane", [(i, i ^ 3) for i in range(4)])
        bit = 1
        while bit < planes:
            v = v + lax.ppermute(v, "plane", [(i, i ^ bit) for i in range(planes)])
            bit *= 2
        return v

    def over_parts(v):
        def turn(k):
            return lax.ppermute(v, "tensor", [(i, i ^ k) for i in range(parts)])

        one, two, three = turn(1), turn(2), turn(3)
        return (v + one) + (two + three)

    def fence(*values):
        return lax.optimization_barrier(values) if quick else values

    def column_of(shard):
        return lax.all_gather(shard, "tensor", axis=0)

    def planes_of(column):
        every = lax.all_gather(column, "plane", axis=0)
        rows, cols = column.shape[1:]
        every = every.reshape(PLANE_BLOCKS, planes // PLANE_BLOCKS, parts, rows, cols)
        every = every.transpose(0, 2, 1, 3, 4).reshape(PLANE_BLOCKS, parts, -1, cols)
        return every[0], every[1], every[2], every[3, :2], every[3, 2:]

    def near(column):
        return step_x(column), step_y(column)

    def far(pair):
        return step_y(pair[0][:2]), step_x(pair[1][2:])

    def share(total):
        n = total.shape[0] // 2
        keep = lax.dynamic_slice_in_dim(total, core * n, n, 0)
        came = other_core(lax.dynamic_slice_in_dim(total, (1 - core) * n, n, 0))
        first = jnp.where(core == 0, keep, came).astype(WIDE)
        second = jnp.where(core == 0, came, keep).astype(WIDE)
        return first, second

    def tensor_sum(total):
        return lax.psum_scatter(total, "tensor", scatter_dimension=0)

    def across_x(every):
        return step_x(every[1::2]) if quick else ()

    def across_y(every, rx):
        return step_y(add(every[2], rx[1])) if quick else ()

    def across_end(every, rx, ry):
        if quick:
            return (every[0].astype(WIDE) + rx[0].astype(WIDE) + ry.astype(WIDE)).astype(NARROW)
        return lax.psum_scatter(
            every.reshape(planes, -1, every.shape[-1]), "plane", scatter_dimension=0
        )

    def hop1(grads):
        return (step_x(grads[1]), step_y(grads[3])) if quick else ()

    def hop2(grads, came):
        if not quick:
            return ()
        return step_y(add(grads[4], came[0][1])), step_x(add(grads[2], came[1][1]))

    def hop3(grads, came, last):
        return tensor_sum(gathered(grads, came, last))

    def gathered(grads, came, last):
        own, sx, kx, sy, ky = grads
        if quick:
            return combine(own, came[0], came[1], last[0], last[1])
        blocks = [
            own,
            jnp.concatenate([sx[0], kx]),
            jnp.concatenate([ky, sy[0]]),
            jnp.concatenate([sx[1], sy[1]]),
        ]
        every = jnp.stack(blocks)
        rows = width // planes
        cols = own.shape[-1]
        every = every.reshape(PLANE_BLOCKS, parts, planes // PLANE_BLOCKS, rows, cols)
        every = every.transpose(0, 2, 1, 3, 4).reshape(planes, parts, rows, cols)
        return lax.psum_scatter(every, "plane", scatter_dimension=0)

    def add(a, b):
        return (a.astype(WIDE) + b.astype(WIDE)).astype(NARROW)

    def rejoin(halves, start, cols, groups):
        pieces = [h[:, start : start + cols].reshape(h.shape[0], groups, -1) for h in halves]
        joined = jnp.concatenate(pieces, axis=2)
        return joined[:, 0] if groups == 1 else joined

    def spot(c, t):
        return c * parts + t

    def route(turn):
        pairs = []
        for c in range(2):
            for t in range(parts):
                mb = (turn + t) % 2
                pairs.append((spot(c, t), spot(t // 2, 2 * mb + c)))
        return pairs

    def bring_one(v, turn):
        mb = lax.rem(turn + part, 2)
        block = lax.dynamic_index_in_dim(v[:, 0], mb, 0, False)
        return lax.ppermute(block, ("pair", "tensor"), route(turn))

    def bring(v):
        return [bring_one(v, turn) for turn in range(2)]

    def settle(blocks):
        swap = part // 2 == 1
        mine = jnp.concatenate(
            [jnp.where(swap, blocks[1], blocks[0]), jnp.where(swap, blocks[0], blocks[1])], axis=0
        )
        theirs = other_core(mine)
        return jnp.concatenate(
            [jnp.where(core == 0, mine, theirs), jnp.where(core == 0, theirs, mine)], axis=0
        )

    def send_home(v):
        half = v.shape[0] // 2
        mine = lax.dynamic_slice_in_dim(v, core * half, half, 0)
        first, second = mine[: half // 2], mine[half // 2 :]
        swap = part // 2 == 1
        blocks = [jnp.where(swap, second, first), jnp.where(swap, first, second)]
        came = []
        for turn in range(2):
            back = [(b, a) for a, b in route(turn)]
            came.append(lax.ppermute(blocks[turn], ("pair", "tensor"), back))
        return came

    def home(came):
        odd = lax.rem(part, 2) == 1
        return jnp.stack([jnp.where(odd, came[1], came[0]), jnp.where(odd, came[0], came[1])])[:, None]

    (w_e1, w_r1, w_proj, w_merge, w_fe, w_fr, w_e2, w_r2) = shards
    core1 = core.astype(jnp.int32).reshape(1)
    ffc = w_e1.shape[1] // 2
    qc = w_proj.shape[2] // 2
    cc = w_fe.shape[2] // 2
    groups = [
        [w_e1],
        [w_r1],
        [w_proj[:, 0], w_proj[:, 1], w_proj[:, 2], w_merge],
        [w_fe[:, 0], w_fe[:, 1], w_fr, w_e2],
        [w_r2],
    ]
    keeps, sends = halve(groups, core1)
    pieces = fence(*[join(k, other_core(v), core1) for k, v in zip(keeps, sends)])

    gains = norm_gains.astype(WIDE)
    bias = biases.astype(WIDE)
    gain_row = lambda i: gains[i : i + 1]
    bias_row = lambda i: bias[i : i + 1]
    stride = w_e1.shape[1] * parts // width

    def pick(v):
        lead = v.shape[0]
        v = v.reshape(lead, parts, 2, -1)
        return lax.dynamic_index_in_dim(v, core, 2, False).reshape(lead, -1)

    hidden1 = pick(bias[11 : 11 + stride].reshape(1, -1))
    hidden2 = pick(bias[11 + stride : 11 + 2 * stride].reshape(1, -1))
    qb = pick(bias_row(6)).reshape(parts, 1, -1)
    vb = pick(bias_row(7)).reshape(parts, 1, -1)
    qkv_bias = jnp.concatenate([qb, jnp.zeros_like(qb), vb], axis=1).reshape(1, -1)
    taps_count = kernel.shape[0]
    taps = jnp.pad(pick(kernel.astype(WIDE)), ((0, PAD - taps_count), (0, 0)))
    depth_gain = pick(gain_row(3))
    depth_bias = pick(bias_row(3))
    buckets = distance_table.shape[0]
    table = jnp.pad(distance_table, ((0, NEAR - buckets), (0, 0)))

    pair_lengths = jnp.stack([lengths[:, 0], other_core(lengths[:, 0])])
    from_pair = jnp.bitwise_xor(lax.rem(part, 2), core)
    length = pair_lengths[from_pair, part // 2]
    rows_all = parts * inputs.shape[2]
    live = (jnp.arange(rows_all) < length).astype(WIDE)[:, None]

    col_e1 = column_of(pieces[0])
    r1c = column_of(pieces[1])
    attc = column_of(pieces[2])
    col_c = column_of(pieces[3])
    if quick:
        sd = pieces[4]
        sx, sy = step_x(sd), step_y(sd)
        sz = step_y(sx)
        col_e1, sx, sy, sz, source = fence(col_e1, sx, sy, sz, inputs)
        r2 = (column_of(jnp.stack([sd, sx, sy, sz])),) * PLANE_BLOCKS
        e1n, block0 = near(col_e1), bring_one(source, 0)
        e1n, r1c, block0, source = fence(e1n, r1c, block0, source)
        e1f, r1n, block1 = far(e1n), near(r1c), bring_one(source, 1)
        e1f, e1n, r1n, attc, block1, source = fence(e1f, e1n, r1n, attc, block1, cotangent)
        x0, cot0 = settle([block0, block1]), bring_one(source, 0)
        e1 = (col_e1, *e1n, *e1f)
        r1f, attn = far(r1n), near(attc)
    else:
        rows, cols = pieces[4].shape
        every = lax.all_gather(pieces[4], "plane", axis=0).reshape(PLANE_BLOCKS, -1, cols)
        r2 = (column_of(every),) * PLANE_BLOCKS
        x0 = settle(bring(inputs))
        e1 = planes_of(col_e1)
        r1 = planes_of(r1c)
        att = planes_of(attc)
        fil = planes_of(col_c[:, :, : 3 * cc])
        e2 = planes_of(col_c[:, :, 3 * cc :])
    x0 = x0.astype(WIDE)
    a1, u1, s1 = norm_expand("ff", x0, None, 0.5, gain_row(0), bias_row(0), e1, ffc, 0, p, hidden1)
    if quick:
        r1f, r1n, attn, s1, cot0, source = fence(r1f, r1n, attn, s1, cot0, source)
        cot1 = bring_one(source, 1)
        r1, attf = (r1c, *r1n, *r1f), far(attn)
    f1 = reduce_mm(s1, r1, ffc, 0, p, width)
    if quick:
        attf, attn, f1, col_c, cot1 = fence(attf, attn, f1, col_c, cot1)
        cot = settle([cot0, cot1])
        att = (attc, *attn, *attf)
    f1o = other_core(f1)
    x1, bn, qkv = norm_expand(
        "qkv", x0, (f1, f1o, bias_row(9)), 0.5, gain_row(1), bias_row(1), att, 3 * qc, 0, p, qkv_bias
    )
    if quick:
        qkv, col_c = fence(qkv, col_c)
        filc, e2c = col_c[:, :, : 3 * cc], col_c[:, :, 3 * cc :]
        filn = near(filc)
    o, chances = attend(qkv, table, length.reshape(1))
    if quick:
        filn, o, e2c = fence(filn, o, e2c)
        filf, e2n = far(filn), near(e2c)
    f2 = reduce_mm(o, att, qc, 3, p, width)
    if quick:
        filf, filn, f2 = fence(filf, filn, f2)
        fil = (filc, *filn, *filf)
    f2o = other_core(f2)
    x2, cn, gate, z = norm_expand(
        "conv", x1, (f2, f2o, bias_row(8)), 1.0, gain_row(2), bias_row(2), fil, 2 * cc, 0, p, None
    )
    y, y_sums = causal_mix(z, taps, taps_count)
    if quick:
        e2n, y_sums = fence(e2n, y_sums)
        e2f = far(e2n)
    y_sums = (y_sums, other_core(y_sums))
    f3, w = filter_out(y, y_sums, depth_gain, depth_bias, fil, cc, 2, p, width)
    if quick:
        e2f, f3 = fence(e2f, f3)
        e2 = (e2c, *e2n, *e2f)
    else:
        cot = settle(bring(cotangent))
    f3o = other_core(f3)
    x3, a2, u2, f4 = norm_expand(
        "ff", x2, (f3, f3o, jnp.zeros((1, width), WIDE)), 1.0, gain_row(4), bias_row(4),
        e2, ffc, 0, p, hidden2, r2,
    )
    out_rows, gx4, gf2, sums_final = final_norm(
        x3, f4, other_core(f4), bias_row(10), cot, live, gain_row(5), bias_row(5)
    )

    b4, gc2, g_r2, g_e2 = ff_back(gf2, a2, u2, r2, e2, p, True)
    g_r2, g_e2, b4 = fence(g_r2, g_e2, b4)
    z_r2 = tensor_sum(g_r2)
    e2h1 = hop1(g_e2)
    gx3, gw, sums3 = norm_back(1.0, x3, gx4, b4, other_core(b4), gain_row(4))
    gyn, depth_cols, depth_rows = filter_in(
        gw, y, y_sums, depth_gain, depth_bias, fil, cc, 2, p
    )
    depth_rows = (depth_rows, other_core(depth_rows))
    b3, taps_grad, g_fil = mix_back(
        gyn, y, y_sums, depth_rows, depth_gain, z, gate, taps, taps_count, cn, gw, w, fil, p
    )
    e2h1, b3, g_fil = fence(e2h1, b3, g_fil)
    e2h2 = hop2(g_e2, e2h1)
    z_fil = tensor_sum(g_fil)
    gx2, gm, sums2 = norm_back(1.0, x2, gx3, b3, other_core(b3), gain_row(2))
    e2h2, gm = fence(e2h2, gm)
    z_e2 = hop3(g_e2, e2h1, e2h2)
    b2, gqkv_sums, table_grad, g_att = attend_back(gm, bn, qkv, chances, o, table, att, p)
    g_att, b2, z_r2 = fence(g_att, b2, z_r2)
    atth1 = hop1(g_att)
    gx1, gf1, sums1 = norm_back(0.5, x1, gx2, b2, other_core(b2), gain_row(1))
    b1, gc1, g_r1, g_e1 = ff_back(gf1, a1, u1, r1, e1, p, False)
    g_r1, g_e1, b1, atth1 = fence(g_r1, g_e1, b1, atth1)
    outputs = send_home(out_rows)
    r1h1 = hop1(g_r1)
    atth2 = hop2(g_att, atth1)
    gx0, _, sums0 = norm_back(1.0, x0, gx1, b1, other_core(b1), gain_row(0))
    atth2, r1h1, gx0, z_fil, outputs = fence(atth2, r1h1, gx0, z_fil, outputs)
    e1h1 = hop1(g_e1)
    r1h2 = hop2(g_r1, r1h1)
    z_att = hop3(g_att, atth1, atth2)

    table_rows = -(-buckets // 8)
    tail = jnp.transpose(table_grad[:HD])[1 : buckets - 1]
    ends = table_grad[HD : HD + 2, :HD]
    for e in range(1, qc // HD):
        ends = ends + table_grad[HD + 2 * e : HD + 2 * e + 2, e * HD : (e + 1) * HD]
    tail = jnp.concatenate([ends[:1], tail, ends[1:]], axis=0)
    tail = jnp.pad(tail, ((0, 8 * table_rows - buckets), (0, 0)))
    tail = tail.reshape(table_rows, 8, HD).transpose(1, 0, 2).reshape(8, table_rows * HD)
    tail = jnp.pad(tail, ((0, 0), (0, width - table_rows * HD)))
    small = pack(
        64, width, core1,
        [
            (sums_final, [("once", 0, 5), ("once", 1, 11), ("once", 2, 16)]),
            (sums3, [("once", 0, 4), ("once", 1, 10)]),
            (sums2, [("once", 0, 2), ("once", 1, 8), ("once", 2, 14)]),
            (sums1, [("once", 0, 1), ("once", 1, 7), ("once", 2, 15)]),
            (sums0, [("once", 0, 0), ("once", 1, 6)]),
            (gqkv_sums, [("row", (0, 0, 3 * qc, qc), 12), ("row", (0, 2 * qc, 3 * qc, qc), 13)]),
            (depth_cols, [("row", (0, 0, cc, cc), 3), ("row", (1, 0, cc, cc), 9)]),
            (gc1, [("hidden", 0, 17)]),
            (gc2, [("hidden", 0, 21)]),
            (taps_grad, [("taps", taps_count, 25)]),
            (tail, [("all", 0, 56)]),
        ],
    )
    half = small.shape[0] // 2
    mine = lax.dynamic_slice_in_dim(small, core * half, half, 0)
    came = other_core(lax.dynamic_slice_in_dim(small, (1 - core) * half, half, 0))
    homeward = send_home(gx0.astype(NARROW))
    r1h2, e1h1, came, z_e2, homeward = fence(r1h2, e1h1, came, z_e2, homeward)
    e1h2 = hop2(g_e1, e1h1)
    z_r1 = hop3(g_r1, r1h1, r1h2)
    planes_came = over_planes(mine + came)
    e1h2, planes_came = fence(e1h2, planes_came)
    t_e1, planes_came = fence(gathered(g_e1, e1h1, e1h2), planes_came)
    z_e1 = tensor_sum(t_e1)
    filx, r2x = across_x(z_fil), across_x(z_r2)
    mine = over_parts(planes_came)
    filx, r2x, mine, z_att = fence(filx, r2x, mine, z_att)
    fily, r2y = across_y(z_fil, filx), across_y(z_r2, r2x)
    e2_grad, att_grad = share(z_e2), share(z_att)
    theirs = other_core(mine)
    r2_grad = share(across_end(z_r2, r2x, r2y))
    fil_grad = share(across_end(z_fil, filx, fily))
    small = jnp.concatenate(
        [jnp.where(core == 0, mine, theirs), jnp.where(core == 0, theirs, mine)], axis=0
    )
    outputs = home(outputs)
    input_grad = home(homeward).astype(WIDE)
    r1_grad, e1_grad = share(z_r1), share(z_e1)
    gains_grad = small[0:6]
    bias_grad = small[6:25]
    taps_t = small[25 : 25 + taps_count]
    table_t = small[56:64, : table_rows * HD].reshape(8, table_rows, HD).transpose(1, 0, 2)
    table_t = table_t.reshape(8 * table_rows, HD)[:buckets]
    return (
        outputs,
        input_grad,
        rejoin(e1_grad, 0, ffc, 1),
        rejoin(r1_grad, 0, ffc, 1),
        rejoin(att_grad, 0, 3 * qc, 3),
        rejoin(att_grad, 3 * qc, qc, 1),
        rejoin(fil_grad, 0, 2 * cc, 2),
        rejoin(fil_grad, 2 * cc, cc, 1),
        rejoin(e2_grad, 0, ffc, 1),
        rejoin(r2_grad, 0, ffc, 1),
        gains_grad,
        bias_grad,
        taps_t,
        table_t,
    )


def solution(mesh):
    dp = mesh.shape["dp"]
    tensor = mesh.shape["tensor"]
    split = Mesh(mesh.devices.reshape(dp // 2, 2, tensor), ("plane", "pair", "tensor"))
    both = ("plane", "pair")
    rows = P(None, both, "tensor", None)
    flat = P(both, "tensor")
    deep = P(both, None, "tensor")
    weights = (flat, flat, deep, flat, deep, flat, flat, flat)
    small = (P(), P(), P(), P())
    return jax.shard_map(
        functools.partial(on_device, dp // 2),
        mesh=split,
        in_specs=(rows, P(None, both), rows, *weights, *small),
        out_specs=(rows, rows, *weights, *small),
        check_vma=False,
    )
```

```python
import functools

import jax
import jax.numpy as jnp
from jax import lax
from jax.experimental import pallas as pl
from jax.experimental.pallas import tpu as pltpu
from jax.sharding import Mesh
from jax.sharding import PartitionSpec as P

HD = 64
LEFT = 64
RIGHT = 8
EPSILON = 1e-05
MASKED = -1e30
WIDE = jnp.float32
NARROW = jnp.bfloat16
CHUNK = 256
MIX_CHUNK = 64
QROWS = 256
BROWS = 512
NEAR = 128
VMEM_BYTES = 48 * 1024 * 1024
MOST_VMEM = 60 * 1024 * 1024
PLANE_BLOCKS = 4
LANES = 128
COST_PART = 0.0005
PAD = 32


def sds(shape, dtype):
    return jax.ShapeDtypeStruct(shape, dtype)


def params(limit=VMEM_BYTES):
    return pltpu.CompilerParams(dimension_semantics=("arbitrary",), vmem_limit_bytes=limit)


def cost(flops, moved, exps=0):
    return pl.CostEstimate(
        flops=int(flops * COST_PART), bytes_accessed=int(moved * COST_PART), transcendentals=0
    )


def whole(shape):
    return pl.BlockSpec(shape, lambda *_: (0,) * len(shape))


def rel_cols(p, r, width):
    return pl.ds(pl.multiple_of(jnp.bitwise_xor(p, r) * width, width), width)


def weight_specs(w, cols, col_block):
    if len(w) == PLANE_BLOCKS:
        shape = (1, 1, w[0].shape[2], cols)
        return [
            pl.BlockSpec(shape, functools.partial(lambda r, t, p: (t, r, 0, col_block), r))
            for r in range(PLANE_BLOCKS)
        ]
    shape = (1, w[0].shape[1], cols)
    return [
        pl.BlockSpec(shape, lambda t, p: (t, 0, col_block)),
        pl.BlockSpec(shape, lambda t, p: (t, 0, col_block)),
        pl.BlockSpec(shape, lambda t, p: (t, 0, col_block)),
        pl.BlockSpec(shape, lambda t, p: (jnp.minimum(t, 1), 0, col_block)),
        pl.BlockSpec(shape, lambda t, p: (jnp.maximum(t - 2, 0), 0, col_block)),
    ]


def weight_blocks(w_refs, t):
    if len(w_refs) == PLANE_BLOCKS:
        return [ref[0, 0] for ref in w_refs]
    own, wx, wy, da, db = w_refs
    return own[0], wx[0], wy[0], jnp.where(t < 2, da[0], db[0])


def sigmoid(v):
    return 1.0 / (1.0 + jnp.exp(-v))


def norm_stats(v):
    mean = jnp.mean(v, axis=-1, keepdims=True)
    center = v - mean
    inv_std = lax.rsqrt(jnp.mean(center * center, axis=-1, keepdims=True) + EPSILON)
    return center * inv_std, inv_std


def expand_body(kind, merged, scale, nw, nr, p_ref, *refs):
    refs = list(refs)
    x_ref = refs.pop(0)
    if merged:
        pa_ref, pb_ref, ob_ref = refs[:3]
        refs = refs[3:]
    g_ref, b_ref = refs[:2]
    w_refs = refs[2 : 2 + nw]
    r_refs = refs[2 + nw : 2 + nw + nr]
    refs = refs[2 + nw + nr :]
    if kind != "conv":
        hb_ref = refs.pop(0)
    if merged:
        xn_ref = refs.pop(0)
    a_ref = refs.pop(0)
    outs = refs
    t = pl.program_id(0)
    p = p_ref[0]
    width = x_ref.shape[1] // PLANE_BLOCKS

    @pl.when(t == 0)
    def _():
        def step(i, carry):
            rows = pl.ds(pl.multiple_of(i * CHUNK, CHUNK), CHUNK)
            v = x_ref[rows, :]
            if merged:
                branch = pa_ref[rows, :].astype(WIDE) + pb_ref[rows, :].astype(WIDE)
                v = v + scale * (branch + ob_ref[...])
                xn_ref[rows, :] = v
            unit, _ = norm_stats(v)
            a_ref[rows, :] = (unit * g_ref[...] + b_ref[...]).astype(NARROW)
            return carry

        lax.fori_loop(0, x_ref.shape[0] // CHUNK, step, 0)

    acc = None
    for r, w in enumerate(weight_blocks(w_refs, t)):
        term = jnp.dot(a_ref[:, rel_cols(p, r, width)], w, preferred_element_type=WIDE)
        acc = term if acc is None else acc + term
    if kind == "ff":
        u = acc + hb_ref[...]
        outs[0][...] = u
        s = (u * sigmoid(u)).astype(NARROW)
        if nr == 0:
            outs[1][...] = s
        else:
            f_ref, acc_ref = outs[1:]
            reduce_into(acc_ref, s, r_refs, t, p)

            @pl.when(t == 3)
            def _():
                f_ref[...] = acc_ref[...].astype(NARROW)
    elif kind == "qkv":
        outs[0][...] = (acc + hb_ref[...]).astype(NARROW)
    else:
        half = acc.shape[1] // 2
        gate = sigmoid(acc[:, half:])
        outs[0][...] = gate
        outs[1][...] = acc[:, :half] * gate


def norm_expand(kind, x, merge, scale, gain, bias, w, cols, col_block, p, hidden_bias, wr=()):
    rows, width = x.shape
    merged = merge is not None
    ins = [x]
    specs = [whole((rows, width))]
    if merged:
        ins += list(merge)
        specs += [whole((rows, width)), whole((rows, width)), whole((1, width))]
    ins += [gain, bias, *w, *wr]
    specs += [whole((1, width)), whole((1, width)), *weight_specs(w, cols, col_block)]
    if wr:
        specs += weight_specs(wr, cols, 0)
    if kind != "conv":
        ins.append(hidden_bias)
        specs.append(pl.BlockSpec((1, cols), lambda t, p: (0, t)))
    shapes, out_specs = [], []
    if merged:
        shapes.append(sds((rows, width), WIDE))
        out_specs.append(whole((rows, width)))
    shapes.append(sds((rows, width), NARROW))
    out_specs.append(whole((rows, width)))
    if kind == "ff":
        outs = [(cols, WIDE)] if wr else [(cols, WIDE), (cols, NARROW)]
    elif kind == "qkv":
        outs = [(cols, NARROW)]
    else:
        outs = [(cols // 2, WIDE), (cols // 2, WIDE)]
    for out_cols, dtype in outs:
        shapes.append(sds((rows, 4 * out_cols), dtype))
        out_specs.append(pl.BlockSpec((rows, out_cols), lambda t, p: (0, t)))
    if wr:
        shapes.append(sds((rows, width), NARROW))
        out_specs.append(whole((rows, width)))
    return pl.pallas_call(
        functools.partial(expand_body, kind, merged, scale, len(w), len(wr)),
        grid_spec=pltpu.PrefetchScalarGridSpec(
            num_scalar_prefetch=1, grid=(4,), in_specs=specs, out_specs=out_specs,
            scratch_shapes=[pltpu.VMEM((rows, width), WIDE)] if wr else [],
        ),
        out_shape=shapes,
        compiler_params=params(),
        cost_estimate=cost(2 * rows * width * 4 * cols, 8 * width * cols + 12 * rows * width),
        name="norm_expand_" + kind,
    )(p, *ins)


def reduce_body(nw, p_ref, s_ref, *refs):
    w_refs = refs[:nw]
    out_ref, acc_ref = refs[nw:]
    t = pl.program_id(0)
    p = p_ref[0]
    width = out_ref.shape[1] // PLANE_BLOCKS
    s = s_ref[...]

    @pl.when(t == 0)
    def _():
        acc_ref[...] = jnp.zeros_like(acc_ref)

    for r, w in enumerate(weight_blocks(w_refs, t)):
        cols = rel_cols(p, r, width)
        acc_ref[:, cols] += lax.dot_general(
            s, w, (((1,), (1,)), ((), ())), preferred_element_type=WIDE
        )

    @pl.when(t == 3)
    def _():
        out_ref[...] = acc_ref[...].astype(NARROW)


def reduce_mm(s, w, cols, col_block, p, width):
    rows = s.shape[0]
    return pl.pallas_call(
        functools.partial(reduce_body, len(w)),
        grid_spec=pltpu.PrefetchScalarGridSpec(
            num_scalar_prefetch=1,
            grid=(4,),
            in_specs=[
                pl.BlockSpec((rows, cols), lambda t, p: (0, t)),
                *weight_specs(w, cols, col_block),
            ],
            out_specs=whole((rows, width)),
            scratch_shapes=[pltpu.VMEM((rows, width), WIDE)],
        ),
        out_shape=sds((rows, width), NARROW),
        compiler_params=params(),
        cost_estimate=cost(2 * rows * width * 4 * cols, 8 * width * cols + 2 * rows * width),
        name="reduce_mm",
    )(p, s, *w)


def combine_body(own_ref, rx_ref, ry_ref, fx_ref, fy_ref, out_ref):
    t = pl.program_id(0)
    near = jnp.where(t < 2, rx_ref[0, 0], ry_ref[0, 0])
    far = jnp.where(t < 2, fx_ref[0], fy_ref[0])
    total = own_ref[0].astype(WIDE) + near.astype(WIDE) + far.astype(WIDE)
    out_ref[0] = total.astype(NARROW)


def combine(own, rx, ry, fx, fy):
    rows, cols = own.shape[1:]
    first = lambda t: jnp.minimum(t, 1)
    last = lambda t: jnp.maximum(t - 2, 0)
    return pl.pallas_call(
        combine_body,
        grid=(4,),
        in_specs=[
            pl.BlockSpec((1, rows, cols), lambda t: (t, 0, 0)),
            pl.BlockSpec((1, 1, rows, cols), lambda t: (0, first(t), 0, 0)),
            pl.BlockSpec((1, 1, rows, cols), lambda t: (0, last(t), 0, 0)),
            pl.BlockSpec((1, rows, cols), lambda t: (first(t), 0, 0)),
            pl.BlockSpec((1, rows, cols), lambda t: (last(t), 0, 0)),
        ],
        out_specs=pl.BlockSpec((1, rows, cols), lambda t: (t, 0, 0)),
        out_shape=sds(own.shape, NARROW),
        compiler_params=params(),
        cost_estimate=cost(8 * rows * cols, 32 * rows * cols),
        name="combine",
    )(own, rx, ry, fx, fy)


def write_grads(t, p, pairs, refs):
    def grad(r, put):
        start = 0
        for x_ref, value in pairs:
            width = x_ref.shape[1] // PLANE_BLOCKS
            cols = value.shape[1]
            term = lax.dot_general(
                x_ref[:, rel_cols(p, r, width)],
                value,
                (((0,), (0,)), ((), ())),
                preferred_element_type=WIDE,
            ).astype(NARROW)
            put(slice(start, start + cols), term)
            start += cols

    def into(ref, *place):
        def put(cols, term):
            ref[(*place, slice(None), cols)] = term

        return put

    if len(refs) == 1:
        for r in range(PLANE_BLOCKS):
            grad(r, into(refs[0], 0, r))
        return
    own_ref, sx_ref, kx_ref, sy_ref, ky_ref = refs
    grad(0, into(own_ref, 0))

    @pl.when(t < 2)
    def _():
        grad(1, into(sx_ref, 0, 0))
        grad(3, into(sx_ref, 1, 0))
        grad(2, into(ky_ref, 0))

    @pl.when(t >= 2)
    def _():
        grad(2, into(sy_ref, 0, 0))
        grad(3, into(sy_ref, 1, 0))
        grad(1, into(kx_ref, 0))


def grad_outs(wrows, cols, flat):
    if flat:
        shape = (4, PLANE_BLOCKS, wrows, cols)
        spec = pl.BlockSpec((1, PLANE_BLOCKS, wrows, cols), lambda t, p: (t, 0, 0, 0))
        return [spec], [sds(shape, NARROW)]
    first = lambda t: jnp.minimum(t, 1)
    last = lambda t: jnp.maximum(t - 2, 0)
    specs = [
        pl.BlockSpec((1, wrows, cols), lambda t, p: (t, 0, 0)),
        pl.BlockSpec((2, 1, wrows, cols), lambda t, p: (0, first(t), 0, 0)),
        pl.BlockSpec((1, wrows, cols), lambda t, p: (last(t), 0, 0)),
        pl.BlockSpec((2, 1, wrows, cols), lambda t, p: (0, last(t), 0, 0)),
        pl.BlockSpec((1, wrows, cols), lambda t, p: (first(t), 0, 0)),
    ]
    shapes = [
        sds((4, wrows, cols), NARROW),
        sds((2, 2, wrows, cols), NARROW),
        sds((2, wrows, cols), NARROW),
        sds((2, 2, wrows, cols), NARROW),
        sds((2, wrows, cols), NARROW),
    ]
    return specs, shapes


def expand_from(g_ref, w_refs, t, p):
    width = g_ref.shape[1] // PLANE_BLOCKS
    acc = None
    for r, w in enumerate(weight_blocks(w_refs, t)):
        term = jnp.dot(g_ref[:, rel_cols(p, r, width)], w, preferred_element_type=WIDE)
        acc = term if acc is None else acc + term
    return acc


def reduce_into(acc_ref, value, w_refs, t, p):
    width = acc_ref.shape[1] // PLANE_BLOCKS

    @pl.when(t == 0)
    def _():
        acc_ref[...] = jnp.zeros_like(acc_ref)

    for r, w in enumerate(weight_blocks(w_refs, t)):
        acc_ref[:, rel_cols(p, r, width)] += lax.dot_general(
            value, w, (((1,), (1,)), ((), ())), preferred_element_type=WIDE
        )


def ff_back_body(nr, ne, fr, p_ref, g_ref, a_ref, u_ref, *refs):
    r_refs, e_refs = refs[:nr], refs[nr : nr + ne]
    b_ref, gc_ref = refs[nr + ne : nr + ne + 2]
    outs, acc_ref = refs[nr + ne + 2 : -1], refs[-1]
    t = pl.program_id(0)
    p = p_ref[0]
    grad = expand_from(g_ref, r_refs, t, p)
    u = u_ref[...]
    logistic = sigmoid(u)
    gu = grad * (logistic * (1.0 + u * (1.0 - logistic)))
    gc_ref[...] = jnp.sum(gu, axis=0, keepdims=True)
    low = gu.astype(NARROW)
    reduce_into(acc_ref, low, e_refs, t, p)
    write_grads(t, p, [(g_ref, (u * logistic).astype(NARROW))], outs[:fr])
    write_grads(t, p, [(a_ref, low)], outs[fr:])

    @pl.when(t == 3)
    def _():
        b_ref[...] = acc_ref[...].astype(NARROW)


def ff_back(g, a, u, wr, we, p, flat):
    rows, width = g.shape
    cols = u.shape[1] // 4
    wrows = width // PLANE_BLOCKS
    r_specs, r_shapes = grad_outs(wrows, cols, flat)
    e_specs, e_shapes = grad_outs(wrows, cols, False)
    out = pl.pallas_call(
        functools.partial(ff_back_body, len(wr), len(we), len(r_specs)),
        grid_spec=pltpu.PrefetchScalarGridSpec(
            num_scalar_prefetch=1,
            grid=(4,),
            in_specs=[
                whole((rows, width)),
                whole((rows, width)),
                pl.BlockSpec((rows, cols), lambda t, p: (0, t)),
                *weight_specs(wr, cols, 0),
                *weight_specs(we, cols, 0),
            ],
            out_specs=[
                whole((rows, width)),
                pl.BlockSpec((1, cols), lambda t, p: (0, t)),
                *r_specs,
                *e_specs,
            ],
            scratch_shapes=[pltpu.VMEM((rows, width), WIDE)],
        ),
        out_shape=[sds((rows, width), NARROW), sds((1, 4 * cols), WIDE), *r_shapes, *e_shapes],
        compiler_params=params(MOST_VMEM),
        cost_estimate=cost(32 * rows * width * cols, 32 * width * cols),
        name="ff_back",
    )(p, g, a, u, *wr, *we)
    g_r = out[2 : 2 + len(r_specs)]
    return out[0], out[1], (g_r[0] if flat else g_r), out[2 + len(r_specs) :]


def norm_back_body(scale, x_ref, gx_ref, pa_ref, pb_ref, g_ref, out_ref, low_ref, sums_ref):
    @pl.when(pl.program_id(0) == 0)
    def _():
        sums_ref[...] = jnp.zeros_like(sums_ref)

    unit, inv_std = norm_stats(x_ref[...])
    grad = pa_ref[...].astype(WIDE) + pb_ref[...].astype(WIDE)
    scaled = grad * g_ref[...]
    gx = gx_ref[...] + inv_std * (
        scaled
        - jnp.mean(scaled, axis=-1, keepdims=True)
        - unit * jnp.mean(scaled * unit, axis=-1, keepdims=True)
    )
    out_ref[...] = gx
    branch = scale * gx
    low_ref[...] = branch.astype(NARROW)
    sums_ref[0:1, :] += jnp.sum(grad * unit, axis=0, keepdims=True)
    sums_ref[1:2, :] += jnp.sum(grad, axis=0, keepdims=True)
    sums_ref[2:3, :] += jnp.sum(branch, axis=0, keepdims=True)


def norm_back(scale, x, gx, pa, pb, gain):
    rows, width = x.shape
    block = pl.BlockSpec((CHUNK, width), lambda i: (i, 0))
    return pl.pallas_call(
        functools.partial(norm_back_body, scale),
        grid=(rows // CHUNK,),
        in_specs=[block, block, block, block, whole((1, width))],
        out_specs=[block, block, whole((8, width))],
        out_shape=[sds((rows, width), WIDE), sds((rows, width), NARROW), sds((8, width), WIDE)],
        compiler_params=params(),
        cost_estimate=cost(20 * rows * width, 18 * rows * width),
        name="norm_back",
    )(x, gx, pa, pb, gain)


def final_body(
    x_ref, pa_ref, pb_ref, ob_ref, cot_ref, live_ref, g_ref, b_ref, y_ref, gx_ref, low_ref, sums_ref
):
    @pl.when(pl.program_id(0) == 0)
    def _():
        sums_ref[...] = jnp.zeros_like(sums_ref)

    branch = pa_ref[...].astype(WIDE) + pb_ref[...].astype(WIDE)
    v = x_ref[...] + 0.5 * (branch + ob_ref[...])
    unit, inv_std = norm_stats(v)
    live = live_ref[...]
    y_ref[...] = ((unit * g_ref[...] + b_ref[...]) * live).astype(NARROW)
    grad = cot_ref[...].astype(WIDE) * live
    scaled = grad * g_ref[...]
    gx = inv_std * (
        scaled
        - jnp.mean(scaled, axis=-1, keepdims=True)
        - unit * jnp.mean(scaled * unit, axis=-1, keepdims=True)
    )
    gx_ref[...] = gx
    half = 0.5 * gx
    low_ref[...] = half.astype(NARROW)
    sums_ref[0:1, :] += jnp.sum(grad * unit, axis=0, keepdims=True)
    sums_ref[1:2, :] += jnp.sum(grad, axis=0, keepdims=True)
    sums_ref[2:3, :] += jnp.sum(half, axis=0, keepdims=True)


def final_norm(x, pa, pb, ob, cot, live, gain, bias):
    rows, width = x.shape
    block = pl.BlockSpec((CHUNK, width), lambda i: (i, 0))
    row = whole((1, width))
    return pl.pallas_call(
        final_body,
        grid=(rows // CHUNK,),
        in_specs=[
            block, block, block, row, block,
            pl.BlockSpec((CHUNK, 1), lambda i: (i, 0)), row, row,
        ],
        out_specs=[block, block, block, whole((8, width))],
        out_shape=[
            sds((rows, width), NARROW),
            sds((rows, width), WIDE),
            sds((rows, width), NARROW),
            sds((8, width), WIDE),
        ],
        compiler_params=params(),
        cost_estimate=cost(24 * rows * width, 18 * rows * width),
        name="final_norm",
    )(x, pa, pb, ob, cot, live, gain, bias)


def distances(i0, keys, rows_here):
    rows = lax.broadcasted_iota(jnp.int32, (rows_here, keys), 0) + i0
    cols = lax.broadcasted_iota(jnp.int32, (rows_here, keys), 1)
    return cols - rows, cols


def head_lanes(rows, width, e):
    lane = lax.broadcasted_iota(jnp.int32, (rows, width), 1)
    return (lane >= e * HD) & (lane < (e + 1) * HD)


def doubled(table, heads):
    return jnp.concatenate([table] * heads, axis=1)


def attend_body(len_ref, qkv_ref, table_ref, o_ref, p_out_ref):
    keys = qkv_ref.shape[0]
    width = qkv_ref.shape[1] // 3
    heads = width // HD
    length = len_ref[0]
    table_turned = jnp.transpose(doubled(table_ref[...], heads))
    k_turned = jnp.transpose(qkv_ref[:, width : 2 * width])
    v = qkv_ref[:, 2 * width :]
    key_live = lax.broadcasted_iota(jnp.int32, (QROWS, keys), 1) < length
    masks = [head_lanes(QROWS, width, e) for e in range(heads)]
    for n in range(keys // QROWS):
        i0 = n * QROWS
        rows = slice(i0, i0 + QROWS)
        begin = max(0, i0 - NEAR)
        end = min(keys, i0 + QROWS + NEAR)
        span = end - begin
        apart = distances(i0 - begin, span, QROWS)[0]
        far_left = apart <= -LEFT
        far_right = apart >= RIGHT
        q_all = qkv_ref[rows, :width]
        merged = None
        for e in range(heads):
            q = jnp.where(masks[e], q_all, jnp.zeros_like(q_all))
            near = jnp.dot(q, table_turned, preferred_element_type=WIDE)
            left, right = near[:, 0:1], near[:, LEFT + RIGHT : LEFT + RIGHT + 1]
            band = jnp.concatenate([near, jnp.zeros((QROWS, span - NEAR), WIDE)], axis=1)
            band = pltpu.roll(band, (i0 - begin + span - LEFT) % span, 1, stride=1, stride_axis=0)
            pieces = [jnp.where(far_left, left, jnp.where(far_right, right, band))]
            if begin > 0:
                pieces.insert(0, jnp.broadcast_to(left, (QROWS, begin)))
            if end < keys:
                pieces.append(jnp.broadcast_to(right, (QROWS, keys - end)))
            rel = jnp.concatenate(pieces, axis=1) if len(pieces) > 1 else pieces[0]
            s = jnp.dot(q, k_turned, preferred_element_type=WIDE)
            s = jnp.where(key_live, (s + rel) * HD ** (-0.5), MASKED)
            top = jnp.max(s, axis=-1, keepdims=True)
            ex = jnp.exp(s - top)
            chance = (ex * (1.0 / row_sum(ex))).astype(NARROW)
            p_out_ref[e, rows, :] = chance
            part = jnp.dot(chance, v, preferred_element_type=WIDE)
            merged = part if merged is None else jnp.where(masks[e], part, merged)
        o_ref[rows, :] = merged.astype(NARROW)


def attend(qkv, table, length):
    rows = qkv.shape[0]
    width = qkv.shape[1] // 12
    heads = width // HD
    return pl.pallas_call(
        attend_body,
        grid_spec=pltpu.PrefetchScalarGridSpec(
            num_scalar_prefetch=1,
            grid=(4,),
            in_specs=[
                pl.BlockSpec((rows, 3 * width), lambda t, n: (0, t)),
                whole(table.shape),
            ],
            out_specs=[
                pl.BlockSpec((rows, width), lambda t, n: (0, t)),
                pl.BlockSpec((heads, rows, rows), lambda t, n: (t, 0, 0)),
            ],
        ),
        out_shape=[sds((rows, 4 * width), NARROW), sds((4 * heads, rows, rows), NARROW)],
        compiler_params=params(),
        cost_estimate=cost(16 * heads * rows * rows * HD, 10 * heads * rows * rows, 4 * heads * rows * rows),
        name="attend",
    )(length, qkv, table)


def attend_back_parts(qkv_ref, go_ref, p_ref, table_ref, out_ref, sums_ref, dist_ref, gk_ref, gv_ref):
    keys = qkv_ref.shape[0]
    width = qkv_ref.shape[1] // 3
    heads = width // HD
    table = doubled(table_ref[...], heads)
    scale = HD ** (-0.5)
    flip = (
        lax.broadcasted_iota(jnp.int32, (BROWS, BROWS), 0)
        + lax.broadcasted_iota(jnp.int32, (BROWS, BROWS), 1)
        == BROWS - 1
    ).astype(NARROW)
    bucket = lax.broadcasted_iota(jnp.int32, (BROWS, NEAR), 1)
    first_row = table[0:1, :].astype(WIDE)
    last_row = table[LEFT + RIGHT : LEFT + RIGHT + 1, :].astype(WIDE)
    masks = [head_lanes(BROWS, width, e) for e in range(heads)]

    @pl.when(pl.program_id(0) == 0)
    def _():
        dist_ref[...] = jnp.zeros_like(dist_ref)

    q_turned = jnp.transpose(qkv_ref[:, :width])
    go_turned = jnp.transpose(go_ref[...])
    v_turned = jnp.transpose(qkv_ref[:, 2 * width :])
    k = qkv_ref[:, width : 2 * width]
    for n in range(keys // BROWS):
        i0 = n * BROWS
        rows = slice(i0, i0 + BROWS)
        begin = max(0, i0 - NEAR)
        end = min(keys, i0 + BROWS + NEAR)
        span = end - begin
        apart = distances(i0 - begin, span, BROWS)[0]
        far_left = apart <= -LEFT
        far_right = apart >= RIGHT
        key_of = lax.broadcasted_iota(jnp.int32, (BROWS, NEAR), 0) + bucket + (i0 - LEFT)
        inside = (bucket > 0) & (bucket < LEFT + RIGHT) & (key_of >= 0) & (key_of < keys)
        q_wide = qkv_ref[rows, :width].astype(WIDE)
        go_all = go_ref[rows, :]
        merged = None
        for e in range(heads):
            some = slice(e * HD, (e + 1) * HD)
            go = jnp.where(masks[e], go_all, jnp.zeros_like(go_all))
            chance = p_ref[e, rows, :]
            wide = chance.astype(WIDE)
            gp = jnp.dot(go, v_turned, preferred_element_type=WIDE)
            gs = (wide * (gp - row_sum(gp * wide))).astype(NARROW)
            gsw = gs.astype(WIDE)
            window = gsw[:, begin:end]
            turned = jnp.dot(flip, gs[:, begin:end], preferred_element_type=WIDE)
            turned = pltpu.roll(
                turned, (LEFT + 1 - BROWS - (i0 - begin)) % span, 1, stride=1, stride_axis=0
            )[:, :NEAR]
            back = jnp.dot(flip, turned.astype(NARROW), preferred_element_type=WIDE)
            left_sum = row_sum(jnp.where(far_left, window, 0.0))
            right_sum = row_sum(jnp.where(far_right, window, 0.0))
            if begin > 0:
                left_sum += row_sum(gsw[:, :begin])
            if end < keys:
                right_sum += row_sum(gsw[:, end:])
            left_sum *= scale
            right_sum *= scale
            near = (jnp.where(inside, back, 0.0) * scale).astype(NARROW)
            gq = jnp.dot(gs, k, preferred_element_type=WIDE) * scale
            gq += jnp.dot(near, table, preferred_element_type=WIDE)
            gq += left_sum * first_row + right_sum * last_row
            merged = gq if merged is None else jnp.where(masks[e], gq, merged)
            q_part = q_turned[some, rows]
            dist_ref[:HD, :] += jnp.dot(q_part, near, preferred_element_type=WIDE)
            ends = HD + 2 * e
            dist_ref[ends : ends + 1, :] += jnp.sum(left_sum * q_wide, axis=0, keepdims=True)
            dist_ref[ends + 1 : ends + 2, :] += jnp.sum(right_sum * q_wide, axis=0, keepdims=True)
            gk = jnp.dot(q_part, gs, preferred_element_type=WIDE)
            gv = jnp.dot(go_turned[some, rows], chance, preferred_element_type=WIDE)
            if n == 0:
                gk_ref[some, :] = gk
                gv_ref[some, :] = gv
            else:
                gk_ref[some, :] += gk
                gv_ref[some, :] += gv
        out_ref[rows, :width] = merged.astype(NARROW)

    out_ref[:, width : 2 * width] = jnp.transpose(gk_ref[...] * scale).astype(NARROW)
    out_ref[:, 2 * width :] = jnp.transpose(gv_ref[...]).astype(NARROW)
    sums_ref[...] = jnp.sum(out_ref[...].astype(WIDE), axis=0, keepdims=True)


def attend_back_body(
    nw, s_ref, gm_ref, bn_ref, qkv_ref, chance_ref, o_ref, table_ref, *refs
):
    m_refs, w_refs = refs[:nw], refs[nw : 2 * nw]
    b_ref, sums_ref, dist_ref = refs[2 * nw : 2 * nw + 3]
    outs = refs[2 * nw + 3 : -5]
    acc_ref, go_ref, out_ref, gk_ref, gv_ref = refs[-5:]
    t = pl.program_id(0)
    p = s_ref[0]
    go_ref[...] = expand_from(gm_ref, m_refs, t, p).astype(NARROW)
    attend_back_parts(
        qkv_ref, go_ref, chance_ref, table_ref, out_ref, sums_ref, dist_ref, gk_ref, gv_ref
    )
    grad = out_ref[...]
    reduce_into(acc_ref, grad, w_refs, t, p)
    write_grads(t, p, [(bn_ref, grad), (gm_ref, o_ref[...])], outs)

    @pl.when(t == 3)
    def _():
        b_ref[...] = acc_ref[...].astype(NARROW)


def attend_back(gm, bn, qkv, chances, o, table, w, p):
    rows, width = gm.shape
    wrows = width // PLANE_BLOCKS
    cols = qkv.shape[1] // 12
    heads = cols // HD
    g_specs, g_shapes = grad_outs(wrows, 4 * cols, False)
    out = pl.pallas_call(
        functools.partial(attend_back_body, len(w)),
        grid_spec=pltpu.PrefetchScalarGridSpec(
            num_scalar_prefetch=1,
            grid=(4,),
            in_specs=[
                whole((rows, width)),
                whole((rows, width)),
                pl.BlockSpec((rows, 3 * cols), lambda t, p: (0, t)),
                pl.BlockSpec((heads, rows, rows), lambda t, p: (t, 0, 0)),
                pl.BlockSpec((rows, cols), lambda t, p: (0, t)),
                whole(table.shape),
                *weight_specs(w, cols, 3),
                *weight_specs(w, 3 * cols, 0),
            ],
            out_specs=[
                whole((rows, width)),
                pl.BlockSpec((1, 3 * cols), lambda t, p: (0, t)),
                whole((HD + 8, NEAR)),
                *g_specs,
            ],
            scratch_shapes=[
                pltpu.VMEM((rows, width), WIDE),
                pltpu.VMEM((rows, cols), NARROW),
                pltpu.VMEM((rows, 3 * cols), NARROW),
                pltpu.VMEM((cols, rows), WIDE),
                pltpu.VMEM((cols, rows), WIDE),
            ],
        ),
        out_shape=[
            sds((rows, width), NARROW),
            sds((1, 12 * cols), WIDE),
            sds((HD + 8, NEAR), WIDE),
            *g_shapes,
        ],
        compiler_params=params(MOST_VMEM),
        cost_estimate=cost(40 * heads * rows * rows * HD, 10 * heads * rows * rows),
        name="attend_back",
    )(p, gm, bn, qkv, chances, o, table, *w, *w)
    return out[0], out[1], out[2], out[3:]


def lane_pair(first, second, rows):
    lane = lax.broadcasted_iota(jnp.int32, (rows, LANES), 1)
    return jnp.where(lane == 0, first, jnp.where(lane == 1, second, 0.0))


def row_sum(v):
    return jnp.sum(v, axis=-1, keepdims=True)


def mix_body(taps_count, z_ref, taps_ref, y_ref, sums_ref, pad_ref):
    rows = z_ref.shape[0]

    @pl.when(pl.program_id(0) == 0)
    def _():
        sums_ref[...] = jnp.zeros_like(sums_ref)

    pad_ref[0:PAD, :] = jnp.zeros((PAD, pad_ref.shape[1]), WIDE)
    pad_ref[PAD:, :] = z_ref[...]
    for start in range(0, rows, MIX_CHUNK):
        total = None
        for i in range(taps_count):
            begin = start + PAD - taps_count + 1 + i
            term = taps_ref[i : i + 1, :] * pad_ref[begin : begin + MIX_CHUNK, :]
            total = term if total is None else total + term
        here = slice(start, start + MIX_CHUNK)
        y_ref[here, :] = total
        sums_ref[here, :] += lane_pair(row_sum(total), row_sum(total * total), MIX_CHUNK)


def causal_mix(z, taps, taps_count):
    rows, cols = z.shape
    block = pl.BlockSpec((rows, cols // 4), lambda t: (0, t))
    return pl.pallas_call(
        functools.partial(mix_body, taps_count),
        grid=(4,),
        in_specs=[block, pl.BlockSpec((taps.shape[0], cols // 4), lambda t: (0, t))],
        out_specs=[block, whole((rows, LANES))],
        out_shape=[sds((rows, cols), WIDE), sds((rows, LANES), WIDE)],
        scratch_shapes=[pltpu.VMEM((rows + PAD, cols // 4), WIDE)],
        compiler_params=params(),
        cost_estimate=cost(2 * taps_count * rows * cols, 8 * rows * cols),
        name="causal_mix",
    )(z, taps)


def depth_stats(sa_ref, sb_ref, here, width):
    sums = (sa_ref[here, :] + sb_ref[here, :]) * (1.0 / width)
    mean = sums[:, 0:1]
    return mean, lax.rsqrt(sums[:, 1:2] - mean * mean + EPSILON)


def filter_out_body(p_ref, y_ref, sa_ref, sb_ref, g_ref, b_ref, *refs):
    w_refs = refs[:5]
    out_ref, low_ref, acc_ref = refs[5:]
    t = pl.program_id(0)
    p = p_ref[0]
    width = out_ref.shape[1]
    mean, std = depth_stats(sa_ref, sb_ref, slice(None), width)
    yn = (y_ref[...] - mean) * std * g_ref[...] + b_ref[...]
    low = (yn * sigmoid(yn)).astype(NARROW)
    low_ref[...] = low

    @pl.when(t == 0)
    def _():
        acc_ref[...] = jnp.zeros_like(acc_ref)

    for r, w in enumerate(weight_blocks(w_refs, t)):
        cols = rel_cols(p, r, width // PLANE_BLOCKS)
        acc_ref[:, cols] += lax.dot_general(
            low, w, (((1,), (1,)), ((), ())), preferred_element_type=WIDE
        )

    @pl.when(t == 3)
    def _():
        out_ref[...] = acc_ref[...].astype(NARROW)


def filter_out(y, sums, gain, bias, w, cols, col_block, p, width):
    rows = y.shape[0]
    block = pl.BlockSpec((rows, cols), lambda t, p: (0, t))
    row = pl.BlockSpec((1, cols), lambda t, p: (0, t))
    return pl.pallas_call(
        filter_out_body,
        grid_spec=pltpu.PrefetchScalarGridSpec(
            num_scalar_prefetch=1,
            grid=(4,),
            in_specs=[
                block, whole((rows, LANES)), whole((rows, LANES)), row, row,
                *weight_specs(w, cols, col_block),
            ],
            out_specs=[whole((rows, width)), block],
            scratch_shapes=[pltpu.VMEM((rows, width), WIDE)],
        ),
        out_shape=[sds((rows, width), NARROW), sds(y.shape, NARROW)],
        compiler_params=params(),
        cost_estimate=cost(2 * rows * width * 4 * cols, 8 * width * cols + 6 * rows * width),
        name="filter_out",
    )(p, y, *sums, gain, bias, *w)


def filter_in_body(p_ref, grad_ref, y_ref, sa_ref, sb_ref, g_ref, b_ref, *refs):
    w_refs = refs[:5]
    gyn_ref, cols_ref, rows_ref = refs[5:]
    t = pl.program_id(0)
    p = p_ref[0]
    width = grad_ref.shape[1]
    acc = None
    for r, w in enumerate(weight_blocks(w_refs, t)):
        cols = rel_cols(p, r, width // PLANE_BLOCKS)
        term = jnp.dot(grad_ref[:, cols], w, preferred_element_type=WIDE)
        acc = term if acc is None else acc + term
    mean, std = depth_stats(sa_ref, sb_ref, slice(None), width)
    unit = (y_ref[...] - mean) * std
    yn = unit * g_ref[...] + b_ref[...]
    logistic = sigmoid(yn)
    gyn = acc * (logistic * (1.0 + yn * (1.0 - logistic)))
    gyn_ref[...] = gyn
    cols_ref[0:1, :] = jnp.sum(gyn * unit, axis=0, keepdims=True)
    cols_ref[1:2, :] = jnp.sum(gyn, axis=0, keepdims=True)
    scaled = gyn * g_ref[...]
    pair = lane_pair(row_sum(scaled), row_sum(scaled * unit), gyn.shape[0])

    @pl.when(t == 0)
    def _():
        rows_ref[...] = pair

    @pl.when(t > 0)
    def _():
        rows_ref[...] += pair


def filter_in(grad, y, sums, gain, bias, w, cols, col_block, p):
    rows, width = grad.shape
    block = pl.BlockSpec((rows, cols), lambda t, p: (0, t))
    row = pl.BlockSpec((1, cols), lambda t, p: (0, t))
    return pl.pallas_call(
        filter_in_body,
        grid_spec=pltpu.PrefetchScalarGridSpec(
            num_scalar_prefetch=1,
            grid=(4,),
            in_specs=[
                whole((rows, width)), block, whole((rows, LANES)), whole((rows, LANES)), row, row,
                *weight_specs(w, cols, col_block),
            ],
            out_specs=[
                block,
                pl.BlockSpec((8, cols), lambda t, p: (0, t)),
                whole((rows, LANES)),
            ],
        ),
        out_shape=[sds(y.shape, WIDE), sds((8, 4 * cols), WIDE), sds((rows, LANES), WIDE)],
        compiler_params=params(),
        cost_estimate=cost(2 * rows * width * 4 * cols, 8 * width * cols + 6 * rows * width),
        name="filter_in",
    )(p, grad, y, *sums, gain, bias, *w)


def mix_back_parts(
    taps_count, width, gyn_ref, y_ref, sa_ref, sb_ref, ra_ref, rb_ref, g_ref, z_ref, gate_ref,
    taps_ref, out_ref, grad_ref, gpad_ref, zpad_ref,
):
    rows, cols = z_ref.shape
    zpad_ref[0:PAD, :] = jnp.zeros((PAD, cols), WIDE)
    zpad_ref[PAD:, :] = z_ref[...]
    gpad_ref[rows:, :] = jnp.zeros((PAD, cols), WIDE)
    mean, std = depth_stats(sa_ref, sb_ref, slice(None), width)
    pair = (ra_ref[...] + rb_ref[...]) * (1.0 / width)
    unit = (y_ref[...] - mean) * std
    gpad_ref[0:rows, :] = std * (gyn_ref[...] * g_ref[...] - pair[:, 0:1] - unit * pair[:, 1:2])
    sums = [None] * taps_count
    for start in range(0, rows, MIX_CHUNK):
        here = slice(start, start + MIX_CHUNK)
        gy = gpad_ref[here, :]
        total = None
        for i in range(taps_count):
            begin = start + taps_count - 1 - i
            term = taps_ref[i : i + 1, :] * gpad_ref[begin : begin + MIX_CHUNK, :]
            total = term if total is None else total + term
        for i in range(taps_count):
            begin = start + PAD - taps_count + 1 + i
            part = zpad_ref[begin : begin + MIX_CHUNK, :] * gy
            part = jnp.sum(part.reshape(MIX_CHUNK // 8, 8, cols), axis=0)
            sums[i] = part if sums[i] is None else sums[i] + part
        gate = gate_ref[here, :]
        first = total * gate
        out_ref[here, :cols] = first.astype(NARROW)
        out_ref[here, cols:] = (total * z_ref[here, :] * (1.0 - gate)).astype(NARROW)
    for i in range(taps_count):
        grad_ref[i : i + 1, :] = jnp.sum(sums[i], axis=0, keepdims=True)


def mix_back_body(taps_count, width, nw, s_ref, *refs):
    parts, gate_taps = refs[:8], refs[8:10]
    cn_ref, gw_ref, wact_ref = refs[10:13]
    w_refs = refs[13 : 13 + nw]
    b_ref, grad_ref, flat_ref = refs[13 + nw : 16 + nw]
    acc_ref, out_ref, gpad_ref, zpad_ref = refs[16 + nw :]
    t = pl.program_id(0)
    p = s_ref[0]
    mix_back_parts(
        taps_count, width, *parts, *gate_taps, out_ref, grad_ref, gpad_ref, zpad_ref
    )
    grad = out_ref[...]
    reduce_into(acc_ref, grad, w_refs, t, p)
    write_grads(t, p, [(cn_ref, grad), (gw_ref, wact_ref[...])], [flat_ref])

    @pl.when(t == 3)
    def _():
        b_ref[...] = acc_ref[...].astype(NARROW)


def mix_back(gyn, y, sums, pairs, gain, z, gate, taps, taps_count, cn, gw, act, w, p):
    rows, cols = z.shape
    width = cn.shape[1]
    wrows = width // PLANE_BLOCKS
    n = cols // 4
    block = pl.BlockSpec((rows, n), lambda t, p: (0, t))
    row = pl.BlockSpec((1, n), lambda t, p: (0, t))
    lanes = whole((rows, LANES))
    tap_block = pl.BlockSpec((taps.shape[0], n), lambda t, p: (0, t))
    g_specs, g_shapes = grad_outs(wrows, 3 * n, True)
    return pl.pallas_call(
        functools.partial(mix_back_body, taps_count, width, len(w)),
        grid_spec=pltpu.PrefetchScalarGridSpec(
            num_scalar_prefetch=1,
            grid=(4,),
            in_specs=[
                block, block, lanes, lanes, lanes, lanes, row, block, block, tap_block,
                whole((rows, width)), whole((rows, width)), block,
                *weight_specs(w, 2 * n, 0),
            ],
            out_specs=[whole((rows, width)), tap_block, *g_specs],
            scratch_shapes=[
                pltpu.VMEM((rows, width), WIDE),
                pltpu.VMEM((rows, 2 * n), NARROW),
                pltpu.VMEM((rows + PAD, n), WIDE),
                pltpu.VMEM((rows + PAD, n), WIDE),
            ],
        ),
        out_shape=[sds((rows, width), NARROW), sds(taps.shape, WIDE), *g_shapes],
        compiler_params=params(MOST_VMEM),
        cost_estimate=cost(4 * taps_count * rows * cols, 20 * rows * cols),
        name="mix_back",
    )(p, gyn, y, *sums, *pairs, gain, z, gate, taps, cn, gw, act, *w)


def halve_body(groups, core_ref, *refs):
    count = sum(len(g) for g in groups)
    ins = list(refs[:count])
    keeps = refs[count : count + len(groups)]
    sends = refs[count + len(groups) :]
    low = core_ref[0] == 0
    for group, keep, send in zip(groups, keeps, sends):
        start = 0
        for n in group:
            ref = ins.pop(0)
            left, right = ref[:, :n], ref[:, n:]
            keep[:, start : start + n] = jnp.where(low, left, right)
            send[:, start : start + n] = jnp.where(low, right, left)
            start += n


def halve(groups, core):
    rows = groups[0][0].shape[0]
    halves = tuple(tuple(w.shape[1] // 2 for w in g) for g in groups)
    flat = [w for g in groups for w in g]
    shapes = [sds((rows, sum(h)), NARROW) for h in halves] * 2
    out = pl.pallas_call(
        functools.partial(halve_body, halves),
        grid_spec=pltpu.PrefetchScalarGridSpec(
            num_scalar_prefetch=1,
            grid=(1,),
            in_specs=[whole(w.shape) for w in flat],
            out_specs=[whole(s.shape) for s in shapes],
        ),
        out_shape=shapes,
        compiler_params=params(),
        cost_estimate=cost(0, 4 * sum(w.size for w in flat)),
        name="halve",
    )(core, *flat)
    return out[: len(groups)], out[len(groups) :]


def join_body(core_ref, keep_ref, came_ref, out_ref):
    low = core_ref[0] == 0
    rows = keep_ref.shape[0]
    keep, came = keep_ref[...], came_ref[...]
    out_ref[:rows, :] = jnp.where(low, keep, came)
    out_ref[rows:, :] = jnp.where(low, came, keep)


def join(keep, came, core):
    rows, cols = keep.shape
    return pl.pallas_call(
        join_body,
        grid_spec=pltpu.PrefetchScalarGridSpec(
            num_scalar_prefetch=1,
            grid=(1,),
            in_specs=[whole((rows, cols)), whole((rows, cols))],
            out_specs=whole((2 * rows, cols)),
        ),
        out_shape=sds((2 * rows, cols), keep.dtype),
        compiler_params=params(),
        cost_estimate=cost(0, 8 * rows * cols),
        name="join",
    )(core, keep, came)


def pack_body(lead, plan, core_ref, *refs):
    out_ref = refs[-1]
    low = core_ref[0] == 0
    out_ref[...] = jnp.zeros_like(out_ref)
    for ref, items in zip(refs[:-1], plan):
        for kind, src, dst in items:
            if kind == "once":
                v = ref[src : src + 1, :]
                out_ref[dst : dst + 1, :] = jnp.where(low, v, 0.0)
            elif kind == "all":
                out_ref[dst : dst + 8, :] = ref[...]
            elif kind == "taps":
                n = ref.shape[1] // 4
                for t in range(4):
                    v = ref[: src, t * n : (t + 1) * n]
                    out_ref[dst : dst + src, 2 * t * n : (2 * t + 1) * n] = jnp.where(low, v, 0.0)
                    out_ref[dst : dst + src, (2 * t + 1) * n : (2 * t + 2) * n] = jnp.where(low, 0.0, v)
            elif kind == "hidden":
                n = ref.shape[1] // 4
                for t in range(4):
                    v = ref[0:1, t * n : (t + 1) * n]
                    out_ref[dst + t : dst + t + 1, :n] = jnp.where(low, v, 0.0)
                    out_ref[dst + t : dst + t + 1, n:] = jnp.where(low, 0.0, v)
            else:
                row, first, step, n = src
                for t in range(4):
                    begin = t * step + first
                    v = ref[row : row + 1, begin : begin + n]
                    out_ref[dst : dst + 1, 2 * t * n : (2 * t + 1) * n] = jnp.where(low, v, 0.0)
                    out_ref[dst : dst + 1, (2 * t + 1) * n : (2 * t + 2) * n] = jnp.where(low, 0.0, v)


def pack(rows, width, core, sources):
    arrays = [a for a, _ in sources]
    plan = tuple(tuple(items) for _, items in sources)
    return pl.pallas_call(
        functools.partial(pack_body, rows, plan),
        grid_spec=pltpu.PrefetchScalarGridSpec(
            num_scalar_prefetch=1,
            grid=(1,),
            in_specs=[whole(a.shape) for a in arrays],
            out_specs=whole((rows, width)),
        ),
        out_shape=sds((rows, width), WIDE),
        compiler_params=params(),
        cost_estimate=cost(0, 8 * rows * width),
        name="pack",
    )(core, *arrays)


def on_device(planes, inputs, lengths, cotangent, *weights_and_rest):
    shards = weights_and_rest[:8]
    norm_gains, biases, kernel, distance_table = weights_and_rest[8:]
    batches, _, rows_here, width = inputs.shape
    parts = 4
    core = lax.axis_index("pair")
    plane = lax.axis_index("plane")
    part = lax.axis_index("tensor")
    quick = planes == PLANE_BLOCKS
    place = plane if quick else plane * 0
    p = place.astype(jnp.int32).reshape(1)

    def other_core(v):
        return lax.ppermute(v, "pair", [(0, 1), (1, 0)])

    def step_x(v):
        return lax.ppermute(v, "plane", [(i, i ^ 1) for i in range(planes)])

    def step_y(v):
        return lax.ppermute(v, "plane", [(i, i ^ 2) for i in range(planes)])

    def over_planes(v):
        if quick:
            return v + step_x(v) + step_y(v) + lax.ppermute(v, "plane", [(i, i ^ 3) for i in range(4)])
        bit = 1
        while bit < planes:
            v = v + lax.ppermute(v, "plane", [(i, i ^ bit) for i in range(planes)])
            bit *= 2
        return v

    def over_parts(v):
        def turn(k):
            return lax.ppermute(v, "tensor", [(i, i ^ k) for i in range(parts)])

        one, two, three = turn(1), turn(2), turn(3)
        return (v + one) + (two + three)

    def fence(*values):
        return lax.optimization_barrier(values) if quick else values

    def column_of(shard):
        return lax.all_gather(shard, "tensor", axis=0)

    def planes_of(column):
        every = lax.all_gather(column, "plane", axis=0)
        rows, cols = column.shape[1:]
        every = every.reshape(PLANE_BLOCKS, planes // PLANE_BLOCKS, parts, rows, cols)
        every = every.transpose(0, 2, 1, 3, 4).reshape(PLANE_BLOCKS, parts, -1, cols)
        return every[0], every[1], every[2], every[3, :2], every[3, 2:]

    def near(column):
        return step_x(column), step_y(column)

    def far(pair):
        return step_y(pair[0][:2]), step_x(pair[1][2:])

    def share(total):
        n = total.shape[0] // 2
        keep = lax.dynamic_slice_in_dim(total, core * n, n, 0)
        came = other_core(lax.dynamic_slice_in_dim(total, (1 - core) * n, n, 0))
        first = jnp.where(core == 0, keep, came).astype(WIDE)
        second = jnp.where(core == 0, came, keep).astype(WIDE)
        return first, second

    def tensor_sum(total):
        return lax.psum_scatter(total, "tensor", scatter_dimension=0)

    def across_x(every):
        return step_x(every[1::2]) if quick else ()

    def across_y(every, rx):
        return step_y(add(every[2], rx[1])) if quick else ()

    def across_end(every, rx, ry):
        if quick:
            return (every[0].astype(WIDE) + rx[0].astype(WIDE) + ry.astype(WIDE)).astype(NARROW)
        return lax.psum_scatter(
            every.reshape(planes, -1, every.shape[-1]), "plane", scatter_dimension=0
        )

    def hop1(grads):
        return (step_x(grads[1]), step_y(grads[3])) if quick else ()

    def hop2(grads, came):
        if not quick:
            return ()
        return step_y(add(grads[4], came[0][1])), step_x(add(grads[2], came[1][1]))

    def hop3(grads, came, last):
        return tensor_sum(gathered(grads, came, last))

    def gathered(grads, came, last):
        own, sx, kx, sy, ky = grads
        if quick:
            return combine(own, came[0], came[1], last[0], last[1])
        blocks = [
            own,
            jnp.concatenate([sx[0], kx]),
            jnp.concatenate([ky, sy[0]]),
            jnp.concatenate([sx[1], sy[1]]),
        ]
        every = jnp.stack(blocks)
        rows = width // planes
        cols = own.shape[-1]
        every = every.reshape(PLANE_BLOCKS, parts, planes // PLANE_BLOCKS, rows, cols)
        every = every.transpose(0, 2, 1, 3, 4).reshape(planes, parts, rows, cols)
        return lax.psum_scatter(every, "plane", scatter_dimension=0)

    def add(a, b):
        return (a.astype(WIDE) + b.astype(WIDE)).astype(NARROW)

    def rejoin(halves, start, cols, groups):
        pieces = [h[:, start : start + cols].reshape(h.shape[0], groups, -1) for h in halves]
        joined = jnp.concatenate(pieces, axis=2)
        return joined[:, 0] if groups == 1 else joined

    def spot(c, t):
        return c * parts + t

    def route(turn):
        pairs = []
        for c in range(2):
            for t in range(parts):
                mb = (turn + t) % 2
                pairs.append((spot(c, t), spot(t // 2, 2 * mb + c)))
        return pairs

    def bring_one(v, turn):
        mb = lax.rem(turn + part, 2)
        block = lax.dynamic_index_in_dim(v[:, 0], mb, 0, False)
        return lax.ppermute(block, ("pair", "tensor"), route(turn))

    def bring(v):
        return [bring_one(v, turn) for turn in range(2)]

    def settle(blocks):
        swap = part // 2 == 1
        mine = jnp.concatenate(
            [jnp.where(swap, blocks[1], blocks[0]), jnp.where(swap, blocks[0], blocks[1])], axis=0
        )
        theirs = other_core(mine)
        return jnp.concatenate(
            [jnp.where(core == 0, mine, theirs), jnp.where(core == 0, theirs, mine)], axis=0
        )

    def send_home(v):
        half = v.shape[0] // 2
        mine = lax.dynamic_slice_in_dim(v, core * half, half, 0)
        first, second = mine[: half // 2], mine[half // 2 :]
        swap = part // 2 == 1
        blocks = [jnp.where(swap, second, first), jnp.where(swap, first, second)]
        came = []
        for turn in range(2):
            back = [(b, a) for a, b in route(turn)]
            came.append(lax.ppermute(blocks[turn], ("pair", "tensor"), back))
        return came

    def send_one(v, turn):
        half = v.shape[0] // 2
        mine = lax.dynamic_slice_in_dim(v, core * half, half, 0)
        first, second = mine[: half // 2], mine[half // 2 :]
        other = (part // 2 == 1) == (turn == 0)
        block = jnp.where(other, second, first)
        return lax.ppermute(block, ("pair", "tensor"), [(b, a) for a, b in route(turn)])

    def home(came):
        odd = lax.rem(part, 2) == 1
        return jnp.stack([jnp.where(odd, came[1], came[0]), jnp.where(odd, came[0], came[1])])[:, None]

    (w_e1, w_r1, w_proj, w_merge, w_fe, w_fr, w_e2, w_r2) = shards
    core1 = core.astype(jnp.int32).reshape(1)
    ffc = w_e1.shape[1] // 2
    qc = w_proj.shape[2] // 2
    cc = w_fe.shape[2] // 2
    groups = [
        [w_e1],
        [w_r1],
        [w_proj[:, 0], w_proj[:, 1], w_proj[:, 2], w_merge],
        [w_fe[:, 0], w_fe[:, 1], w_fr, w_e2],
        [w_r2],
    ]
    keeps, sends = halve(groups, core1)
    pieces = fence(*[join(k, other_core(v), core1) for k, v in zip(keeps, sends)])

    gains = norm_gains.astype(WIDE)
    bias = biases.astype(WIDE)
    gain_row = lambda i: gains[i : i + 1]
    bias_row = lambda i: bias[i : i + 1]
    stride = w_e1.shape[1] * parts // width

    def pick(v):
        lead = v.shape[0]
        v = v.reshape(lead, parts, 2, -1)
        return lax.dynamic_index_in_dim(v, core, 2, False).reshape(lead, -1)

    hidden1 = pick(bias[11 : 11 + stride].reshape(1, -1))
    hidden2 = pick(bias[11 + stride : 11 + 2 * stride].reshape(1, -1))
    qb = pick(bias_row(6)).reshape(parts, 1, -1)
    vb = pick(bias_row(7)).reshape(parts, 1, -1)
    qkv_bias = jnp.concatenate([qb, jnp.zeros_like(qb), vb], axis=1).reshape(1, -1)
    taps_count = kernel.shape[0]
    taps = jnp.pad(pick(kernel.astype(WIDE)), ((0, PAD - taps_count), (0, 0)))
    depth_gain = pick(gain_row(3))
    depth_bias = pick(bias_row(3))
    buckets = distance_table.shape[0]
    table = jnp.pad(distance_table, ((0, NEAR - buckets), (0, 0)))

    pair_lengths = jnp.stack([lengths[:, 0], other_core(lengths[:, 0])])
    from_pair = jnp.bitwise_xor(lax.rem(part, 2), core)
    length = pair_lengths[from_pair, part // 2]
    rows_all = parts * inputs.shape[2]
    live = (jnp.arange(rows_all) < length).astype(WIDE)[:, None]

    col_e1 = column_of(pieces[0])
    r1c = column_of(pieces[1])
    attc = column_of(pieces[2])
    col_c = column_of(pieces[3])
    if quick:
        sd = pieces[4]
        sx, sy = step_x(sd), step_y(sd)
        sz = step_y(sx)
        col_e1, sx, sy, sz, source = fence(col_e1, sx, sy, sz, inputs)
        r2 = (column_of(jnp.stack([sd, sx, sy, sz])),) * PLANE_BLOCKS
        e1n, block0 = near(col_e1), bring_one(source, 0)
        e1n, r1c, block0, source = fence(e1n, r1c, block0, source)
        e1f, r1n, block1 = far(e1n), near(r1c), bring_one(source, 1)
        e1f, e1n, r1n, attc, block1, source = fence(e1f, e1n, r1n, attc, block1, cotangent)
        x0, cot0 = settle([block0, block1]), bring_one(source, 0)
        e1 = (col_e1, *e1n, *e1f)
        r1f, attn = far(r1n), near(attc)
    else:
        rows, cols = pieces[4].shape
        every = lax.all_gather(pieces[4], "plane", axis=0).reshape(PLANE_BLOCKS, -1, cols)
        r2 = (column_of(every),) * PLANE_BLOCKS
        x0 = settle(bring(inputs))
        e1 = planes_of(col_e1)
        r1 = planes_of(r1c)
        att = planes_of(attc)
        fil = planes_of(col_c[:, :, : 3 * cc])
        e2 = planes_of(col_c[:, :, 3 * cc :])
    x0 = x0.astype(WIDE)
    a1, u1, s1 = norm_expand("ff", x0, None, 0.5, gain_row(0), bias_row(0), e1, ffc, 0, p, hidden1)
    if quick:
        r1f, r1n, attn, s1, cot0, source = fence(r1f, r1n, attn, s1, cot0, source)
        cot1 = bring_one(source, 1)
        r1, attf = (r1c, *r1n, *r1f), far(attn)
    f1 = reduce_mm(s1, r1, ffc, 0, p, width)
    if quick:
        attf, attn, f1, col_c, cot1 = fence(attf, attn, f1, col_c, cot1)
        cot = settle([cot0, cot1])
        att = (attc, *attn, *attf)
    f1o = other_core(f1)
    x1, bn, qkv = norm_expand(
        "qkv", x0, (f1, f1o, bias_row(9)), 0.5, gain_row(1), bias_row(1), att, 3 * qc, 0, p, qkv_bias
    )
    if quick:
        qkv, col_c = fence(qkv, col_c)
        filc, e2c = col_c[:, :, : 3 * cc], col_c[:, :, 3 * cc :]
        filn = near(filc)
    o, chances = attend(qkv, table, length.reshape(1))
    if quick:
        filn, o, e2c = fence(filn, o, e2c)
        filf, e2n = far(filn), near(e2c)
    f2 = reduce_mm(o, att, qc, 3, p, width)
    if quick:
        filf, filn, f2 = fence(filf, filn, f2)
        fil = (filc, *filn, *filf)
    f2o = other_core(f2)
    x2, cn, gate, z = norm_expand(
        "conv", x1, (f2, f2o, bias_row(8)), 1.0, gain_row(2), bias_row(2), fil, 2 * cc, 0, p, None
    )
    y, y_sums = causal_mix(z, taps, taps_count)
    if quick:
        e2n, y_sums = fence(e2n, y_sums)
        e2f = far(e2n)
    y_sums = (y_sums, other_core(y_sums))
    f3, w = filter_out(y, y_sums, depth_gain, depth_bias, fil, cc, 2, p, width)
    if quick:
        e2f, f3 = fence(e2f, f3)
        e2 = (e2c, *e2n, *e2f)
    else:
        cot = settle(bring(cotangent))
    f3o = other_core(f3)
    x3, a2, u2, f4 = norm_expand(
        "ff", x2, (f3, f3o, jnp.zeros((1, width), WIDE)), 1.0, gain_row(4), bias_row(4),
        e2, ffc, 0, p, hidden2, r2,
    )
    out_rows, gx4, gf2, sums_final = final_norm(
        x3, f4, other_core(f4), bias_row(10), cot, live, gain_row(5), bias_row(5)
    )

    b4, gc2, g_r2, g_e2 = ff_back(gf2, a2, u2, r2, e2, p, True)
    g_r2, g_e2, b4 = fence(g_r2, g_e2, b4)
    z_r2 = tensor_sum(g_r2)
    e2h1 = hop1(g_e2)
    gx3, gw, sums3 = norm_back(1.0, x3, gx4, b4, other_core(b4), gain_row(4))
    gyn, depth_cols, depth_rows = filter_in(
        gw, y, y_sums, depth_gain, depth_bias, fil, cc, 2, p
    )
    depth_rows = (depth_rows, other_core(depth_rows))
    b3, taps_grad, g_fil = mix_back(
        gyn, y, y_sums, depth_rows, depth_gain, z, gate, taps, taps_count, cn, gw, w, fil, p
    )
    e2h1, b3, g_fil = fence(e2h1, b3, g_fil)
    e2h2 = hop2(g_e2, e2h1)
    z_fil = tensor_sum(g_fil)
    gx2, gm, sums2 = norm_back(1.0, x2, gx3, b3, other_core(b3), gain_row(2))
    e2h2, gm = fence(e2h2, gm)
    z_e2 = hop3(g_e2, e2h1, e2h2)
    b2, gqkv_sums, table_grad, g_att = attend_back(gm, bn, qkv, chances, o, table, att, p)
    g_att, b2, z_r2 = fence(g_att, b2, z_r2)
    atth1 = hop1(g_att)
    gx1, gf1, sums1 = norm_back(0.5, x1, gx2, b2, other_core(b2), gain_row(1))
    home0 = send_one(out_rows, 0)
    b1, gc1, g_r1, g_e1 = ff_back(gf1, a1, u1, r1, e1, p, False)
    g_r1, g_e1, b1, atth1, home0, out_rows = fence(g_r1, g_e1, b1, atth1, home0, out_rows)
    home1 = send_one(out_rows, 1)
    r1h1 = hop1(g_r1)
    atth2 = hop2(g_att, atth1)
    gx0, _, sums0 = norm_back(1.0, x0, gx1, b1, other_core(b1), gain_row(0))
    atth2, r1h1, gx0, z_fil, home1 = fence(atth2, r1h1, gx0, z_fil, home1)
    outputs = [home0, home1]
    e1h1 = hop1(g_e1)
    r1h2 = hop2(g_r1, r1h1)
    z_att = hop3(g_att, atth1, atth2)

    table_rows = -(-buckets // 8)
    tail = jnp.transpose(table_grad[:HD])[1 : buckets - 1]
    ends = table_grad[HD : HD + 2, :HD]
    for e in range(1, qc // HD):
        ends = ends + table_grad[HD + 2 * e : HD + 2 * e + 2, e * HD : (e + 1) * HD]
    tail = jnp.concatenate([ends[:1], tail, ends[1:]], axis=0)
    tail = jnp.pad(tail, ((0, 8 * table_rows - buckets), (0, 0)))
    tail = tail.reshape(table_rows, 8, HD).transpose(1, 0, 2).reshape(8, table_rows * HD)
    tail = jnp.pad(tail, ((0, 0), (0, width - table_rows * HD)))
    small = pack(
        64, width, core1,
        [
            (sums_final, [("once", 0, 5), ("once", 1, 11), ("once", 2, 16)]),
            (sums3, [("once", 0, 4), ("once", 1, 10)]),
            (sums2, [("once", 0, 2), ("once", 1, 8), ("once", 2, 14)]),
            (sums1, [("once", 0, 1), ("once", 1, 7), ("once", 2, 15)]),
            (sums0, [("once", 0, 0), ("once", 1, 6)]),
            (gqkv_sums, [("row", (0, 0, 3 * qc, qc), 12), ("row", (0, 2 * qc, 3 * qc, qc), 13)]),
            (depth_cols, [("row", (0, 0, cc, cc), 3), ("row", (1, 0, cc, cc), 9)]),
            (gc1, [("hidden", 0, 17)]),
            (gc2, [("hidden", 0, 21)]),
            (taps_grad, [("taps", taps_count, 25)]),
            (tail, [("all", 0, 56)]),
        ],
    )
    half = small.shape[0] // 2
    mine = lax.dynamic_slice_in_dim(small, core * half, half, 0)
    came = other_core(lax.dynamic_slice_in_dim(small, (1 - core) * half, half, 0))
    homeward = send_home(gx0.astype(NARROW))
    r1h2, e1h1, came, z_e2, homeward = fence(r1h2, e1h1, came, z_e2, homeward)
    e1h2 = hop2(g_e1, e1h1)
    z_r1 = hop3(g_r1, r1h1, r1h2)
    planes_came = over_planes(mine + came)
    e1h2, planes_came = fence(e1h2, planes_came)
    t_e1, planes_came = fence(gathered(g_e1, e1h1, e1h2), planes_came)
    z_e1 = tensor_sum(t_e1)
    filx, r2x = across_x(z_fil), across_x(z_r2)
    mine = over_parts(planes_came)
    filx, r2x, mine, z_att = fence(filx, r2x, mine, z_att)
    fily, r2y = across_y(z_fil, filx), across_y(z_r2, r2x)
    e2_grad, att_grad = share(z_e2), share(z_att)
    theirs = other_core(mine)
    r2_grad = share(across_end(z_r2, r2x, r2y))
    fil_grad = share(across_end(z_fil, filx, fily))
    small = jnp.concatenate(
        [jnp.where(core == 0, mine, theirs), jnp.where(core == 0, theirs, mine)], axis=0
    )
    outputs = home(outputs)
    input_grad = home(homeward).astype(WIDE)
    r1_grad, e1_grad = share(z_r1), share(z_e1)
    gains_grad = small[0:6]
    bias_grad = small[6:25]
    taps_t = small[25 : 25 + taps_count]
    table_t = small[56:64, : table_rows * HD].reshape(8, table_rows, HD).transpose(1, 0, 2)
    table_t = table_t.reshape(8 * table_rows, HD)[:buckets]
    return (
        outputs,
        input_grad,
        rejoin(e1_grad, 0, ffc, 1),
        rejoin(r1_grad, 0, ffc, 1),
        rejoin(att_grad, 0, 3 * qc, 3),
        rejoin(att_grad, 3 * qc, qc, 1),
        rejoin(fil_grad, 0, 2 * cc, 2),
        rejoin(fil_grad, 2 * cc, cc, 1),
        rejoin(e2_grad, 0, ffc, 1),
        rejoin(r2_grad, 0, ffc, 1),
        gains_grad,
        bias_grad,
        taps_t,
        table_t,
    )


def solution(mesh):
    dp = mesh.shape["dp"]
    tensor = mesh.shape["tensor"]
    split = Mesh(mesh.devices.reshape(dp // 2, 2, tensor), ("plane", "pair", "tensor"))
    both = ("plane", "pair")
    rows = P(None, both, "tensor", None)
    flat = P(both, "tensor")
    deep = P(both, None, "tensor")
    weights = (flat, flat, deep, flat, deep, flat, flat, flat)
    small = (P(), P(), P(), P())
    return jax.shard_map(
        functools.partial(on_device, dp // 2),
        mesh=split,
        in_specs=(rows, P(None, both), rows, *weights, *small),
        out_specs=(rows, rows, *weights, *small),
        check_vma=False,
    )
```
